32 devices in a mesh: grp: 2 (over core), dp: 16 (over z, y, x).
Axes of the slice: x: 2, y: 2, z: 4, core: 2. Of those that a mesh axis runs over, the one named last changes fastest.
Arguments:
- hidden: bfloat16 [32768, 768], P(('grp', 'dp')), may hold values from -6 to 6
- grad_out: bfloat16 [32768, 768], P(('grp', 'dp')), may hold values from -6 to 6
- seq_lens: int32 [64], P(('grp', 'dp')), may hold values from 128 to 512, as said below
- mix_state: float32 [4, 5, 768, 384], P(None, None, ('grp', 'dp')), as said below
- out_state: float32 [4, 768, 768], P(None, ('grp', 'dp')), as said below
- depth_state: float32 [4, 9, 768], replicated, as said below
- span_state: float32 [4, 384, 54], replicated, as said below
- norm_state: float32 [4, 4, 768], replicated, as said below
- up_state: float32 [4, 2, 384, 1536], P(None, 'grp', None, 'dp'), as said below
- bias_state: float32 [4, 2, 1536], P(None, 'grp', 'dp'), as said below
- down_state: float32 [4, 2, 1536, 384], P(None, 'grp', 'dp'), as said below
Outputs:
- out: bfloat16 [32768, 768], P(('grp', 'dp'))
- input_grad: bfloat16 [32768, 768], P(('grp', 'dp'))
- mix_new: float32 [2, 5, 768, 384], P(None, None, ('grp', 'dp'))
- mix_moments: float32 [2, 5, 768, 384], P(None, None, ('grp', 'dp'))
- out_new: float32 [2, 768, 768], P(None, ('grp', 'dp'))
- out_moments: float32 [2, 768, 768], P(None, ('grp', 'dp'))
- depth_new: float32 [2, 9, 768], replicated
- depth_moments: float32 [2, 9, 768], replicated
- span_new: float32 [2, 384, 54], replicated
- span_moments: float32 [2, 384, 54], replicated
- norm_new: float32 [2, 4, 768], replicated
- norm_moments: float32 [2, 4, 768], replicated
- up_new: float32 [2, 2, 384, 1536], P(None, 'grp', None, 'dp')
- up_moments: float32 [2, 2, 384, 1536], P(None, 'grp', None, 'dp')
- bias_new: float32 [2, 2, 1536], P(None, 'grp', 'dp')
- bias_moments: float32 [2, 2, 1536], P(None, 'grp', 'dp')
- down_new: float32 [2, 2, 1536, 384], P(None, 'grp', 'dp')
- down_moments: float32 [2, 2, 1536, 384], P(None, 'grp', 'dp')
The draws below stay inside these ranges and needn't reach their ends.
Inputs may be any that keep to these rules, and one draw needn't show every extreme that they name: The first seq_lens positions of a sequence are live keys, the rest padding; the first sequence is full. `mix_state`: slot 2 is positive. `out_state`: slot 2 is positive. `depth_state`: slot 2 is positive. `span_state`: slot 2 is positive. `norm_state`: slot 2 is positive. `up_state`: slot 2 is positive. `bias_state`: slot 2 is positive. `down_state`: slot 2 is positive.
All inputs are finite; a program needn't handle non-finite values.
Results may differ from the reference program's by a relative error of at most 0.029.
Values may be sent and summed in bfloat16 or wider, within the bound.
No kernel may reach another device: no remote copies, remote signals or barrier semaphores. Data moves between devices by JAX's collectives and lax.ppermute only.
A program may use at most 192 MiB of HBM per device.

```python
import math
import jax
import jax.numpy as jnp
from jax import lax

D = 768
HEADS = 6
HS = 64
HID = 1536
GROUPS = 2
KERNEL = 9
SEQ_LEN = 512
STEP = 7
SEQ_DEV = 2
SEQS = 64
TOKENS = 32768


def draw_seq_lens(key, part):
    lengths_drawn = jax.random.randint(key, (SEQS,), SEQ_LEN // 4, SEQ_LEN + 1)
    return lengths_drawn.at[0].set(SEQ_LEN).astype(jnp.int32)


def state_stack(key, weight, scale_w, grad_scale):
    keys_all = jax.random.split(key, 3)
    moment_one = grad_scale / 9.0 * jax.random.uniform(keys_all[0], weight.shape, minval=-1.5, maxval=1.5)
    factors = jnp.exp(jax.random.uniform(keys_all[1], weight.shape, minval=0.0, maxval=math.log(4.0)))
    moment_two = grad_scale * grad_scale * (0.001 / 0.999) * factors
    average = weight + 0.3 * scale_w * jax.random.normal(keys_all[2], weight.shape)
    return jnp.stack([weight, moment_one, moment_two, average]).astype(jnp.float32)


def drawn_state(key, shape, scale_w, grad_factor):
    keys_all = jax.random.split(key, 2)
    weight = scale_w * jax.random.truncated_normal(keys_all[0], -3.0, 3.0, shape)
    return state_stack(keys_all[1], weight, scale_w, grad_factor * math.sqrt(TOKENS))


def draw_mix_state(key, part):
    keys_all = jax.random.split(key, 2)
    scale_w = D ** (-0.5)
    weight = scale_w * jax.random.truncated_normal(keys_all[0], -3.0, 3.0, (5, D, D // 2))
    grad_scale = jnp.array([0.2, 0.1, 0.1, 0.3, 0.6], jnp.float32).reshape(5, 1, 1) * math.sqrt(TOKENS)
    return state_stack(keys_all[1], weight, scale_w, grad_scale)


def draw_out_state(key, part):
    return drawn_state(key, (D, D), (D // 4) ** (-0.5), 0.25)


def draw_depth_state(key, part):
    return drawn_state(key, (KERNEL, D), KERNEL ** (-0.5), 0.3)


def draw_span_state(key, part):
    return drawn_state(key, (D // 2, HEADS * KERNEL), (D // 2) ** (-0.5), 0.3)


def draw_norm_state(key, part):
    keys_all = jax.random.split(key, 3)
    gains = 1.0 + 0.1 * jax.random.uniform(keys_all[0], (2, D), minval=-1.0, maxval=1.0)
    shifts = 0.2 * jax.random.normal(keys_all[1], (2, D))
    weight = jnp.stack([gains[0], shifts[0], gains[1], shifts[1]])
    return state_stack(keys_all[2], weight, 0.2, math.sqrt(TOKENS))


def draw_up_state(key, part):
    return drawn_state(key, (GROUPS, D // 2, HID), (D // 2) ** (-0.5), 0.3)


def draw_bias_state(key, part):
    return drawn_state(key, (GROUPS, HID), 0.3, 0.3)


def draw_down_state(key, part):
    return drawn_state(key, (GROUPS, HID, D // 2), HID ** (-0.5), 0.6)


def block_levels(stream_key, extent, cuts, low, high):
    def one(dim, blocks):
        heights = jax.random.uniform(jax.random.fold_in(jax.random.fold_in(stream_key, 6), dim), (blocks,), jnp.float32, low / len(cuts), high / len(cuts))
        return jnp.repeat(jnp.exp(heights), extent[dim] // blocks).reshape((-1,) + (1,) * (len(extent) - dim - 1))

    level = one(*cuts[0])
    for cut in cuts[1:]:
        level = level * one(*cut)
    return level


def bell_draw(own_key, extent, deviation, most, cuts=(), kind=jnp.bfloat16):
    loudness = block_levels(own_key, extent, cuts, -0.22, 0.18) if cuts else 1.0
    values = jax.random.normal(own_key, extent, jnp.float32) * deviation * loudness
    return jnp.minimum(jnp.maximum(values, -most), most).astype(kind)


def setup_inputs(seed: int = 0) -> dict:
    key_list = jax.random.split(jax.random.key(seed), 12)
    return {
        "hidden": bell_draw(key_list[0], (TOKENS, D), 1.0, 6.0, ((0, 32),)),
        "grad_out": bell_draw(key_list[1], (TOKENS, D), 1.0, 6.0, ((0, 32),)),
        "seq_lens": draw_seq_lens(jax.random.fold_in(key_list[11], 71), 0),
        "mix_state": draw_mix_state(jax.random.fold_in(key_list[11], 71), 0),
        "out_state": draw_out_state(jax.random.fold_in(key_list[11], 71), 0),
        "depth_state": draw_depth_state(jax.random.fold_in(key_list[11], 71), 0),
        "span_state": draw_span_state(jax.random.fold_in(key_list[11], 71), 0),
        "norm_state": draw_norm_state(jax.random.fold_in(key_list[11], 71), 0),
        "up_state": draw_up_state(jax.random.fold_in(key_list[11], 71), 0),
        "bias_state": draw_bias_state(jax.random.fold_in(key_list[11], 71), 0),
        "down_state": draw_down_state(jax.random.fold_in(key_list[11], 71), 0),
    }


@jax.custom_vjp
def low(v):
    return lax.optimization_barrier(v.astype(jnp.bfloat16)).astype(jnp.float32)

@jax.custom_vjp
def low_back(v):
    return v

def low_keep(v):
    return (low(v), None)

def low_pass(kept, grad):
    return (grad,)

def back_keep(v):
    return (v, None)

def back_low(kept, grad):
    return (low(grad),)
low.defvjp(low_keep, low_pass)
low_back.defvjp(back_keep, back_low)
HIGHEST = lax.Precision.HIGHEST
beta_one = 0.9
beta_two = 0.999
adam_eps = 1e-06
ema_rate = 0.99
decay_rate = 0.01
rate_mix = 0.06
rate_out = 0.12
rate_depth = 0.4
rate_span = 0.08
rate_norm = 0.5
rate_up = 0.08
rate_bias = 0.3
rate_down = 0.04

def both_ways(value):
    return low_back(low(value))

def product(left, right):
    return jnp.dot(left, right, precision=HIGHEST)

def softmax_rows(scores):
    top_score = lax.optimization_barrier(jnp.max(scores, axis=-1, keepdims=True))
    powers = jnp.exp(scores - top_score)
    return powers / lax.optimization_barrier(jnp.sum(powers, axis=-1, keepdims=True))

def gelu_exact(value):
    return 0.5 * value * (1.0 + lax.erf(value * 2.0 ** (-0.5)))

def layer_norm(value, scale_row, shift_row):
    centered = value - lax.optimization_barrier(jnp.mean(value, axis=-1, keepdims=True))
    variance = lax.optimization_barrier(jnp.mean(centered * centered, axis=-1, keepdims=True))
    return centered * lax.rsqrt(variance + 1e-12) * scale_row + shift_row

def attend(queries, key_rows, value_rows, seq_len):
    scores = jnp.einsum('qhd,khd->hqk', queries, key_rows, precision=HIGHEST) * HS ** (-0.5)
    places = lax.broadcasted_iota(jnp.int32, scores.shape, 2)
    scores = low_back(jnp.where(places < seq_len, scores, -1000000000.0))
    weights = both_ways(softmax_rows(scores))
    return jnp.einsum('hqk,khd->qhd', weights, value_rows, precision=HIGHEST)

def mixer(inputs, seq_lens, mix, w_out, depth, span, norms):
    count, length, width = inputs.shape
    half = width // 2
    reach = KERNEL // 2
    flat = inputs.reshape(count * length, width)
    queries = both_ways(product(flat, mix[0]))
    key_rows = both_ways(product(flat, mix[1]))
    value_rows = both_ways(product(flat, mix[2]))
    padded = jnp.pad(inputs, ((0, 0), (reach, reach), (0, 0)))
    spread = depth[0] * padded[:, 0:length]
    for offset in range(1, KERNEL):
        spread = spread + depth[offset] * padded[:, offset:offset + length]
    conv_in = both_ways(spread.reshape(count * length, width))
    conv_keys = both_ways(product(conv_in, mix[3]))
    joined = both_ways(conv_keys * queries)
    logits = both_ways(product(joined, span)).reshape(count, length, HEADS, KERNEL)
    kernel_w = softmax_rows(logits)
    conv_vals = both_ways(product(flat, mix[4])).reshape(count, length, HEADS, HS)
    conv_pad = jnp.pad(conv_vals, ((0, 0), (reach, reach), (0, 0), (0, 0)))
    convolved = kernel_w[..., 0:1] * conv_pad[:, 0:length]
    for offset in range(1, KERNEL):
        convolved = convolved + kernel_w[..., offset:offset + 1] * conv_pad[:, offset:offset + length]
    shaped = (count, length, HEADS, HS)
    context = jax.vmap(jax.checkpoint(attend))(queries.reshape(shaped), key_rows.reshape(shaped), value_rows.reshape(shaped), seq_lens)
    mixed = both_ways(jnp.concatenate([context.reshape(count * length, half), convolved.reshape(count * length, half)], axis=1))
    branch = both_ways(product(mixed, w_out))
    return layer_norm(branch + flat, norms[0], norms[1])

def feed_forward(normed, w_up, b_up, w_down):
    sent = both_ways(normed)
    part_width = normed.shape[1] // GROUPS
    outputs = []
    for group in range(GROUPS):
        part = sent[:, group * part_width:(group + 1) * part_width]
        pre_act = low_back(product(part, w_up[group]) + b_up[group])
        act_low = low(gelu_exact(pre_act))
        outputs.append(product(act_low, w_down[group]))
    return both_ways(jnp.concatenate(outputs, axis=1))

def forward(inputs, seq_lens, mix, w_out, depth, span, norms, w_up, b_up, w_down):
    blocks = inputs.reshape(-1, SEQ_DEV, SEQ_LEN, D)
    len_blocks = seq_lens.reshape(-1, SEQ_DEV)

    def one_block(pair):
        block_in, block_lens = pair
        normed = mixer(block_in, block_lens, mix, w_out, depth, span, norms).reshape(-1, D)
        return layer_norm(normed + feed_forward(normed, w_up, b_up, w_down), norms[2], norms[3])
    return lax.map(jax.checkpoint(one_block), (blocks, len_blocks)).reshape(-1, D)

def adamw(opt_state, gradient, step_rate, wd_rate):
    moment_one = beta_one * opt_state[1] + (1.0 - beta_one) * gradient
    moment_two = beta_two * opt_state[2] + (1.0 - beta_two) * gradient * gradient
    scaled_one = moment_one / (1.0 - beta_one ** STEP)
    scaled_two = moment_two / (1.0 - beta_two ** STEP)
    weight = opt_state[0] - step_rate * (scaled_one / (jnp.sqrt(scaled_two) + adam_eps) + wd_rate * opt_state[0])
    average = ema_rate * opt_state[3] + (1.0 - ema_rate) * weight
    return (jnp.stack([weight, average]), jnp.stack([moment_one, moment_two]))

def reference(hidden, grad_out, seq_lens, mix_state, out_state, depth_state, span_state, norm_state, up_state, bias_state, down_state):

    def whole_pass(inputs, mix, w_out, depth, span, norms, w_up, b_up, w_down):
        return forward(inputs, seq_lens, low(mix), low(w_out), low(depth), low(span), norms, low(w_up), low(b_up), low(w_down))
    result, pullback = jax.vjp(whole_pass, hidden.astype(jnp.float32), mix_state[0], out_state[0], depth_state[0], span_state[0], norm_state[0], up_state[0], bias_state[0], down_state[0])
    gradients = pullback(grad_out.astype(jnp.float32))
    mix_update = adamw(mix_state, gradients[1], rate_mix, decay_rate)
    out_update = adamw(out_state, gradients[2], rate_out, decay_rate)
    depth_update = adamw(depth_state, gradients[3], rate_depth, decay_rate)
    span_update = adamw(span_state, gradients[4], rate_span, decay_rate)
    norm_update = adamw(norm_state, gradients[5], rate_norm, 0.0)
    up_update = adamw(up_state, gradients[6], rate_up, decay_rate)
    bias_update = adamw(bias_state, gradients[7], rate_bias, 0.0)
    down_update = adamw(down_state, gradients[8], rate_down, decay_rate)
    return (result.astype(jnp.bfloat16), gradients[0].astype(jnp.bfloat16), mix_update[0], mix_update[1], out_update[0], out_update[1], depth_update[0], depth_update[1], span_update[0], span_update[1], norm_update[0], norm_update[1], up_update[0], up_update[1], bias_update[0], bias_update[1], down_update[0], down_update[1])
```

```python
import functools

import jax
import jax.numpy as jnp
from jax import lax
from jax.experimental import pallas as pl
from jax.experimental.pallas import tpu as pltpu
from jax.sharding import PartitionSpec as P

HEADS = 6
HS = 64
KERNEL = 9
STEP = 7
REACH = KERNEL // 2
TAP = 8
LANES = 128
PAD = 8
EDGE = REACH * PAD

beta_one = 0.9
beta_two = 0.999
adam_eps = 1e-06
ema_rate = 0.99
decay_rate = 0.01
rate_mix = 0.06
rate_out = 0.12
rate_depth = 0.4
rate_span = 0.08
rate_norm = 0.5
rate_up = 0.08
rate_bias = 0.3
rate_down = 0.04

low = jnp.bfloat16
full = jnp.float32
NN = (((1,), (0,)), ((), ()))
NT = (((1,), (1,)), ((), ()))
TN = (((0,), (0,)), ((), ()))


def dot(left, right, dims=NN):
    return lax.dot_general(left, right, dims, preferred_element_type=full)


def row_loop(rows, chunk, body):
    def step(i, carry):
        body(pl.multiple_of(i * chunk, chunk))
        return carry

    lax.fori_loop(0, rows // chunk, step, 0)


def spread_matrix(width):
    row = lax.broadcasted_iota(jnp.int32, (LANES, KERNEL * width), 0)
    col = lax.broadcasted_iota(jnp.int32, (LANES, KERNEL * width), 1)
    tap = col // width
    head = (col - tap * width) // HS
    return (row == tap * TAP + head).astype(full).astype(low)


def multiple(r):
    return pl.multiple_of(r, PAD)


def fill_padded(ref, value):
    rows = value.shape[0]
    value = value.astype(full)
    place = lax.broadcasted_iota(jnp.int32, (PAD, 1), 0)
    ref[EDGE : EDGE + rows, :] = value
    for i in range(REACH):
        before = value[rows - EDGE + i * PAD : rows - EDGE + (i + 1) * PAD]
        ref[i * PAD : (i + 1) * PAD, :] = jnp.where(place == 0, 0.0, pltpu.roll(before, 1, 0))
        after = value[i * PAD : (i + 1) * PAD]
        ref[EDGE + rows + i * PAD : EDGE + rows + (i + 1) * PAD, :] = jnp.where(
            place == PAD - 1, 0.0, pltpu.roll(after, PAD - 1, 0))


def order_matrix(rows):
    row = lax.broadcasted_iota(jnp.int32, (rows, rows), 0)
    col = lax.broadcasted_iota(jnp.int32, (rows, rows), 1)
    return ((row % PAD) * (rows // PAD) + row // PAD == col).astype(full).astype(low)


def order_kernel(x_ref, g_ref, depth_ref, xo_ref, go_ref, e_ref, xpad):
    rows, width = x_ref.shape
    order = order_matrix(rows)
    x = dot(order, x_ref[...])
    xo_ref[...] = x.astype(low)
    go_ref[...] = dot(order, g_ref[...]).astype(low)
    fill_padded(xpad, x)

    def depth_rows(r):
        acc = depth_ref[0:1, :] * xpad[pl.ds(r, 32), :]
        for j in range(1, KERNEL):
            acc = acc + depth_ref[j : j + 1, :] * xpad[pl.ds(multiple(r + PAD * j), 32), :]
        e_ref[pl.ds(r, 32), :] = acc.astype(low)

    row_loop(rows, 32, depth_rows)


def front_kernel(x_ref, e_ref, wa_ref, wb_ref, span_ref, spread_ref,
                 qkvw_ref, u_ref, p_ref, conv_ref,
                 wpad, taps):
    rows, width = x_ref.shape
    half = width // 2
    x = x_ref[...]
    for c in range(4):
        qkvw_ref[:, c * half : (c + 1) * half] = dot(x, wa_ref[:, c * half : (c + 1) * half]).astype(low)
    u = dot(e_ref[...], wb_ref[...]).astype(low)
    u_ref[...] = u
    r = (u.astype(full) * qkvw_ref[:, 0:half].astype(full)).astype(low)
    logits = dot(r, span_ref[...]).astype(low).astype(full)
    lt = logits.T[0 : KERNEL * TAP].reshape(KERNEL, TAP, rows)
    top = jnp.max(lt, axis=0, keepdims=True)
    ex = jnp.exp(lt - top)
    pt = (ex / jnp.sum(ex, axis=0, keepdims=True)).reshape(KERNEL * TAP, rows)
    p = jnp.concatenate([pt, jnp.zeros((LANES - KERNEL * TAP, rows), full)], axis=0).T
    p_ref[...] = p
    fill_padded(wpad, qkvw_ref[:, 3 * half : 4 * half])
    p_low = p.astype(low)
    for j in range(KERNEL):
        taps[:, j * half : (j + 1) * half] = dot(p_low, spread_ref[:, j * half : (j + 1) * half])

    def conv_rows(r):
        acc = taps[pl.ds(r, 32), 0:half] * wpad[pl.ds(r, 32), :]
        for j in range(1, KERNEL):
            acc = acc + taps[pl.ds(r, 32), j * half : (j + 1) * half] * wpad[pl.ds(multiple(r + PAD * j), 32), :]
        conv_ref[pl.ds(r, 32), :] = acc.astype(low)

    row_loop(rows, 32, conv_rows)


def attend_kernel(lens_ref, qkvw_ref, a_ref, ctx_ref):
    rows = qkvw_ref.shape[0]
    half = HEADS * HS
    seq_len = lens_ref[pl.program_id(0)]
    lane = lax.broadcasted_iota(jnp.int32, (1, LANES), 1)
    row = lax.broadcasted_iota(jnp.int32, (1, rows), 1)
    live = (row % PAD) * (rows // PAD) + row // PAD < seq_len
    for pair in range(HEADS // 2):
        at = pair * LANES
        q = qkvw_ref[:, at : at + LANES]
        k = qkvw_ref[:, half + at : half + at + LANES]
        v = qkvw_ref[:, 2 * half + at : 2 * half + at + LANES]
        outs = []
        for side in range(2):
            pick = jnp.where((lane // HS) == side, HS ** (-0.5), 0.0).astype(low)
            scores = dot(q * pick, k, NT)
            scores = jnp.where(live, scores, -1000000000.0)
            top = jnp.max(scores, axis=1, keepdims=True)
            ex = jnp.exp(scores - top)
            a = (ex * (1.0 / jnp.sum(ex, axis=1, keepdims=True))).astype(low)
            a_ref[0, 2 * pair + side] = a
            outs.append(dot(a, v))
        ctx_ref[:, at : at + LANES] = jnp.where((lane // HS) == 0, outs[0], outs[1]).astype(low)


def join_kernel(x_ref, ctx_ref, conv_ref, wb_ref, zh_ref, rstd_ref):
    half = ctx_ref.shape[1]
    branch = dot(ctx_ref[...], wb_ref[0:half, :]) + dot(conv_ref[...], wb_ref[half:, :])
    z = branch.astype(low).astype(full) + x_ref[...].astype(full)
    centered = z - jnp.mean(z, axis=1, keepdims=True)
    variance = jnp.mean(centered * centered, axis=1, keepdims=True)
    rstd = lax.rsqrt(variance + 1e-12)
    zh_ref[...] = centered * rstd
    rstd_ref[...] = jnp.broadcast_to(rstd, rstd_ref.shape)


def feed_kernel(zh_ref, rstd_ref, g_ref, norm_ref, up_ref, bias_ref, down_ref,
                out_ref, gy_ref, gb_ref, dup_ref, ddown_ref, dnorm_ref, dbias_ref,
                act_s, slope_s, gpre_s, dup_s, ddown_s):
    step, last = pl.program_id(0), pl.num_programs(0) - 1
    tile, width = zh_ref.shape
    half = width // 2
    hid = bias_ref.shape[1]
    chunk = 512

    @pl.when(step == 0)
    def _():
        dup_s[...] = jnp.zeros_like(dup_s)
        ddown_s[...] = jnp.zeros_like(ddown_s)
        dnorm_ref[...] = jnp.zeros_like(dnorm_ref)
        dbias_ref[...] = jnp.zeros_like(dbias_ref)

    zh1 = zh_ref[...]
    g1, c1, g2, c2 = (norm_ref[i : i + 1, :] for i in range(4))
    h1 = zh1 * g1 + c1
    f = h1.astype(low)
    outs = []
    for g in range(2):
        fg = f[:, g * half : (g + 1) * half]
        for c in range(0, hid, chunk):
            at = g * hid + c
            pre = dot(fg, up_ref[at : at + chunk, :], NT) + bias_ref[g : g + 1, c : c + chunk]
            cdf = 0.5 * (1.0 + lax.erf(pre * 2.0 ** (-0.5)))
            act_s[:, at : at + chunk] = (pre * cdf).astype(low)
            slope_s[:, at : at + chunk] = cdf + pre * (jnp.exp(-0.5 * pre * pre) * 0.3989422804014327)
        outs.append(dot(act_s[:, g * hid : (g + 1) * hid], down_ref[g * hid : (g + 1) * hid, :]).astype(low).astype(full))
    s = h1 + jnp.concatenate(outs, axis=1)
    centered = s - jnp.mean(s, axis=1, keepdims=True)
    variance = jnp.mean(centered * centered, axis=1, keepdims=True)
    rstd2 = lax.rsqrt(variance + 1e-12)
    zh2 = centered * rstd2
    out_ref[...] = (zh2 * g2 + c2).astype(low)
    grad = g_ref[...].astype(full)
    dnorm_ref[2:3, :] += jnp.sum(grad * zh2, axis=0, keepdims=True)
    dnorm_ref[3:4, :] += jnp.sum(grad, axis=0, keepdims=True)
    dz = grad * g2
    gz = (dz - jnp.mean(dz, axis=1, keepdims=True) - zh2 * jnp.mean(dz * zh2, axis=1, keepdims=True)) * rstd2
    go = gz.astype(low)
    backs = []
    for g in range(2):
        gog = go[:, g * half : (g + 1) * half]
        fg = f[:, g * half : (g + 1) * half]
        for c in range(0, hid, chunk):
            at = g * hid + c
            d_act = dot(gog, down_ref[at : at + chunk, :], NT)
            gpre = (d_act * slope_s[:, at : at + chunk]).astype(low)
            gpre_s[:, at : at + chunk] = gpre
            dbias_ref[g : g + 1, c : c + chunk] += jnp.sum(gpre.astype(full), axis=0, keepdims=True)
            ddown_s[at : at + chunk, :] += dot(act_s[:, at : at + chunk], gog, TN)
            dup_s[at : at + chunk, :] += dot(gpre, fg, TN)
        backs.append(dot(gpre_s[:, g * hid : (g + 1) * hid], up_ref[g * hid : (g + 1) * hid, :]).astype(low).astype(full))
    gh1 = gz + jnp.concatenate(backs, axis=1)
    dnorm_ref[0:1, :] += jnp.sum(gh1 * zh1, axis=0, keepdims=True)
    dnorm_ref[1:2, :] += jnp.sum(gh1, axis=0, keepdims=True)
    dz1 = gh1 * g1
    gy = (dz1 - jnp.mean(dz1, axis=1, keepdims=True) - zh1 * jnp.mean(dz1 * zh1, axis=1, keepdims=True)) * rstd_ref[:, 0:1]
    gy_ref[...] = gy
    gb_ref[...] = gy.astype(low)

    @pl.when(step == last)
    def _():
        dup_ref[...] = dup_s[...].astype(low)
        ddown_ref[...] = ddown_s[...].astype(low)


def split_kernel(gb_ref, ctx_ref, conv_ref, wb_ref, res_ref, gm_ref, dout_ref, result_ref, acc):
    step, last = pl.program_id(0), pl.num_programs(0) - 1
    half = ctx_ref.shape[1]

    @pl.when(step == 0)
    def _():
        acc[...] = jnp.zeros_like(acc)

    result_ref[...] = dot(order_matrix(gb_ref.shape[0]), res_ref[...], TN).astype(low)
    gb = gb_ref[...]
    gm_ref[...] = dot(gb, wb_ref[...], NT).astype(low)
    acc[0:half, :] += dot(ctx_ref[...], gb, TN)
    acc[half:, :] += dot(conv_ref[...], gb, TN)

    @pl.when(step == last)
    def _():
        dout_ref[...] = acc[...].astype(low)


def attend_back_kernel(qkvw_ref, a_ref, gctx_ref, gq_ref, gk_ref, gv_ref):
    half = HEADS * HS
    lane = lax.broadcasted_iota(jnp.int32, (1, LANES), 1)
    for pair in range(HEADS // 2):
        at = pair * LANES
        q = qkvw_ref[:, at : at + LANES]
        k = qkvw_ref[:, half + at : half + at + LANES]
        v = qkvw_ref[:, 2 * half + at : 2 * half + at + LANES]
        gctx = gctx_ref[:, at : at + LANES]
        gqs, gks, gvs = [], [], []
        for side in range(2):
            pick = jnp.where((lane // HS) == side, 1.0, 0.0).astype(low)
            a_low = a_ref[0, 2 * pair + side]
            a = a_low.astype(full)
            ga = dot(gctx * pick, v, NT)
            gs = (a * (ga - jnp.sum(a * ga, axis=1, keepdims=True))).astype(low)
            gqs.append(dot(gs, k))
            gks.append(dot(gs, q, TN))
            gvs.append(dot(a_low, gctx, TN))
        first = (lane // HS) == 0
        gq_ref[:, at : at + LANES] = jnp.where(first, gqs[0], gqs[1]) * HS ** (-0.5)
        gk_ref[:, at : at + LANES] = (jnp.where(first, gks[0], gks[1]) * HS ** (-0.5)).astype(low)
        gv_ref[:, at : at + LANES] = jnp.where(first, gvs[0], gvs[1]).astype(low)


def conv_back_kernel(gm_ref, qkvw_ref, u_ref, p_ref, gqa_ref, wb_ref, spant_ref, spread_ref,
                     gq_ref, gw_ref, gu_ref, ge_ref, dspan_ref,
                     wpad, gpad, taps, prods):
    rows = u_ref.shape[0]
    half = u_ref.shape[1]

    @pl.when(pl.program_id(0) == 0)
    def _():
        dspan_ref[...] = jnp.zeros_like(dspan_ref)

    fill_padded(wpad, qkvw_ref[:, 3 * half : 4 * half])
    fill_padded(gpad, gm_ref[...])
    p = p_ref[...]
    p_low = p.astype(low)
    for j in range(KERNEL):
        cols = slice(j * half, (j + 1) * half)
        fill_padded(taps.at[:, cols], dot(p_low, spread_ref[:, cols]))

    def conv_rows(r):
        here = gpad[pl.ds(multiple(r + EDGE), 32), :]
        acc = None
        for j in range(KERNEL):
            cols = slice(j * half, (j + 1) * half)
            prods[pl.ds(r, 32), cols] = (here * wpad[pl.ds(multiple(r + PAD * j), 32), :]).astype(low)
            back = pl.ds(multiple(r + PAD * (2 * REACH - j)), 32)
            term = taps[back, cols] * gpad[back, :]
            acc = term if acc is None else acc + term
        gw_ref[pl.ds(r, 32), :] = acc.astype(low)

    row_loop(rows, 32, conv_rows)
    gp = dot(prods[...], spread_ref[...], NT)
    gpt = gp.T[0 : KERNEL * TAP].reshape(KERNEL, TAP, rows)
    pt = p.T[0 : KERNEL * TAP].reshape(KERNEL, TAP, rows)
    glt = pt * (gpt - jnp.sum(pt * gpt, axis=0, keepdims=True))
    glt = jnp.concatenate([glt.reshape(KERNEL * TAP, rows), jnp.zeros((LANES - KERNEL * TAP, rows), full)], axis=0)
    gl = glt.T.astype(low)
    q = qkvw_ref[:, 0:half].astype(full)
    u = u_ref[...].astype(full)
    r = (u * q).astype(low)
    dspan_ref[...] += dot(glt.astype(low), r)
    gr = dot(gl, spant_ref[...]).astype(low).astype(full)
    gq_ref[...] = (gqa_ref[...] + gr * u).astype(low)
    gu = (gr * q).astype(low)
    gu_ref[...] = gu
    ge_ref[...] = dot(gu, wb_ref[...], NT).astype(low)


def front_back_kernel(x_ref, e_ref, gy_ref, gq_ref, gk_ref, gv_ref, gw_ref, gu_ref, ge_ref, wa_ref, depth_ref,
                      gx_ref, dwa_ref, dwb_ref, ddepth_ref,
                      gepad, xpad, gx_s, acc_a, acc_b):
    step, last = pl.program_id(0), pl.num_programs(0) - 1
    rows, width = x_ref.shape
    half = width // 2

    @pl.when(step == 0)
    def _():
        acc_a[...] = jnp.zeros_like(acc_a)
        acc_b[...] = jnp.zeros_like(acc_b)
        ddepth_ref[...] = jnp.zeros_like(ddepth_ref)

    x = x_ref[...]
    total = gy_ref[...]
    for c, ref in enumerate((gq_ref, gk_ref, gv_ref, gw_ref)):
        g = ref[...]
        acc_a[:, c * half : (c + 1) * half] += dot(x, g, TN)
        total = total + dot(g, wa_ref[:, c * half : (c + 1) * half], NT)
    acc_b[...] += dot(e_ref[...], gu_ref[...], TN)
    fill_padded(xpad, total)
    fill_padded(gepad, ge_ref[...])

    def shift_rows(r):
        acc = xpad[pl.ds(multiple(r + EDGE), 32), :]
        for j in range(KERNEL):
            acc = acc + depth_ref[j : j + 1, :] * gepad[pl.ds(multiple(r + PAD * (2 * REACH - j)), 32), :]
        gx_s[pl.ds(r, 32), :] = acc.astype(low)

    row_loop(rows, 32, shift_rows)
    gx_ref[...] = dot(order_matrix(rows), gx_s[...], TN).astype(low)
    fill_padded(xpad, x)
    for c in range(0, width, LANES):
        cols = slice(c, c + LANES)

        def depth_sum(i, sums):
            r = pl.multiple_of(i * 64, 64)
            ge = gepad[pl.ds(multiple(r + EDGE), 64), cols]
            new = []
            for j in range(KERNEL):
                prod = ge * xpad[pl.ds(multiple(r + PAD * j), 64), cols]
                new.append(sums[j] + jnp.sum(prod.reshape(8, 8, LANES), axis=0))
            return tuple(new)

        sums = lax.fori_loop(0, rows // 64, depth_sum, tuple(jnp.zeros((8, LANES), full) for _ in range(KERNEL)))
        for j in range(KERNEL):
            ddepth_ref[j : j + 1, cols] += jnp.sum(sums[j], axis=0, keepdims=True)

    @pl.when(step == last)
    def _():
        dwa_ref[...] = acc_a[...].astype(low)
        dwb_ref[...] = acc_b[...].astype(low)


def struct(shape, dtype):
    return jax.ShapeDtypeStruct(shape, dtype)


def rows_spec(rows, width, at=0):
    return pl.BlockSpec((rows, width), lambda i, *_: (i, at))


def whole(shape, index=None):
    index = index or (0,) * len(shape)
    return pl.BlockSpec(shape, lambda i, *_: index)


def call(kernel, grid, in_specs, out_specs, out_shape, scratch, flops, moved, limit, prefetch=0):
    return pl.pallas_call(
        kernel,
        grid_spec=pltpu.PrefetchScalarGridSpec(
            num_scalar_prefetch=prefetch, grid=grid, in_specs=in_specs, out_specs=out_specs, scratch_shapes=scratch),
        out_shape=out_shape,
        compiler_params=pltpu.CompilerParams(dimension_semantics=("arbitrary",), vmem_limit_bytes=limit << 20),
        cost_estimate=pl.CostEstimate(flops=int(flops), transcendentals=0, bytes_accessed=int(moved)),
    )


def on_tokens(hidden, grad_out, seq_lens, depth_w, span_w, norm_w, get_a, get_b, get_feed, send_feed, send_out):
    tokens, width = hidden.shape
    count = seq_lens.shape[0]
    length = tokens // count
    half = width // 2
    V = pltpu.VMEM
    padded = length + 2 * EDGE
    depth16 = jnp.pad(depth_w, ((0, 16 - KERNEL), (0, 0)))
    by_tap = jnp.swapaxes(span_w.reshape(half, HEADS, KERNEL), 1, 2)
    by_tap = jnp.pad(by_tap, ((0, 0), (0, 0), (0, TAP - HEADS))).reshape(half, KERNEL * TAP)
    span_cols = jnp.pad(by_tap, ((0, 0), (0, LANES - KERNEL * TAP))).astype(low)
    span_rows = span_cols.T
    spread = spread_matrix(half)

    hidden, grad_out, e = call(
        order_kernel, (count,),
        [rows_spec(length, width), rows_spec(length, width), whole((16, width))],
        [rows_spec(length, width)] * 3,
        [struct((tokens, width), low)] * 3,
        [V((padded, width), full)], 2e9, 8e6, 32,
    )(hidden, grad_out, depth16)
    wa = get_a()
    w3, w_out = get_b()
    qkvw, u, p, conv = call(
        front_kernel, (count,),
        [rows_spec(length, width), rows_spec(length, width), whole((width, 4 * half)), whole((width, half)),
         whole((half, LANES)), whole((LANES, KERNEL * half))],
        [rows_spec(length, 4 * half), rows_spec(length, half), rows_spec(length, LANES), rows_spec(length, half)],
        [struct((tokens, 4 * half), low), struct((tokens, half), low), struct((tokens, LANES), full), struct((tokens, half), low)],
        [V((padded, half), full), V((length, KERNEL * half), full)],
        12e9, 12e6, 48,
    )(hidden, e, wa, w3, span_cols, spread)
    a, ctx = call(
        attend_kernel, (count,),
        [rows_spec(length, 4 * half)],
        [pl.BlockSpec((1, HEADS, length, length), lambda i, *_: (i, 0, 0, 0)), rows_spec(length, half)],
        [struct((count, HEADS, length, length), low), struct((tokens, half), low)],
        [], 10e9, 12e6, 48, prefetch=1,
    )(seq_lens, qkvw)
    zh, rstd = call(
        join_kernel, (count,),
        [rows_spec(length, width), rows_spec(length, half), rows_spec(length, half), whole((width, width))],
        [rows_spec(length, width), rows_spec(length, LANES)],
        [struct((tokens, width), full), struct((tokens, LANES), full)],
        [], 3e9, 6e6, 48,
    )(hidden, ctx, conv, w_out)
    up, down, bias = get_feed()
    hid = bias.shape[1]
    tile = 256
    result, gy, gb, d_up, d_down, d_norm, d_bias = call(
        feed_kernel, (tokens // tile,),
        [rows_spec(tile, width), rows_spec(tile, LANES), rows_spec(tile, width), whole((8, width)),
         whole((2 * hid, half)), whole((2, hid)), whole((2 * hid, half))],
        [rows_spec(tile, width), rows_spec(tile, width), rows_spec(tile, width), whole((2 * hid, half)),
         whole((2 * hid, half)), whole((8, width)), whole((2, hid))],
        [struct((tokens, width), low), struct((tokens, width), full), struct((tokens, width), low),
         struct((2 * hid, half), low), struct((2 * hid, half), low), struct((8, width), full), struct((2, hid), full)],
        [V((tile, 2 * hid), low), V((tile, 2 * hid), full), V((tile, 2 * hid), low),
         V((2 * hid, half), full), V((2 * hid, half), full)],
        30e9, 20e6, 60,
    )(zh, rstd, grad_out, norm_w, up, bias, down)
    feed_grads = send_feed(d_up, d_down)
    gm, d_out, result = call(
        split_kernel, (count,),
        [rows_spec(length, width), rows_spec(length, half), rows_spec(length, half), whole((width, width)), rows_spec(length, width)],
        [rows_spec(length, width), whole((width, width)), rows_spec(length, width)],
        [struct((tokens, width), low), struct((width, width), low), struct((tokens, width), low)],
        [V((width, width), full)], 4e9, 6e6, 48,
    )(gb, ctx, conv, w_out, result)
    gqa, gk, gv = call(
        attend_back_kernel, (count,),
        [rows_spec(length, 4 * half), pl.BlockSpec((1, HEADS, length, length), lambda i, *_: (i, 0, 0, 0)), rows_spec(length, half)],
        [rows_spec(length, half)] * 3,
        [struct((tokens, half), full), struct((tokens, half), low), struct((tokens, half), low)],
        [], 15e9, 12e6, 48,
    )(qkvw, a, gm)
    gq, gw, gu, ge, d_span = call(
        conv_back_kernel, (count,),
        [rows_spec(length, half, 1), rows_spec(length, 4 * half), rows_spec(length, half), rows_spec(length, LANES),
         rows_spec(length, half), whole((width, half)), whole((LANES, half)), whole((LANES, KERNEL * half))],
        [rows_spec(length, half), rows_spec(length, half), rows_spec(length, half), rows_spec(length, width), whole((LANES, half))],
        [struct((tokens, half), low), struct((tokens, half), low), struct((tokens, half), low),
         struct((tokens, width), low), struct((LANES, half), full)],
        [V((padded, half), full), V((padded, half), full), V((padded, KERNEL * half), full), V((length, KERNEL * half), low)],
        12e9, 12e6, 48,
    )(gm, qkvw, u, p, gqa, w3, span_rows, spread)
    gx, d_wa, d_w3, d_depth = call(
        front_back_kernel, (count,),
        [rows_spec(length, width), rows_spec(length, width), rows_spec(length, width)]
        + [rows_spec(length, half)] * 5 + [rows_spec(length, width), whole((width, 4 * half)), whole((16, width))],
        [rows_spec(length, width), whole((width, 4 * half)), whole((width, half)), whole((16, width))],
        [struct((tokens, width), low), struct((width, 4 * half), low), struct((width, half), low), struct((16, width), full)],
        [V((padded, width), full), V((padded, width), full), V((length, width), low), V((width, 4 * half), full), V((width, half), full)],
        16e9, 20e6, 56,
    )(hidden, e, gy, gq, gk, gv, gw, gu, ge, wa, depth16)
    return result, gx, d_wa, d_w3, d_out, d_depth, d_span, d_norm, d_bias, feed_grads


def adamw(opt_state, gradient, step_rate, wd_rate):
    moment_one = beta_one * opt_state[1] + (1.0 - beta_one) * gradient
    moment_two = beta_two * opt_state[2] + (1.0 - beta_two) * gradient * gradient
    scaled_one = moment_one / (1.0 - beta_one**STEP)
    scaled_two = moment_two / (1.0 - beta_two**STEP)
    weight = opt_state[0] - step_rate * (
        scaled_one / (jnp.sqrt(scaled_two) + adam_eps) + wd_rate * opt_state[0]
    )
    average = ema_rate * opt_state[3] + (1.0 - ema_rate) * weight
    return (jnp.stack([weight, average]), jnp.stack([moment_one, moment_two]))


class Links:
    def __init__(self, mesh):
        self.size = mesh.shape["dp"]
        self.grp = mesh.shape["grp"]
        deep = 4 if self.size % 4 == 0 else 1
        rest = self.size // deep
        wide = 1 << ((rest.bit_length() - 1) // 2)
        self.sizes = (self.grp, deep, rest // wide, wide)
        self.strides = (0, rest, wide, 1)

    def place(self, dim):
        if dim == 0:
            return lax.axis_index("grp")
        return (lax.axis_index("dp") // self.strides[dim]) % self.sizes[dim]

    def swap(self, value, dim, shift):
        if dim == 0:
            return lax.ppermute(value, "grp", [(i, i ^ shift) for i in range(self.grp)])
        size, stride = self.sizes[dim], self.strides[dim]
        pairs = []
        for i in range(self.size):
            at = (i // stride) % size
            pairs.append((i, i + ((at ^ shift) - at) * stride))
        return lax.ppermute(value, "dp", pairs)

    def gather(self, block, dim):
        size, here = self.sizes[dim], self.place(dim)
        got = [block] + [self.swap(block, dim, k) for k in range(1, size)]
        slots = []
        for j in range(size):
            value = got[size - 1]
            for k in range(size - 1):
                value = jnp.where(here == (j ^ k), got[k], value)
            slots.append(value)
        return jnp.concatenate(slots, axis=dim)

    def scatter(self, block, dim, dtype):
        size, here = self.sizes[dim], self.place(dim)
        got = [lax.dynamic_slice_in_dim(block, here, 1, dim).astype(full)]
        for k in range(1, size):
            piece = lax.dynamic_slice_in_dim(block, here ^ k, 1, dim)
            got.append(self.swap(piece, dim, k).astype(full))
        while len(got) > 1:
            got = [got[i] + got[i + 1] for i in range(0, len(got), 2)]
        return got[0].astype(dtype)

    def total(self, value):
        for dim in (0, 3, 2, 1):
            value = value.astype(low)
            got = [value.astype(full)]
            for k in range(1, self.sizes[dim]):
                got.append(self.swap(value, dim, k).astype(full))
            while len(got) > 1:
                got = [got[i] + got[i + 1] for i in range(0, len(got), 2)]
            value = got[0]
        return value

    def gather_all(self, shard, order):
        block = shard.reshape((1, 1, 1, 1) + shard.shape)
        for dim in order:
            block = self.gather(block, dim)
        return block.reshape((-1,) + shard.shape[1:])

    def scatter_all(self, grads, order):
        block = grads.reshape(self.sizes + (-1,) + grads.shape[1:])
        for dim in order[:-1]:
            block = self.scatter(block, dim, low)
        block = self.scatter(block, order[-1], full)
        return block.reshape((-1,) + grads.shape[1:])


def on_device(links, hidden, grad_out, seq_lens, mix_state, out_state, depth_state, span_state, norm_state,
              up_state, bias_state, down_state):
    width = hidden.shape[1]
    half = width // 2
    hid_dev = up_state.shape[3]
    rows_dev = mix_state.shape[2]
    mix_low = mix_state[0].astype(low)
    shard_a = jnp.concatenate([mix_low[i] for i in (0, 1, 2, 4)], axis=1)
    bias_row = jnp.pad(bias_state[0].astype(low), ((0, rows_dev - 1), (0, LANES - hid_dev)))
    shard_a = jnp.concatenate([shard_a, bias_row], axis=1)
    shard_b = jnp.concatenate([mix_low[3], out_state[0].astype(low)], axis=1)
    all_a = links.gather_all(shard_a, (1, 2, 3, 0))
    all_b = links.gather_all(shard_b, (1, 3, 2, 0))
    up_all = links.gather_all(up_state[0, 0].astype(low).T, (1, 2, 3, 0))
    down_all = links.gather_all(down_state[0, 0].astype(low), (1, 3, 2, 0))
    devices = links.grp * links.size
    bias_all = all_a.reshape(devices, rows_dev, -1)[:, 0, 4 * half : 4 * half + hid_dev].reshape(links.grp, -1).astype(full)

    def send_feed(d_up, d_down):
        return links.scatter_all(d_up, (0, 3, 2, 1)), links.scatter_all(d_down, (0, 2, 3, 1))

    norm_w = jnp.pad(norm_state[0], ((0, 4), (0, 0)))
    depth_w = depth_state[0].astype(low).astype(full)
    span_w = span_state[0].astype(low)
    result, gx, d_wa, d_w3, d_out, d_depth, d_span, d_norm, d_bias, feed_grads = on_tokens(
        hidden, grad_out, seq_lens, depth_w, span_w, norm_w,
        lambda: all_a, lambda: (all_b[:, :half], all_b[:, half:]),
        lambda: (up_all, down_all, bias_all), send_feed, None)

    grad_a = links.scatter_all(d_wa, (0, 3, 2, 1))
    grad_b = links.scatter_all(jnp.concatenate([d_w3, d_out], axis=1), (0, 2, 3, 1))
    small = jnp.concatenate(
        [d_depth[:KERNEL], d_norm[:4], d_bias.reshape(-1, width), d_span[: KERNEL * TAP].reshape(-1, width)], axis=0)
    small = links.total(small)
    depth_grad = small[:KERNEL]
    norm_grad = small[KERNEL : KERNEL + 4]
    at = KERNEL + 4
    bias_rows = d_bias.size // width
    bias_grad = small[at : at + bias_rows].reshape(links.grp, links.size, hid_dev)
    bias_grad = lax.dynamic_slice(bias_grad, (links.place(0), lax.axis_index("dp"), 0), (1, 1, hid_dev)).reshape(1, hid_dev)
    span_grad = small[at + bias_rows :].reshape(KERNEL, TAP, half)[:, :HEADS]
    span_grad = jnp.transpose(span_grad, (2, 1, 0)).reshape(half, HEADS * KERNEL)
    mix_parts = [grad_a[:, i * half : (i + 1) * half] for i in range(3)] + [grad_b[:, :half], grad_a[:, 3 * half :]]
    mix_update = adamw(mix_state, jnp.stack(mix_parts), rate_mix, decay_rate)
    out_update = adamw(out_state, grad_b[:, half:], rate_out, decay_rate)
    depth_update = adamw(depth_state, depth_grad, rate_depth, decay_rate)
    span_update = adamw(span_state, span_grad, rate_span, decay_rate)
    norm_update = adamw(norm_state, norm_grad, rate_norm, 0.0)
    up_update = adamw(up_state, feed_grads[0].T[None], rate_up, decay_rate)
    bias_update = adamw(bias_state, bias_grad, rate_bias, 0.0)
    down_update = adamw(down_state, feed_grads[1][None], rate_down, decay_rate)
    return (result, gx, *mix_update, *out_update, *depth_update, *span_update, *norm_update,
            *up_update, *bias_update, *down_update)


def solution(mesh):
    both = ("grp", "dp")
    mix, out = P(None, None, both, None), P(None, both, None)
    up, bias, down = P(None, "grp", None, "dp"), P(None, "grp", "dp"), P(None, "grp", "dp", None)
    rows = P(both, None)
    return jax.shard_map(
        functools.partial(on_device, Links(mesh)),
        mesh=mesh,
        in_specs=(rows, rows, P(both), mix, out, P(), P(), P(), up, bias, down),
        out_specs=(rows, rows, mix, mix, out, out, P(), P(), P(), P(), P(), P(), up, up, bias, bias, down, down),
        check_vma=False,
    )
```

```python
import functools

import jax
import jax.numpy as jnp
from jax import lax
from jax.experimental import pallas as pl
from jax.experimental.pallas import tpu as pltpu
from jax.sharding import PartitionSpec as P

HEADS = 6
HS = 64
KERNEL = 9
STEP = 7
REACH = KERNEL // 2
TAP = 8
LANES = 128
PAD = 8
EDGE = REACH * PAD

beta_one = 0.9
beta_two = 0.999
adam_eps = 1e-06
ema_rate = 0.99
decay_rate = 0.01
rate_mix = 0.06
rate_out = 0.12
rate_depth = 0.4
rate_span = 0.08
rate_norm = 0.5
rate_up = 0.08
rate_bias = 0.3
rate_down = 0.04

low = jnp.bfloat16
full = jnp.float32
NN = (((1,), (0,)), ((), ()))
NT = (((1,), (1,)), ((), ()))
TN = (((0,), (0,)), ((), ()))


def dot(left, right, dims=NN):
    return lax.dot_general(left, right, dims, preferred_element_type=full)


def row_loop(rows, chunk, body):
    def step(i, carry):
        body(pl.multiple_of(i * chunk, chunk))
        return carry

    lax.fori_loop(0, rows // chunk, step, 0)


def spread_matrix(width):
    row = lax.broadcasted_iota(jnp.int32, (LANES, KERNEL * width), 0)
    col = lax.broadcasted_iota(jnp.int32, (LANES, KERNEL * width), 1)
    tap = col // width
    head = (col - tap * width) // HS
    return (row == tap * TAP + head).astype(full).astype(low)


def multiple(r):
    return pl.multiple_of(r, PAD)


def fill_padded(ref, value):
    rows = value.shape[0]
    value = value.astype(full)
    place = lax.broadcasted_iota(jnp.int32, (PAD, 1), 0)
    ref[EDGE : EDGE + rows, :] = value
    for i in range(REACH):
        before = value[rows - EDGE + i * PAD : rows - EDGE + (i + 1) * PAD]
        ref[i * PAD : (i + 1) * PAD, :] = jnp.where(place == 0, 0.0, pltpu.roll(before, 1, 0))
        after = value[i * PAD : (i + 1) * PAD]
        ref[EDGE + rows + i * PAD : EDGE + rows + (i + 1) * PAD, :] = jnp.where(
            place == PAD - 1, 0.0, pltpu.roll(after, PAD - 1, 0))


def order_matrix(rows):
    row = lax.broadcasted_iota(jnp.int32, (rows, rows), 0)
    col = lax.broadcasted_iota(jnp.int32, (rows, rows), 1)
    return ((row % PAD) * (rows // PAD) + row // PAD == col).astype(full).astype(low)


def order_kernel(x_ref, g_ref, depth_ref, xo_ref, go_ref, e_ref, xpad):
    rows, width = x_ref.shape
    order = order_matrix(rows)
    x = dot(order, x_ref[...])
    xo_ref[...] = x.astype(low)
    go_ref[...] = dot(order, g_ref[...]).astype(low)
    fill_padded(xpad, x)

    def depth_rows(r):
        acc = depth_ref[0:1, :] * xpad[pl.ds(r, 32), :]
        for j in range(1, KERNEL):
            acc = acc + depth_ref[j : j + 1, :] * xpad[pl.ds(multiple(r + PAD * j), 32), :]
        e_ref[pl.ds(r, 32), :] = acc.astype(low)

    row_loop(rows, 32, depth_rows)


def forward_kernel(lens_ref, x_ref, e_ref, wa_ref, wo_ref, w3_ref, span_ref, spread_ref,
                   qwkv_ref, u_ref, p_ref, conv_ref, a_ref, ctx_ref, zh_ref, rstd_ref,
                   wpad, taps):
    rows, width = x_ref.shape
    half = width // 2
    x = x_ref[...]
    for c in range(4):
        qwkv_ref[:, c * half : (c + 1) * half] = dot(x, wa_ref[:, c * half : (c + 1) * half]).astype(low)
    u = dot(e_ref[...], w3_ref[...]).astype(low)
    u_ref[...] = u
    r = (u.astype(full) * qwkv_ref[:, 0:half].astype(full)).astype(low)
    logits = dot(r, span_ref[...]).astype(low).astype(full)
    lt = logits.T[0 : KERNEL * TAP].reshape(KERNEL, TAP, rows)
    top = jnp.max(lt, axis=0, keepdims=True)
    ex = jnp.exp(lt - top)
    pt = (ex / jnp.sum(ex, axis=0, keepdims=True)).reshape(KERNEL * TAP, rows)
    p = jnp.concatenate([pt, jnp.zeros((LANES - KERNEL * TAP, rows), full)], axis=0).T
    p_ref[...] = p
    fill_padded(wpad, qwkv_ref[:, half : 2 * half])
    p_low = p.astype(low)
    for j in range(KERNEL):
        taps[:, j * half : (j + 1) * half] = dot(p_low, spread_ref[:, j * half : (j + 1) * half])

    def conv_rows(r):
        acc = taps[pl.ds(r, 32), 0:half] * wpad[pl.ds(r, 32), :]
        for j in range(1, KERNEL):
            acc = acc + taps[pl.ds(r, 32), j * half : (j + 1) * half] * wpad[pl.ds(multiple(r + PAD * j), 32), :]
        conv_ref[pl.ds(r, 32), :] = acc.astype(low)

    row_loop(rows, 32, conv_rows)
    seq_len = lens_ref[pl.program_id(0)]
    lane = lax.broadcasted_iota(jnp.int32, (1, LANES), 1)
    row = lax.broadcasted_iota(jnp.int32, (1, rows), 1)
    live = (row % PAD) * (rows // PAD) + row // PAD < seq_len
    for pair in range(HEADS // 2):
        at = pair * LANES
        q = qwkv_ref[:, at : at + LANES]
        k = qwkv_ref[:, 2 * half + at : 2 * half + at + LANES]
        v = qwkv_ref[:, 3 * half + at : 3 * half + at + LANES]
        outs = []
        for side in range(2):
            pick = jnp.where((lane // HS) == side, HS ** (-0.5), 0.0).astype(low)
            scores = dot(q * pick, k, NT)
            scores = jnp.where(live, scores, -1000000000.0)
            top = jnp.max(scores, axis=1, keepdims=True)
            ex = jnp.exp(scores - top)
            a = (ex * (1.0 / jnp.sum(ex, axis=1, keepdims=True))).astype(low)
            a_ref[0, 2 * pair + side] = a
            outs.append(dot(a, v))
        ctx_ref[:, at : at + LANES] = jnp.where((lane // HS) == 0, outs[0], outs[1]).astype(low)
    branch = dot(ctx_ref[...], wo_ref[0:half, :]) + dot(conv_ref[...], wo_ref[half:, :])
    z = branch.astype(low).astype(full) + x.astype(full)
    centered = z - jnp.mean(z, axis=1, keepdims=True)
    variance = jnp.mean(centered * centered, axis=1, keepdims=True)
    rstd = lax.rsqrt(variance + 1e-12)
    zh_ref[...] = centered * rstd
    rstd_ref[...] = jnp.broadcast_to(rstd, rstd_ref.shape)


def feed_kernel(zh_ref, rstd_ref, g_ref, norm_ref, up_ref, bias_ref, down_ref,
                out_ref, gy_ref, gb_ref, dfeed_ref, dnorm_ref, dbias_ref,
                act_s, slope_s, gpre_s, dup_s, ddown_s):
    step, last = pl.program_id(0), pl.num_programs(0) - 1
    tile, width = zh_ref.shape
    half = width // 2
    hid = bias_ref.shape[1]
    chunk = 512

    @pl.when(step == 0)
    def _():
        dup_s[...] = jnp.zeros_like(dup_s)
        ddown_s[...] = jnp.zeros_like(ddown_s)
        dnorm_ref[...] = jnp.zeros_like(dnorm_ref)
        dbias_ref[...] = jnp.zeros_like(dbias_ref)

    zh1 = zh_ref[...]
    g1, c1, g2, c2 = (norm_ref[i : i + 1, :] for i in range(4))
    h1 = zh1 * g1 + c1
    f = h1.astype(low)
    outs = []
    for g in range(2):
        fg = f[:, g * half : (g + 1) * half]
        for c in range(0, hid, chunk):
            at = g * hid + c
            pre = dot(fg, up_ref[at : at + chunk, :], NT) + bias_ref[g : g + 1, c : c + chunk]
            cdf = 0.5 * (1.0 + lax.erf(pre * 2.0 ** (-0.5)))
            act_s[:, at : at + chunk] = (pre * cdf).astype(low)
            slope_s[:, at : at + chunk] = cdf + pre * (jnp.exp(-0.5 * pre * pre) * 0.3989422804014327)
        outs.append(dot(act_s[:, g * hid : (g + 1) * hid], down_ref[g * hid : (g + 1) * hid, :]).astype(low).astype(full))
    s = h1 + jnp.concatenate(outs, axis=1)
    centered = s - jnp.mean(s, axis=1, keepdims=True)
    variance = jnp.mean(centered * centered, axis=1, keepdims=True)
    rstd2 = lax.rsqrt(variance + 1e-12)
    zh2 = centered * rstd2
    out_ref[...] = (zh2 * g2 + c2).astype(low)
    grad = g_ref[...].astype(full)
    dnorm_ref[2:3, :] += jnp.sum(grad * zh2, axis=0, keepdims=True)
    dnorm_ref[3:4, :] += jnp.sum(grad, axis=0, keepdims=True)
    dz = grad * g2
    gz = (dz - jnp.mean(dz, axis=1, keepdims=True) - zh2 * jnp.mean(dz * zh2, axis=1, keepdims=True)) * rstd2
    go = gz.astype(low)
    backs = []
    for g in range(2):
        gog = go[:, g * half : (g + 1) * half]
        fg = f[:, g * half : (g + 1) * half]
        for c in range(0, hid, chunk):
            at = g * hid + c
            d_act = dot(gog, down_ref[at : at + chunk, :], NT)
            gpre = (d_act * slope_s[:, at : at + chunk]).astype(low)
            gpre_s[:, at : at + chunk] = gpre
            dbias_ref[g : g + 1, c : c + chunk] += jnp.sum(gpre.astype(full), axis=0, keepdims=True)
            ddown_s[at : at + chunk, :] += dot(act_s[:, at : at + chunk], gog, TN)
            dup_s[at : at + chunk, :] += dot(gpre, fg, TN)
        backs.append(dot(gpre_s[:, g * hid : (g + 1) * hid], up_ref[g * hid : (g + 1) * hid, :]).astype(low).astype(full))
    gh1 = gz + jnp.concatenate(backs, axis=1)
    dnorm_ref[0:1, :] += jnp.sum(gh1 * zh1, axis=0, keepdims=True)
    dnorm_ref[1:2, :] += jnp.sum(gh1, axis=0, keepdims=True)
    dz1 = gh1 * g1
    gy = (dz1 - jnp.mean(dz1, axis=1, keepdims=True) - zh1 * jnp.mean(dz1 * zh1, axis=1, keepdims=True)) * rstd_ref[:, 0:1]
    gy_ref[...] = gy
    gb_ref[...] = gy.astype(low)

    @pl.when(step == last)
    def _():
        dfeed_ref[:, 0:half] = dup_s[...].astype(low)
        dfeed_ref[:, half:] = ddown_s[...].astype(low)


def split_kernel(gb_ref, ctx_ref, conv_ref, res_ref, wo_ref, gm_ref, dout_ref, result_ref, acc):
    step, last = pl.program_id(0), pl.num_programs(0) - 1
    half = ctx_ref.shape[1]

    @pl.when(step == 0)
    def _():
        acc[...] = jnp.zeros_like(acc)

    gb = gb_ref[...]
    gm_ref[...] = dot(gb, wo_ref[...], NT).astype(low)
    acc[0:half, :] += dot(ctx_ref[...].T, gb)
    acc[half:, :] += dot(conv_ref[...].T, gb)
    result_ref[...] = dot(order_matrix(gb.shape[0]), res_ref[...], TN).astype(low)

    @pl.when(step == last)
    def _():
        dout_ref[...] = acc[...].astype(low)


def attend_back_kernel(qwkv_ref, a_ref, gctx_ref, gqa_ref, gkv_ref):
    half = HEADS * HS
    lane = lax.broadcasted_iota(jnp.int32, (1, LANES), 1)
    for pair in range(HEADS // 2):
        at = pair * LANES
        q = qwkv_ref[:, at : at + LANES]
        k = qwkv_ref[:, 2 * half + at : 2 * half + at + LANES]
        v = qwkv_ref[:, 3 * half + at : 3 * half + at + LANES]
        gctx = gctx_ref[:, at : at + LANES]
        gqs, gks, gvs = [], [], []
        for side in range(2):
            pick = jnp.where((lane // HS) == side, 1.0, 0.0).astype(low)
            a_low = a_ref[0, 2 * pair + side]
            a = a_low.astype(full)
            ga = dot(gctx * pick, v, NT)
            gs = (a * (ga - jnp.sum(a * ga, axis=1, keepdims=True))).astype(low)
            gqs.append(dot(gs, k))
            gks.append(dot(gs, q, TN))
            gvs.append(dot(a_low, gctx, TN))
        first = (lane // HS) == 0
        gqa_ref[:, at : at + LANES] = jnp.where(first, gqs[0], gqs[1]) * HS ** (-0.5)
        gkv_ref[:, at : at + LANES] = (jnp.where(first, gks[0], gks[1]) * HS ** (-0.5)).astype(low)
        gkv_ref[:, half + at : half + at + LANES] = jnp.where(first, gvs[0], gvs[1]).astype(low)


def conv_back_kernel(gconv_ref, qw_ref, u_ref, p_ref, gqa_ref, w3_ref, spant_ref, spread_ref,
                     gqw_ref, gu_ref, ge_ref, dspan_ref,
                     wpad, gpad, taps, prods):
    rows, half = u_ref.shape

    @pl.when(pl.program_id(0) == 0)
    def _():
        dspan_ref[...] = jnp.zeros_like(dspan_ref)

    fill_padded(wpad, qw_ref[:, half:])
    fill_padded(gpad, gconv_ref[...])
    p = p_ref[...]
    p_low = p.astype(low)
    for j in range(KERNEL):
        cols = slice(j * half, (j + 1) * half)
        fill_padded(taps.at[:, cols], dot(p_low, spread_ref[:, cols]))

    def conv_rows(r):
        here = gpad[pl.ds(multiple(r + EDGE), 32), :]
        acc = None
        for j in range(KERNEL):
            cols = slice(j * half, (j + 1) * half)
            prods[pl.ds(r, 32), cols] = (here * wpad[pl.ds(multiple(r + PAD * j), 32), :]).astype(low)
            back = pl.ds(multiple(r + PAD * (2 * REACH - j)), 32)
            term = taps[back, cols] * gpad[back, :]
            acc = term if acc is None else acc + term
        gqw_ref[pl.ds(r, 32), half:] = acc.astype(low)

    row_loop(rows, 32, conv_rows)
    gp = dot(prods[...], spread_ref[...], NT)
    gpt = gp.T[0 : KERNEL * TAP].reshape(KERNEL, TAP, rows)
    pt = p.T[0 : KERNEL * TAP].reshape(KERNEL, TAP, rows)
    glt = pt * (gpt - jnp.sum(pt * gpt, axis=0, keepdims=True))
    glt = jnp.concatenate([glt.reshape(KERNEL * TAP, rows), jnp.zeros((LANES - KERNEL * TAP, rows), full)], axis=0)
    gl = glt.T.astype(low)
    q = qw_ref[:, 0:half].astype(full)
    u = u_ref[...].astype(full)
    r = (u * q).astype(low)
    dspan_ref[...] += dot(glt.astype(low), r)
    gr = dot(gl, spant_ref[...]).astype(low).astype(full)
    gqw_ref[:, 0:half] = (gqa_ref[...] + gr * u).astype(low)
    gu = (gr * q).astype(low)
    gu_ref[...] = gu
    ge_ref[...] = dot(gu, w3_ref[...], NT).astype(low)


SMALL_ROWS = 40


def weight_kernel(x_ref, e_ref, gqw_ref, gkv_ref, gu_ref, ge_ref, dspan_ref,
                  da_ref, db_ref, small_ref,
                  xpad, acc_a, acc_b, small):
    step, last = pl.program_id(0), pl.num_programs(0) - 1
    rows, width = x_ref.shape
    half = width // 2

    @pl.when(step == 0)
    def _():
        acc_a[...] = jnp.zeros_like(acc_a)
        acc_b[...] = jnp.zeros_like(acc_b)
        small[...] = jnp.zeros_like(small)

    x = x_ref[...]
    xt = x.T
    acc_a[:, 0:width] += dot(xt, gqw_ref[...])
    acc_a[:, width:] += dot(xt, gkv_ref[:, 0:half])
    acc_b[:, 0:half] += dot(xt, gkv_ref[:, half:])
    acc_b[:, half:] += dot(e_ref[...].T, gu_ref[...])
    fill_padded(xpad, x)
    for c in range(0, width, LANES):
        cols = slice(c, c + LANES)

        def depth_sum(i, sums):
            r = multiple(i * 64)
            ge = ge_ref[pl.ds(r, 64), cols].astype(full)
            new = []
            for j in range(KERNEL):
                prod = ge * xpad[pl.ds(multiple(r + PAD * j), 64), cols]
                new.append(sums[j] + jnp.sum(prod.reshape(8, 8, LANES), axis=0))
            return tuple(new)

        sums = lax.fori_loop(0, rows // 64, depth_sum, tuple(jnp.zeros((8, LANES), full) for _ in range(KERNEL)))
        for j in range(KERNEL):
            small[j : j + 1, cols] += jnp.sum(sums[j], axis=0, keepdims=True)

    @pl.when(step == last)
    def _():
        da_ref[...] = acc_a[...].astype(low)
        db_ref[...] = acc_b[...].astype(low)
        count = HEADS * KERNEL
        row = lax.broadcasted_iota(jnp.int32, (count, LANES), 0)
        col = lax.broadcasted_iota(jnp.int32, (count, LANES), 1)
        pick = ((row % KERNEL) * TAP + row // KERNEL == col).astype(full).astype(low)
        taps = dot(pick, dspan_ref[...].astype(low))
        small[KERNEL : KERNEL + count // 2, 0:half] = taps[0 : count // 2]
        small[KERNEL : KERNEL + count // 2, half:] = taps[count // 2 :]
        small_ref[...] = small[...].astype(low)


def input_kernel(gy_ref, gqw_ref, gkv_ref, ge_ref, wa_ref, depth_ref,
                 gx_ref, gepad, gx_s):
    rows, width = gy_ref.shape
    fill_padded(gepad, ge_ref[...])
    gx_s[...] = gy_ref[...] + dot(gqw_ref[...], wa_ref[:, 0:width], NT) + dot(gkv_ref[...], wa_ref[:, width:], NT)

    def shift_rows(r):
        acc = gx_s[pl.ds(r, 32), :]
        for j in range(KERNEL):
            acc = acc + depth_ref[j : j + 1, :] * gepad[pl.ds(multiple(r + PAD * (2 * REACH - j)), 32), :]
        gx_s[pl.ds(r, 32), :] = acc

    row_loop(rows, 32, shift_rows)
    gx_ref[...] = dot(order_matrix(rows), gx_s[...].astype(low), TN).astype(low)


def adam_step(old, one, two, mean, grad, step_rate, wd_rate):
    moment_one = beta_one * one + (1.0 - beta_one) * grad
    moment_two = beta_two * two + (1.0 - beta_two) * grad * grad
    scaled_one = moment_one / (1.0 - beta_one**STEP)
    scaled_two = moment_two / (1.0 - beta_two**STEP)
    weight = old - step_rate * (scaled_one / (jnp.sqrt(scaled_two) + adam_eps) + wd_rate * old)
    return weight, ema_rate * mean + (1.0 - ema_rate) * weight, moment_one, moment_two


def adam_at(state, new, moments, at, grad, step_rate, wd_rate):
    values = adam_step(*(state[at(slot)] for slot in range(4)), grad, step_rate, wd_rate)
    new[at(0)], new[at(1)], moments[at(0)], moments[at(1)] = values


def adam_mix_kernel(mix, depth, span, ga_ref, gb_ref, small,
                    mix_new, mix_moments, depth_new, depth_moments, span_new, span_moments):
    half = mix.shape[3]
    width = 2 * half
    sources = [ga_ref[:, 0:half], ga_ref[:, width:], gb_ref[:, 0:half], gb_ref[:, half:], ga_ref[:, half:width]]
    for i, grad in enumerate(sources):
        adam_at(mix, mix_new, mix_moments, lambda slot: (slot, i), grad, rate_mix, decay_rate)
    adam_at(depth, depth_new, depth_moments, lambda slot: (slice(None), slot), small[0:KERNEL, :], rate_depth, decay_rate)
    count = HEADS * KERNEL
    grad = jnp.concatenate([small[KERNEL : KERNEL + count // 2, 0:half], small[KERNEL : KERNEL + count // 2, half:]], axis=0)
    adam_at(span, span_new, span_moments, lambda slot: (slice(None), slot), grad, rate_span, decay_rate)


def adam_feed_kernel(place_ref, out, norm, up, bias, down, ga_ref, gb_ref, small,
                     out_new, out_moments, norm_new, norm_moments,
                     up_new, up_moments, bias_new, bias_moments, down_new, down_moments):
    half = down.shape[3]
    width = 2 * half
    hid_dev = down.shape[2]
    adam_at(up, up_new, up_moments, lambda slot: (slot, 0), ga_ref[0:hid_dev, :], rate_up, decay_rate)
    adam_at(down, down_new, down_moments, lambda slot: (slot, 0), gb_ref[0:hid_dev, :], rate_down, decay_rate)
    grad = jnp.concatenate([ga_ref[hid_dev:, :], gb_ref[hid_dev:, :]], axis=1)
    adam_at(out, out_new, out_moments, lambda slot: slot, grad, rate_out, decay_rate)
    adam_at(norm, norm_new, norm_moments, lambda slot: slot, small[0:4, :], rate_norm, 0.0)
    row = lax.broadcasted_iota(jnp.int32, (width, hid_dev), 0)
    col = lax.broadcasted_iota(jnp.int32, (width, hid_dev), 1)
    grad = jnp.zeros((1, hid_dev), full)
    for i in range(4):
        group, side = divmod(i, 2)
        line = jnp.where(place_ref[0] == group, small[4 + i : 5 + i, :], 0.0)
        here = (row + side * width == col + place_ref[1] * hid_dev).astype(full).astype(low)
        high = line.astype(low)
        rest = (line - high.astype(full)).astype(low)
        both = dot(jnp.concatenate([high, rest] + [jnp.zeros_like(high)] * 6, axis=0), here)
        grad = grad + both[0:1] + both[1:2]
    adam_at(bias, bias_new, bias_moments, lambda slot: slot, grad, rate_bias, 0.0)


def adam_call(kernel, inputs, shapes, scalars=0):
    vmem = pl.BlockSpec(memory_space=pltpu.VMEM)
    moved = sum(value.size for value in inputs) * 6
    return pl.pallas_call(
        kernel,
        in_specs=[pl.BlockSpec(memory_space=pltpu.SMEM)] * scalars + [vmem] * (len(inputs) - scalars),
        out_specs=[vmem] * len(shapes),
        out_shape=[struct(shape, full) for shape in shapes],
        compiler_params=pltpu.CompilerParams(vmem_limit_bytes=40 << 20),
        cost_estimate=pl.CostEstimate(flops=2 * moved, transcendentals=0, bytes_accessed=moved),
    )(*inputs)


def struct(shape, dtype):
    return jax.ShapeDtypeStruct(shape, dtype)


def rows_spec(rows, width, at=0):
    return pl.BlockSpec((rows, width), lambda i, *_: (i, at))


def whole(shape, index=None):
    index = index or (0,) * len(shape)
    return pl.BlockSpec(shape, lambda i, *_: index)


def call(kernel, grid, in_specs, out_specs, out_shape, scratch, flops, moved, limit, prefetch=0):
    return pl.pallas_call(
        kernel,
        grid_spec=pltpu.PrefetchScalarGridSpec(
            num_scalar_prefetch=prefetch, grid=grid, in_specs=in_specs, out_specs=out_specs, scratch_shapes=scratch),
        out_shape=out_shape,
        compiler_params=pltpu.CompilerParams(dimension_semantics=("arbitrary",), vmem_limit_bytes=limit << 20),
        cost_estimate=pl.CostEstimate(flops=int(flops), transcendentals=0, bytes_accessed=int(moved)),
    )


def once(shape, index=None):
    index = index or (0,) * len(shape)
    return pl.BlockSpec(shape, lambda i, *_: index, pipeline_mode=pl.Buffered(1))


class Tokens:
    def __init__(self, hidden, seq_lens, depth_w, span_w, norm_w):
        self.tokens, self.width = hidden.shape
        self.count = seq_lens.shape[0]
        self.length = self.tokens // self.count
        self.half = half = self.width // 2
        self.padded = self.length + 2 * EDGE
        self.lens = seq_lens
        self.depth = jnp.pad(depth_w, ((0, 16 - KERNEL), (0, 0)))
        self.norm = jnp.pad(norm_w, ((0, 4), (0, 0)))
        by_tap = jnp.swapaxes(span_w.reshape(half, HEADS, KERNEL), 1, 2)
        by_tap = jnp.pad(by_tap, ((0, 0), (0, 0), (0, TAP - HEADS))).reshape(half, KERNEL * TAP)
        self.span_cols = jnp.pad(by_tap, ((0, 0), (0, LANES - KERNEL * TAP)))
        self.span_rows = self.span_cols.T
        self.spread = spread_matrix(half)

    def order(self, hidden, grad_out):
        length, width = self.length, self.width
        return call(
            order_kernel, (self.count,),
            [rows_spec(length, width), rows_spec(length, width), once((16, width))],
            [rows_spec(length, width)] * 3,
            [struct((self.tokens, width), low)] * 3,
            [pltpu.VMEM((self.padded, width), full)], 4e9, 8e6, 32,
        )(hidden, grad_out, self.depth)

    def forward(self, hidden, e, wa, wb):
        tokens, length, width, half = self.tokens, self.length, self.width, self.half
        heads = pl.BlockSpec((1, HEADS, length, length), lambda i, *_: (i, 0, 0, 0))
        return call(
            forward_kernel, (self.count,),
            [rows_spec(length, width), rows_spec(length, width), once((width, 4 * half)), once((width, width)),
             once((width, half), (0, 2)), once((half, LANES)), once((LANES, KERNEL * half))],
            [rows_spec(length, 4 * half), rows_spec(length, half), rows_spec(length, LANES), rows_spec(length, half),
             heads, rows_spec(length, half), rows_spec(length, width), rows_spec(length, LANES)],
            [struct((tokens, 4 * half), low), struct((tokens, half), low), struct((tokens, LANES), full),
             struct((tokens, half), low), struct((self.count, HEADS, length, length), low), struct((tokens, half), low),
             struct((tokens, width), full), struct((tokens, LANES), full)],
            [pltpu.VMEM((self.padded, half), full), pltpu.VMEM((length, KERNEL * half), full)],
            25e9, 25e6, 60, prefetch=1,
        )(self.lens, hidden, e, wa, wb, wb, self.span_cols, self.spread)

    def feed(self, zh, rstd, grad_out, feed, bias):
        tokens, width, half = self.tokens, self.width, self.half
        hid = bias.shape[1]
        tile = 256
        return call(
            feed_kernel, (tokens // tile,),
            [rows_spec(tile, width), rows_spec(tile, LANES), rows_spec(tile, width), once((8, width)),
             once((2 * hid, half)), once((2, hid)), once((2 * hid, half), (0, 1))],
            [rows_spec(tile, width), rows_spec(tile, width), rows_spec(tile, width), whole((2 * hid, width)),
             whole((8, width)), whole((2, hid))],
            [struct((tokens, width), low), struct((tokens, width), full), struct((tokens, width), low),
             struct((2 * hid, width), low), struct((8, width), full), struct((2, hid), full)],
            [pltpu.VMEM((tile, 2 * hid), low), pltpu.VMEM((tile, 2 * hid), full), pltpu.VMEM((tile, 2 * hid), low),
             pltpu.VMEM((2 * hid, half), full), pltpu.VMEM((2 * hid, half), full)],
            30e9, 20e6, 60,
        )(zh, rstd, grad_out, self.norm, feed, bias, feed)

    def split(self, gb, ctx, conv, result, wb):
        tokens, length, width, half = self.tokens, self.length, self.width, self.half
        wide, slim = rows_spec(length, width), rows_spec(length, half)
        return call(
            split_kernel, (self.count,),
            [wide, slim, slim, wide, once((width, width))],
            [wide, whole((width, width)), wide],
            [struct((tokens, width), low), struct((width, width), low), struct((tokens, width), low)],
            [pltpu.VMEM((width, width), full)], 6e9, 9e6, 60,
        )(gb, ctx, conv, result, wb)

    def attend_back(self, qwkv, a, gm):
        tokens, length, width, half = self.tokens, self.length, self.width, self.half
        heads = pl.BlockSpec((1, HEADS, length, length), lambda i, *_: (i, 0, 0, 0))
        return call(
            attend_back_kernel, (self.count,),
            [rows_spec(length, 4 * half), heads, rows_spec(length, half)],
            [rows_spec(length, half), rows_spec(length, width)],
            [struct((tokens, half), full), struct((tokens, width), low)],
            [], 15e9, 12e6, 60,
        )(qwkv, a, gm)

    def conv_back(self, gm, qwkv, u, p, gqa, wb):
        tokens, length, width, half = self.tokens, self.length, self.width, self.half
        V = pltpu.VMEM
        slim = rows_spec(length, half)
        return call(
            conv_back_kernel, (self.count,),
            [rows_spec(length, half, 1), rows_spec(length, width), slim, rows_spec(length, LANES), slim,
             once((width, half), (0, 2)), once((LANES, half)), once((LANES, KERNEL * half))],
            [rows_spec(length, width), slim, rows_spec(length, width), whole((LANES, half))],
            [struct((tokens, width), low), struct((tokens, half), low), struct((tokens, width), low), struct((LANES, half), full)],
            [V((self.padded, half), full), V((self.padded, half), full), V((self.padded, KERNEL * half), full),
             V((length, KERNEL * half), low)],
            16e9, 12e6, 60,
        )(gm, qwkv, u, p, gqa, wb, self.span_rows, self.spread)

    def weights(self, hidden, e, gqw, gkv, gu, ge, d_span):
        length, width, half = self.length, self.width, self.half
        V = pltpu.VMEM
        wide = rows_spec(length, width)
        return call(
            weight_kernel, (self.count,),
            [wide, wide, wide, wide, rows_spec(length, half), wide, whole((LANES, half))],
            [whole((width, 3 * half)), whole((width, width)), whole((SMALL_ROWS, width))],
            [struct((width, 3 * half), low), struct((width, width), low), struct((SMALL_ROWS, width), low)],
            [V((self.padded, width), full), V((width, 3 * half), full), V((width, width), full), V((SMALL_ROWS, width), full)],
            12e9, 16e6, 60,
        )(hidden, e, gqw, gkv, gu, ge, d_span)

    def input_grad(self, n, gy, gqw, gkv, ge, wa):
        length, width, half = self.length, self.width, self.half

        def part(cols):
            return pl.BlockSpec((length, cols), lambda i, *_: (n, 0))

        return call(
            input_kernel, (1,),
            [part(width), part(width), part(width), part(width), whole((width, 4 * half)), whole((16, width))],
            [whole((length, width))], [struct((length, width), low)],
            [pltpu.VMEM((self.padded, width), full), pltpu.VMEM((length, width), full)],
            5e9, 9e6, 32,
        )(gy, gqw, gkv, ge, wa, self.depth)[0]


class Links:
    def __init__(self, mesh):
        self.size = mesh.shape["dp"]
        self.grp = mesh.shape["grp"]
        deep = 4 if self.size % 4 == 0 else 1
        rest = self.size // deep
        wide = 1 << ((rest.bit_length() - 1) // 2)
        self.sizes = (self.grp, deep, rest // wide, wide)
        self.strides = (0, rest, wide, 1)

    def place(self, dim):
        if dim == 0:
            return lax.axis_index("grp")
        return (lax.axis_index("dp") // self.strides[dim]) % self.sizes[dim]

    def swap(self, value, dim, shift):
        if dim == 0:
            return lax.ppermute(value, "grp", [(i, i ^ shift) for i in range(self.grp)])
        size, stride = self.sizes[dim], self.strides[dim]
        pairs = []
        for i in range(self.size):
            at = (i // stride) % size
            pairs.append((i, i + ((at ^ shift) - at) * stride))
        return lax.ppermute(value, "dp", pairs)

    def gather(self, block, dim):
        size, here = self.sizes[dim], self.place(dim)
        got = [block] + [self.swap(block, dim, k) for k in range(1, size)]
        slots = []
        for j in range(size):
            value = got[size - 1]
            for k in range(size - 1):
                value = jnp.where(here == (j ^ k), got[k], value)
            slots.append(value)
        return jnp.concatenate(slots, axis=dim)

    def scatter(self, block, dim, dtype):
        size, here = self.sizes[dim], self.place(dim)
        got = [lax.dynamic_slice_in_dim(block, here, 1, dim).astype(full)]
        for k in range(1, size):
            piece = lax.dynamic_slice_in_dim(block, here ^ k, 1, dim)
            got.append(self.swap(piece, dim, k).astype(full))
        while len(got) > 1:
            got = [got[i] + got[i + 1] for i in range(0, len(got), 2)]
        return got[0].astype(dtype)

    def halves(self, block):
        here = self.place(0)
        return (lax.dynamic_slice_in_dim(block, here, 1, 0), lax.dynamic_slice_in_dim(block, here ^ 1, 1, 0))

    def join(self, keep, piece):
        return keep.astype(full) + self.swap(piece, 0, 1).astype(full)

    def scatter_both(self, a, b, small, dim_a, dim_b, end):
        a = self.scatter(a, dim_a, end)
        cols = b.shape[-1]
        size, here = self.sizes[dim_b], self.place(dim_b)
        small = small.astype(low)
        keep = lax.dynamic_slice_in_dim(b, here, 1, dim_b)
        got, sums = [keep.astype(full)], [small.astype(full)]
        for k in range(1, size):
            piece = lax.dynamic_slice_in_dim(b, here ^ k, 1, dim_b).reshape(-1, cols)
            message = self.swap(jnp.concatenate([piece, small], axis=0), dim_b, k)
            got.append(message[: -small.shape[0]].reshape(keep.shape).astype(full))
            sums.append(message[-small.shape[0] :].astype(full))
        while len(got) > 1:
            got = [got[i] + got[i + 1] for i in range(0, len(got), 2)]
            sums = [sums[i] + sums[i + 1] for i in range(0, len(sums), 2)]
        return a, got[0].astype(end), sums[0].astype(end)


def on_device(links, hidden, grad_out, seq_lens, mix_state, out_state, depth_state, span_state, norm_state,
              up_state, bias_state, down_state):
    both = ("grp", "dp")
    barrier = lax.optimization_barrier
    width = hidden.shape[1]
    half = width // 2
    hid_dev = up_state.shape[3]
    rows_dev = mix_state.shape[2]
    up_state = jnp.swapaxes(up_state, 2, 3)
    depth_state = jnp.swapaxes(depth_state, 0, 1)
    span_state = jnp.transpose(span_state, (2, 0, 1))
    tokens = Tokens(hidden, seq_lens, depth_state[:, 0].astype(low).astype(full), span_state[:, 0].astype(low).T, norm_state[0])

    mix_low = mix_state[0].astype(low)
    bias_row = jnp.pad(bias_state[0].astype(low), ((0, rows_dev - 1), (0, LANES - hid_dev)))
    shard = jnp.concatenate(
        [mix_low[0], mix_low[4], mix_low[1], mix_low[2], bias_row, out_state[0].astype(low), mix_low[3]], axis=1)
    feed_shard = jnp.concatenate([up_state[0, 0], down_state[0, 0]], axis=1).astype(low)
    feed = lax.all_gather(feed_shard, both, axis=0, tiled=True)
    block = links.gather(shard.reshape((1, 1, 1, 1) + shard.shape), 1)
    block, hidden_o, grad_o, e = barrier((block, *tokens.order(hidden, grad_out)))
    split = 4 * half + LANES
    wa, wb = block[..., :split], block[..., split:]
    for dim_a, dim_b in ((2, 3), (3, 2), (0, 0)):
        wa, wb = links.gather(wa, dim_a), links.gather(wb, dim_b)
    wa, wb = wa.reshape(width, -1), wb.reshape(width, -1)
    devices = links.grp * links.size
    bias = wa.reshape(devices, rows_dev, -1)[:, 0, 4 * half : 4 * half + hid_dev].reshape(links.grp, -1).astype(full)

    qwkv, u, p, conv, a, ctx, zh, rstd = tokens.forward(hidden_o, e, wa, wb)
    result, gy, gb, d_feed, d_norm, d_bias = tokens.feed(zh, rstd, grad_o, feed, bias)

    def blocks(value):
        return value.reshape(links.sizes + (-1, value.shape[-1]))

    small = jnp.concatenate([d_norm[:4], d_bias.reshape(4, width)], axis=0).reshape(-1, half)
    keep, piece = links.halves(blocks(d_feed))
    keep, piece, gb, result, small = barrier((keep, piece, gb, result, small))
    d_feed = links.join(keep, piece)
    small = links.join(small, small.astype(low)).astype(low)
    gm, d_out, result = tokens.split(gb, ctx, conv, result, wb)
    d_out = links.join(*links.halves(blocks(d_out)))
    rows = jnp.concatenate([d_feed, d_out], axis=4).astype(low)
    *sums, gm = barrier((rows[..., :half], rows[..., half:], small, gm))
    sums = links.scatter_both(*sums, 3, 2, low)
    gqa, gkv = tokens.attend_back(qwkv, a, gm)
    *sums, gqa, gkv = barrier((*sums, gqa, gkv))
    sums = links.scatter_both(*sums, 2, 3, low)
    gqw, gu, ge, d_span = tokens.conv_back(gm, qwkv, u, p, gqa, wb)
    *sums, gqw, gu, ge, d_span = barrier((*sums, gqw, gu, ge, d_span))
    feed_sums = links.scatter_both(*sums, 1, 1, full)
    d_a, d_b, small = tokens.weights(hidden_o, e, gqw, gkv, gu, ge, d_span)
    *feed_sums, d_a, d_b, small = barrier((*feed_sums, d_a, d_b, small))

    sums = links.scatter_both(blocks(d_a), blocks(d_b), small, 0, 0, low)
    *sums, gy, gqw, ge = barrier((*sums, gy, gqw, ge))
    sums = links.scatter_both(*sums, 3, 2, low)
    parts = [tokens.input_grad(n, gy, gqw, gkv, ge, wa) for n in range(tokens.count)]
    *sums, gx = barrier((*sums, jnp.concatenate(parts, axis=0)))
    sums = barrier(links.scatter_both(*sums, 2, 3, low))
    grad_a, grad_b, small = links.scatter_both(*sums, 1, 1, full)

    def twice(state, at=0):
        shape = state.shape[:at] + (2,) + state.shape[at + 1 :]
        return [shape, shape]

    def flat(value):
        return value.reshape(-1, value.shape[-1])

    place = jnp.stack([links.place(0), lax.axis_index("dp")]).astype(jnp.int32)
    feed_a, feed_b, feed_small = feed_sums
    feed_out = adam_call(
        adam_feed_kernel,
        [place, out_state, norm_state, up_state, bias_state, down_state, flat(feed_a), flat(feed_b), feed_small.reshape(-1, width)],
        twice(out_state) + twice(norm_state) + twice(up_state) + twice(bias_state) + twice(down_state), scalars=1)
    mixed = adam_call(
        adam_mix_kernel,
        [mix_state, depth_state, span_state, flat(grad_a), flat(grad_b), small],
        twice(mix_state) + twice(depth_state, 1) + twice(span_state, 1))
    depth_out = [jnp.swapaxes(value, 0, 1) for value in mixed[2:4]]
    span_out = [jnp.transpose(value, (1, 2, 0)) for value in mixed[4:]]
    up_out = [jnp.swapaxes(value, 2, 3) for value in feed_out[4:6]]
    return (result, gx, *mixed[:2], *feed_out[:2], *depth_out, *span_out, *feed_out[2:4], *up_out, *feed_out[6:])


def solution(mesh):
    both = ("grp", "dp")
    mix, out = P(None, None, both, None), P(None, both, None)
    up, bias, down = P(None, "grp", None, "dp"), P(None, "grp", "dp"), P(None, "grp", "dp", None)
    rows = P(both, None)
    return jax.shard_map(
        functools.partial(on_device, Links(mesh)),
        mesh=mesh,
        in_specs=(rows, rows, P(both), mix, out, P(), P(), P(), up, bias, down),
        out_specs=(rows, rows, mix, mix, out, out, P(), P(), P(), P(), P(), P(), up, up, bias, bias, down, down),
        check_vma=False,
    )
```

```python
import functools

import jax
import jax.numpy as jnp
from jax import lax
from jax.experimental import pallas as pl
from jax.experimental.pallas import tpu as pltpu
from jax.sharding import PartitionSpec as P

HEADS = 6
HS = 64
KERNEL = 9
STEP = 7
REACH = KERNEL // 2
TAP = 8
LANES = 128
PAD = 8
EDGE = REACH * PAD

beta_one = 0.9
beta_two = 0.999
adam_eps = 1e-06
ema_rate = 0.99
decay_rate = 0.01
rate_mix = 0.06
rate_out = 0.12
rate_depth = 0.4
rate_span = 0.08
rate_norm = 0.5
rate_up = 0.08
rate_bias = 0.3
rate_down = 0.04

low = jnp.bfloat16
full = jnp.float32
NN = (((1,), (0,)), ((), ()))
NT = (((1,), (1,)), ((), ()))
TN = (((0,), (0,)), ((), ()))


def dot(left, right, dims=NN):
    return lax.dot_general(left, right, dims, preferred_element_type=full)


def rounded(value):
    return value.astype(low).astype(full)


def row_loop(rows, chunk, body):
    for r in range(0, rows, chunk):
        body(r)


def spread_table(width):
    row = lax.broadcasted_iota(jnp.int32, (LANES, 1), 0)
    col = lax.broadcasted_iota(jnp.int32, (1, KERNEL * width), 1)
    head = row % TAP
    first = (row // TAP) * width + head * HS
    first = jnp.where(head < HEADS, first, -HS)
    return ((col >= first) & (col < first + HS)).astype(full).astype(low)


def tap_table():
    row = lax.broadcasted_iota(jnp.int32, (LANES, HEADS * KERNEL), 0)
    col = lax.broadcasted_iota(jnp.int32, (LANES, HEADS * KERNEL), 1)
    return ((col % KERNEL) * TAP + col // KERNEL == row).astype(full).astype(low)


def copy_halves(place_ref, mine, other, target, sems, first, cols):
    rows = mine.shape[0]
    copies = []
    for i, (half, at) in enumerate(((mine, place_ref[0]), (other, 1 - place_ref[0]))):
        copy = pltpu.make_async_copy(
            half.at[:, pl.ds(first, cols)], target.at[pl.ds(pl.multiple_of(at * rows, rows), rows), :], sems.at[i])
        copy.start()
        copies.append(copy)
    return copies


def put_halves(place_ref, value_ref, keep_ref, piece_ref):
    rows = keep_ref.shape[0]
    here = pl.ds(pl.multiple_of(place_ref[0] * rows, rows), rows)
    there = pl.ds(pl.multiple_of((1 - place_ref[0]) * rows, rows), rows)
    keep_ref[...] = value_ref[here, :].astype(low)
    piece_ref[...] = value_ref[there, :].astype(low)


def fill_padded(ref, value):
    rows = value.shape[0]
    value = value.astype(full)
    place = lax.broadcasted_iota(jnp.int32, (PAD, 1), 0)
    ref[EDGE : EDGE + rows, :] = value
    for i in range(REACH):
        before = value[rows - EDGE + i * PAD : rows - EDGE + (i + 1) * PAD]
        ref[i * PAD : (i + 1) * PAD, :] = jnp.where(place == 0, 0.0, pltpu.roll(before, 1, 0))
        after = value[i * PAD : (i + 1) * PAD]
        ref[EDGE + rows + i * PAD : EDGE + rows + (i + 1) * PAD, :] = jnp.where(
            place == PAD - 1, 0.0, pltpu.roll(after, PAD - 1, 0))


def order_matrix(rows, back=False):
    row = lax.broadcasted_iota(jnp.int32, (rows, rows), 0)
    col = lax.broadcasted_iota(jnp.int32, (1, rows), 1)
    places = rows // PAD
    at = (col % PAD) * places + col // PAD if back else (col % places) * PAD + col // places
    return (row == at).astype(full).astype(low)


def order_kernel(x_ref, g_ref, depth_ref, xo_ref, go_ref, e_ref, xpad):
    rows, width = x_ref.shape
    order = order_matrix(rows)
    x = dot(order, x_ref[...])
    xo_ref[...] = x.astype(low)
    go_ref[...] = dot(order, g_ref[...]).astype(low)
    fill_padded(xpad, x)

    rates = [rounded(depth_ref[j, 0:1]) for j in range(KERNEL)]

    def depth_rows(r):
        acc = rates[0] * xpad[pl.ds(r, 32), :]
        for j in range(1, KERNEL):
            acc = acc + rates[j] * xpad[pl.ds(r + PAD * j, 32), :]
        e_ref[pl.ds(r, 32), :] = acc.astype(low)

    row_loop(rows, 32, depth_rows)


def forward_kernel(lens_ref, place_ref, x_ref, e_ref, wam_ref, wao_ref, wbm_ref, wbo_ref, bm_ref, bo_ref, span_ref,
                   qwkv_ref, u_ref, p_ref, conv_ref, a_ref, ctx_ref, y_ref, bias_ref, spant_ref,
                   wpad, taps, wa_ref, wo_ref, w3_ref, spread_ref, sems):
    rows, width = x_ref.shape
    half = width // 2

    @pl.when(pl.program_id(0) == 0)
    def _():
        copies = copy_halves(place_ref, wam_ref, wao_ref, wa_ref, sems.at[0], 0, 4 * half)
        copies += copy_halves(place_ref, wbm_ref, wbo_ref, wo_ref, sems.at[1], 0, width)
        copies += copy_halves(place_ref, wbm_ref, wbo_ref, w3_ref, sems.at[2], width, half)
        spread_ref[...] = spread_table(half)
        spant_ref[...] = dot(tap_table(), span_ref[:, 0, :].astype(low)).astype(low)
        hid_dev = bias_ref.shape[1] // bm_ref.shape[0]
        for n in range(bm_ref.shape[0]):
            cols = slice(n * hid_dev, (n + 1) * hid_dev)
            mine, other = bm_ref[n].astype(full)[0:1, 0:hid_dev], bo_ref[n].astype(full)[0:1, 0:hid_dev]
            bias_ref[0:1, cols] = jnp.where(place_ref[0] == 0, mine, other)
            bias_ref[1:2, cols] = jnp.where(place_ref[0] == 0, other, mine)
        for copy in copies:
            copy.wait()

    x = x_ref[...]
    for c in range(4):
        qwkv_ref[:, c * half : (c + 1) * half] = dot(x, wa_ref[:, c * half : (c + 1) * half]).astype(low)
    u = dot(e_ref[...], w3_ref[...]).astype(low)
    u_ref[...] = u
    r = (u.astype(full) * qwkv_ref[:, 0:half].astype(full)).astype(low)
    logits = rounded(dot(r, spant_ref[...], NT))
    lt = logits.T[0 : KERNEL * TAP].reshape(KERNEL, TAP, rows)
    top = jnp.max(lt, axis=0, keepdims=True)
    ex = jnp.exp(lt - top)
    pt = (ex / jnp.sum(ex, axis=0, keepdims=True)).reshape(KERNEL * TAP, rows)
    p = jnp.concatenate([pt, jnp.zeros((LANES - KERNEL * TAP, rows), full)], axis=0).T
    p_ref[...] = p
    fill_padded(wpad, qwkv_ref[:, half : 2 * half])
    p_low = p.astype(low)
    for j in range(KERNEL):
        taps[:, j * half : (j + 1) * half] = dot(p_low, spread_ref[:, j * half : (j + 1) * half])

    def conv_rows(r):
        acc = taps[pl.ds(r, 32), 0:half] * wpad[pl.ds(r, 32), :]
        for j in range(1, KERNEL):
            acc = acc + taps[pl.ds(r, 32), j * half : (j + 1) * half] * wpad[pl.ds(r + PAD * j, 32), :]
        conv_ref[pl.ds(r, 32), :] = acc.astype(low)

    row_loop(rows, 32, conv_rows)
    seq_len = lens_ref[pl.program_id(0)]
    lane = lax.broadcasted_iota(jnp.int32, (1, LANES), 1)
    row = lax.broadcasted_iota(jnp.int32, (1, rows), 1)
    live = (row % PAD) * (rows // PAD) + row // PAD < seq_len
    for pair in range(HEADS // 2):
        at = pair * LANES
        q = qwkv_ref[:, at : at + LANES]
        k = qwkv_ref[:, 2 * half + at : 2 * half + at + LANES]
        v = qwkv_ref[:, 3 * half + at : 3 * half + at + LANES]
        outs = []
        for side in range(2):
            pick = jnp.where((lane // HS) == side, HS ** (-0.5), 0.0).astype(low)
            scores = dot(q * pick, k, NT)
            scores = jnp.where(live, scores, -1000000000.0)
            top = jnp.max(scores, axis=1, keepdims=True)
            ex = jnp.exp(scores - top)
            a = (ex * (1.0 / jnp.sum(ex, axis=1, keepdims=True))).astype(low)
            a_ref[0, 2 * pair + side] = a
            outs.append(dot(a, v))
        ctx_ref[:, at : at + LANES] = jnp.where((lane // HS) == 0, outs[0], outs[1]).astype(low)
    y_ref[...] = (dot(ctx_ref[...], wo_ref[0:half, :]) + dot(conv_ref[...], wo_ref[half:, :])).astype(low)


def normed(value):
    centered = value - jnp.mean(value, axis=1, keepdims=True)
    variance = jnp.mean(centered * centered, axis=1, keepdims=True)
    rstd = lax.rsqrt(variance + 1e-12)
    return centered * rstd, rstd


def feed_kernel(place_ref, y_ref, x_ref, g_ref, norm_ref, up_ref, bias_ref, down_ref,
                out_ref, gb_ref, keep_ref, piece_ref, small_ref,
                act_s, slope_s, gpre_s, dup_s, ddown_s, dbias_s):
    step, last = pl.program_id(0), pl.num_programs(0) - 1
    width = y_ref.shape[1]
    half = width // 2
    hid = bias_ref.shape[1]

    @pl.when(step == 0)
    def _():
        dup_s[...] = jnp.zeros_like(dup_s)
        ddown_s[...] = jnp.zeros_like(ddown_s)
        dbias_s[...] = jnp.zeros_like(dbias_s)
        small_ref[...] = jnp.zeros_like(small_ref)

    zh1, rstd1 = normed(y_ref[...].astype(full) + x_ref[...].astype(full))
    g1, c1, g2, c2 = (norm_ref[0, i : i + 1] for i in range(4))
    h1 = zh1 * g1 + c1
    f = h1.astype(low)
    outs = []
    for g in range(2):
        rows = slice(g * hid, (g + 1) * hid)
        pre = dot(f[:, g * half : (g + 1) * half], up_ref[rows, :], NT) + bias_ref[g : g + 1, :]
        cdf = 0.5 * (1.0 + lax.erf(pre * 2.0 ** (-0.5)))
        act_s[:, rows] = (pre * cdf).astype(low)
        slope_s[:, rows] = cdf + pre * (jnp.exp(-0.5 * pre * pre) * 0.3989422804014327)
        outs.append(rounded(dot(act_s[:, rows], down_ref[rows, :])))
    zh2, rstd2 = normed(h1 + jnp.concatenate(outs, axis=1))
    out_ref[...] = (zh2 * g2 + c2).astype(low)
    grad = g_ref[...].astype(full)
    small_ref[2:3, :] += jnp.sum(grad * zh2, axis=0, keepdims=True)
    small_ref[3:4, :] += jnp.sum(grad, axis=0, keepdims=True)
    dz = grad * g2
    gz = (dz - jnp.mean(dz, axis=1, keepdims=True) - zh2 * jnp.mean(dz * zh2, axis=1, keepdims=True)) * rstd2
    go = gz.astype(low)
    ft, got = f.T, go.T
    backs = []
    for g in range(2):
        rows, cols = slice(g * hid, (g + 1) * hid), slice(g * half, (g + 1) * half)
        gpre = (dot(go[:, cols], down_ref[rows, :], NT) * slope_s[:, rows]).astype(low)
        gpre_s[:, rows] = gpre
        dbias_s[g : g + 1, :] += jnp.sum(gpre.astype(full), axis=0, keepdims=True)
        ddown_s[cols, :] += dot(got[cols], act_s[:, rows])
        dup_s[cols, :] += dot(ft[cols], gpre)
        backs.append(rounded(dot(gpre_s[:, rows], up_ref[rows, :])))
    gh1 = gz + jnp.concatenate(backs, axis=1)
    small_ref[0:1, :] += jnp.sum(gh1 * zh1, axis=0, keepdims=True)
    small_ref[1:2, :] += jnp.sum(gh1, axis=0, keepdims=True)
    dz1 = gh1 * g1
    gy = (dz1 - jnp.mean(dz1, axis=1, keepdims=True) - zh1 * jnp.mean(dz1 * zh1, axis=1, keepdims=True)) * rstd1
    gb_ref[...] = gy.astype(low)

    @pl.when(step == last)
    def _():
        for ref, group in ((keep_ref, place_ref[0]), (piece_ref, 1 - place_ref[0])):
            rows = pl.ds(pl.multiple_of(group * half, half), half)
            ref[:, 0:half] = dup_s[rows, :].T.astype(low)
            ref[:, half:] = ddown_s[rows, :].T.astype(low)
        for i in range(4):
            g, side = divmod(i, 2)
            small_ref[4 + i : 5 + i, :] = dbias_s[g : g + 1, side * width : (side + 1) * width]


def split_kernel(place_ref, gb_ref, ctx_ref, conv_ref, res_ref, wbm_ref, wbo_ref,
                 gm_ref, keep_ref, piece_ref, result_ref,
                 acc, wo_ref, sems):
    step, last = pl.program_id(0), pl.num_programs(0) - 1
    half = ctx_ref.shape[1]

    @pl.when(step == 0)
    def _():
        copies = copy_halves(place_ref, wbm_ref, wbo_ref, wo_ref, sems, 0, 2 * half)
        acc[...] = jnp.zeros_like(acc)
        for copy in copies:
            copy.wait()

    gb = gb_ref[...]
    gm_ref[...] = dot(gb, wo_ref[...], NT).astype(low)
    acc[0:half, :] += dot(ctx_ref[...].T, gb)
    acc[half:, :] += dot(conv_ref[...].T, gb)
    result_ref[...] = dot(order_matrix(gb.shape[0], True), res_ref[...]).astype(low)

    @pl.when(step == last)
    def _():
        put_halves(place_ref, acc, keep_ref, piece_ref)


def attend_back_kernel(qwkv_ref, a_ref, gctx_ref, gqa_ref, gkv_ref):
    half = HEADS * HS
    lane = lax.broadcasted_iota(jnp.int32, (1, LANES), 1)
    for pair in range(HEADS // 2):
        at = pair * LANES
        q = qwkv_ref[:, at : at + LANES]
        k = qwkv_ref[:, 2 * half + at : 2 * half + at + LANES]
        v = qwkv_ref[:, 3 * half + at : 3 * half + at + LANES]
        gctx = gctx_ref[:, at : at + LANES]
        qt, gctxt = q.T, gctx.T
        gqs, gks, gvs = [], [], []
        for side in range(2):
            pick = jnp.where((lane // HS) == side, 1.0, 0.0).astype(low)
            a_low = a_ref[0, 2 * pair + side]
            a = a_low.astype(full)
            ga = dot(gctx * pick, v, NT)
            gs = (a * (ga - jnp.sum(a * ga, axis=1, keepdims=True))).astype(low)
            gqs.append(dot(gs, k))
            gks.append(dot(qt, gs))
            gvs.append(dot(gctxt, a_low))
        first = (lane // HS) == 0
        gqa_ref[:, at : at + LANES] = jnp.where(first, gqs[0], gqs[1]) * HS ** (-0.5)
        gk = jnp.concatenate([gks[0][0:HS], gks[1][HS:]], axis=0) * HS ** (-0.5)
        gv = jnp.concatenate([gvs[0][0:HS], gvs[1][HS:]], axis=0)
        gkv_ref[:, at : at + LANES] = gk.T.astype(low)
        gkv_ref[:, half + at : half + at + LANES] = gv.T.astype(low)


def conv_back_kernel(place_ref, gconv_ref, qw_ref, u_ref, p_ref, gqa_ref, wbm_ref, wbo_ref, spant_ref,
                     gqw_ref, gu_ref, ge_ref, dspan_ref,
                     wpad, gpad, taps, prods, w3_ref, spread_ref, sems):
    rows, half = u_ref.shape

    @pl.when(pl.program_id(0) == 0)
    def _():
        copies = copy_halves(place_ref, wbm_ref, wbo_ref, w3_ref, sems, 2 * half, half)
        dspan_ref[...] = jnp.zeros_like(dspan_ref)
        spread_ref[...] = spread_table(half)
        for copy in copies:
            copy.wait()

    fill_padded(wpad, qw_ref[:, half:])
    fill_padded(gpad, gconv_ref[...])
    p = p_ref[...]
    p_low = p.astype(low)
    for j in range(KERNEL):
        cols = slice(j * half, (j + 1) * half)
        fill_padded(taps.at[:, cols], dot(p_low, spread_ref[:, cols]))

    def conv_rows(r):
        here = gpad[pl.ds(r + EDGE, 32), :]
        acc = None
        for j in range(KERNEL):
            cols = slice(j * half, (j + 1) * half)
            prods[pl.ds(r, 32), cols] = (here * wpad[pl.ds(r + PAD * j, 32), :]).astype(low)
            back = pl.ds(r + PAD * (2 * REACH - j), 32)
            term = taps[back, cols] * gpad[back, :]
            acc = term if acc is None else acc + term
        gqw_ref[pl.ds(r, 32), half:] = acc.astype(low)

    row_loop(rows, 32, conv_rows)
    gp = dot(prods[...], spread_ref[...], NT)
    gpt = gp.T[0 : KERNEL * TAP].reshape(KERNEL, TAP, rows)
    pt = p.T[0 : KERNEL * TAP].reshape(KERNEL, TAP, rows)
    glt = pt * (gpt - jnp.sum(pt * gpt, axis=0, keepdims=True))
    glt = jnp.concatenate([glt.reshape(KERNEL * TAP, rows), jnp.zeros((LANES - KERNEL * TAP, rows), full)], axis=0)
    gl = glt.T.astype(low)
    q = qw_ref[:, 0:half].astype(full)
    u = u_ref[...].astype(full)
    r = (u * q).astype(low)
    dspan_ref[...] += dot(glt.astype(low), r)
    gr = dot(gl, spant_ref[...]).astype(low).astype(full)
    gqw_ref[:, 0:half] = (gqa_ref[...] + gr * u).astype(low)
    gu = (gr * q).astype(low)
    gu_ref[...] = gu
    ge_ref[...] = dot(gu, w3_ref[...], NT).astype(low)


SMALL_ROWS = 40


def weight_kernel(place_ref, x_ref, e_ref, gqw_ref, gkv_ref, gu_ref, ge_ref, dspan_ref,
                  keep_a_ref, piece_a_ref, keep_b_ref, piece_b_ref, small_ref,
                  xpad, acc_a, acc_b, small):
    step, last = pl.program_id(0), pl.num_programs(0) - 1
    rows, width = x_ref.shape
    half = width // 2

    @pl.when(step == 0)
    def _():
        acc_a[...] = jnp.zeros_like(acc_a)
        acc_b[...] = jnp.zeros_like(acc_b)
        small[...] = jnp.zeros_like(small)

    x = x_ref[...]
    xt = x.T
    acc_a[:, 0:width] += dot(xt, gqw_ref[...])
    acc_a[:, width:] += dot(xt, gkv_ref[:, 0:half])
    acc_b[:, 0:half] += dot(xt, gkv_ref[:, half:])
    acc_b[:, half:] += dot(e_ref[...].T, gu_ref[...])
    fill_padded(xpad, x)
    for c in range(0, width, LANES):
        cols = slice(c, c + LANES)

        sums = [jnp.zeros((PAD, LANES), full) for _ in range(KERNEL)]
        for r in range(0, rows, 64):
            ge = ge_ref[pl.ds(r, 64), cols].astype(full)
            for j in range(KERNEL):
                prod = ge * xpad[pl.ds(r + PAD * j, 64), cols]
                sums[j] = sums[j] + jnp.sum(prod.reshape(PAD, PAD, LANES), axis=0)
        for j in range(KERNEL):
            small[j : j + 1, cols] += jnp.sum(sums[j], axis=0, keepdims=True)

    @pl.when(step == last)
    def _():
        put_halves(place_ref, acc_a, keep_a_ref, piece_a_ref)
        put_halves(place_ref, acc_b, keep_b_ref, piece_b_ref)
        count = HEADS * KERNEL
        taps = dot(tap_table(), dspan_ref[...].astype(low), TN)
        small[KERNEL : KERNEL + count // 2, 0:half] = taps[0 : count // 2]
        small[KERNEL : KERNEL + count // 2, half:] = taps[count // 2 :]
        small_ref[...] = small[...].astype(low)


def input_kernel(place_ref, gb_ref, gqw_ref, gkv_ref, ge_ref, wam_ref, wao_ref, depth_ref,
                 gx_ref, gepad, gx_s, wa_ref, sems):
    rows, width = gb_ref.shape

    @pl.when(pl.program_id(0) == 0)
    def _():
        for copy in copy_halves(place_ref, wam_ref, wao_ref, wa_ref, sems, 0, 2 * width):
            copy.wait()

    fill_padded(gepad, ge_ref[...])
    gx_s[...] = gb_ref[...].astype(full) + dot(gqw_ref[...], wa_ref[:, 0:width], NT) + dot(gkv_ref[...], wa_ref[:, width:], NT)

    rates = [rounded(depth_ref[j, 0:1]) for j in range(KERNEL)]

    def shift_rows(r):
        acc = gx_s[pl.ds(r, 32), :]
        for j in range(KERNEL):
            acc = acc + rates[j] * gepad[pl.ds(r + PAD * (2 * REACH - j), 32), :]
        gx_s[pl.ds(r, 32), :] = acc

    row_loop(rows, 32, shift_rows)
    gx_ref[...] = dot(order_matrix(rows, True), gx_s[...].astype(low)).astype(low)


def adam_step(old, one, two, mean, grad, step_rate, wd_rate):
    moment_one = beta_one * one + (1.0 - beta_one) * grad
    moment_two = beta_two * two + (1.0 - beta_two) * grad * grad
    scaled_one = moment_one / (1.0 - beta_one**STEP)
    scaled_two = moment_two / (1.0 - beta_two**STEP)
    weight = old - step_rate * (scaled_one / (jnp.sqrt(scaled_two) + adam_eps) + wd_rate * old)
    return weight, ema_rate * mean + (1.0 - ema_rate) * weight, moment_one, moment_two


def adam_at(state, new, moments, at, grad, step_rate, wd_rate):
    values = adam_step(*(state[at(slot)] for slot in range(4)), grad, step_rate, wd_rate)
    new[at(0)], new[at(1)], moments[at(0)], moments[at(1)] = values


def adam_mix_kernel(mix, depth, span, ga_ref, gb_ref, small,
                    mix_new, mix_moments, depth_new, depth_moments, span_new, span_moments):
    half = mix.shape[3]
    width = 2 * half
    sources = [ga_ref[:, 0:half], ga_ref[:, width:], gb_ref[:, 0:half], gb_ref[:, half:], ga_ref[:, half:width]]
    for i, grad in enumerate(sources):
        adam_at(mix, mix_new, mix_moments, lambda slot: (slot, i), grad, rate_mix, decay_rate)
    adam_at(depth, depth_new, depth_moments, lambda slot: (slice(None), slot), small[0:KERNEL, :], rate_depth, decay_rate)
    count = HEADS * KERNEL
    grad = jnp.concatenate([small[KERNEL : KERNEL + count // 2, 0:half], small[KERNEL : KERNEL + count // 2, half:]], axis=0)
    adam_at(span, span_new, span_moments, lambda slot: (slice(None), slot), grad, rate_span, decay_rate)


def adam_feed_kernel(place_ref, out, norm, up, bias, down, ga_ref, gb_ref, small,
                     out_new, out_moments, norm_new, norm_moments,
                     up_new, up_moments, bias_new, bias_moments, down_new, down_moments):
    half = down.shape[3]
    width = 2 * half
    hid_dev = down.shape[2]
    adam_at(up, up_new, up_moments, lambda slot: (slot, 0), ga_ref[0:hid_dev, :], rate_up, decay_rate)
    adam_at(down, down_new, down_moments, lambda slot: (slot, 0), gb_ref[0:hid_dev, :], rate_down, decay_rate)
    grad = jnp.concatenate([ga_ref[hid_dev:, :], gb_ref[hid_dev:, :]], axis=1)
    adam_at(out, out_new, out_moments, lambda slot: slot, grad, rate_out, decay_rate)
    adam_at(norm, norm_new, norm_moments, lambda slot: slot, small[0:4, :], rate_norm, 0.0)
    row = lax.broadcasted_iota(jnp.int32, (width, hid_dev), 0)
    col = lax.broadcasted_iota(jnp.int32, (width, hid_dev), 1)
    grad = jnp.zeros((1, hid_dev), full)
    for i in range(4):
        group, side = divmod(i, 2)
        line = jnp.where(place_ref[0] == group, small[4 + i : 5 + i, :], 0.0)
        here = (row + side * width == col + place_ref[1] * hid_dev).astype(full).astype(low)
        high = line.astype(low)
        rest = (line - high.astype(full)).astype(low)
        both = dot(jnp.concatenate([high, rest] + [jnp.zeros_like(high)] * 6, axis=0), here)
        grad = grad + both[0:1] + both[1:2]
    adam_at(bias, bias_new, bias_moments, lambda slot: slot, grad, rate_bias, 0.0)


def adam_call(kernel, inputs, shapes, scalars=0):
    vmem = pl.BlockSpec(memory_space=pltpu.VMEM)
    moved = sum(value.size for value in inputs) * 6
    return pl.pallas_call(
        kernel,
        in_specs=[pl.BlockSpec(memory_space=pltpu.SMEM)] * scalars + [vmem] * (len(inputs) - scalars),
        out_specs=[vmem] * len(shapes),
        out_shape=[struct(shape, full) for shape in shapes],
        compiler_params=pltpu.CompilerParams(vmem_limit_bytes=40 << 20),
        cost_estimate=pl.CostEstimate(flops=2 * moved, transcendentals=0, bytes_accessed=moved),
    )(*inputs)


def struct(shape, dtype):
    return jax.ShapeDtypeStruct(shape, dtype)


def rows_spec(rows, width, at=0):
    return pl.BlockSpec((rows, width), lambda i, *_: (i, at))


def whole(shape, index=None):
    index = index or (0,) * len(shape)
    return pl.BlockSpec(shape, lambda i, *_: index)


def call(kernel, grid, in_specs, out_specs, out_shape, scratch, flops, moved, limit, prefetch=0):
    return pl.pallas_call(
        kernel,
        grid_spec=pltpu.PrefetchScalarGridSpec(
            num_scalar_prefetch=prefetch, grid=grid, in_specs=in_specs, out_specs=out_specs, scratch_shapes=scratch),
        out_shape=out_shape,
        compiler_params=pltpu.CompilerParams(dimension_semantics=("arbitrary",), vmem_limit_bytes=limit << 20),
        cost_estimate=pl.CostEstimate(flops=int(flops), transcendentals=0, bytes_accessed=int(moved)),
    )


def once(shape, index=None):
    index = index or (0,) * len(shape)
    return pl.BlockSpec(shape, lambda i, *_: index, pipeline_mode=pl.Buffered(1))


class Tokens:
    def __init__(self, tokens, width, count, place):
        self.tokens, self.width, self.count, self.place = tokens, width, count, place
        self.length = length = tokens // count
        self.half = half = width // 2
        self.padded = length + 2 * EDGE
        self.wide, self.slim, self.lane = rows_spec(length, width), rows_spec(length, half), rows_spec(length, LANES)
        self.all_cols = rows_spec(length, 4 * half)
        self.heads = pl.BlockSpec((1, HEADS, length, length), lambda i, *_: (i, 0, 0, 0))
        self.any = pl.BlockSpec(memory_space=pl.ANY)
        self.low_wide, self.low_slim = struct((tokens, width), low), struct((tokens, half), low)
        self.low_half = struct((half, width), low)

    def order(self, hidden, grad_out, depth):
        return call(
            order_kernel, (self.count,),
            [self.wide, self.wide, once(depth.shape)],
            [self.wide] * 3, [self.low_wide] * 3,
            [pltpu.VMEM((self.padded, self.width), full)], 4e9, 8e6, 60,
        )(hidden, grad_out, depth)

    def forward(self, lens, hidden, e, wa, wb, span, hid):
        tokens, length, width, half = self.tokens, self.length, self.width, self.half
        V = pltpu.VMEM
        devices = 2 * hid // self.hid_dev
        blocks = [value.reshape(devices // 2, -1, value.shape[1]) for value in wa]
        bias = pl.BlockSpec((devices // 2, blocks[0].shape[1], LANES), lambda i, *_: (0, 0, 4 * half // LANES),
                            pipeline_mode=pl.Buffered(1))
        return call(
            forward_kernel, (self.count,),
            [self.wide, self.wide] + [self.any] * 4 + [bias, bias, once(span.shape)],
            [self.all_cols, self.slim, self.lane, self.slim, self.heads, self.slim, self.wide,
             whole((2, hid)), whole((LANES, half))],
            [struct((tokens, 4 * half), low), self.low_slim, struct((tokens, LANES), full), self.low_slim,
             struct((self.count, HEADS, length, length), low), self.low_slim, self.low_wide,
             struct((2, hid), full), struct((LANES, half), low)],
            [V((self.padded, half), full), V((length, KERNEL * half), full), V((width, 4 * half), low), V((width, width), low),
             V((width, half), low), V((LANES, KERNEL * half), low), pltpu.SemaphoreType.DMA((3, 2))],
            25e9, 25e6, 60, prefetch=2,
        )(lens, self.place, hidden, e, *wa, *wb, *blocks, span)

    def feed(self, y, hidden, grad_out, norm, feed, bias):
        width, half = self.width, self.half
        hid = bias.shape[1]
        V = pltpu.VMEM
        return call(
            feed_kernel, (self.count,),
            [self.wide, self.wide, self.wide, once(norm.shape), once((2 * hid, half)), once((2, hid)), once((2 * hid, half), (0, 1))],
            [self.wide, self.wide, whole((hid, width)), whole((hid, width)), whole((8, width))],
            [self.low_wide, self.low_wide, struct((hid, width), low), struct((hid, width), low), struct((8, width), full)],
            [V((self.length, 2 * hid), low), V((self.length, 2 * hid), full), V((self.length, 2 * hid), low),
             V((width, hid), full), V((width, hid), full), V((2, hid), full)],
            30e9, 20e6, 62, prefetch=1,
        )(self.place, y, hidden, grad_out, norm, feed, bias, feed)

    def split(self, gb, ctx, conv, result, wb):
        width, half = self.width, self.half
        V = pltpu.VMEM
        return call(
            split_kernel, (self.count,),
            [self.wide, self.slim, self.slim, self.wide, self.any, self.any],
            [self.wide, whole((half, width)), whole((half, width)), self.wide],
            [self.low_wide, self.low_half, self.low_half, self.low_wide],
            [V((width, width), full), V((width, width), low), pltpu.SemaphoreType.DMA((2,))], 6e9, 9e6, 60, prefetch=1,
        )(self.place, gb, ctx, conv, result, *wb)

    def attend_back(self, qwkv, a, gm):
        return call(
            attend_back_kernel, (self.count,),
            [self.all_cols, self.heads, self.slim], [self.slim, self.wide],
            [struct((self.tokens, self.half), full), self.low_wide],
            [], 15e9, 12e6, 60,
        )(qwkv, a, gm)

    def conv_back(self, gm, qwkv, u, p, gqa, wb, spant):
        length, width, half = self.length, self.width, self.half
        V = pltpu.VMEM
        return call(
            conv_back_kernel, (self.count,),
            [rows_spec(length, half, 1), self.wide, self.slim, self.lane, self.slim, self.any, self.any, once((LANES, half))],
            [self.wide, self.slim, self.wide, whole((LANES, half))],
            [self.low_wide, self.low_slim, self.low_wide, struct((LANES, half), full)],
            [V((self.padded, half), full), V((self.padded, half), full), V((self.padded, KERNEL * half), full),
             V((length, KERNEL * half), low), V((width, half), low), V((LANES, KERNEL * half), low), pltpu.SemaphoreType.DMA((2,))],
            16e9, 12e6, 60, prefetch=1,
        )(self.place, gm, qwkv, u, p, gqa, *wb, spant)

    def weights(self, hidden, e, gqw, gkv, gu, ge, d_span):
        width, half = self.width, self.half
        V = pltpu.VMEM
        return call(
            weight_kernel, (self.count,),
            [self.wide, self.wide, self.wide, self.wide, self.slim, self.wide, whole((LANES, half))],
            [whole((half, 3 * half))] * 2 + [whole((half, width))] * 2 + [whole((SMALL_ROWS, width))],
            [struct((half, 3 * half), low)] * 2 + [self.low_half] * 2 + [struct((SMALL_ROWS, width), low)],
            [V((self.padded, width), full), V((width, 3 * half), full), V((width, width), full), V((SMALL_ROWS, width), full)],
            12e9, 16e6, 60, prefetch=1,
        )(self.place, hidden, e, gqw, gkv, gu, ge, d_span)

    def input_grad(self, gb, gqw, gkv, ge, wa, depth):
        length, width = self.length, self.width
        V = pltpu.VMEM
        return call(
            input_kernel, (self.count,),
            [self.wide, self.wide, self.wide, self.wide, self.any, self.any, once(depth.shape)],
            [self.wide], [self.low_wide],
            [V((self.padded, width), full), V((length, width), full), V((width, 2 * width), low), pltpu.SemaphoreType.DMA((2,))],
            10e9, 14e6, 60, prefetch=1,
        )(self.place, gb, gqw, gkv, ge, *wa, depth)[0]


class Links:
    def __init__(self, mesh):
        self.size = mesh.shape["dp"]
        self.grp = mesh.shape["grp"]
        deep = 4 if self.size % 4 == 0 else 1
        rest = self.size // deep
        wide = 1 << ((rest.bit_length() - 1) // 2)
        self.sizes = (self.grp, deep, rest // wide, wide)
        self.strides = (0, rest, wide, 1)

    def place(self, dim):
        if dim == 0:
            return lax.axis_index("grp")
        return (lax.axis_index("dp") // self.strides[dim]) % self.sizes[dim]

    def swap(self, value, dim, shift):
        if dim == 0:
            return lax.ppermute(value, "grp", [(i, i ^ shift) for i in range(self.grp)])
        size, stride = self.sizes[dim], self.strides[dim]
        pairs = []
        for i in range(self.size):
            at = (i // stride) % size
            pairs.append((i, i + ((at ^ shift) - at) * stride))
        return lax.ppermute(value, "dp", pairs)

    def gather(self, block, dim):
        size, here = self.sizes[dim], self.place(dim)
        got = [block] + [self.swap(block, dim, k) for k in range(1, size)]
        slots = []
        for j in range(size):
            value = got[size - 1]
            for k in range(size - 1):
                value = jnp.where(here == (j ^ k), got[k], value)
            slots.append(value)
        return jnp.concatenate(slots, axis=dim)

    def scatter(self, block, dim, dtype):
        size, here = self.sizes[dim], self.place(dim)
        got = [lax.dynamic_slice_in_dim(block, here, 1, dim).astype(full)]
        for k in range(1, size):
            piece = lax.dynamic_slice_in_dim(block, here ^ k, 1, dim)
            got.append(self.swap(piece, dim, k).astype(full))
        while len(got) > 1:
            got = [got[i] + got[i + 1] for i in range(0, len(got), 2)]
        return got[0].astype(dtype)

    def join(self, keep, piece):
        return keep.astype(full) + self.swap(piece, 0, 1).astype(full)

    def scatter_both(self, a, b, small, dim_a, dim_b, end):
        a = self.scatter(a, dim_a, end)
        cols = b.shape[-1]
        size, here = self.sizes[dim_b], self.place(dim_b)
        small = small.astype(low)
        keep = lax.dynamic_slice_in_dim(b, here, 1, dim_b)
        got, sums = [keep.astype(full)], [small.astype(full)]
        for k in range(1, size):
            piece = lax.dynamic_slice_in_dim(b, here ^ k, 1, dim_b).reshape(-1, cols)
            message = self.swap(jnp.concatenate([piece, small], axis=0), dim_b, k)
            got.append(message[: -small.shape[0]].reshape(keep.shape).astype(full))
            sums.append(message[-small.shape[0] :].astype(full))
        while len(got) > 1:
            got = [got[i] + got[i + 1] for i in range(0, len(got), 2)]
            sums = [sums[i] + sums[i + 1] for i in range(0, len(sums), 2)]
        return a, got[0].astype(end), sums[0].astype(end)


def on_device(links, hidden, grad_out, seq_lens, mix_state, out_state, depth_state, span_state, norm_state,
              up_state, bias_state, down_state):
    both = ("grp", "dp")
    barrier = lax.optimization_barrier
    width = hidden.shape[1]
    half = width // 2
    hid_dev = up_state.shape[3]
    rows_dev = mix_state.shape[2]
    up_state = jnp.swapaxes(up_state, 2, 3)
    depth_state = jnp.swapaxes(depth_state, 0, 1)
    span_state = jnp.transpose(span_state, (2, 0, 1))
    place = jnp.stack([links.place(0), lax.axis_index("dp")]).astype(jnp.int32)
    tokens = Tokens(hidden.shape[0], width, seq_lens.shape[0], place)
    tokens.hid_dev = hid_dev

    mix_low = mix_state[0].astype(low)
    bias_row = jnp.pad(bias_state[0].astype(low), ((0, rows_dev - 1), (0, LANES - hid_dev)))
    shard = jnp.concatenate(
        [mix_low[0], mix_low[4], mix_low[1], mix_low[2], bias_row, out_state[0].astype(low), mix_low[3]], axis=1)
    feed_shard = jnp.concatenate([up_state[0, 0], down_state[0, 0]], axis=1).astype(low)
    feed = lax.all_gather(feed_shard, both, axis=0, tiled=True)
    block = links.gather(shard.reshape((1, 1, 1, 1) + shard.shape), 1)
    block, hidden_o, grad_o, e = barrier((block, *tokens.order(hidden, grad_out, depth_state)))
    split = 4 * half + LANES
    wa, wb = block[..., :split], block[..., split:]
    for dim_a, dim_b in ((2, 3), (3, 2)):
        wa, wb = links.gather(wa, dim_a), links.gather(wb, dim_b)
    wa, wb = wa.reshape(half, -1), wb.reshape(half, -1)
    wa, wb = (wa, links.swap(wa, 0, 1)), (wb, links.swap(wb, 0, 1))

    qwkv, u, p, conv, a, ctx, y, bias, spant = tokens.forward(
        seq_lens, hidden_o, e, wa, wb, span_state, hid_dev * links.size)
    result, gb, keep_f, piece_f, small = tokens.feed(y, hidden_o, grad_o, norm_state, feed, bias)

    def blocks(value):
        return value.reshape((1,) + links.sizes[1:] + (-1, value.shape[-1]))

    small = small.astype(low).reshape(-1, half)
    d_feed = links.join(keep_f, piece_f)
    small = links.join(small, small)
    gm, keep_o, piece_o, result = tokens.split(gb, ctx, conv, result, wb)
    d_out = links.join(keep_o, piece_o)
    rows = jnp.concatenate([blocks(d_feed), blocks(d_out)], axis=4).astype(low)
    *sums, gm = barrier((rows[..., :half], rows[..., half:], small.astype(low), gm))
    sums = links.scatter_both(*sums, 3, 2, low)
    gqa, gkv = tokens.attend_back(qwkv, a, gm)
    *sums, gqa, gkv = barrier((*sums, gqa, gkv))
    sums = links.scatter_both(*sums, 2, 3, low)
    gqw, gu, ge, d_span = tokens.conv_back(gm, qwkv, u, p, gqa, wb, spant)
    *sums, gqw, gu, ge, d_span = barrier((*sums, gqw, gu, ge, d_span))
    feed_sums = links.scatter_both(*sums, 1, 1, full)
    keep_a, piece_a, keep_b, piece_b, small = tokens.weights(hidden_o, e, gqw, gkv, gu, ge, d_span)
    *feed_sums, keep_a, piece_a, keep_b, piece_b, small = barrier((*feed_sums, keep_a, piece_a, keep_b, piece_b, small))

    sums = (blocks(links.join(keep_a, piece_a).astype(low)), blocks(links.join(keep_b, piece_b).astype(low)),
            links.join(small, small).astype(low))
    *sums, gqw, ge = barrier((*sums, gqw, ge))
    sums = links.scatter_both(*sums, 3, 2, low)
    gx = tokens.input_grad(gb, gqw, gkv, ge, wa, depth_state)
    *sums, gx = barrier((*sums, gx))
    sums = barrier(links.scatter_both(*sums, 2, 3, low))
    grad_a, grad_b, small = links.scatter_both(*sums, 1, 1, full)

    def twice(state, at=0):
        shape = state.shape[:at] + (2,) + state.shape[at + 1 :]
        return [shape, shape]

    def flat(value):
        return value.reshape(-1, value.shape[-1])

    feed_a, feed_b, feed_small = feed_sums
    feed_out = adam_call(
        adam_feed_kernel,
        [place, out_state, norm_state, up_state, bias_state, down_state, flat(feed_a), flat(feed_b), feed_small.reshape(-1, width)],
        twice(out_state) + twice(norm_state) + twice(up_state) + twice(bias_state) + twice(down_state), scalars=1)
    mixed = adam_call(
        adam_mix_kernel,
        [mix_state, depth_state, span_state, flat(grad_a), flat(grad_b), small],
        twice(mix_state) + twice(depth_state, 1) + twice(span_state, 1))
    depth_out = [jnp.swapaxes(value, 0, 1) for value in mixed[2:4]]
    span_out = [jnp.transpose(value, (1, 2, 0)) for value in mixed[4:]]
    up_out = [jnp.swapaxes(value, 2, 3) for value in feed_out[4:6]]
    return (result, gx, *mixed[:2], *feed_out[:2], *depth_out, *span_out, *feed_out[2:4], *up_out, *feed_out[6:])


def solution(mesh):
    both = ("grp", "dp")
    mix, out = P(None, None, both, None), P(None, both, None)
    up, bias, down = P(None, "grp", None, "dp"), P(None, "grp", "dp"), P(None, "grp", "dp", None)
    rows = P(both, None)
    return jax.shard_map(
        functools.partial(on_device, Links(mesh)),
        mesh=mesh,
        in_specs=(rows, rows, P(both), mix, out, P(), P(), P(), up, bias, down),
        out_specs=(rows, rows, mix, mix, out, out, P(), P(), P(), P(), P(), P(), up, up, bias, bias, down, down),
        check_vma=False,
    )
```

```python
import functools

import jax
import jax.numpy as jnp
from jax import lax
from jax.experimental import pallas as pl
from jax.experimental.pallas import tpu as pltpu
from jax.sharding import PartitionSpec as P

HEADS = 6
HS = 64
KERNEL = 9
STEP = 7
REACH = KERNEL // 2
TAP = 8
LANES = 128
PAD = 8
EDGE = REACH * PAD

beta_one = 0.9
beta_two = 0.999
adam_eps = 1e-06
ema_rate = 0.99
decay_rate = 0.01
rate_mix = 0.06
rate_out = 0.12
rate_depth = 0.4
rate_span = 0.08
rate_norm = 0.5
rate_up = 0.08
rate_bias = 0.3
rate_down = 0.04

low = jnp.bfloat16
full = jnp.float32
NN = (((1,), (0,)), ((), ()))
NT = (((1,), (1,)), ((), ()))
TN = (((0,), (0,)), ((), ()))


def dot(left, right, dims=NN):
    return lax.dot_general(left, right, dims, preferred_element_type=full)


def rounded(value):
    return value.astype(low).astype(full)


def row_loop(rows, chunk, body):
    for r in range(0, rows, chunk):
        body(r)


def spread_table(width):
    row = lax.broadcasted_iota(jnp.int32, (LANES, 1), 0)
    col = lax.broadcasted_iota(jnp.int32, (1, KERNEL * width), 1)
    head = row % TAP
    first = (row // TAP) * width + head * HS
    first = jnp.where(head < HEADS, first, -HS)
    return ((col >= first) & (col < first + HS)).astype(full).astype(low)


def tap_table():
    row = lax.broadcasted_iota(jnp.int32, (LANES, HEADS * KERNEL), 0)
    col = lax.broadcasted_iota(jnp.int32, (LANES, HEADS * KERNEL), 1)
    return ((col % KERNEL) * TAP + col // KERNEL == row).astype(full).astype(low)


def copy_halves(place_ref, mine, other, target, sems, first, cols):
    rows = mine.shape[0]
    copies = []
    for i, (half, at) in enumerate(((mine, place_ref[0]), (other, 1 - place_ref[0]))):
        copy = pltpu.make_async_copy(
            half.at[:, pl.ds(first, cols)], target.at[pl.ds(pl.multiple_of(at * rows, rows), rows), :], sems.at[i])
        copy.start()
        copies.append(copy)
    return copies


def put_blocks(place_ref, value_ref, keep_ref, piece_ref):
    devices, _, half = keep_ref.shape
    parts = value_ref.shape[1] // half
    rows = half // devices
    for ref, at in ((keep_ref, place_ref[0]), (piece_ref, 1 - place_ref[0])):
        for m in range(parts):
            value = value_ref[pl.ds(pl.multiple_of(at * half, half), half), m * half : (m + 1) * half]
            for n in range(devices):
                ref[n, m * rows : (m + 1) * rows, :] = value[n * rows : (n + 1) * rows].astype(low)


def fill_padded(ref, value):
    rows = value.shape[0]
    value = value.astype(full)
    place = lax.broadcasted_iota(jnp.int32, (PAD, 1), 0)
    ref[EDGE : EDGE + rows, :] = value
    for i in range(REACH):
        before = value[rows - EDGE + i * PAD : rows - EDGE + (i + 1) * PAD]
        ref[i * PAD : (i + 1) * PAD, :] = jnp.where(place == 0, 0.0, pltpu.roll(before, 1, 0))
        after = value[i * PAD : (i + 1) * PAD]
        ref[EDGE + rows + i * PAD : EDGE + rows + (i + 1) * PAD, :] = jnp.where(
            place == PAD - 1, 0.0, pltpu.roll(after, PAD - 1, 0))


def order_matrix(rows, back=False):
    row = lax.broadcasted_iota(jnp.int32, (rows, rows), 0)
    col = lax.broadcasted_iota(jnp.int32, (1, rows), 1)
    places = rows // PAD
    at = (col % PAD) * places + col // PAD if back else (col % places) * PAD + col // places
    return (row == at).astype(full).astype(low)


def order_kernel(x_ref, g_ref, depth_ref, xo_ref, go_ref, e_ref, xpad):
    rows, width = x_ref.shape
    order = order_matrix(rows)
    x = dot(order, x_ref[...])
    xo_ref[...] = x.astype(low)
    go_ref[...] = dot(order, g_ref[...]).astype(low)
    fill_padded(xpad, x)

    rates = [rounded(depth_ref[j, 0:1]) for j in range(KERNEL)]

    def depth_rows(r):
        acc = rates[0] * xpad[pl.ds(r, 32), :]
        for j in range(1, KERNEL):
            acc = acc + rates[j] * xpad[pl.ds(r + PAD * j, 32), :]
        e_ref[pl.ds(r, 32), :] = acc.astype(low)

    row_loop(rows, 32, depth_rows)


def forward_kernel(lens_ref, place_ref, x_ref, e_ref, wam_ref, wao_ref, wbm_ref, wbo_ref, bm_ref, bo_ref, span_ref,
                   qwkv_ref, u_ref, p_ref, conv_ref, a_ref, ctx_ref, y_ref, bias_ref, spant_ref,
                   wpad, taps, wa_ref, wo_ref, w3_ref, spread_ref, sems):
    rows, width = x_ref.shape
    half = width // 2

    @pl.when(pl.program_id(0) == 0)
    def _():
        copies = copy_halves(place_ref, wam_ref, wao_ref, wa_ref, sems.at[0], 0, 4 * half)
        copies += copy_halves(place_ref, wbm_ref, wbo_ref, wo_ref, sems.at[1], 0, width)
        copies += copy_halves(place_ref, wbm_ref, wbo_ref, w3_ref, sems.at[2], width, half)
        spread_ref[...] = spread_table(half)
        spant_ref[...] = dot(tap_table(), span_ref[:, 0, :].astype(low)).astype(low)
        hid_dev = bias_ref.shape[1] // bm_ref.shape[0]
        for n in range(bm_ref.shape[0]):
            cols = slice(n * hid_dev, (n + 1) * hid_dev)
            mine, other = bm_ref[n].astype(full)[0:1, 0:hid_dev], bo_ref[n].astype(full)[0:1, 0:hid_dev]
            bias_ref[0:1, cols] = jnp.where(place_ref[0] == 0, mine, other)
            bias_ref[1:2, cols] = jnp.where(place_ref[0] == 0, other, mine)
        for copy in copies:
            copy.wait()

    x = x_ref[...]
    for c in range(4):
        qwkv_ref[:, c * half : (c + 1) * half] = dot(x, wa_ref[:, c * half : (c + 1) * half]).astype(low)
    u = dot(e_ref[...], w3_ref[...]).astype(low)
    u_ref[...] = u
    r = (u.astype(full) * qwkv_ref[:, 0:half].astype(full)).astype(low)
    logits = rounded(dot(r, spant_ref[...], NT))
    lt = logits.T[0 : KERNEL * TAP].reshape(KERNEL, TAP, rows)
    top = jnp.max(lt, axis=0, keepdims=True)
    ex = jnp.exp(lt - top)
    pt = (ex / jnp.sum(ex, axis=0, keepdims=True)).reshape(KERNEL * TAP, rows)
    p = jnp.concatenate([pt, jnp.zeros((LANES - KERNEL * TAP, rows), full)], axis=0).T
    p_ref[...] = p
    fill_padded(wpad, qwkv_ref[:, half : 2 * half])
    p_low = p.astype(low)
    for j in range(KERNEL):
        taps[:, j * half : (j + 1) * half] = dot(p_low, spread_ref[:, j * half : (j + 1) * half])

    def conv_rows(r):
        acc = taps[pl.ds(r, 32), 0:half] * wpad[pl.ds(r, 32), :]
        for j in range(1, KERNEL):
            acc = acc + taps[pl.ds(r, 32), j * half : (j + 1) * half] * wpad[pl.ds(r + PAD * j, 32), :]
        conv_ref[pl.ds(r, 32), :] = acc.astype(low)

    row_loop(rows, 32, conv_rows)
    seq_len = lens_ref[pl.program_id(0)]
    lane = lax.broadcasted_iota(jnp.int32, (1, LANES), 1)
    row = lax.broadcasted_iota(jnp.int32, (1, rows), 1)
    live = (row % PAD) * (rows // PAD) + row // PAD < seq_len
    for pair in range(HEADS // 2):
        at = pair * LANES
        q = qwkv_ref[:, at : at + LANES]
        k = qwkv_ref[:, 2 * half + at : 2 * half + at + LANES]
        v = qwkv_ref[:, 3 * half + at : 3 * half + at + LANES]
        outs = []
        for side in range(2):
            pick = jnp.where((lane // HS) == side, HS ** (-0.5), 0.0).astype(low)
            scores = dot(q * pick, k, NT)
            scores = jnp.where(live, scores, -1000000000.0)
            top = jnp.max(scores, axis=1, keepdims=True)
            ex = jnp.exp(scores - top)
            a = (ex * (1.0 / jnp.sum(ex, axis=1, keepdims=True))).astype(low)
            a_ref[0, 2 * pair + side] = a
            outs.append(dot(a, v))
        ctx_ref[:, at : at + LANES] = jnp.where((lane // HS) == 0, outs[0], outs[1]).astype(low)
    y_ref[...] = (dot(ctx_ref[...], wo_ref[0:half, :]) + dot(conv_ref[...], wo_ref[half:, :])).astype(low)


def normed(value):
    centered = value - jnp.mean(value, axis=1, keepdims=True)
    variance = jnp.mean(centered * centered, axis=1, keepdims=True)
    rstd = lax.rsqrt(variance + 1e-12)
    return centered * rstd, rstd


def feed_kernel(count, place_ref, norm_ref, bias_ref, y_hbm, x_hbm, g_hbm, ctx_hbm, conv_hbm, feed_hbm, wbm_hbm, wbo_hbm,
                small_ref, res_hbm, gb_hbm, gm_hbm, keep_hbm, piece_hbm, keep_o_hbm, piece_o_hbm,
                y_s, x_s, g_s, m_s, up_s, down_s, wo_s, act_s, gpre_s, res_s, gb_s, gm_s, ft_s, got_s, df_s, do_s,
                in_sems, out_sems):
    tokens, width = y_s.shape
    half = width // 2
    hid = bias_ref.shape[1]
    length = tokens // count
    waits, outs = {}, []

    def fetch(name, source, target):
        copy = pltpu.make_async_copy(source, target, in_sems.at[len(waits)])
        copy.start()
        waits[name] = copy

    def put(source, target):
        copy = pltpu.make_async_copy(source, target, out_sems.at[len(outs)])
        copy.start()
        outs.append(copy)

    seqs = [slice(n * length, (n + 1) * length) for n in range(count)]
    for n, rows in enumerate(seqs):
        fetch(("y", n), y_hbm.at[rows], y_s.at[rows])
        fetch(("x", n), x_hbm.at[rows], x_s.at[rows])
        if n == 0:
            fetch("up", feed_hbm.at[:, pl.ds(0, half)], up_s)
            fetch("down", feed_hbm.at[:, pl.ds(half, half)], down_s)
        fetch(("g", n), g_hbm.at[rows], g_s.at[rows])
        if n == 0:
            for i, (part, at) in enumerate(((wbm_hbm, place_ref[0]), (wbo_hbm, 1 - place_ref[0]))):
                fetch(("wo", i), part.at[:, pl.ds(0, width)], wo_s.at[pl.ds(pl.multiple_of(at * half, half), half), :])
    fetch("ctx", ctx_hbm, m_s.at[:, pl.ds(0, half)])
    fetch("conv", conv_hbm, m_s.at[:, pl.ds(half, half)])

    g1, c1, g2, c2 = (norm_ref[0, i : i + 1] for i in range(4))
    sums = [jnp.zeros((1, width), full) for _ in range(4)]
    dbias = [jnp.zeros((1, hid), full) for _ in range(2)]
    groups = [(slice(g * hid, (g + 1) * hid), slice(g * half, (g + 1) * half)) for g in range(2)]
    kept = [{} for _ in seqs]

    def wait(name):
        if name in waits:
            waits.pop(name).wait()

    def enter(n):
        wait(("y", n))
        wait(("x", n))
        zh1, rstd1 = normed(y_s[seqs[n]].astype(full) + x_s[seqs[n]].astype(full))
        f = (zh1 * g1 + c1).astype(low)
        kept[n].update(zh1=zh1, rstd1=rstd1, f=f, parts=[])
        ft_s[:, seqs[n]] = f.T

    def ahead(n, g):
        hidden, cols = groups[g]
        wait("up")
        pre = dot(kept[n]["f"][:, cols], up_s[hidden, :], NT) + bias_ref[g : g + 1, :]
        cdf = 0.5 * (1.0 + lax.erf(pre * 2.0 ** (-0.5)))
        act_s[seqs[n], hidden] = (pre * cdf).astype(low)
        gpre_s[seqs[n], hidden] = (cdf + pre * (jnp.exp(-0.5 * pre * pre) * 0.3989422804014327)).astype(low)
        wait("down")
        kept[n]["parts"].append(rounded(dot(act_s[seqs[n], hidden], down_s[hidden, :])))

    def turn(n):
        rows = seqs[n]
        h1 = kept[n]["zh1"] * g1 + c1
        zh2, rstd2 = normed(h1 + jnp.concatenate(kept[n]["parts"], axis=1))
        result = (zh2 * g2 + c2).astype(low)
        res_s[rows] = dot(order_matrix(length, True), result).astype(low)
        put(res_s.at[rows], res_hbm.at[rows])
        wait(("g", n))
        grad = g_s[rows].astype(full)
        sums[2] = sums[2] + jnp.sum(grad * zh2, axis=0, keepdims=True)
        sums[3] = sums[3] + jnp.sum(grad, axis=0, keepdims=True)
        dz = grad * g2
        gz = (dz - jnp.mean(dz, axis=1, keepdims=True) - zh2 * jnp.mean(dz * zh2, axis=1, keepdims=True)) * rstd2
        go = gz.astype(low)
        got_s[:, rows] = go.T
        kept[n].update(gz=gz, go=go, parts=[])

    def behind(n, g):
        hidden, cols = groups[g]
        slope = gpre_s[seqs[n], hidden].astype(full)
        gpre = (dot(kept[n]["go"][:, cols], down_s[hidden, :], NT) * slope).astype(low)
        gpre_s[seqs[n], hidden] = gpre
        dbias[g] = dbias[g] + jnp.sum(gpre.astype(full), axis=0, keepdims=True)
        kept[n]["parts"].append(rounded(dot(gpre, up_s[hidden, :])))

    def leave(n):
        rows, zh1 = seqs[n], kept[n]["zh1"]
        gh1 = kept[n]["gz"] + jnp.concatenate(kept[n]["parts"], axis=1)
        sums[0] = sums[0] + jnp.sum(gh1 * zh1, axis=0, keepdims=True)
        sums[1] = sums[1] + jnp.sum(gh1, axis=0, keepdims=True)
        dz1 = gh1 * g1
        gy = (dz1 - jnp.mean(dz1, axis=1, keepdims=True) - zh1 * jnp.mean(dz1 * zh1, axis=1, keepdims=True)) * kept[n]["rstd1"]
        gb_s[rows] = gy.astype(low)
        put(gb_s.at[rows], gb_hbm.at[rows])

    def through(n):
        rows = seqs[n]
        wait(("wo", 0))
        wait(("wo", 1))
        gm_s[rows] = dot(gb_s[rows], wo_s[...], NT).astype(low)
        put(gm_s.at[rows], gm_hbm.at[rows])

    first, *rest = range(count)
    enter(first)
    ahead(first, 0)
    for n in rest:
        enter(n)
    ahead(first, 1)
    for n in rest:
        ahead(n, 0)
        turn(n - 1)
        ahead(n, 1)
        behind(n - 1, 0)
        if n == rest[-1]:
            turn(n)
        behind(n - 1, 1)
        if n == rest[-1]:
            behind(n, 0)
        leave(n - 1)
        if n == rest[-1]:
            behind(n, 1)
        through(n - 1)
    if not rest:
        turn(first)
        behind(first, 0)
        behind(first, 1)
    leave(count - 1)
    through(count - 1)

    for i, (at, target) in enumerate(((1 - place_ref[0], piece_hbm), (place_ref[0], keep_hbm))):
        hidden = pl.ds(pl.multiple_of(at * hid, LANES), hid)
        cols = pl.ds(pl.multiple_of(at * half, half), half)
        df_s[i, :, 0:half] = dot(ft_s[cols, :], gpre_s[:, hidden]).astype(low).T
        df_s[i, :, half:] = dot(got_s[cols, :], act_s[:, hidden]).astype(low).T
        put(df_s.at[i], target)
    wait("ctx")
    wait("conv")
    do_s[...] = dot(m_s[...].T, gb_s[...]).astype(low)
    for at, target in ((1 - place_ref[0], piece_o_hbm), (place_ref[0], keep_o_hbm)):
        put(do_s.at[pl.ds(pl.multiple_of(at * half, half), half), :], target)
    for i in range(4):
        g, side = divmod(i, 2)
        for j in range(2):
            small_ref[8 * j + i : 8 * j + i + 1, :] = sums[i][:, j * half : (j + 1) * half]
            at = side * width + j * half
            small_ref[8 * j + 4 + i : 8 * j + 5 + i, :] = dbias[g][:, at : at + half]
    for copy in outs:
        copy.wait()


def attend_back_kernel(qwkv_ref, a_ref, gctx_ref, gqa_ref, gkv_ref):
    half = HEADS * HS
    lane = lax.broadcasted_iota(jnp.int32, (1, LANES), 1)
    for pair in range(HEADS // 2):
        at = pair * LANES
        q = qwkv_ref[:, at : at + LANES]
        k = qwkv_ref[:, 2 * half + at : 2 * half + at + LANES]
        v = qwkv_ref[:, 3 * half + at : 3 * half + at + LANES]
        gctx = gctx_ref[:, at : at + LANES]
        qt, gctxt = q.T, gctx.T
        gqs, gks, gvs = [], [], []
        for side in range(2):
            pick = jnp.where((lane // HS) == side, 1.0, 0.0).astype(low)
            a_low = a_ref[0, 2 * pair + side]
            a = a_low.astype(full)
            ga = dot(gctx * pick, v, NT)
            gs = (a * (ga - jnp.sum(a * ga, axis=1, keepdims=True))).astype(low)
            gqs.append(dot(gs, k))
            gks.append(dot(qt, gs))
            gvs.append(dot(gctxt, a_low))
        first = (lane // HS) == 0
        gqa_ref[:, at : at + LANES] = jnp.where(first, gqs[0], gqs[1]) * HS ** (-0.5)
        gk = jnp.concatenate([gks[0][0:HS], gks[1][HS:]], axis=0) * HS ** (-0.5)
        gv = jnp.concatenate([gvs[0][0:HS], gvs[1][HS:]], axis=0)
        gkv_ref[:, at : at + LANES] = gk.T.astype(low)
        gkv_ref[:, half + at : half + at + LANES] = gv.T.astype(low)


def conv_back_kernel(place_ref, gconv_ref, qw_ref, u_ref, p_ref, gqa_ref, wbm_ref, wbo_ref, spant_ref,
                     gqw_ref, gu_ref, ge_ref, dspan_ref,
                     wpad, gpad, taps, prods, w3_ref, spread_ref, sems):
    rows, half = u_ref.shape

    @pl.when(pl.program_id(0) == 0)
    def _():
        copies = copy_halves(place_ref, wbm_ref, wbo_ref, w3_ref, sems, 2 * half, half)
        dspan_ref[...] = jnp.zeros_like(dspan_ref)
        spread_ref[...] = spread_table(half)
        for copy in copies:
            copy.wait()

    fill_padded(wpad, qw_ref[:, half:])
    fill_padded(gpad, gconv_ref[...])
    p = p_ref[...]
    p_low = p.astype(low)
    for j in range(KERNEL):
        cols = slice(j * half, (j + 1) * half)
        fill_padded(taps.at[:, cols], dot(p_low, spread_ref[:, cols]))

    def conv_rows(r):
        here = gpad[pl.ds(r + EDGE, 32), :]
        acc = None
        for j in range(KERNEL):
            cols = slice(j * half, (j + 1) * half)
            prods[pl.ds(r, 32), cols] = (here * wpad[pl.ds(r + PAD * j, 32), :]).astype(low)
            back = pl.ds(r + PAD * (2 * REACH - j), 32)
            term = taps[back, cols] * gpad[back, :]
            acc = term if acc is None else acc + term
        gqw_ref[pl.ds(r, 32), half:] = acc.astype(low)

    row_loop(rows, 32, conv_rows)
    gp = dot(prods[...], spread_ref[...], NT)
    gpt = gp.T[0 : KERNEL * TAP].reshape(KERNEL, TAP, rows)
    pt = p.T[0 : KERNEL * TAP].reshape(KERNEL, TAP, rows)
    glt = pt * (gpt - jnp.sum(pt * gpt, axis=0, keepdims=True))
    glt = jnp.concatenate([glt.reshape(KERNEL * TAP, rows), jnp.zeros((LANES - KERNEL * TAP, rows), full)], axis=0)
    gl = glt.T.astype(low)
    q = qw_ref[:, 0:half].astype(full)
    u = u_ref[...].astype(full)
    r = (u * q).astype(low)
    dspan_ref[...] += dot(glt.astype(low), r)
    gr = dot(gl, spant_ref[...]).astype(low).astype(full)
    gqw_ref[:, 0:half] = (gqa_ref[...] + gr * u).astype(low)
    gu = (gr * q).astype(low)
    gu_ref[...] = gu
    ge_ref[...] = dot(gu, w3_ref[...], NT).astype(low)


SMALL_ROWS = 2 * KERNEL + HEADS * KERNEL


def weight_kernel(place_ref, x_ref, e_ref, gqw_ref, gkv_ref, gu_ref, ge_ref, dspan_ref,
                  keep_a_ref, piece_a_ref, keep_b_ref, piece_b_ref, small_ref,
                  xpad, acc_a, acc_b, small):
    step, last = pl.program_id(0), pl.num_programs(0) - 1
    rows, width = x_ref.shape
    half = width // 2

    @pl.when(step == 0)
    def _():
        acc_a[...] = jnp.zeros_like(acc_a)
        acc_b[...] = jnp.zeros_like(acc_b)
        small[...] = jnp.zeros_like(small)

    x = x_ref[...]
    xt = x.T
    acc_a[:, 0:width] += dot(xt, gqw_ref[...])
    acc_a[:, width:] += dot(xt, gkv_ref[:, 0:half])
    acc_b[:, 0:half] += dot(xt, gkv_ref[:, half:])
    acc_b[:, half:] += dot(e_ref[...].T, gu_ref[...])
    fill_padded(xpad, x)
    for c in range(0, width, LANES):
        cols = slice(c, c + LANES)

        sums = [jnp.zeros((PAD, LANES), full) for _ in range(KERNEL)]
        for r in range(0, rows, 64):
            ge = ge_ref[pl.ds(r, 64), cols].astype(full)
            for j in range(KERNEL):
                prod = ge * xpad[pl.ds(r + PAD * j, 64), cols]
                sums[j] = sums[j] + jnp.sum(prod.reshape(PAD, PAD, LANES), axis=0)
        for j in range(KERNEL):
            small[j : j + 1, cols] += jnp.sum(sums[j], axis=0, keepdims=True)

    @pl.when(step == last)
    def _():
        put_blocks(place_ref, acc_a, keep_a_ref, piece_a_ref)
        put_blocks(place_ref, acc_b, keep_b_ref, piece_b_ref)
        for side in range(2):
            small_ref[side * KERNEL : (side + 1) * KERNEL, :] = small[0:KERNEL, side * half : (side + 1) * half]
        small_ref[2 * KERNEL :, :] = dot(tap_table(), dspan_ref[...].astype(low), TN)


def input_kernel(place_ref, gb_ref, gqw_ref, gkv_ref, ge_ref, wam_ref, wao_ref, depth_ref,
                 gx_ref, gepad, gx_s, wa_ref, sems):
    rows, width = gb_ref.shape

    @pl.when(pl.program_id(0) == 0)
    def _():
        for copy in copy_halves(place_ref, wam_ref, wao_ref, wa_ref, sems, 0, 2 * width):
            copy.wait()

    fill_padded(gepad, ge_ref[...])
    gx_s[...] = gb_ref[...].astype(full) + dot(gqw_ref[...], wa_ref[:, 0:width], NT) + dot(gkv_ref[...], wa_ref[:, width:], NT)

    rates = [rounded(depth_ref[j, 0:1]) for j in range(KERNEL)]

    def shift_rows(r):
        acc = gx_s[pl.ds(r, 32), :]
        for j in range(KERNEL):
            acc = acc + rates[j] * gepad[pl.ds(r + PAD * (2 * REACH - j), 32), :]
        gx_s[pl.ds(r, 32), :] = acc

    row_loop(rows, 32, shift_rows)
    gx_ref[...] = dot(order_matrix(rows, True), gx_s[...].astype(low)).astype(low)


def adam_step(old, one, two, mean, grad, step_rate, wd_rate):
    moment_one = beta_one * one + (1.0 - beta_one) * grad
    moment_two = beta_two * two + (1.0 - beta_two) * grad * grad
    scaled_one = moment_one / (1.0 - beta_one**STEP)
    scaled_two = moment_two / (1.0 - beta_two**STEP)
    weight = old - step_rate * (scaled_one / (jnp.sqrt(scaled_two) + adam_eps) + wd_rate * old)
    return weight, ema_rate * mean + (1.0 - ema_rate) * weight, moment_one, moment_two


def adam_at(state, new, moments, at, grad, step_rate, wd_rate):
    values = adam_step(*(state[at(slot)] for slot in range(4)), grad, step_rate, wd_rate)
    new[at(0)], new[at(1)], moments[at(0)], moments[at(1)] = values


def adam_mix_kernel(mix, depth, span, ga_ref, gb_ref, small,
                    mix_new, mix_moments, depth_new, depth_moments, span_new, span_moments):
    rows = mix.shape[2]
    sources = [(ga_ref, 0), (ga_ref, 2), (gb_ref, 0), (gb_ref, 1), (ga_ref, 1)]
    for i, (ref, at) in enumerate(sources):
        adam_at(mix, mix_new, mix_moments, lambda slot: (slot, i), ref[at * rows : (at + 1) * rows, :], rate_mix, decay_rate)
    grad = jnp.concatenate([small[0:KERNEL], small[KERNEL : 2 * KERNEL]], axis=1)
    adam_at(depth, depth_new, depth_moments, lambda slot: (slice(None), slot), grad, rate_depth, decay_rate)
    adam_at(span, span_new, span_moments, lambda slot: (slice(None), slot), small[2 * KERNEL :], rate_span, decay_rate)


def adam_feed_kernel(place_ref, out, norm, up, bias, down, ga_ref, gb_ref, small,
                     out_new, out_moments, norm_new, norm_moments,
                     up_new, up_moments, bias_new, bias_moments, down_new, down_moments):
    half = down.shape[3]
    width = 2 * half
    hid_dev = down.shape[2]
    adam_at(up, up_new, up_moments, lambda slot: (slot, 0), ga_ref[0:hid_dev, :], rate_up, decay_rate)
    adam_at(down, down_new, down_moments, lambda slot: (slot, 0), gb_ref[0:hid_dev, :], rate_down, decay_rate)
    grad = jnp.concatenate([ga_ref[hid_dev:, :], gb_ref[hid_dev:, :]], axis=1)
    adam_at(out, out_new, out_moments, lambda slot: slot, grad, rate_out, decay_rate)
    lines = jnp.concatenate([small[0:8], small[8:16]], axis=1)
    adam_at(norm, norm_new, norm_moments, lambda slot: slot, lines[0:4], rate_norm, 0.0)
    row = lax.broadcasted_iota(jnp.int32, (width, hid_dev), 0)
    col = lax.broadcasted_iota(jnp.int32, (width, hid_dev), 1)
    grad = jnp.zeros((1, hid_dev), full)
    for i in range(4):
        group, side = divmod(i, 2)
        line = jnp.where(place_ref[0] == group, lines[4 + i : 5 + i, :], 0.0)
        here = (row + side * width == col + place_ref[1] * hid_dev).astype(full).astype(low)
        high = line.astype(low)
        rest = (line - high.astype(full)).astype(low)
        both = dot(jnp.concatenate([high, rest] + [jnp.zeros_like(high)] * 6, axis=0), here)
        grad = grad + both[0:1] + both[1:2]
    adam_at(bias, bias_new, bias_moments, lambda slot: slot, grad, rate_bias, 0.0)


def adam_call(kernel, inputs, shapes, scalars=0):
    vmem = pl.BlockSpec(memory_space=pltpu.VMEM)
    moved = sum(value.size for value in inputs) * 6
    return pl.pallas_call(
        kernel,
        in_specs=[pl.BlockSpec(memory_space=pltpu.SMEM)] * scalars + [vmem] * (len(inputs) - scalars),
        out_specs=[vmem] * len(shapes),
        out_shape=[struct(shape, full) for shape in shapes],
        compiler_params=pltpu.CompilerParams(vmem_limit_bytes=40 << 20),
        cost_estimate=pl.CostEstimate(flops=2 * moved, transcendentals=0, bytes_accessed=moved),
    )(*inputs)


def struct(shape, dtype):
    return jax.ShapeDtypeStruct(shape, dtype)


def rows_spec(rows, width, at=0):
    return pl.BlockSpec((rows, width), lambda i, *_: (i, at))


def whole(shape, index=None):
    index = index or (0,) * len(shape)
    return pl.BlockSpec(shape, lambda i, *_: index)


def call(kernel, grid, in_specs, out_specs, out_shape, scratch, flops, moved, limit, prefetch=0):
    return pl.pallas_call(
        kernel,
        grid_spec=pltpu.PrefetchScalarGridSpec(
            num_scalar_prefetch=prefetch, grid=grid, in_specs=in_specs, out_specs=out_specs, scratch_shapes=scratch),
        out_shape=out_shape,
        compiler_params=pltpu.CompilerParams(dimension_semantics=("arbitrary",), vmem_limit_bytes=limit << 20),
        cost_estimate=pl.CostEstimate(flops=int(flops), transcendentals=0, bytes_accessed=int(moved)),
    )


def once(shape, index=None):
    index = index or (0,) * len(shape)
    return pl.BlockSpec(shape, lambda i, *_: index, pipeline_mode=pl.Buffered(1))


class Tokens:
    def __init__(self, tokens, width, count, place):
        self.tokens, self.width, self.count, self.place = tokens, width, count, place
        self.length = length = tokens // count
        self.half = half = width // 2
        self.padded = length + 2 * EDGE
        self.wide, self.slim, self.lane = rows_spec(length, width), rows_spec(length, half), rows_spec(length, LANES)
        self.all_cols = rows_spec(length, 4 * half)
        self.heads = pl.BlockSpec((1, HEADS, length, length), lambda i, *_: (i, 0, 0, 0))
        self.any = pl.BlockSpec(memory_space=pl.ANY)
        self.low_wide, self.low_slim = struct((tokens, width), low), struct((tokens, half), low)
        self.low_half = struct((half, width), low)

    def order(self, hidden, grad_out, depth):
        return call(
            order_kernel, (self.count,),
            [self.wide, self.wide, once(depth.shape)],
            [self.wide] * 3, [self.low_wide] * 3,
            [pltpu.VMEM((self.padded, self.width), full)], 4e9, 8e6, 60,
        )(hidden, grad_out, depth)

    def forward(self, lens, hidden, e, wa, wb, span, hid):
        tokens, length, width, half = self.tokens, self.length, self.width, self.half
        V = pltpu.VMEM
        devices = 2 * hid // self.hid_dev
        blocks = [value.reshape(devices // 2, -1, value.shape[1]) for value in wa]
        bias = pl.BlockSpec((devices // 2, blocks[0].shape[1], LANES), lambda i, *_: (0, 0, 4 * half // LANES),
                            pipeline_mode=pl.Buffered(1))
        return call(
            forward_kernel, (self.count,),
            [self.wide, self.wide] + [self.any] * 4 + [bias, bias, once(span.shape)],
            [self.all_cols, self.slim, self.lane, self.slim, self.heads, self.slim, self.wide,
             whole((2, hid)), whole((LANES, half))],
            [struct((tokens, 4 * half), low), self.low_slim, struct((tokens, LANES), full), self.low_slim,
             struct((self.count, HEADS, length, length), low), self.low_slim, self.low_wide,
             struct((2, hid), full), struct((LANES, half), low)],
            [V((self.padded, half), full), V((length, KERNEL * half), full), V((width, 4 * half), low), V((width, width), low),
             V((width, half), low), V((LANES, KERNEL * half), low), pltpu.SemaphoreType.DMA((3, 2))],
            25e9, 25e6, 60, prefetch=2,
        )(lens, self.place, hidden, e, *wa, *wb, *blocks, span)

    def feed(self, y, hidden, grad_out, norm, feed, bias, ctx, conv, wb):
        tokens, width, half = self.tokens, self.width, self.half
        hid = bias.shape[1]
        V = pltpu.VMEM
        vmem = pl.BlockSpec(memory_space=V)
        wide = V((tokens, width), low)
        return pl.pallas_call(
            functools.partial(feed_kernel, self.count),
            in_specs=[pl.BlockSpec(memory_space=pltpu.SMEM), vmem, vmem] + [self.any] * 8,
            out_specs=[vmem] + [self.any] * 7,
            out_shape=[struct((16, half), full)] + [self.low_wide] * 3 + [struct((hid, width), low)] * 2 + [self.low_half] * 2,
            scratch_shapes=[wide, wide, wide, wide, V((2 * hid, half), low), V((2 * hid, half), low), V((width, width), low),
                            V((tokens, 2 * hid), low), V((tokens, 2 * hid), low), wide, wide, wide,
                            V((width, tokens), low), V((width, tokens), low), V((2, hid, width), low), V((width, width), low),
                            pltpu.SemaphoreType.DMA((6 + 3 * self.count,)), pltpu.SemaphoreType.DMA((4 + 3 * self.count,))],
            compiler_params=pltpu.CompilerParams(vmem_limit_bytes=63 << 20),
            cost_estimate=pl.CostEstimate(flops=int(30e9), transcendentals=0, bytes_accessed=int(25e6)),
        )(self.place, norm, bias, y, hidden, grad_out, ctx, conv, feed, *wb)

    def attend_back(self, qwkv, a, gm):
        return call(
            attend_back_kernel, (self.count,),
            [self.all_cols, self.heads, self.slim], [self.slim, self.wide],
            [struct((self.tokens, self.half), full), self.low_wide],
            [], 15e9, 12e6, 60,
        )(qwkv, a, gm)

    def conv_back(self, gm, qwkv, u, p, gqa, wb, spant):
        length, width, half = self.length, self.width, self.half
        V = pltpu.VMEM
        return call(
            conv_back_kernel, (self.count,),
            [rows_spec(length, half, 1), self.wide, self.slim, self.lane, self.slim, self.any, self.any, once((LANES, half))],
            [self.wide, self.slim, self.wide, whole((LANES, half))],
            [self.low_wide, self.low_slim, self.low_wide, struct((LANES, half), full)],
            [V((self.padded, half), full), V((self.padded, half), full), V((self.padded, KERNEL * half), full),
             V((length, KERNEL * half), low), V((width, half), low), V((LANES, KERNEL * half), low), pltpu.SemaphoreType.DMA((2,))],
            16e9, 12e6, 60, prefetch=1,
        )(self.place, gm, qwkv, u, p, gqa, *wb, spant)

    def weights(self, hidden, e, gqw, gkv, gu, ge, d_span, devices):
        width, half = self.width, self.half
        shapes = [(devices, parts * half // devices, half) for parts in (3, 3, 2, 2)]
        V = pltpu.VMEM
        return call(
            weight_kernel, (self.count,),
            [self.wide, self.wide, self.wide, self.wide, self.slim, self.wide, whole((LANES, half))],
            [whole(shape) for shape in shapes] + [whole((SMALL_ROWS, half))],
            [struct(shape, low) for shape in shapes] + [struct((SMALL_ROWS, half), full)],
            [V((self.padded, width), full), V((width, 3 * half), full), V((width, width), full), V((16, width), full)],
            12e9, 16e6, 60, prefetch=1,
        )(self.place, hidden, e, gqw, gkv, gu, ge, d_span)

    def input_grad(self, gb, gqw, gkv, ge, wa, depth):
        length, width = self.length, self.width
        V = pltpu.VMEM
        return call(
            input_kernel, (self.count,),
            [self.wide, self.wide, self.wide, self.wide, self.any, self.any, once(depth.shape)],
            [self.wide], [self.low_wide],
            [V((self.padded, width), full), V((length, width), full), V((width, 2 * width), low), pltpu.SemaphoreType.DMA((2,))],
            10e9, 14e6, 60, prefetch=1,
        )(self.place, gb, gqw, gkv, ge, *wa, depth)[0]


class Links:
    def __init__(self, mesh):
        self.size = mesh.shape["dp"]
        self.grp = mesh.shape["grp"]
        deep = 4 if self.size % 4 == 0 else 1
        rest = self.size // deep
        wide = 1 << ((rest.bit_length() - 1) // 2)
        self.sizes = (self.grp, deep, rest // wide, wide)
        self.strides = (0, rest, wide, 1)

    def place(self, dim):
        if dim == 0:
            return lax.axis_index("grp")
        return (lax.axis_index("dp") // self.strides[dim]) % self.sizes[dim]

    def swap(self, value, dim, shift):
        if dim == 0:
            return lax.ppermute(value, "grp", [(i, i ^ shift) for i in range(self.grp)])
        size, stride = self.sizes[dim], self.strides[dim]
        pairs = []
        for i in range(self.size):
            at = (i // stride) % size
            pairs.append((i, i + ((at ^ shift) - at) * stride))
        return lax.ppermute(value, "dp", pairs)

    def gather(self, block, dim):
        size, here = self.sizes[dim], self.place(dim)
        got = [block] + [self.swap(block, dim, k) for k in range(1, size)]
        slots = []
        for j in range(size):
            value = got[size - 1]
            for k in range(size - 1):
                value = jnp.where(here == (j ^ k), got[k], value)
            slots.append(value)
        return jnp.concatenate(slots, axis=dim)

    def join(self, keep, piece):
        return keep.astype(full) + self.swap(piece, 0, 1).astype(full)

    def scatter_both(self, a, b, small, dim_a, dim_b, end=low):
        small = small.astype(low)
        cols = b.shape[-1]

        def slices(block, dim):
            here = self.place(dim)
            return [lax.dynamic_slice_in_dim(block, here ^ k, 1, dim) for k in range(self.sizes[dim])]

        def add(got):
            got = [value.astype(full) for value in got]
            while len(got) > 1:
                got = [got[i] + got[i + 1] for i in range(0, len(got), 2)]
            return got[0].astype(end)

        parts_a, parts_b, sums = slices(a, dim_a), slices(b, dim_b), [small]
        if dim_a != dim_b:
            parts_a = parts_a[:1] + [self.swap(parts_a[k], dim_a, k) for k in range(1, len(parts_a))]
        size_a, size_b = parts_a[0].size // cols, parts_b[0].size // cols
        for k in range(1, len(parts_b)):
            pieces = [parts_b[k].reshape(-1, cols), small]
            if dim_a == dim_b:
                pieces = [parts_a[k].reshape(-1, cols)] + pieces
            message = self.swap(jnp.concatenate(pieces, axis=0), dim_b, k)
            if dim_a == dim_b:
                parts_a[k], message = message[:size_a].reshape(parts_a[0].shape), message[size_a:]
            parts_b[k] = message[:size_b].reshape(parts_b[0].shape)
            sums.append(message[size_b:])
        return add(parts_a), add(parts_b), add(sums)


def on_device(links, hidden, grad_out, seq_lens, mix_state, out_state, depth_state, span_state, norm_state,
              up_state, bias_state, down_state):
    both = ("grp", "dp")
    barrier = lax.optimization_barrier
    width = hidden.shape[1]
    half = width // 2
    hid_dev = up_state.shape[3]
    rows_dev = mix_state.shape[2]
    up_state = jnp.swapaxes(up_state, 2, 3)
    depth_state = jnp.swapaxes(depth_state, 0, 1)
    span_state = jnp.transpose(span_state, (2, 0, 1))
    place = jnp.stack([links.place(0), lax.axis_index("dp")]).astype(jnp.int32)
    tokens = Tokens(hidden.shape[0], width, seq_lens.shape[0], place)
    tokens.hid_dev = hid_dev

    mix_low = mix_state[0].astype(low)
    bias_row = jnp.pad(bias_state[0].astype(low), ((0, rows_dev - 1), (0, LANES - hid_dev)))
    shard = jnp.concatenate(
        [mix_low[0], mix_low[4], mix_low[1], mix_low[2], bias_row, out_state[0].astype(low), mix_low[3]], axis=1)
    feed_shard = jnp.concatenate([up_state[0, 0], down_state[0, 0]], axis=1).astype(low)
    feed = lax.all_gather(feed_shard, both, axis=0, tiled=True)
    block = links.gather(shard.reshape((1, 1, 1, 1) + shard.shape), 1)
    block, hidden_o, grad_o, e = barrier((block, *tokens.order(hidden, grad_out, depth_state)))
    split = 4 * half + LANES
    wa, wb = block[..., :split], block[..., split:]
    for dim_a, dim_b in ((2, 3), (3, 2)):
        wa, wb = links.gather(wa, dim_a), links.gather(wb, dim_b)
    wa, wb = wa.reshape(half, -1), wb.reshape(half, -1)
    wa, wb = (wa, links.swap(wa, 0, 1)), (wb, links.swap(wb, 0, 1))

    qwkv, u, p, conv, a, ctx, y, bias, spant = tokens.forward(
        seq_lens, hidden_o, e, wa, wb, span_state, hid_dev * links.size)
    small, result, gb, gm, keep_f, piece_f, keep_o, piece_o = tokens.feed(
        y, hidden_o, grad_o, norm_state, feed, bias, ctx, conv, wb)

    def blocks(value):
        return value.reshape((1,) + links.sizes[1:] + (-1, value.shape[-1]))

    d_feed, d_out = blocks(links.join(keep_f, piece_f)), blocks(links.join(keep_o, piece_o))
    small = small.astype(low)
    small = links.join(small, small)
    gqa, gkv = tokens.attend_back(qwkv, a, gm)
    sums = [jnp.concatenate([d_feed[..., cols], d_out[..., cols]], axis=4).astype(low) for cols in (slice(0, half), slice(half, width))]
    *sums, gqa, gkv = barrier((*sums, small.astype(low), gqa, gkv))
    sums = links.scatter_both(*sums, 3, 2)
    gqw, gu, ge, d_span = tokens.conv_back(gm, qwkv, u, p, gqa, wb, spant)
    *sums, gqw, gu, ge, d_span = barrier((*sums, gqw, gu, ge, d_span))
    sums = links.scatter_both(*sums, 2, 3)
    keep_a, piece_a, keep_b, piece_b, small = tokens.weights(hidden_o, e, gqw, gkv, gu, ge, d_span, links.size)
    *feed_sums, keep_a, piece_a, keep_b, piece_b, small = barrier((*sums, keep_a, piece_a, keep_b, piece_b, small))

    small = small.astype(low)
    sums = (blocks(links.join(keep_a, piece_a).astype(low)), blocks(links.join(keep_b, piece_b).astype(low)),
            links.join(small, small).astype(low))
    *sums, gqw, ge = barrier((*sums, gqw, ge))
    feed_sums = links.scatter_both(*feed_sums, 1, 1, full)
    sums = links.scatter_both(*sums, 3, 2)
    gx = tokens.input_grad(gb, gqw, gkv, ge, wa, depth_state)
    *sums, gx = barrier((*sums, gx))
    sums = barrier(links.scatter_both(*sums, 2, 3))
    grad_a, grad_b, small = links.scatter_both(*sums, 1, 1, full)

    def twice(state, at=0):
        shape = state.shape[:at] + (2,) + state.shape[at + 1 :]
        return [shape, shape]

    def flat(value):
        return value.reshape(-1, value.shape[-1])

    feed_a, feed_b, feed_small = feed_sums
    feed_out = adam_call(
        adam_feed_kernel,
        [place, out_state, norm_state, up_state, bias_state, down_state, flat(feed_a), flat(feed_b), feed_small],
        twice(out_state) + twice(norm_state) + twice(up_state) + twice(bias_state) + twice(down_state), scalars=1)
    mixed = adam_call(
        adam_mix_kernel,
        [mix_state, depth_state, span_state, flat(grad_a), flat(grad_b), small],
        twice(mix_state) + twice(depth_state, 1) + twice(span_state, 1))
    depth_out = [jnp.swapaxes(value, 0, 1) for value in mixed[2:4]]
    span_out = [jnp.transpose(value, (1, 2, 0)) for value in mixed[4:]]
    up_out = [jnp.swapaxes(value, 2, 3) for value in feed_out[4:6]]
    return (result, gx, *mixed[:2], *feed_out[:2], *depth_out, *span_out, *feed_out[2:4], *up_out, *feed_out[6:])


def solution(mesh):
    both = ("grp", "dp")
    mix, out = P(None, None, both, None), P(None, both, None)
    up, bias, down = P(None, "grp", None, "dp"), P(None, "grp", "dp"), P(None, "grp", "dp", None)
    rows = P(both, None)
    return jax.shard_map(
        functools.partial(on_device, Links(mesh)),
        mesh=mesh,
        in_specs=(rows, rows, P(both), mix, out, P(), P(), P(), up, bias, down),
        out_specs=(rows, rows, mix, mix, out, out, P(), P(), P(), P(), P(), P(), up, up, bias, bias, down, down),
        check_vma=False,
    )
```

```python
import functools

import jax
import jax.numpy as jnp
from jax import lax
from jax.experimental import pallas as pl
from jax.experimental.pallas import tpu as pltpu
from jax.sharding import PartitionSpec as P

HEADS = 6
HS = 64
KERNEL = 9
STEP = 7
REACH = KERNEL // 2
TAP = 8
LANES = 128
PAD = 8
EDGE = REACH * PAD

beta_one = 0.9
beta_two = 0.999
adam_eps = 1e-06
ema_rate = 0.99
decay_rate = 0.01
rate_mix = 0.06
rate_out = 0.12
rate_depth = 0.4
rate_span = 0.08
rate_norm = 0.5
rate_up = 0.08
rate_bias = 0.3
rate_down = 0.04

low = jnp.bfloat16
full = jnp.float32
NN = (((1,), (0,)), ((), ()))
NT = (((1,), (1,)), ((), ()))
TN = (((0,), (0,)), ((), ()))


def dot(left, right, dims=NN):
    return lax.dot_general(left, right, dims, preferred_element_type=full)


def rounded(value):
    return value.astype(low).astype(full)


def row_loop(rows, chunk, body):
    for r in range(0, rows, chunk):
        body(r)


def spread_table(width):
    row = lax.broadcasted_iota(jnp.int32, (LANES, 1), 0)
    col = lax.broadcasted_iota(jnp.int32, (1, KERNEL * width), 1)
    head = row % TAP
    first = (row // TAP) * width + head * HS
    first = jnp.where(head < HEADS, first, -HS)
    return ((col >= first) & (col < first + HS)).astype(full).astype(low)


def tap_table():
    row = lax.broadcasted_iota(jnp.int32, (LANES, HEADS * KERNEL), 0)
    col = lax.broadcasted_iota(jnp.int32, (LANES, HEADS * KERNEL), 1)
    return ((col % KERNEL) * TAP + col // KERNEL == row).astype(full).astype(low)


def copy_halves(place_ref, mine, other, target, sems, first, cols):
    rows = mine.shape[0]
    copies = []
    for i, (half, at) in enumerate(((mine, place_ref[0]), (other, 1 - place_ref[0]))):
        copy = pltpu.make_async_copy(
            half.at[:, pl.ds(first, cols)], target.at[pl.ds(pl.multiple_of(at * rows, rows), rows), :], sems.at[i])
        copy.start()
        copies.append(copy)
    return copies


def put_blocks(place_ref, value_ref, keep_ref, piece_ref):
    devices, _, half = keep_ref.shape
    parts = value_ref.shape[1] // half
    rows = half // devices
    for ref, at in ((keep_ref, place_ref[0]), (piece_ref, 1 - place_ref[0])):
        for m in range(parts):
            value = value_ref[pl.ds(pl.multiple_of(at * half, half), half), m * half : (m + 1) * half]
            for n in range(devices):
                ref[n, m * rows : (m + 1) * rows, :] = value[n * rows : (n + 1) * rows].astype(low)


def fill_padded(ref, value):
    rows = value.shape[0]
    value = value.astype(full)
    place = lax.broadcasted_iota(jnp.int32, (PAD, 1), 0)
    ref[EDGE : EDGE + rows, :] = value
    for i in range(REACH):
        before = value[rows - EDGE + i * PAD : rows - EDGE + (i + 1) * PAD]
        ref[i * PAD : (i + 1) * PAD, :] = jnp.where(place == 0, 0.0, pltpu.roll(before, 1, 0))
        after = value[i * PAD : (i + 1) * PAD]
        ref[EDGE + rows + i * PAD : EDGE + rows + (i + 1) * PAD, :] = jnp.where(
            place == PAD - 1, 0.0, pltpu.roll(after, PAD - 1, 0))


def order_matrix(rows, back=False):
    row = lax.broadcasted_iota(jnp.int32, (rows, rows), 0)
    col = lax.broadcasted_iota(jnp.int32, (1, rows), 1)
    places = rows // PAD
    at = (col % PAD) * places + col // PAD if back else (col % places) * PAD + col // places
    return (row == at).astype(full).astype(low)


def order_kernel(x_ref, g_ref, depth_ref, xo_ref, go_ref, e_ref, xpad):
    rows, width = x_ref.shape
    order = order_matrix(rows)
    x = dot(order, x_ref[...])
    xo_ref[...] = x.astype(low)
    go_ref[...] = dot(order, g_ref[...]).astype(low)
    fill_padded(xpad, x)

    rates = [rounded(depth_ref[j, 0:1]) for j in range(KERNEL)]

    def depth_rows(r):
        acc = rates[0] * xpad[pl.ds(r, 32), :]
        for j in range(1, KERNEL):
            acc = acc + rates[j] * xpad[pl.ds(r + PAD * j, 32), :]
        e_ref[pl.ds(r, 32), :] = acc.astype(low)

    row_loop(rows, 32, depth_rows)


def project_kernel(place_ref, x_ref, e_ref, wam_ref, wao_ref, wbm_ref, wbo_ref, bm_ref, bo_ref, span_ref,
                   qwkv_ref, u_ref, bias_ref, spant_ref,
                   wa_ref, w3_ref, sems):
    rows, width = x_ref.shape
    half = width // 2

    @pl.when(pl.program_id(0) == 0)
    def _():
        copies = copy_halves(place_ref, wam_ref, wao_ref, wa_ref, sems.at[0], 0, 4 * half)
        copies += copy_halves(place_ref, wbm_ref, wbo_ref, w3_ref, sems.at[1], width, half)
        spant_ref[...] = dot(tap_table(), span_ref[:, 0, :].astype(low)).astype(low)
        hid_dev = bias_ref.shape[1] // bm_ref.shape[0]
        for n in range(bm_ref.shape[0]):
            cols = slice(n * hid_dev, (n + 1) * hid_dev)
            mine, other = bm_ref[n].astype(full)[0:1, 0:hid_dev], bo_ref[n].astype(full)[0:1, 0:hid_dev]
            bias_ref[0:1, cols] = jnp.where(place_ref[0] == 0, mine, other)
            bias_ref[1:2, cols] = jnp.where(place_ref[0] == 0, other, mine)
        for copy in copies:
            copy.wait()

    x = x_ref[...]
    for c in range(4):
        qwkv_ref[:, c * half : (c + 1) * half] = dot(x, wa_ref[:, c * half : (c + 1) * half]).astype(low)
    u_ref[...] = dot(e_ref[...], w3_ref[...]).astype(low)


def mix_kernel(lens_ref, place_ref, qwkv_ref, u_ref, spant_ref, wbm_ref, wbo_ref,
               p_ref, conv_ref, a_ref, ctx_ref, y_ref,
               wpad, taps, wo_ref, spread_ref, sems):
    rows, half = u_ref.shape

    @pl.when(pl.program_id(0) == 0)
    def _():
        copies = copy_halves(place_ref, wbm_ref, wbo_ref, wo_ref, sems, 0, 2 * half)
        spread_ref[...] = spread_table(half)
        for copy in copies:
            copy.wait()

    r = (u_ref[...].astype(full) * qwkv_ref[:, 0:half].astype(full)).astype(low)
    logits = rounded(dot(r, spant_ref[...], NT))
    lt = logits.T[0 : KERNEL * TAP].reshape(KERNEL, TAP, rows)
    top = jnp.max(lt, axis=0, keepdims=True)
    ex = jnp.exp(lt - top)
    pt = (ex / jnp.sum(ex, axis=0, keepdims=True)).reshape(KERNEL * TAP, rows)
    p = jnp.concatenate([pt, jnp.zeros((LANES - KERNEL * TAP, rows), full)], axis=0).T
    p_ref[...] = p
    fill_padded(wpad, qwkv_ref[:, half : 2 * half])
    p_low = p.astype(low)
    for j in range(KERNEL):
        taps[:, j * half : (j + 1) * half] = dot(p_low, spread_ref[:, j * half : (j + 1) * half])

    def conv_rows(r):
        acc = taps[pl.ds(r, 32), 0:half] * wpad[pl.ds(r, 32), :]
        for j in range(1, KERNEL):
            acc = acc + taps[pl.ds(r, 32), j * half : (j + 1) * half] * wpad[pl.ds(r + PAD * j, 32), :]
        conv_ref[pl.ds(r, 32), :] = acc.astype(low)

    row_loop(rows, 32, conv_rows)
    seq_len = lens_ref[pl.program_id(0)]
    lane = lax.broadcasted_iota(jnp.int32, (1, LANES), 1)
    row = lax.broadcasted_iota(jnp.int32, (1, rows), 1)
    live = (row % PAD) * (rows // PAD) + row // PAD < seq_len
    for pair in range(HEADS // 2):
        at = pair * LANES
        q = qwkv_ref[:, at : at + LANES]
        k = qwkv_ref[:, 2 * half + at : 2 * half + at + LANES]
        v = qwkv_ref[:, 3 * half + at : 3 * half + at + LANES]
        outs = []
        for side in range(2):
            pick = jnp.where((lane // HS) == side, HS ** (-0.5), 0.0).astype(low)
            scores = dot(q * pick, k, NT)
            scores = jnp.where(live, scores, -1000000000.0)
            top = jnp.max(scores, axis=1, keepdims=True)
            ex = jnp.exp(scores - top)
            a = (ex * (1.0 / jnp.sum(ex, axis=1, keepdims=True))).astype(low)
            a_ref[0, 2 * pair + side] = a
            outs.append(dot(a, v))
        ctx_ref[:, at : at + LANES] = jnp.where((lane // HS) == 0, outs[0], outs[1]).astype(low)
    y_ref[...] = (dot(ctx_ref[...], wo_ref[0:half, :]) + dot(conv_ref[...], wo_ref[half:, :])).astype(low)


def normed(value):
    centered = value - jnp.mean(value, axis=1, keepdims=True)
    variance = jnp.mean(centered * centered, axis=1, keepdims=True)
    rstd = lax.rsqrt(variance + 1e-12)
    return centered * rstd, rstd


def feed_kernel(count, place_ref, norm_ref, bias_ref, y_hbm, x_hbm, g_hbm, ctx_hbm, conv_hbm, upm_hbm, upo_hbm, downm_hbm, downo_hbm, wbm_hbm, wbo_hbm,
                small_ref, res_hbm, gb_hbm, gm_hbm, keep_hbm, piece_hbm, keep_o_hbm, piece_o_hbm,
                small_s, y_s, x_s, g_s, m_s, up_s, down_s, wo_s, act_s, gpre_s, res_s, gb_s, gm_s, ft_s, got_s, df_s, do_s,
                in_sems, out_sems):
    tokens, width = y_s.shape
    half = width // 2
    hid = bias_ref.shape[1]
    length = tokens // count
    waits, outs = {}, []

    def fetch(name, source, target):
        copy = pltpu.make_async_copy(source, target, in_sems.at[len(waits)])
        copy.start()
        waits[name] = copy

    def put(source, target):
        copy = pltpu.make_async_copy(source, target, out_sems.at[len(outs)])
        copy.start()
        outs.append(copy)

    seqs = [slice(n * length, (n + 1) * length) for n in range(count)]
    for n, rows in enumerate(seqs):
        fetch(("y", n), y_hbm.at[rows], y_s.at[rows])
        fetch(("x", n), x_hbm.at[rows], x_s.at[rows])
        if n == 0:
            for name, pair, target in (("up", (upm_hbm, upo_hbm), up_s), ("down", (downm_hbm, downo_hbm), down_s)):
                for i, at in enumerate((place_ref[0], 1 - place_ref[0])):
                    fetch((name, i), pair[i], target.at[pl.ds(pl.multiple_of(at * hid, hid), hid), :])
        fetch(("g", n), g_hbm.at[rows], g_s.at[rows])
        if n == 0:
            for i, (part, at) in enumerate(((wbm_hbm, place_ref[0]), (wbo_hbm, 1 - place_ref[0]))):
                fetch(("wo", i), part.at[:, pl.ds(0, width)], wo_s.at[pl.ds(pl.multiple_of(at * half, half), half), :])
    fetch("ctx", ctx_hbm, m_s.at[:, pl.ds(0, half)])
    fetch("conv", conv_hbm, m_s.at[:, pl.ds(half, half)])

    g1, c1, g2, c2 = (norm_ref[0, i : i + 1] for i in range(4))
    sums = [jnp.zeros((1, width), full) for _ in range(4)]
    dbias = [jnp.zeros((1, hid), full) for _ in range(2)]
    groups = [(slice(g * hid, (g + 1) * hid), slice(g * half, (g + 1) * half)) for g in range(2)]
    kept = [{} for _ in seqs]

    def wait(name):
        if name in waits:
            waits.pop(name).wait()

    def enter(n):
        wait(("y", n))
        wait(("x", n))
        zh1, rstd1 = normed(y_s[seqs[n]].astype(full) + x_s[seqs[n]].astype(full))
        f = (zh1 * g1 + c1).astype(low)
        kept[n].update(zh1=zh1, rstd1=rstd1, f=f, parts=[])
        ft_s[:, seqs[n]] = f.T

    def ahead(n, g):
        hidden, cols = groups[g]
        wait(("up", 0))
        wait(("up", 1))
        pre = dot(kept[n]["f"][:, cols], up_s[hidden, :], NT) + bias_ref[g : g + 1, :]
        cdf = 0.5 * (1.0 + lax.erf(pre * 2.0 ** (-0.5)))
        act_s[seqs[n], hidden] = (pre * cdf).astype(low)
        gpre_s[seqs[n], hidden] = (cdf + pre * (jnp.exp(-0.5 * pre * pre) * 0.3989422804014327)).astype(low)
        wait(("down", 0))
        wait(("down", 1))
        kept[n]["parts"].append(rounded(dot(act_s[seqs[n], hidden], down_s[hidden, :])))

    def turn(n):
        rows = seqs[n]
        h1 = kept[n]["zh1"] * g1 + c1
        zh2, rstd2 = normed(h1 + jnp.concatenate(kept[n]["parts"], axis=1))
        result = (zh2 * g2 + c2).astype(low)
        res_s[rows] = dot(order_matrix(length, True), result).astype(low)
        put(res_s.at[rows], res_hbm.at[rows])
        wait(("g", n))
        grad = g_s[rows].astype(full)
        sums[2] = sums[2] + jnp.sum(grad * zh2, axis=0, keepdims=True)
        sums[3] = sums[3] + jnp.sum(grad, axis=0, keepdims=True)
        dz = grad * g2
        gz = (dz - jnp.mean(dz, axis=1, keepdims=True) - zh2 * jnp.mean(dz * zh2, axis=1, keepdims=True)) * rstd2
        go = gz.astype(low)
        got_s[:, rows] = go.T
        kept[n].update(gz=gz, go=go, parts=[])

    def behind(n, g):
        hidden, cols = groups[g]
        slope = gpre_s[seqs[n], hidden].astype(full)
        gpre = (dot(kept[n]["go"][:, cols], down_s[hidden, :], NT) * slope).astype(low)
        gpre_s[seqs[n], hidden] = gpre
        dbias[g] = dbias[g] + jnp.sum(gpre.astype(full), axis=0, keepdims=True)
        kept[n]["parts"].append(rounded(dot(gpre, up_s[hidden, :])))

    def leave(n):
        rows, zh1 = seqs[n], kept[n]["zh1"]
        gh1 = kept[n]["gz"] + jnp.concatenate(kept[n]["parts"], axis=1)
        sums[0] = sums[0] + jnp.sum(gh1 * zh1, axis=0, keepdims=True)
        sums[1] = sums[1] + jnp.sum(gh1, axis=0, keepdims=True)
        dz1 = gh1 * g1
        gy = (dz1 - jnp.mean(dz1, axis=1, keepdims=True) - zh1 * jnp.mean(dz1 * zh1, axis=1, keepdims=True)) * kept[n]["rstd1"]
        gb_s[rows] = gy.astype(low)
        put(gb_s.at[rows], gb_hbm.at[rows])

    def through(n):
        rows = seqs[n]
        wait(("wo", 0))
        wait(("wo", 1))
        gm_s[rows] = dot(gb_s[rows], wo_s[...], NT).astype(low)
        put(gm_s.at[rows], gm_hbm.at[rows])

    first, *rest = range(count)
    enter(first)
    ahead(first, 0)
    for n in rest:
        enter(n)
    ahead(first, 1)
    for n in rest:
        ahead(n, 0)
        turn(n - 1)
        ahead(n, 1)
        behind(n - 1, 0)
        if n == rest[-1]:
            turn(n)
        behind(n - 1, 1)
        if n == rest[-1]:
            behind(n, 0)
        leave(n - 1)
        if n == rest[-1]:
            behind(n, 1)
        through(n - 1)
    if not rest:
        turn(first)
        behind(first, 0)
        behind(first, 1)
    leave(count - 1)
    through(count - 1)

    for i, (at, target) in enumerate(((1 - place_ref[0], piece_hbm), (place_ref[0], keep_hbm))):
        hidden = pl.ds(pl.multiple_of(at * hid, LANES), hid)
        cols = pl.ds(pl.multiple_of(at * half, half), half)
        df_s[i, :, 0:half] = dot(ft_s[cols, :], gpre_s[:, hidden]).astype(low).T
        df_s[i, :, half:] = dot(got_s[cols, :], act_s[:, hidden]).astype(low).T
        put(df_s.at[i], target)
    wait("ctx")
    wait("conv")
    do_s[...] = dot(m_s[...].T, gb_s[...]).astype(low)
    for at, target in ((1 - place_ref[0], piece_o_hbm), (place_ref[0], keep_o_hbm)):
        put(do_s.at[pl.ds(pl.multiple_of(at * half, half), half), :], target)
    for i in range(4):
        g, side = divmod(i, 2)
        for j in range(2):
            small_s[8 * j + i : 8 * j + i + 1, :] = sums[i][:, j * half : (j + 1) * half]
            at = side * width + j * half
            small_s[8 * j + 4 + i : 8 * j + 5 + i, :] = dbias[g][:, at : at + half]
    small_ref[...] = small_s[...].astype(low)
    for copy in outs:
        copy.wait()


def mixer_back_kernel(place_ref, qwkv_ref, a_ref, gm_ref, u_ref, p_ref, wbm_ref, wbo_ref, spant_ref,
                      gqw_ref, gkv_ref, gu_ref, ge_ref, dspan_ref,
                      gqa, wpad, gpad, taps, prods, w3_ref, spread_ref, sems):
    rows, half = u_ref.shape

    @pl.when(pl.program_id(0) == 0)
    def _():
        copies = copy_halves(place_ref, wbm_ref, wbo_ref, w3_ref, sems, 2 * half, half)
        dspan_ref[...] = jnp.zeros_like(dspan_ref)
        spread_ref[...] = spread_table(half)
        for copy in copies:
            copy.wait()

    lane = lax.broadcasted_iota(jnp.int32, (1, LANES), 1)
    for pair in range(HEADS // 2):
        at = pair * LANES
        q = qwkv_ref[:, at : at + LANES]
        k = qwkv_ref[:, 2 * half + at : 2 * half + at + LANES]
        v = qwkv_ref[:, 3 * half + at : 3 * half + at + LANES]
        gctx = gm_ref[:, at : at + LANES]
        qt, gctxt = q.T, gctx.T
        gqs, gks, gvs = [], [], []
        for side in range(2):
            pick = jnp.where((lane // HS) == side, 1.0, 0.0).astype(low)
            a_low = a_ref[0, 2 * pair + side]
            a = a_low.astype(full)
            ga = dot(gctx * pick, v, NT)
            gs = (a * (ga - jnp.sum(a * ga, axis=1, keepdims=True))).astype(low)
            gqs.append(dot(gs, k))
            gks.append(dot(qt, gs))
            gvs.append(dot(gctxt, a_low))
        first = (lane // HS) == 0
        gqa[:, at : at + LANES] = jnp.where(first, gqs[0], gqs[1]) * HS ** (-0.5)
        gk = jnp.concatenate([gks[0][0:HS], gks[1][HS:]], axis=0) * HS ** (-0.5)
        gv = jnp.concatenate([gvs[0][0:HS], gvs[1][HS:]], axis=0)
        gkv_ref[:, at : at + LANES] = gk.T.astype(low)
        gkv_ref[:, half + at : half + at + LANES] = gv.T.astype(low)
    fill_padded(wpad, qwkv_ref[:, half : 2 * half])
    fill_padded(gpad, gm_ref[:, half:])
    p = p_ref[...]
    p_low = p.astype(low)
    for j in range(KERNEL):
        cols = slice(j * half, (j + 1) * half)
        fill_padded(taps.at[:, cols], dot(p_low, spread_ref[:, cols]))

    def conv_rows(r):
        here = gpad[pl.ds(r + EDGE, 32), :]
        acc = None
        for j in range(KERNEL):
            cols = slice(j * half, (j + 1) * half)
            prods[pl.ds(r, 32), cols] = (here * wpad[pl.ds(r + PAD * j, 32), :]).astype(low)
            back = pl.ds(r + PAD * (2 * REACH - j), 32)
            term = taps[back, cols] * gpad[back, :]
            acc = term if acc is None else acc + term
        gqw_ref[pl.ds(r, 32), half:] = acc.astype(low)

    row_loop(rows, 32, conv_rows)
    gp = dot(prods[...], spread_ref[...], NT)
    gpt = gp.T[0 : KERNEL * TAP].reshape(KERNEL, TAP, rows)
    pt = p.T[0 : KERNEL * TAP].reshape(KERNEL, TAP, rows)
    glt = pt * (gpt - jnp.sum(pt * gpt, axis=0, keepdims=True))
    glt = jnp.concatenate([glt.reshape(KERNEL * TAP, rows), jnp.zeros((LANES - KERNEL * TAP, rows), full)], axis=0)
    gl = glt.T.astype(low)
    q = qwkv_ref[:, 0:half].astype(full)
    u = u_ref[...].astype(full)
    r = (u * q).astype(low)
    dspan_ref[...] += dot(glt.astype(low), r)
    gr = rounded(dot(gl, spant_ref[...]))
    gqw_ref[:, 0:half] = (gqa[...] + gr * u).astype(low)
    gu = (gr * q).astype(low)
    gu_ref[...] = gu
    ge_ref[...] = dot(gu, w3_ref[...], NT).astype(low)


SMALL_ROWS = 2 * KERNEL + HEADS * KERNEL


def weight_kernel(place_ref, x_ref, e_ref, gqw_ref, gkv_ref, gu_ref, ge_ref, dspan_ref,
                  keep_a_ref, piece_a_ref, keep_b_ref, piece_b_ref, small_ref,
                  xpad, acc_a, acc_b, small, rows_s):
    step, last = pl.program_id(0), pl.num_programs(0) - 1
    rows, width = x_ref.shape
    half = width // 2

    @pl.when(step == 0)
    def _():
        acc_a[...] = jnp.zeros_like(acc_a)
        acc_b[...] = jnp.zeros_like(acc_b)
        small[...] = jnp.zeros_like(small)

    x = x_ref[...]
    xt = x.T
    acc_a[:, 0:width] += dot(xt, gqw_ref[...])
    acc_a[:, width:] += dot(xt, gkv_ref[:, 0:half])
    acc_b[:, 0:half] += dot(xt, gkv_ref[:, half:])
    acc_b[:, half:] += dot(e_ref[...].T, gu_ref[...])
    fill_padded(xpad, x)
    for c in range(0, width, LANES):
        cols = slice(c, c + LANES)

        sums = [jnp.zeros((PAD, LANES), full) for _ in range(KERNEL)]
        for r in range(0, rows, 64):
            ge = ge_ref[pl.ds(r, 64), cols].astype(full)
            for j in range(KERNEL):
                prod = ge * xpad[pl.ds(r + PAD * j, 64), cols]
                sums[j] = sums[j] + jnp.sum(prod.reshape(PAD, PAD, LANES), axis=0)
        for j in range(KERNEL):
            small[j : j + 1, cols] += jnp.sum(sums[j], axis=0, keepdims=True)

    @pl.when(step == last)
    def _():
        put_blocks(place_ref, acc_a, keep_a_ref, piece_a_ref)
        put_blocks(place_ref, acc_b, keep_b_ref, piece_b_ref)
        for side in range(2):
            rows_s[side * KERNEL : (side + 1) * KERNEL, :] = small[0:KERNEL, side * half : (side + 1) * half]
        rows_s[2 * KERNEL :, :] = dot(tap_table(), dspan_ref[...].astype(low), TN)
        small_ref[...] = rows_s[...].astype(low)


def input_kernel(place_ref, gb_ref, gqw_ref, gkv_ref, ge_ref, wam_ref, wao_ref, depth_ref,
                 gx_ref, gepad, gx_s, wa_ref, sems):
    rows, width = gb_ref.shape

    @pl.when(pl.program_id(0) == 0)
    def _():
        for copy in copy_halves(place_ref, wam_ref, wao_ref, wa_ref, sems, 0, 2 * width):
            copy.wait()

    fill_padded(gepad, ge_ref[...])
    gx_s[...] = gb_ref[...].astype(full) + dot(gqw_ref[...], wa_ref[:, 0:width], NT) + dot(gkv_ref[...], wa_ref[:, width:], NT)

    rates = [rounded(depth_ref[j, 0:1]) for j in range(KERNEL)]

    def shift_rows(r):
        acc = gx_s[pl.ds(r, 32), :]
        for j in range(KERNEL):
            acc = acc + rates[j] * gepad[pl.ds(r + PAD * (2 * REACH - j), 32), :]
        gx_s[pl.ds(r, 32), :] = acc

    row_loop(rows, 32, shift_rows)
    gx_ref[...] = dot(order_matrix(rows, True), gx_s[...].astype(low)).astype(low)


def adam_step(old, one, two, mean, grad, step_rate, wd_rate):
    moment_one = beta_one * one + (1.0 - beta_one) * grad
    moment_two = beta_two * two + (1.0 - beta_two) * grad * grad
    scaled_one = moment_one / (1.0 - beta_one**STEP)
    scaled_two = moment_two / (1.0 - beta_two**STEP)
    weight = old - step_rate * (scaled_one / (jnp.sqrt(scaled_two) + adam_eps) + wd_rate * old)
    return weight, ema_rate * mean + (1.0 - ema_rate) * weight, moment_one, moment_two


def adam_at(state, new, moments, at, grad, step_rate, wd_rate):
    values = adam_step(*(state[at(slot)] for slot in range(4)), grad, step_rate, wd_rate)
    new[at(0)], new[at(1)], moments[at(0)], moments[at(1)] = values


def adam_mix_kernel(mix, depth, span, ga_ref, gb_ref, small,
                    mix_new, mix_moments, depth_new, depth_moments, span_new, span_moments):
    rows = mix.shape[2]
    sources = [(ga_ref, 0), (ga_ref, 2), (gb_ref, 0), (gb_ref, 1), (ga_ref, 1)]
    for i, (ref, at) in enumerate(sources):
        adam_at(mix, mix_new, mix_moments, lambda slot: (slot, i), ref[at * rows : (at + 1) * rows, :], rate_mix, decay_rate)
    grad = jnp.concatenate([small[0:KERNEL], small[KERNEL : 2 * KERNEL]], axis=1)
    adam_at(depth, depth_new, depth_moments, lambda slot: (slice(None), slot), grad, rate_depth, decay_rate)
    adam_at(span, span_new, span_moments, lambda slot: (slice(None), slot), small[2 * KERNEL :], rate_span, decay_rate)


def adam_feed_kernel(place_ref, out, norm, up, bias, down, ga_ref, gb_ref, small,
                     out_new, out_moments, norm_new, norm_moments,
                     up_new, up_moments, bias_new, bias_moments, down_new, down_moments):
    half = down.shape[3]
    width = 2 * half
    hid_dev = down.shape[2]
    adam_at(up, up_new, up_moments, lambda slot: (slot, 0), ga_ref[0:hid_dev, :], rate_up, decay_rate)
    adam_at(down, down_new, down_moments, lambda slot: (slot, 0), gb_ref[0:hid_dev, :], rate_down, decay_rate)
    grad = jnp.concatenate([ga_ref[hid_dev:, :], gb_ref[hid_dev:, :]], axis=1)
    adam_at(out, out_new, out_moments, lambda slot: slot, grad, rate_out, decay_rate)
    lines = jnp.concatenate([small[0:8], small[8:16]], axis=1)
    adam_at(norm, norm_new, norm_moments, lambda slot: slot, lines[0:4], rate_norm, 0.0)
    row = lax.broadcasted_iota(jnp.int32, (width, hid_dev), 0)
    col = lax.broadcasted_iota(jnp.int32, (width, hid_dev), 1)
    grad = jnp.zeros((1, hid_dev), full)
    for i in range(4):
        group, side = divmod(i, 2)
        line = jnp.where(place_ref[0] == group, lines[4 + i : 5 + i, :], 0.0)
        here = (row + side * width == col + place_ref[1] * hid_dev).astype(full).astype(low)
        high = line.astype(low)
        rest = (line - high.astype(full)).astype(low)
        both = dot(jnp.concatenate([high, rest] + [jnp.zeros_like(high)] * 6, axis=0), here)
        grad = grad + both[0:1] + both[1:2]
    adam_at(bias, bias_new, bias_moments, lambda slot: slot, grad, rate_bias, 0.0)


def adam_call(kernel, inputs, shapes, scalars=0):
    vmem = pl.BlockSpec(memory_space=pltpu.VMEM)
    moved = sum(value.size for value in inputs) * 6
    return pl.pallas_call(
        kernel,
        in_specs=[pl.BlockSpec(memory_space=pltpu.SMEM)] * scalars + [vmem] * (len(inputs) - scalars),
        out_specs=[vmem] * len(shapes),
        out_shape=[struct(shape, full) for shape in shapes],
        compiler_params=pltpu.CompilerParams(vmem_limit_bytes=40 << 20),
        cost_estimate=pl.CostEstimate(flops=2 * moved, transcendentals=0, bytes_accessed=moved),
    )(*inputs)


def struct(shape, dtype):
    return jax.ShapeDtypeStruct(shape, dtype)


def rows_spec(rows, width, at=0):
    return pl.BlockSpec((rows, width), lambda i, *_: (i, at))


def whole(shape, index=None):
    index = index or (0,) * len(shape)
    return pl.BlockSpec(shape, lambda i, *_: index)


def call(kernel, grid, in_specs, out_specs, out_shape, scratch, flops, moved, limit, prefetch=0):
    return pl.pallas_call(
        kernel,
        grid_spec=pltpu.PrefetchScalarGridSpec(
            num_scalar_prefetch=prefetch, grid=grid, in_specs=in_specs, out_specs=out_specs, scratch_shapes=scratch),
        out_shape=out_shape,
        compiler_params=pltpu.CompilerParams(dimension_semantics=("arbitrary",), vmem_limit_bytes=limit << 20),
        cost_estimate=pl.CostEstimate(flops=int(flops), transcendentals=0, bytes_accessed=int(moved)),
    )


def once(shape, index=None):
    index = index or (0,) * len(shape)
    return pl.BlockSpec(shape, lambda i, *_: index, pipeline_mode=pl.Buffered(1))


class Tokens:
    def __init__(self, tokens, width, count, place):
        self.tokens, self.width, self.count, self.place = tokens, width, count, place
        self.length = length = tokens // count
        self.half = half = width // 2
        self.padded = length + 2 * EDGE
        self.wide, self.slim, self.lane = rows_spec(length, width), rows_spec(length, half), rows_spec(length, LANES)
        self.all_cols = rows_spec(length, 4 * half)
        self.heads = pl.BlockSpec((1, HEADS, length, length), lambda i, *_: (i, 0, 0, 0))
        self.any = pl.BlockSpec(memory_space=pl.ANY)
        self.low_wide, self.low_slim = struct((tokens, width), low), struct((tokens, half), low)
        self.low_half = struct((half, width), low)

    def order(self, hidden, grad_out, depth):
        return call(
            order_kernel, (self.count,),
            [self.wide, self.wide, once(depth.shape)],
            [self.wide] * 3, [self.low_wide] * 3,
            [pltpu.VMEM((self.padded, self.width), full)], 4e9, 8e6, 60,
        )(hidden, grad_out, depth)

    def project(self, hidden, e, wa, wb, span, hid):
        tokens, width, half = self.tokens, self.width, self.half
        V = pltpu.VMEM
        devices = 2 * hid // self.hid_dev
        blocks = [value.reshape(devices // 2, -1, value.shape[1]) for value in wa]
        bias = pl.BlockSpec((devices // 2, blocks[0].shape[1], LANES), lambda i, *_: (0, 0, 4 * half // LANES),
                            pipeline_mode=pl.Buffered(1))
        return call(
            project_kernel, (self.count,),
            [self.wide, self.wide] + [self.any] * 4 + [bias, bias, once(span.shape)],
            [self.all_cols, self.slim, whole((2, hid)), whole((LANES, half))],
            [struct((tokens, 4 * half), low), self.low_slim, struct((2, hid), full), struct((LANES, half), low)],
            [V((width, 4 * half), low), V((width, half), low), pltpu.SemaphoreType.DMA((2, 2))],
            8e9, 10e6, 24, prefetch=1,
        )(self.place, hidden, e, *wa, *wb, *blocks, span)

    def mix(self, lens, qwkv, u, spant, wb):
        tokens, length, width, half = self.tokens, self.length, self.width, self.half
        V = pltpu.VMEM
        return call(
            mix_kernel, (self.count,),
            [self.all_cols, self.slim, once((LANES, half)), self.any, self.any],
            [self.lane, self.slim, self.heads, self.slim, self.wide],
            [struct((tokens, LANES), full), self.low_slim, struct((self.count, HEADS, length, length), low),
             self.low_slim, self.low_wide],
            [V((self.padded, half), full), V((length, KERNEL * half), full), V((width, width), low),
             V((LANES, KERNEL * half), low), pltpu.SemaphoreType.DMA((2,))],
            20e9, 18e6, 44, prefetch=2,
        )(lens, self.place, qwkv, u, spant, *wb)

    def feed(self, y, hidden, grad_out, norm, up, down, bias, ctx, conv, wb):
        tokens, width, half = self.tokens, self.width, self.half
        hid = bias.shape[1]
        V = pltpu.VMEM
        vmem = pl.BlockSpec(memory_space=V)
        wide = V((tokens, width), low)
        return pl.pallas_call(
            functools.partial(feed_kernel, self.count),
            in_specs=[pl.BlockSpec(memory_space=pltpu.SMEM), vmem, vmem] + [self.any] * 11,
            out_specs=[vmem] + [self.any] * 7,
            out_shape=[struct((16, half), low)] + [self.low_wide] * 3 + [struct((hid, width), low)] * 2 + [self.low_half] * 2,
            scratch_shapes=[V((16, half), full), wide, wide, wide, wide, V((2 * hid, half), low), V((2 * hid, half), low), V((width, width), low),
                            V((tokens, 2 * hid), low), V((tokens, 2 * hid), low), wide, wide, wide,
                            V((width, tokens), low), V((width, tokens), low), V((2, hid, width), low), V((width, width), low),
                            pltpu.SemaphoreType.DMA((8 + 3 * self.count,)), pltpu.SemaphoreType.DMA((4 + 3 * self.count,))],
            compiler_params=pltpu.CompilerParams(vmem_limit_bytes=63 << 20),
            cost_estimate=pl.CostEstimate(flops=int(30e9), transcendentals=0, bytes_accessed=int(25e6)),
        )(self.place, norm, bias, y, hidden, grad_out, ctx, conv, *up, *down, *wb)

    def mixer_back(self, qwkv, a, gm, u, p, wb, spant):
        length, width, half = self.length, self.width, self.half
        V = pltpu.VMEM
        return call(
            mixer_back_kernel, (self.count,),
            [self.all_cols, self.heads, self.wide, self.slim, self.lane, self.any, self.any, once((LANES, half))],
            [self.wide, self.wide, self.slim, self.wide, whole((LANES, half))],
            [self.low_wide, self.low_wide, self.low_slim, self.low_wide, struct((LANES, half), full)],
            [V((length, half), full), V((self.padded, half), full), V((self.padded, half), full), V((self.padded, KERNEL * half), full),
             V((length, KERNEL * half), low), V((width, half), low), V((LANES, KERNEL * half), low), pltpu.SemaphoreType.DMA((2,))],
            30e9, 22e6, 44, prefetch=1,
        )(self.place, qwkv, a, gm, u, p, *wb, spant)

    def weights(self, hidden, e, gqw, gkv, gu, ge, d_span, devices):
        width, half = self.width, self.half
        shapes = [(devices, parts * half // devices, half) for parts in (3, 3, 2, 2)]
        V = pltpu.VMEM
        return call(
            weight_kernel, (self.count,),
            [self.wide, self.wide, self.wide, self.wide, self.slim, self.wide, whole((LANES, half))],
            [whole(shape) for shape in shapes] + [whole((SMALL_ROWS, half))],
            [struct(shape, low) for shape in shapes] + [struct((SMALL_ROWS, half), low)],
            [V((self.padded, width), full), V((width, 3 * half), full), V((width, width), full), V((16, width), full), V((SMALL_ROWS, half), full)],
            12e9, 16e6, 40, prefetch=1,
        )(self.place, hidden, e, gqw, gkv, gu, ge, d_span)

    def input_grad(self, gb, gqw, gkv, ge, wa, depth):
        length, width = self.length, self.width
        V = pltpu.VMEM
        return call(
            input_kernel, (self.count,),
            [self.wide, self.wide, self.wide, self.wide, self.any, self.any, once(depth.shape)],
            [self.wide], [self.low_wide],
            [V((self.padded, width), full), V((length, width), full), V((width, 2 * width), low), pltpu.SemaphoreType.DMA((2,))],
            10e9, 14e6, 36, prefetch=1,
        )(self.place, gb, gqw, gkv, ge, *wa, depth)[0]


class Links:
    def __init__(self, mesh):
        self.size = mesh.shape["dp"]
        self.grp = mesh.shape["grp"]
        deep = 4 if self.size % 4 == 0 else 1
        rest = self.size // deep
        wide = 1 << ((rest.bit_length() - 1) // 2)
        self.shape = (1, deep, rest // wide, wide)
        self.axes = {"z": (deep, rest, 1), "y": (rest // wide, wide, 2), "x": (wide, 1, 3),
                     "zl": (2, rest, 1), "zh": (deep // 2, 2 * rest, 1)}

    def place(self, name):
        if name == "grp":
            return lax.axis_index("grp")
        size, stride, _ = self.axes[name]
        return (lax.axis_index("dp") // stride) % size

    def swap(self, value, name, shift):
        if name == "grp":
            return lax.ppermute(value, "grp", [(i, i ^ shift) for i in range(self.grp)])
        size, stride, _ = self.axes[name]
        pairs = []
        for i in range(self.size):
            at = (i // stride) % size
            pairs.append((i, i + ((at ^ shift) - at) * stride))
        return lax.ppermute(value, "dp", pairs)

    def fetch(self, block, name):
        return [block] + [self.swap(block, name, k) for k in range(1, self.axes[name][0])]

    def merge(self, got, name):
        size, _, dim = self.axes[name]
        here = self.place(name)
        slots = []
        for j in range(size):
            value = got[size - 1]
            for k in range(size - 1):
                value = jnp.where(here == (j ^ k), got[k], value)
            slots.append(value)
        return jnp.concatenate(slots, axis=dim)

    def gather(self, block, name):
        return self.merge(self.fetch(block, name), name)

    def slices(self, block, name):
        size, _, dim = self.axes[name]
        here = self.place(name)
        if name == "zl":
            halves = block.reshape((1, block.shape[1] // 2, 2) + block.shape[2:])
            return [jnp.squeeze(lax.dynamic_slice_in_dim(halves, here ^ k, 1, 2), 2) for k in range(size)]
        return [lax.dynamic_slice_in_dim(block, here ^ k, 1, dim) for k in range(size)]

    def join(self, keep, piece):
        return keep.astype(full) + self.swap(piece, "grp", 1).astype(full)

    def send(self, a, b, small, name_a, name_b):
        cols = b.shape[-1]
        parts_a, parts_b = self.slices(a, name_a), self.slices(b, name_b)
        own = [parts_a[0], parts_b[0], small]
        apart = [] if name_a == name_b else [self.swap(part, name_a, k + 1) for k, part in enumerate(parts_a[1:])]
        messages = []
        for k in range(1, len(parts_b)):
            pieces = [parts_b[k].reshape(-1, cols), small]
            if name_a == name_b:
                pieces = [parts_a[k].reshape(-1, cols)] + pieces
            messages.append(self.swap(jnp.concatenate(pieces, axis=0), name_b, k))
        return own, apart, messages

    def finish(self, sent, end=low):
        (own_a, own_b, own_small), apart, messages = sent
        cols = own_b.shape[-1]
        sums_a, sums_b, sums = [own_a] + apart, [own_b], [own_small]
        for message in messages:
            for value, kept in ((own_a, sums_a), (own_b, sums_b), (own_small, sums)):
                if value is own_a and apart:
                    continue
                size = value.size // cols
                kept.append(message[:size].reshape(value.shape))
                message = message[size:]

        def add(got):
            got = [value.astype(full) for value in got]
            while len(got) > 1:
                got = [got[i] + got[i + 1] for i in range(0, len(got), 2)]
            return got[0].astype(end)

        return add(sums_a), add(sums_b), add(sums)


def on_device(links, hidden, grad_out, seq_lens, mix_state, out_state, depth_state, span_state, norm_state,
              up_state, bias_state, down_state):
    barrier = lax.optimization_barrier
    width = hidden.shape[1]
    half = width // 2
    hid_dev = up_state.shape[3]
    rows_dev = mix_state.shape[2]
    up_state = jnp.swapaxes(up_state, 2, 3)
    depth_state = jnp.swapaxes(depth_state, 0, 1)
    span_state = jnp.transpose(span_state, (2, 0, 1))
    place = jnp.stack([links.place("grp"), lax.axis_index("dp")]).astype(jnp.int32)
    tokens = Tokens(hidden.shape[0], width, seq_lens.shape[0], place)
    tokens.hid_dev = hid_dev

    mix_low = mix_state[0].astype(low)
    bias_row = jnp.pad(bias_state[0].astype(low), ((0, rows_dev - 1), (0, LANES - hid_dev)))
    shard = jnp.concatenate(
        [mix_low[0], mix_low[4], mix_low[1], mix_low[2], bias_row, out_state[0].astype(low), mix_low[3]], axis=1)
    feed_shard = jnp.concatenate([up_state[0, 0], down_state[0, 0]], axis=1).astype(low)

    def block(value):
        return value.reshape((1, 1, 1, 1) + value.shape)

    def both_cores(value):
        value = value.reshape(-1, value.shape[-1])
        return value, links.swap(value, "grp", 1)

    mixer = links.fetch(block(shard), "z")
    mixer, hidden_o, grad_o, e = barrier((mixer, *tokens.order(hidden, grad_out, depth_state)))
    mixer = links.merge(mixer, "z")
    split = 4 * half + LANES
    wa, wb = mixer[..., :split], mixer[..., split:]
    wa, wb = links.gather(wa, "y"), links.gather(wb, "x")
    wa, wb, feed_shard = barrier((wa, wb, feed_shard))
    wa, wb, feed = barrier((links.fetch(wa, "x"), links.fetch(wb, "y"), links.fetch(block(feed_shard), "z")))
    wa, wb = both_cores(links.merge(wa, "x")), both_cores(links.merge(wb, "y"))
    wa, wb, feed = barrier((wa, wb, feed))
    feed = links.merge(feed, "z")
    up, down = links.fetch(feed[..., :half], "y"), links.fetch(feed[..., half:], "x")

    qwkv, u, bias, spant = tokens.project(hidden_o, e, wa, wb, span_state, hid_dev * links.size)
    up, down, qwkv, u = barrier((up, down, qwkv, u))
    up, down = links.fetch(links.merge(up, "y"), "x"), links.fetch(links.merge(down, "x"), "y")
    p, conv, a, ctx, y = tokens.mix(seq_lens, qwkv, u, spant, wb)
    up, down, y = barrier((up, down, y))
    up, down = both_cores(links.merge(up, "x")), both_cores(links.merge(down, "y"))
    small, result, gb, gm, keep_f, piece_f, keep_o, piece_o = tokens.feed(
        y, hidden_o, grad_o, norm_state, up, down, bias, ctx, conv, wb)

    def blocks(value):
        return value.reshape(links.shape + (-1, value.shape[-1]))

    d_feed, d_out = blocks(links.join(keep_f, piece_f)), blocks(links.join(keep_o, piece_o))
    small = links.join(small, small)
    sums = [jnp.concatenate([d_feed[..., cols], d_out[..., cols]], axis=4).astype(low) for cols in (slice(0, half), slice(half, width))]
    *sums, gm = barrier((*sums, small.astype(low), gm))
    sent = links.send(*sums, "x", "y")
    gqw, gkv, gu, ge, d_span = tokens.mixer_back(qwkv, a, gm, u, p, wb, spant)
    sent, gqw, gkv, gu, ge, d_span = barrier((sent, gqw, gkv, gu, ge, d_span))
    sent = links.send(*links.finish(sent), "y", "x")
    keep_a, piece_a, keep_b, piece_b, small = tokens.weights(hidden_o, e, gqw, gkv, gu, ge, d_span, links.size)
    sent, keep_a, piece_a, keep_b, piece_b, small = barrier((sent, keep_a, piece_a, keep_b, piece_b, small))

    feed_sent = links.send(*links.finish(sent), "zl", "zl")
    sums = (blocks(links.join(keep_a, piece_a).astype(low)), blocks(links.join(keep_b, piece_b).astype(low)),
            links.join(small, small).astype(low))
    sums, gqw, ge = barrier((sums, gqw, ge))
    sent = links.send(*sums, "x", "y")
    gx = tokens.input_grad(gb, gqw, gkv, ge, wa, depth_state)
    feed_sent, sent, gx = barrier((feed_sent, sent, gx))
    sent = links.send(*links.finish(sent), "y", "x")
    feed_sent = links.send(*links.finish(feed_sent), "zh", "zh")
    sums = barrier(links.finish(sent))
    feed_sums = links.finish(feed_sent, full)
    grad_a, grad_b, small = links.finish(links.send(*sums, "z", "z"), full)

    def twice(state, at=0):
        shape = state.shape[:at] + (2,) + state.shape[at + 1 :]
        return [shape, shape]

    def flat(value):
        return value.reshape(-1, value.shape[-1])

    feed_a, feed_b, feed_small = feed_sums
    feed_out = adam_call(
        adam_feed_kernel,
        [place, out_state, norm_state, up_state, bias_state, down_state, flat(feed_a), flat(feed_b), feed_small],
        twice(out_state) + twice(norm_state) + twice(up_state) + twice(bias_state) + twice(down_state), scalars=1)
    mixed = adam_call(
        adam_mix_kernel,
        [mix_state, depth_state, span_state, flat(grad_a), flat(grad_b), small],
        twice(mix_state) + twice(depth_state, 1) + twice(span_state, 1))
    depth_out = [jnp.swapaxes(value, 0, 1) for value in mixed[2:4]]
    span_out = [jnp.transpose(value, (1, 2, 0)) for value in mixed[4:]]
    up_out = [jnp.swapaxes(value, 2, 3) for value in feed_out[4:6]]
    return (result, gx, *mixed[:2], *feed_out[:2], *depth_out, *span_out, *feed_out[2:4], *up_out, *feed_out[6:])


def solution(mesh):
    both = ("grp", "dp")
    mix, out = P(None, None, both, None), P(None, both, None)
    up, bias, down = P(None, "grp", None, "dp"), P(None, "grp", "dp"), P(None, "grp", "dp", None)
    rows = P(both, None)
    return jax.shard_map(
        functools.partial(on_device, Links(mesh)),
        mesh=mesh,
        in_specs=(rows, rows, P(both), mix, out, P(), P(), P(), up, bias, down),
        out_specs=(rows, rows, mix, mix, out, out, P(), P(), P(), P(), P(), P(), up, up, bias, bias, down, down),
        check_vma=False,
    )
```

```python
import functools

import jax
import jax.numpy as jnp
from jax import lax
from jax.experimental import pallas as pl
from jax.experimental.pallas import tpu as pltpu
from jax.sharding import PartitionSpec as P

HEADS = 6
HS = 64
KERNEL = 9
STEP = 7
REACH = KERNEL // 2
TAP = 8
LANES = 128
PAD = 8
EDGE = REACH * PAD

beta_one = 0.9
beta_two = 0.999
adam_eps = 1e-06
ema_rate = 0.99
decay_rate = 0.01
rate_mix = 0.06
rate_out = 0.12
rate_depth = 0.4
rate_span = 0.08
rate_norm = 0.5
rate_up = 0.08
rate_bias = 0.3
rate_down = 0.04

low = jnp.bfloat16
full = jnp.float32
NN = (((1,), (0,)), ((), ()))
NT = (((1,), (1,)), ((), ()))
TN = (((0,), (0,)), ((), ()))


def dot(left, right, dims=NN):
    return lax.dot_general(left, right, dims, preferred_element_type=full)


def rounded(value):
    return value.astype(low).astype(full)


def row_loop(rows, chunk, body):
    for r in range(0, rows, chunk):
        body(r)


def spread_table(width):
    row = lax.broadcasted_iota(jnp.int32, (LANES, 1), 0)
    col = lax.broadcasted_iota(jnp.int32, (1, KERNEL * width), 1)
    head = row % TAP
    first = (row // TAP) * width + head * HS
    first = jnp.where(head < HEADS, first, -HS)
    return ((col >= first) & (col < first + HS)).astype(full).astype(low)


def tap_table():
    row = lax.broadcasted_iota(jnp.int32, (LANES, HEADS * KERNEL), 0)
    col = lax.broadcasted_iota(jnp.int32, (LANES, HEADS * KERNEL), 1)
    return ((col % KERNEL) * TAP + col // KERNEL == row).astype(full).astype(low)


def copy_halves(place_ref, mine, other, target, sems, first, cols):
    rows = mine.shape[0]
    copies = []
    for i, (half, at) in enumerate(((mine, place_ref[0]), (other, 1 - place_ref[0]))):
        copy = pltpu.make_async_copy(
            half.at[:, pl.ds(first, cols)], target.at[pl.ds(pl.multiple_of(at * rows, rows), rows), :], sems.at[i])
        copy.start()
        copies.append(copy)
    return copies


def put_blocks(place_ref, value_ref, keep_ref, piece_ref):
    devices, _, half = keep_ref.shape
    parts = value_ref.shape[1] // half
    rows = half // devices
    for ref, at in ((keep_ref, place_ref[0]), (piece_ref, 1 - place_ref[0])):
        for m in range(parts):
            value = value_ref[pl.ds(pl.multiple_of(at * half, half), half), m * half : (m + 1) * half]
            for n in range(devices):
                ref[n, m * rows : (m + 1) * rows, :] = value[n * rows : (n + 1) * rows].astype(low)


def fill_padded(ref, value):
    rows = value.shape[0]
    value = value.astype(full)
    place = lax.broadcasted_iota(jnp.int32, (PAD, 1), 0)
    ref[EDGE : EDGE + rows, :] = value
    for i in range(REACH):
        before = value[rows - EDGE + i * PAD : rows - EDGE + (i + 1) * PAD]
        ref[i * PAD : (i + 1) * PAD, :] = jnp.where(place == 0, 0.0, pltpu.roll(before, 1, 0))
        after = value[i * PAD : (i + 1) * PAD]
        ref[EDGE + rows + i * PAD : EDGE + rows + (i + 1) * PAD, :] = jnp.where(
            place == PAD - 1, 0.0, pltpu.roll(after, PAD - 1, 0))


def order_matrix(rows, back=False):
    row = lax.broadcasted_iota(jnp.int32, (rows, rows), 0)
    col = lax.broadcasted_iota(jnp.int32, (1, rows), 1)
    places = rows // PAD
    at = (col % PAD) * places + col // PAD if back else (col % places) * PAD + col // places
    return (row == at).astype(full).astype(low)


def order_kernel(x_ref, g_ref, depth_ref, xo_ref, go_ref, e_ref, xpad):
    rows, width = x_ref.shape
    order = order_matrix(rows)
    x = dot(order, x_ref[...])
    xo_ref[...] = x.astype(low)
    go_ref[...] = dot(order, g_ref[...]).astype(low)
    fill_padded(xpad, x)

    rates = [rounded(depth_ref[j, 0:1]) for j in range(KERNEL)]

    def depth_rows(r):
        acc = rates[0] * xpad[pl.ds(r, 32), :]
        for j in range(1, KERNEL):
            acc = acc + rates[j] * xpad[pl.ds(r + PAD * j, 32), :]
        e_ref[pl.ds(r, 32), :] = acc.astype(low)

    row_loop(rows, 32, depth_rows)


def project_kernel(place_ref, x_ref, e_ref, wam_ref, wao_ref, wbm_ref, wbo_ref, bm_ref, bo_ref, span_ref,
                   qwkv_ref, u_ref, bias_ref, spant_ref,
                   wa_ref, w3_ref, sems):
    rows, width = x_ref.shape
    half = width // 2

    @pl.when(pl.program_id(0) == 0)
    def _():
        copies = copy_halves(place_ref, wam_ref, wao_ref, wa_ref, sems.at[0], 0, 4 * half)
        copies += copy_halves(place_ref, wbm_ref, wbo_ref, w3_ref, sems.at[1], width, half)
        spant_ref[...] = dot(tap_table(), span_ref[:, 0, :].astype(low)).astype(low)
        hid_dev = bias_ref.shape[1] // bm_ref.shape[0]
        for n in range(bm_ref.shape[0]):
            cols = slice(n * hid_dev, (n + 1) * hid_dev)
            mine, other = bm_ref[n].astype(full)[0:1, 0:hid_dev], bo_ref[n].astype(full)[0:1, 0:hid_dev]
            bias_ref[0:1, cols] = jnp.where(place_ref[0] == 0, mine, other)
            bias_ref[1:2, cols] = jnp.where(place_ref[0] == 0, other, mine)
        for copy in copies:
            copy.wait()

    x = x_ref[...]
    for c in range(4):
        qwkv_ref[:, c * half : (c + 1) * half] = dot(x, wa_ref[:, c * half : (c + 1) * half]).astype(low)
    u_ref[...] = dot(e_ref[...], w3_ref[...]).astype(low)


def mix_kernel(lens_ref, place_ref, qwkv_ref, u_ref, spant_ref, wbm_ref, wbo_ref,
               p_ref, conv_ref, a_ref, ctx_ref, y_ref,
               wpad, taps, wo_ref, spread_ref, sems):
    rows, half = u_ref.shape

    @pl.when(pl.program_id(0) == 0)
    def _():
        copies = copy_halves(place_ref, wbm_ref, wbo_ref, wo_ref, sems, 0, 2 * half)
        spread_ref[...] = spread_table(half)
        for copy in copies:
            copy.wait()

    r = (u_ref[...].astype(full) * qwkv_ref[:, 0:half].astype(full)).astype(low)
    logits = rounded(dot(r, spant_ref[...], NT))
    lt = logits.T[0 : KERNEL * TAP].reshape(KERNEL, TAP, rows)
    top = jnp.max(lt, axis=0, keepdims=True)
    ex = jnp.exp(lt - top)
    pt = (ex / jnp.sum(ex, axis=0, keepdims=True)).reshape(KERNEL * TAP, rows)
    p = jnp.concatenate([pt, jnp.zeros((LANES - KERNEL * TAP, rows), full)], axis=0).T
    p_ref[...] = p
    fill_padded(wpad, qwkv_ref[:, half : 2 * half])
    p_low = p.astype(low)
    for j in range(KERNEL):
        taps[:, j * half : (j + 1) * half] = dot(p_low, spread_ref[:, j * half : (j + 1) * half])

    def conv_rows(r):
        acc = taps[pl.ds(r, 32), 0:half] * wpad[pl.ds(r, 32), :]
        for j in range(1, KERNEL):
            acc = acc + taps[pl.ds(r, 32), j * half : (j + 1) * half] * wpad[pl.ds(r + PAD * j, 32), :]
        conv_ref[pl.ds(r, 32), :] = acc.astype(low)

    row_loop(rows, 32, conv_rows)
    seq_len = lens_ref[pl.program_id(0)]
    lane = lax.broadcasted_iota(jnp.int32, (1, LANES), 1)
    row = lax.broadcasted_iota(jnp.int32, (1, rows), 1)
    live = (row % PAD) * (rows // PAD) + row // PAD < seq_len
    for pair in range(HEADS // 2):
        at = pair * LANES
        q = qwkv_ref[:, at : at + LANES]
        k = qwkv_ref[:, 2 * half + at : 2 * half + at + LANES]
        v = qwkv_ref[:, 3 * half + at : 3 * half + at + LANES]
        outs = []
        for side in range(2):
            pick = jnp.where((lane // HS) == side, HS ** (-0.5), 0.0).astype(low)
            scores = dot(q * pick, k, NT)
            scores = jnp.where(live, scores, -1000000000.0)
            top = jnp.max(scores, axis=1, keepdims=True)
            ex = jnp.exp(scores - top)
            a = (ex * (1.0 / jnp.sum(ex, axis=1, keepdims=True))).astype(low)
            a_ref[0, 2 * pair + side] = a
            outs.append(dot(a, v))
        ctx_ref[:, at : at + LANES] = jnp.where((lane // HS) == 0, outs[0], outs[1]).astype(low)
    y_ref[...] = (dot(ctx_ref[...], wo_ref[0:half, :]) + dot(conv_ref[...], wo_ref[half:, :])).astype(low)


def normed(value):
    centered = value - jnp.mean(value, axis=1, keepdims=True)
    variance = jnp.mean(centered * centered, axis=1, keepdims=True)
    rstd = lax.rsqrt(variance + 1e-12)
    return centered * rstd, rstd


def feed_kernel(count, place_ref, norm_ref, bias_ref, y_hbm, x_hbm, g_hbm, ctx_hbm, conv_hbm, upm_hbm, upo_hbm, downm_hbm, downo_hbm, wbm_hbm, wbo_hbm,
                small_ref, res_hbm, gb_hbm, gm_hbm, keep_hbm, piece_hbm, keep_o_hbm, piece_o_hbm,
                small_s, y_s, x_s, g_s, m_s, up_s, down_s, wo_s, act_s, gpre_s, res_s, gb_s, gm_s, ft_s, got_s, df_s, do_s,
                in_sems, out_sems):
    tokens, width = y_s.shape
    half = width // 2
    hid = bias_ref.shape[1]
    length = tokens // count
    waits, outs = {}, []

    def fetch(name, source, target):
        copy = pltpu.make_async_copy(source, target, in_sems.at[len(waits)])
        copy.start()
        waits[name] = copy

    def put(source, target):
        copy = pltpu.make_async_copy(source, target, out_sems.at[len(outs)])
        copy.start()
        outs.append(copy)

    seqs = [slice(n * length, (n + 1) * length) for n in range(count)]
    for n, rows in enumerate(seqs):
        fetch(("y", n), y_hbm.at[rows], y_s.at[rows])
        fetch(("x", n), x_hbm.at[rows], x_s.at[rows])
        if n == 0:
            for name, pair, target in (("up", (upm_hbm, upo_hbm), up_s), ("down", (downm_hbm, downo_hbm), down_s)):
                for i, at in enumerate((place_ref[0], 1 - place_ref[0])):
                    fetch((name, i), pair[i], target.at[pl.ds(pl.multiple_of(at * hid, hid), hid), :])
        fetch(("g", n), g_hbm.at[rows], g_s.at[rows])
        if n == 0:
            for i, (part, at) in enumerate(((wbm_hbm, place_ref[0]), (wbo_hbm, 1 - place_ref[0]))):
                fetch(("wo", i), part.at[:, pl.ds(0, width)], wo_s.at[pl.ds(pl.multiple_of(at * half, half), half), :])
    fetch("ctx", ctx_hbm, m_s.at[:, pl.ds(0, half)])
    fetch("conv", conv_hbm, m_s.at[:, pl.ds(half, half)])

    g1, c1, g2, c2 = (norm_ref[0, i : i + 1] for i in range(4))
    sums = [jnp.zeros((1, width), full) for _ in range(4)]
    dbias = [jnp.zeros((1, hid), full) for _ in range(2)]
    groups = [(slice(g * hid, (g + 1) * hid), slice(g * half, (g + 1) * half)) for g in range(2)]
    kept = [{} for _ in seqs]

    def wait(name):
        if name in waits:
            waits.pop(name).wait()

    def enter(n):
        wait(("y", n))
        wait(("x", n))
        zh1, rstd1 = normed(y_s[seqs[n]].astype(full) + x_s[seqs[n]].astype(full))
        f = (zh1 * g1 + c1).astype(low)
        kept[n].update(zh1=zh1, rstd1=rstd1, f=f, parts=[])
        ft_s[:, seqs[n]] = f.T

    def ahead(n, g):
        hidden, cols = groups[g]
        wait(("up", 0))
        wait(("up", 1))
        pre = dot(kept[n]["f"][:, cols], up_s[hidden, :], NT) + bias_ref[g : g + 1, :]
        cdf = 0.5 * (1.0 + lax.erf(pre * 2.0 ** (-0.5)))
        act_s[seqs[n], hidden] = (pre * cdf).astype(low)
        gpre_s[seqs[n], hidden] = (cdf + pre * (jnp.exp(-0.5 * pre * pre) * 0.3989422804014327)).astype(low)
        wait(("down", 0))
        wait(("down", 1))
        kept[n]["parts"].append(rounded(dot(act_s[seqs[n], hidden], down_s[hidden, :])))

    def turn(n):
        rows = seqs[n]
        h1 = kept[n]["zh1"] * g1 + c1
        zh2, rstd2 = normed(h1 + jnp.concatenate(kept[n]["parts"], axis=1))
        result = (zh2 * g2 + c2).astype(low)
        res_s[rows] = dot(order_matrix(length, True), result).astype(low)
        put(res_s.at[rows], res_hbm.at[rows])
        wait(("g", n))
        grad = g_s[rows].astype(full)
        sums[2] = sums[2] + jnp.sum(grad * zh2, axis=0, keepdims=True)
        sums[3] = sums[3] + jnp.sum(grad, axis=0, keepdims=True)
        dz = grad * g2
        gz = (dz - jnp.mean(dz, axis=1, keepdims=True) - zh2 * jnp.mean(dz * zh2, axis=1, keepdims=True)) * rstd2
        go = gz.astype(low)
        got_s[:, rows] = go.T
        kept[n].update(gz=gz, go=go, parts=[])

    def behind(n, g):
        hidden, cols = groups[g]
        slope = gpre_s[seqs[n], hidden].astype(full)
        gpre = (dot(kept[n]["go"][:, cols], down_s[hidden, :], NT) * slope).astype(low)
        gpre_s[seqs[n], hidden] = gpre
        dbias[g] = dbias[g] + jnp.sum(gpre.astype(full), axis=0, keepdims=True)
        kept[n]["parts"].append(rounded(dot(gpre, up_s[hidden, :])))

    def leave(n):
        rows, zh1 = seqs[n], kept[n]["zh1"]
        gh1 = kept[n]["gz"] + jnp.concatenate(kept[n]["parts"], axis=1)
        sums[0] = sums[0] + jnp.sum(gh1 * zh1, axis=0, keepdims=True)
        sums[1] = sums[1] + jnp.sum(gh1, axis=0, keepdims=True)
        dz1 = gh1 * g1
        gy = (dz1 - jnp.mean(dz1, axis=1, keepdims=True) - zh1 * jnp.mean(dz1 * zh1, axis=1, keepdims=True)) * kept[n]["rstd1"]
        gb_s[rows] = gy.astype(low)
        put(gb_s.at[rows], gb_hbm.at[rows])

    def through(n):
        rows = seqs[n]
        wait(("wo", 0))
        wait(("wo", 1))
        gm_s[rows] = dot(gb_s[rows], wo_s[...], NT).astype(low)
        put(gm_s.at[rows], gm_hbm.at[rows])

    first, *rest = range(count)
    enter(first)
    ahead(first, 0)
    for n in rest:
        enter(n)
    ahead(first, 1)
    for n in rest:
        ahead(n, 0)
        turn(n - 1)
        ahead(n, 1)
        behind(n - 1, 0)
        if n == rest[-1]:
            turn(n)
        behind(n - 1, 1)
        if n == rest[-1]:
            behind(n, 0)
        leave(n - 1)
        if n == rest[-1]:
            behind(n, 1)
        through(n - 1)
    if not rest:
        turn(first)
        behind(first, 0)
        behind(first, 1)
    leave(count - 1)
    through(count - 1)

    for i, (at, target) in enumerate(((1 - place_ref[0], piece_hbm), (place_ref[0], keep_hbm))):
        hidden = pl.ds(pl.multiple_of(at * hid, LANES), hid)
        cols = pl.ds(pl.multiple_of(at * half, half), half)
        df_s[i, :, 0:half] = dot(ft_s[cols, :], gpre_s[:, hidden]).astype(low).T
        df_s[i, :, half:] = dot(got_s[cols, :], act_s[:, hidden]).astype(low).T
        put(df_s.at[i], target)
    wait("ctx")
    wait("conv")
    do_s[...] = dot(m_s[...].T, gb_s[...]).astype(low)
    for at, target in ((1 - place_ref[0], piece_o_hbm), (place_ref[0], keep_o_hbm)):
        put(do_s.at[pl.ds(pl.multiple_of(at * half, half), half), :], target)
    for i in range(4):
        g, side = divmod(i, 2)
        for j in range(2):
            small_s[8 * j + i : 8 * j + i + 1, :] = sums[i][:, j * half : (j + 1) * half]
            at = side * width + j * half
            small_s[8 * j + 4 + i : 8 * j + 5 + i, :] = dbias[g][:, at : at + half]
    small_ref[...] = small_s[...].astype(low)
    for copy in outs:
        copy.wait()


def mixer_back_kernel(place_ref, qwkv_ref, a_ref, gm_ref, u_ref, p_ref, wbm_ref, wbo_ref, spant_ref,
                      gqw_ref, gkv_ref, gu_ref, ge_ref, dspan_ref,
                      gqa, wpad, gpad, taps, prods, w3_ref, spread_ref, sems):
    rows, half = u_ref.shape

    @pl.when(pl.program_id(0) == 0)
    def _():
        copies = copy_halves(place_ref, wbm_ref, wbo_ref, w3_ref, sems, 2 * half, half)
        dspan_ref[...] = jnp.zeros_like(dspan_ref)
        spread_ref[...] = spread_table(half)
        for copy in copies:
            copy.wait()

    lane = lax.broadcasted_iota(jnp.int32, (1, LANES), 1)
    for pair in range(HEADS // 2):
        at = pair * LANES
        q = qwkv_ref[:, at : at + LANES]
        k = qwkv_ref[:, 2 * half + at : 2 * half + at + LANES]
        v = qwkv_ref[:, 3 * half + at : 3 * half + at + LANES]
        gctx = gm_ref[:, at : at + LANES]
        qt, gctxt = q.T, gctx.T
        gqs, gks, gvs = [], [], []
        for side in range(2):
            pick = jnp.where((lane // HS) == side, 1.0, 0.0).astype(low)
            a_low = a_ref[0, 2 * pair + side]
            a = a_low.astype(full)
            ga = dot(gctx * pick, v, NT)
            gs = (a * (ga - jnp.sum(a * ga, axis=1, keepdims=True))).astype(low)
            gqs.append(dot(gs, k))
            gks.append(dot(qt, gs))
            gvs.append(dot(gctxt, a_low))
        first = (lane // HS) == 0
        gqa[:, at : at + LANES] = jnp.where(first, gqs[0], gqs[1]) * HS ** (-0.5)
        gk = jnp.concatenate([gks[0][0:HS], gks[1][HS:]], axis=0) * HS ** (-0.5)
        gv = jnp.concatenate([gvs[0][0:HS], gvs[1][HS:]], axis=0)
        gkv_ref[:, at : at + LANES] = gk.T.astype(low)
        gkv_ref[:, half + at : half + at + LANES] = gv.T.astype(low)
    fill_padded(wpad, qwkv_ref[:, half : 2 * half])
    fill_padded(gpad, gm_ref[:, half:])
    p = p_ref[...]
    p_low = p.astype(low)
    for j in range(KERNEL):
        cols = slice(j * half, (j + 1) * half)
        fill_padded(taps.at[:, cols], dot(p_low, spread_ref[:, cols]))

    def conv_rows(r):
        here = gpad[pl.ds(r + EDGE, 32), :]
        acc = None
        for j in range(KERNEL):
            cols = slice(j * half, (j + 1) * half)
            prods[pl.ds(r, 32), cols] = (here * wpad[pl.ds(r + PAD * j, 32), :]).astype(low)
            back = pl.ds(r + PAD * (2 * REACH - j), 32)
            term = taps[back, cols] * gpad[back, :]
            acc = term if acc is None else acc + term
        gqw_ref[pl.ds(r, 32), half:] = acc.astype(low)

    row_loop(rows, 32, conv_rows)
    gp = dot(prods[...], spread_ref[...], NT)
    gpt = gp.T[0 : KERNEL * TAP].reshape(KERNEL, TAP, rows)
    pt = p.T[0 : KERNEL * TAP].reshape(KERNEL, TAP, rows)
    glt = pt * (gpt - jnp.sum(pt * gpt, axis=0, keepdims=True))
    glt = jnp.concatenate([glt.reshape(KERNEL * TAP, rows), jnp.zeros((LANES - KERNEL * TAP, rows), full)], axis=0)
    gl = glt.T.astype(low)
    q = qwkv_ref[:, 0:half].astype(full)
    u = u_ref[...].astype(full)
    r = (u * q).astype(low)
    dspan_ref[...] += dot(glt.astype(low), r)
    gr = rounded(dot(gl, spant_ref[...]))
    gqw_ref[:, 0:half] = (gqa[...] + gr * u).astype(low)
    gu = (gr * q).astype(low)
    gu_ref[...] = gu
    ge_ref[...] = dot(gu, w3_ref[...], NT).astype(low)


SMALL_ROWS = 2 * KERNEL + HEADS * KERNEL


def weight_kernel(place_ref, x_ref, e_ref, gqw_ref, gkv_ref, gu_ref, ge_ref, dspan_ref,
                  keep_a_ref, piece_a_ref, keep_b_ref, piece_b_ref, small_ref,
                  xpad, acc_a, acc_b, small, rows_s):
    step, last = pl.program_id(0), pl.num_programs(0) - 1
    rows, width = x_ref.shape
    half = width // 2

    @pl.when(step == 0)
    def _():
        acc_a[...] = jnp.zeros_like(acc_a)
        acc_b[...] = jnp.zeros_like(acc_b)
        small[...] = jnp.zeros_like(small)

    x = x_ref[...]
    xt = x.T
    acc_a[:, 0:width] += dot(xt, gqw_ref[...])
    acc_a[:, width:] += dot(xt, gkv_ref[:, 0:half])
    acc_b[:, 0:half] += dot(xt, gkv_ref[:, half:])
    acc_b[:, half:] += dot(e_ref[...].T, gu_ref[...])
    fill_padded(xpad, x)
    for c in range(0, width, LANES):
        cols = slice(c, c + LANES)

        sums = [jnp.zeros((PAD, LANES), full) for _ in range(KERNEL)]
        for r in range(0, rows, 64):
            ge = ge_ref[pl.ds(r, 64), cols].astype(full)
            for j in range(KERNEL):
                prod = ge * xpad[pl.ds(r + PAD * j, 64), cols]
                sums[j] = sums[j] + jnp.sum(prod.reshape(PAD, PAD, LANES), axis=0)
        for j in range(KERNEL):
            small[j : j + 1, cols] += jnp.sum(sums[j], axis=0, keepdims=True)

    @pl.when(step == last)
    def _():
        put_blocks(place_ref, acc_a, keep_a_ref, piece_a_ref)
        put_blocks(place_ref, acc_b, keep_b_ref, piece_b_ref)
        for side in range(2):
            rows_s[side * KERNEL : (side + 1) * KERNEL, :] = small[0:KERNEL, side * half : (side + 1) * half]
        rows_s[2 * KERNEL :, :] = dot(tap_table(), dspan_ref[...].astype(low), TN)
        small_ref[...] = rows_s[...].astype(low)


def input_kernel(place_ref, gb_ref, gqw_ref, gkv_ref, ge_ref, wam_ref, wao_ref, depth_ref,
                 gx_ref, gepad, gx_s, wa_ref, sems):
    rows, width = gb_ref.shape

    @pl.when(pl.program_id(0) == 0)
    def _():
        for copy in copy_halves(place_ref, wam_ref, wao_ref, wa_ref, sems, 0, 2 * width):
            copy.wait()

    fill_padded(gepad, ge_ref[...])
    gx_s[...] = gb_ref[...].astype(full) + dot(gqw_ref[...], wa_ref[:, 0:width], NT) + dot(gkv_ref[...], wa_ref[:, width:], NT)

    rates = [rounded(depth_ref[j, 0:1]) for j in range(KERNEL)]

    def shift_rows(r):
        acc = gx_s[pl.ds(r, 32), :]
        for j in range(KERNEL):
            acc = acc + rates[j] * gepad[pl.ds(r + PAD * (2 * REACH - j), 32), :]
        gx_s[pl.ds(r, 32), :] = acc

    row_loop(rows, 32, shift_rows)
    gx_ref[...] = dot(order_matrix(rows, True), gx_s[...].astype(low)).astype(low)


def adam_step(old, one, two, mean, grad, step_rate, wd_rate):
    moment_one = beta_one * one + (1.0 - beta_one) * grad
    moment_two = beta_two * two + (1.0 - beta_two) * grad * grad
    scaled_one = moment_one / (1.0 - beta_one**STEP)
    scaled_two = moment_two / (1.0 - beta_two**STEP)
    weight = old - step_rate * (scaled_one / (jnp.sqrt(scaled_two) + adam_eps) + wd_rate * old)
    return weight, ema_rate * mean + (1.0 - ema_rate) * weight, moment_one, moment_two


def adam_at(state, new, moments, at, grad, step_rate, wd_rate):
    values = adam_step(*(state[at(slot)] for slot in range(4)), grad, step_rate, wd_rate)
    new[at(0)], new[at(1)], moments[at(0)], moments[at(1)] = values


def adam_mix_kernel(mix, depth, span, ga_ref, gb_ref, small,
                    mix_new, mix_moments, depth_new, depth_moments, span_new, span_moments):
    rows = mix.shape[2]
    sources = [(ga_ref, 0), (ga_ref, 2), (gb_ref, 0), (gb_ref, 1), (ga_ref, 1)]
    for i, (ref, at) in enumerate(sources):
        adam_at(mix, mix_new, mix_moments, lambda slot: (slot, i), ref[at * rows : (at + 1) * rows, :], rate_mix, decay_rate)
    grad = jnp.concatenate([small[0:KERNEL], small[KERNEL : 2 * KERNEL]], axis=1)
    adam_at(depth, depth_new, depth_moments, lambda slot: (slice(None), slot), grad, rate_depth, decay_rate)
    adam_at(span, span_new, span_moments, lambda slot: (slice(None), slot), small[2 * KERNEL :], rate_span, decay_rate)


def adam_feed_kernel(place_ref, out, norm, up, bias, down, ga_ref, gb_ref, small,
                     out_new, out_moments, norm_new, norm_moments,
                     up_new, up_moments, bias_new, bias_moments, down_new, down_moments):
    half = down.shape[3]
    width = 2 * half
    hid_dev = down.shape[2]
    adam_at(up, up_new, up_moments, lambda slot: (slot, 0), ga_ref[0:hid_dev, :], rate_up, decay_rate)
    adam_at(down, down_new, down_moments, lambda slot: (slot, 0), gb_ref[0:hid_dev, :], rate_down, decay_rate)
    grad = jnp.concatenate([ga_ref[hid_dev:, :], gb_ref[hid_dev:, :]], axis=1)
    adam_at(out, out_new, out_moments, lambda slot: slot, grad, rate_out, decay_rate)
    lines = jnp.concatenate([small[0:8], small[8:16]], axis=1)
    adam_at(norm, norm_new, norm_moments, lambda slot: slot, lines[0:4], rate_norm, 0.0)
    row = lax.broadcasted_iota(jnp.int32, (width, hid_dev), 0)
    col = lax.broadcasted_iota(jnp.int32, (width, hid_dev), 1)
    grad = jnp.zeros((1, hid_dev), full)
    for i in range(4):
        group, side = divmod(i, 2)
        line = jnp.where(place_ref[0] == group, lines[4 + i : 5 + i, :], 0.0)
        here = (row + side * width == col + place_ref[1] * hid_dev).astype(full).astype(low)
        high = line.astype(low)
        rest = (line - high.astype(full)).astype(low)
        both = dot(jnp.concatenate([high, rest] + [jnp.zeros_like(high)] * 6, axis=0), here)
        grad = grad + both[0:1] + both[1:2]
    adam_at(bias, bias_new, bias_moments, lambda slot: slot, grad, rate_bias, 0.0)


def adam_call(kernel, inputs, shapes, scalars=0):
    vmem = pl.BlockSpec(memory_space=pltpu.VMEM)
    moved = sum(value.size for value in inputs) * 6
    return pl.pallas_call(
        kernel,
        in_specs=[pl.BlockSpec(memory_space=pltpu.SMEM)] * scalars + [vmem] * (len(inputs) - scalars),
        out_specs=[vmem] * len(shapes),
        out_shape=[struct(shape, full) for shape in shapes],
        compiler_params=pltpu.CompilerParams(vmem_limit_bytes=40 << 20),
        cost_estimate=pl.CostEstimate(flops=2 * moved, transcendentals=0, bytes_accessed=moved),
    )(*inputs)


def struct(shape, dtype):
    return jax.ShapeDtypeStruct(shape, dtype)


def rows_spec(rows, width, at=0):
    return pl.BlockSpec((rows, width), lambda i, *_: (i, at))


def whole(shape, index=None):
    index = index or (0,) * len(shape)
    return pl.BlockSpec(shape, lambda i, *_: index)


def call(kernel, grid, in_specs, out_specs, out_shape, scratch, flops, moved, limit, prefetch=0):
    return pl.pallas_call(
        kernel,
        grid_spec=pltpu.PrefetchScalarGridSpec(
            num_scalar_prefetch=prefetch, grid=grid, in_specs=in_specs, out_specs=out_specs, scratch_shapes=scratch),
        out_shape=out_shape,
        compiler_params=pltpu.CompilerParams(dimension_semantics=("arbitrary",), vmem_limit_bytes=limit << 20),
        cost_estimate=pl.CostEstimate(flops=int(flops), transcendentals=0, bytes_accessed=int(moved)),
    )


def once(shape, index=None):
    index = index or (0,) * len(shape)
    return pl.BlockSpec(shape, lambda i, *_: index, pipeline_mode=pl.Buffered(1))


class Tokens:
    def __init__(self, tokens, width, count, place):
        self.tokens, self.width, self.count, self.place = tokens, width, count, place
        self.length = length = tokens // count
        self.half = half = width // 2
        self.padded = length + 2 * EDGE
        self.wide, self.slim, self.lane = rows_spec(length, width), rows_spec(length, half), rows_spec(length, LANES)
        self.all_cols = rows_spec(length, 4 * half)
        self.heads = pl.BlockSpec((1, HEADS, length, length), lambda i, *_: (i, 0, 0, 0))
        self.any = pl.BlockSpec(memory_space=pl.ANY)
        self.low_wide, self.low_slim = struct((tokens, width), low), struct((tokens, half), low)
        self.low_half = struct((half, width), low)

    def order(self, hidden, grad_out, depth):
        return call(
            order_kernel, (self.count,),
            [self.wide, self.wide, once(depth.shape)],
            [self.wide] * 3, [self.low_wide] * 3,
            [pltpu.VMEM((self.padded, self.width), full)], 4e9, 8e6, 60,
        )(hidden, grad_out, depth)

    def project(self, hidden, e, wa, wb, span, hid):
        tokens, width, half = self.tokens, self.width, self.half
        V = pltpu.VMEM
        devices = 2 * hid // self.hid_dev
        blocks = [value.reshape(devices // 2, -1, value.shape[1]) for value in wa]
        bias = pl.BlockSpec((devices // 2, blocks[0].shape[1], LANES), lambda i, *_: (0, 0, 4 * half // LANES),
                            pipeline_mode=pl.Buffered(1))
        return call(
            project_kernel, (self.count,),
            [self.wide, self.wide] + [self.any] * 4 + [bias, bias, once(span.shape)],
            [self.all_cols, self.slim, whole((2, hid)), whole((LANES, half))],
            [struct((tokens, 4 * half), low), self.low_slim, struct((2, hid), full), struct((LANES, half), low)],
            [V((width, 4 * half), low), V((width, half), low), pltpu.SemaphoreType.DMA((2, 2))],
            8e9, 10e6, 24, prefetch=1,
        )(self.place, hidden, e, *wa, *wb, *blocks, span)

    def mix(self, lens, qwkv, u, spant, wb):
        tokens, length, width, half = self.tokens, self.length, self.width, self.half
        V = pltpu.VMEM
        return call(
            mix_kernel, (self.count,),
            [self.all_cols, self.slim, once((LANES, half)), self.any, self.any],
            [self.lane, self.slim, self.heads, self.slim, self.wide],
            [struct((tokens, LANES), full), self.low_slim, struct((self.count, HEADS, length, length), low),
             self.low_slim, self.low_wide],
            [V((self.padded, half), full), V((length, KERNEL * half), full), V((width, width), low),
             V((LANES, KERNEL * half), low), pltpu.SemaphoreType.DMA((2,))],
            20e9, 18e6, 44, prefetch=2,
        )(lens, self.place, qwkv, u, spant, *wb)

    def feed(self, y, hidden, grad_out, norm, up, down, bias, ctx, conv, wb):
        tokens, width, half = self.tokens, self.width, self.half
        hid = bias.shape[1]
        V = pltpu.VMEM
        vmem = pl.BlockSpec(memory_space=V)
        wide = V((tokens, width), low)
        return pl.pallas_call(
            functools.partial(feed_kernel, self.count),
            in_specs=[pl.BlockSpec(memory_space=pltpu.SMEM), vmem, vmem] + [self.any] * 11,
            out_specs=[vmem] + [self.any] * 7,
            out_shape=[struct((16, half), low)] + [self.low_wide] * 3 + [struct((hid, width), low)] * 2 + [self.low_half] * 2,
            scratch_shapes=[V((16, half), full), wide, wide, wide, wide, V((2 * hid, half), low), V((2 * hid, half), low), V((width, width), low),
                            V((tokens, 2 * hid), low), V((tokens, 2 * hid), low), wide, wide, wide,
                            V((width, tokens), low), V((width, tokens), low), V((2, hid, width), low), V((width, width), low),
                            pltpu.SemaphoreType.DMA((8 + 3 * self.count,)), pltpu.SemaphoreType.DMA((4 + 3 * self.count,))],
            compiler_params=pltpu.CompilerParams(vmem_limit_bytes=63 << 20),
            cost_estimate=pl.CostEstimate(flops=int(30e9), transcendentals=0, bytes_accessed=int(25e6)),
        )(self.place, norm, bias, y, hidden, grad_out, ctx, conv, *up, *down, *wb)

    def mixer_back(self, qwkv, a, gm, u, p, wb, spant):
        length, width, half = self.length, self.width, self.half
        V = pltpu.VMEM
        return call(
            mixer_back_kernel, (self.count,),
            [self.all_cols, self.heads, self.wide, self.slim, self.lane, self.any, self.any, once((LANES, half))],
            [self.wide, self.wide, self.slim, self.wide, whole((LANES, half))],
            [self.low_wide, self.low_wide, self.low_slim, self.low_wide, struct((LANES, half), full)],
            [V((length, half), full), V((self.padded, half), full), V((self.padded, half), full), V((self.padded, KERNEL * half), full),
             V((length, KERNEL * half), low), V((width, half), low), V((LANES, KERNEL * half), low), pltpu.SemaphoreType.DMA((2,))],
            30e9, 22e6, 44, prefetch=1,
        )(self.place, qwkv, a, gm, u, p, *wb, spant)

    def weights(self, hidden, e, gqw, gkv, gu, ge, d_span, devices):
        width, half = self.width, self.half
        shapes = [(devices, parts * half // devices, half) for parts in (3, 3, 2, 2)]
        V = pltpu.VMEM
        return call(
            weight_kernel, (self.count,),
            [self.wide, self.wide, self.wide, self.wide, self.slim, self.wide, whole((LANES, half))],
            [whole(shape) for shape in shapes] + [whole((SMALL_ROWS, half))],
            [struct(shape, low) for shape in shapes] + [struct((SMALL_ROWS, half), low)],
            [V((self.padded, width), full), V((width, 3 * half), full), V((width, width), full), V((16, width), full), V((SMALL_ROWS, half), full)],
            12e9, 16e6, 40, prefetch=1,
        )(self.place, hidden, e, gqw, gkv, gu, ge, d_span)

    def input_grad(self, gb, gqw, gkv, ge, wa, depth):
        length, width = self.length, self.width
        V = pltpu.VMEM
        return call(
            input_kernel, (self.count,),
            [self.wide, self.wide, self.wide, self.wide, self.any, self.any, once(depth.shape)],
            [self.wide], [self.low_wide],
            [V((self.padded, width), full), V((length, width), full), V((width, 2 * width), low), pltpu.SemaphoreType.DMA((2,))],
            10e9, 14e6, 36, prefetch=1,
        )(self.place, gb, gqw, gkv, ge, *wa, depth)[0]


class Links:
    def __init__(self, mesh):
        self.size = mesh.shape["dp"]
        self.grp = mesh.shape["grp"]
        deep = 4 if self.size % 4 == 0 else 1
        rest = self.size // deep
        wide = 1 << ((rest.bit_length() - 1) // 2)
        self.shape = (1, deep, rest // wide, wide)
        self.axes = {"z": (deep, rest, 1), "y": (rest // wide, wide, 2), "x": (wide, 1, 3),
                     "zl": (2, rest, 1), "zh": (deep // 2, 2 * rest, 1)}

    def place(self, name):
        if name == "grp":
            return lax.axis_index("grp")
        size, stride, _ = self.axes[name]
        return (lax.axis_index("dp") // stride) % size

    def swap(self, value, name, shift):
        if name == "grp":
            return lax.ppermute(value, "grp", [(i, i ^ shift) for i in range(self.grp)])
        size, stride, _ = self.axes[name]
        pairs = []
        for i in range(self.size):
            at = (i // stride) % size
            pairs.append((i, i + ((at ^ shift) - at) * stride))
        return lax.ppermute(value, "dp", pairs)

    def fetch(self, block, name):
        return [block] + [self.swap(block, name, k) for k in range(1, self.axes[name][0])]

    def merge(self, got, name):
        size, _, dim = self.axes[name]
        here = self.place(name)
        slots = []
        for j in range(size):
            value = got[size - 1]
            for k in range(size - 1):
                value = jnp.where(here == (j ^ k), got[k], value)
            slots.append(value)
        return jnp.concatenate(slots, axis=dim)

    def gather(self, block, name):
        return self.merge(self.fetch(block, name), name)

    def slices(self, block, name):
        size, _, dim = self.axes[name]
        here = self.place(name)
        if name == "zl":
            halves = block.reshape((1, block.shape[1] // 2, 2) + block.shape[2:])
            return [jnp.squeeze(lax.dynamic_slice_in_dim(halves, here ^ k, 1, 2), 2) for k in range(size)]
        return [lax.dynamic_slice_in_dim(block, here ^ k, 1, dim) for k in range(size)]

    def join(self, keep, piece):
        return keep.astype(full) + self.swap(piece, "grp", 1).astype(full)

    def send(self, a, b, small, name_a, name_b):
        cols = b.shape[-1]
        parts_a, parts_b = self.slices(a, name_a), self.slices(b, name_b)
        own = [parts_a[0], parts_b[0], small]
        apart = [] if name_a == name_b else [self.swap(part, name_a, k + 1) for k, part in enumerate(parts_a[1:])]
        messages = []
        for k in range(1, len(parts_b)):
            pieces = [parts_b[k].reshape(-1, cols), small]
            if name_a == name_b:
                pieces = [parts_a[k].reshape(-1, cols)] + pieces
            messages.append(self.swap(jnp.concatenate(pieces, axis=0), name_b, k))
        return own, apart, messages

    def finish(self, sent, end=low):
        (own_a, own_b, own_small), apart, messages = sent
        cols = own_b.shape[-1]
        sums_a, sums_b, sums = [own_a] + apart, [own_b], [own_small]
        for message in messages:
            for value, kept in ((own_a, sums_a), (own_b, sums_b), (own_small, sums)):
                if value is own_a and apart:
                    continue
                size = value.size // cols
                kept.append(message[:size].reshape(value.shape))
                message = message[size:]

        def add(got):
            got = [value.astype(full) for value in got]
            while len(got) > 1:
                got = [got[i] + got[i + 1] for i in range(0, len(got), 2)]
            return got[0].astype(end)

        return add(sums_a), add(sums_b), add(sums)


def on_device(links, hidden, grad_out, seq_lens, mix_state, out_state, depth_state, span_state, norm_state,
              up_state, bias_state, down_state):
    barrier = lax.optimization_barrier
    width = hidden.shape[1]
    half = width // 2
    hid_dev = up_state.shape[3]
    rows_dev = mix_state.shape[2]
    up_state = jnp.swapaxes(up_state, 2, 3)
    depth_state = jnp.swapaxes(depth_state, 0, 1)
    span_state = jnp.transpose(span_state, (2, 0, 1))
    place = jnp.stack([links.place("grp"), lax.axis_index("dp")]).astype(jnp.int32)
    tokens = Tokens(hidden.shape[0], width, seq_lens.shape[0], place)
    tokens.hid_dev = hid_dev

    mix_low = mix_state[0].astype(low)
    bias_row = jnp.pad(bias_state[0].astype(low), ((0, rows_dev - 1), (0, LANES - hid_dev)))
    shard = jnp.concatenate(
        [mix_low[0], mix_low[4], mix_low[1], mix_low[2], bias_row, out_state[0].astype(low), mix_low[3]], axis=1)
    feed_shard = jnp.concatenate([up_state[0, 0], down_state[0, 0]], axis=1).astype(low)

    def block(value):
        return value.reshape((1, 1, 1, 1) + value.shape)

    def both_cores(value):
        value = value.reshape(-1, value.shape[-1])
        return value, links.swap(value, "grp", 1)

    mixer = links.fetch(block(shard), "z")
    mixer, hidden_o, grad_o, e = barrier((mixer, *tokens.order(hidden, grad_out, depth_state)))
    mixer = links.merge(mixer, "z")
    split = 4 * half + LANES
    wa, wb = mixer[..., :split], mixer[..., split:]
    wa, wb = links.gather(wa, "y"), links.gather(wb, "x")
    wa, wb, feed_shard = barrier((wa, wb, feed_shard))
    wa, wb, feed = barrier((links.fetch(wa, "x"), links.fetch(wb, "y"), links.fetch(block(feed_shard), "z")))
    wa, wb = both_cores(links.merge(wa, "x")), both_cores(links.merge(wb, "y"))
    feed = links.merge(feed, "z")
    up, down = links.fetch(feed[..., :half], "y"), links.fetch(feed[..., half:], "x")

    qwkv, u, bias, spant = tokens.project(hidden_o, e, wa, wb, span_state, hid_dev * links.size)
    up, down, qwkv, u = barrier((up, down, qwkv, u))
    up, down = links.fetch(links.merge(up, "y"), "x"), links.fetch(links.merge(down, "x"), "y")
    p, conv, a, ctx, y = tokens.mix(seq_lens, qwkv, u, spant, wb)
    up, down, y = barrier((up, down, y))
    up, down = both_cores(links.merge(up, "x")), both_cores(links.merge(down, "y"))
    small, result, gb, gm, keep_f, piece_f, keep_o, piece_o = tokens.feed(
        y, hidden_o, grad_o, norm_state, up, down, bias, ctx, conv, wb)

    def blocks(value):
        return value.reshape(links.shape + (-1, value.shape[-1]))

    d_feed, d_out = blocks(links.join(keep_f, piece_f)), blocks(links.join(keep_o, piece_o))
    small = links.join(small, small)
    sums = [jnp.concatenate([d_feed[..., cols], d_out[..., cols]], axis=4).astype(low) for cols in (slice(0, half), slice(half, width))]
    *sums, gm = barrier((*sums, small.astype(low), gm))
    sent = links.send(*sums, "x", "y")
    gqw, gkv, gu, ge, d_span = tokens.mixer_back(qwkv, a, gm, u, p, wb, spant)
    sent, gqw, gkv, gu, ge, d_span = barrier((sent, gqw, gkv, gu, ge, d_span))
    sent = links.send(*links.finish(sent), "y", "x")
    keep_a, piece_a, keep_b, piece_b, small = tokens.weights(hidden_o, e, gqw, gkv, gu, ge, d_span, links.size)
    sent, keep_a, piece_a, keep_b, piece_b, small = barrier((sent, keep_a, piece_a, keep_b, piece_b, small))

    feed_sent = links.send(*links.finish(sent), "z", "z")
    sums = (blocks(links.join(keep_a, piece_a).astype(low)), blocks(links.join(keep_b, piece_b).astype(low)),
            links.join(small, small).astype(low))
    sums, gqw, ge = barrier((sums, gqw, ge))
    sent = links.send(*sums, "x", "y")
    gx = tokens.input_grad(gb, gqw, gkv, ge, wa, depth_state)
    sent, gx = barrier((sent, gx))
    feed_sent, sums = barrier((feed_sent, links.finish(links.send(*links.finish(sent), "y", "x"))))
    feed_sums = links.finish(feed_sent, full)
    grad_a, grad_b, small = links.finish(links.send(*sums, "z", "z"), full)

    def twice(state, at=0):
        shape = state.shape[:at] + (2,) + state.shape[at + 1 :]
        return [shape, shape]

    def flat(value):
        return value.reshape(-1, value.shape[-1])

    feed_a, feed_b, feed_small = feed_sums
    feed_out = adam_call(
        adam_feed_kernel,
        [place, out_state, norm_state, up_state, bias_state, down_state, flat(feed_a), flat(feed_b), feed_small],
        twice(out_state) + twice(norm_state) + twice(up_state) + twice(bias_state) + twice(down_state), scalars=1)
    mixed = adam_call(
        adam_mix_kernel,
        [mix_state, depth_state, span_state, flat(grad_a), flat(grad_b), small],
        twice(mix_state) + twice(depth_state, 1) + twice(span_state, 1))
    depth_out = [jnp.swapaxes(value, 0, 1) for value in mixed[2:4]]
    span_out = [jnp.transpose(value, (1, 2, 0)) for value in mixed[4:]]
    up_out = [jnp.swapaxes(value, 2, 3) for value in feed_out[4:6]]
    return (result, gx, *mixed[:2], *feed_out[:2], *depth_out, *span_out, *feed_out[2:4], *up_out, *feed_out[6:])


def solution(mesh):
    both = ("grp", "dp")
    mix, out = P(None, None, both, None), P(None, both, None)
    up, bias, down = P(None, "grp", None, "dp"), P(None, "grp", "dp"), P(None, "grp", "dp", None)
    rows = P(both, None)
    return jax.shard_map(
        functools.partial(on_device, Links(mesh)),
        mesh=mesh,
        in_specs=(rows, rows, P(both), mix, out, P(), P(), P(), up, bias, down),
        out_specs=(rows, rows, mix, mix, out, out, P(), P(), P(), P(), P(), P(), up, up, bias, bias, down, down),
        check_vma=False,
    )
```

```python
import functools

import jax
import jax.numpy as jnp
from jax import lax
from jax.experimental import pallas as pl
from jax.experimental.pallas import tpu as pltpu
from jax.sharding import PartitionSpec as P

HEADS = 6
HS = 64
KERNEL = 9
STEP = 7
REACH = KERNEL // 2
TAP = 8
LANES = 128
PAD = 8
EDGE = REACH * PAD

beta_one = 0.9
beta_two = 0.999
adam_eps = 1e-06
ema_rate = 0.99
decay_rate = 0.01
rate_mix = 0.06
rate_out = 0.12
rate_depth = 0.4
rate_span = 0.08
rate_norm = 0.5
rate_up = 0.08
rate_bias = 0.3
rate_down = 0.04

low = jnp.bfloat16
full = jnp.float32
NN = (((1,), (0,)), ((), ()))
NT = (((1,), (1,)), ((), ()))
TN = (((0,), (0,)), ((), ()))


def dot(left, right, dims=NN):
    return lax.dot_general(left, right, dims, preferred_element_type=full)


def rounded(value):
    return value.astype(low).astype(full)


def row_loop(rows, chunk, body):
    for r in range(0, rows, chunk):
        body(r)


def spread_table(width):
    row = lax.broadcasted_iota(jnp.int32, (LANES, 1), 0)
    col = lax.broadcasted_iota(jnp.int32, (1, KERNEL * width), 1)
    head = row % TAP
    first = (row // TAP) * width + head * HS
    first = jnp.where(head < HEADS, first, -HS)
    return ((col >= first) & (col < first + HS)).astype(full).astype(low)


def tap_table():
    row = lax.broadcasted_iota(jnp.int32, (LANES, HEADS * KERNEL), 0)
    col = lax.broadcasted_iota(jnp.int32, (LANES, HEADS * KERNEL), 1)
    return ((col % KERNEL) * TAP + col // KERNEL == row).astype(full).astype(low)


def copy_halves(place_ref, mine, other, target, sems, first, cols):
    rows = mine.shape[0]
    copies = []
    for i, (half, at) in enumerate(((mine, place_ref[0]), (other, 1 - place_ref[0]))):
        copy = pltpu.make_async_copy(
            half.at[:, pl.ds(first, cols)], target.at[pl.ds(pl.multiple_of(at * rows, rows), rows), :], sems.at[i])
        copy.start()
        copies.append(copy)
    return copies


def put_blocks(place_ref, value_ref, keep_ref, piece_ref):
    devices, _, half = keep_ref.shape
    parts = value_ref.shape[1] // half
    rows = half // devices
    for ref, at in ((keep_ref, place_ref[0]), (piece_ref, 1 - place_ref[0])):
        for m in range(parts):
            value = value_ref[pl.ds(pl.multiple_of(at * half, half), half), m * half : (m + 1) * half]
            for n in range(devices):
                ref[n, m * rows : (m + 1) * rows, :] = value[n * rows : (n + 1) * rows].astype(low)


def fill_padded(ref, value):
    rows = value.shape[0]
    value = value.astype(full)
    place = lax.broadcasted_iota(jnp.int32, (PAD, 1), 0)
    ref[EDGE : EDGE + rows, :] = value
    for i in range(REACH):
        before = value[rows - EDGE + i * PAD : rows - EDGE + (i + 1) * PAD]
        ref[i * PAD : (i + 1) * PAD, :] = jnp.where(place == 0, 0.0, pltpu.roll(before, 1, 0))
        after = value[i * PAD : (i + 1) * PAD]
        ref[EDGE + rows + i * PAD : EDGE + rows + (i + 1) * PAD, :] = jnp.where(
            place == PAD - 1, 0.0, pltpu.roll(after, PAD - 1, 0))


def order_matrix(rows, back=False):
    row = lax.broadcasted_iota(jnp.int32, (rows, rows), 0)
    col = lax.broadcasted_iota(jnp.int32, (1, rows), 1)
    places = rows // PAD
    at = (col % PAD) * places + col // PAD if back else (col % places) * PAD + col // places
    return (row == at).astype(full).astype(low)


def order_kernel(x_ref, g_ref, depth_ref, xo_ref, go_ref, e_ref, xpad):
    rows, width = x_ref.shape
    order = order_matrix(rows)
    x = dot(order, x_ref[...])
    xo_ref[...] = x.astype(low)
    go_ref[...] = dot(order, g_ref[...]).astype(low)
    fill_padded(xpad, x)

    rates = [rounded(depth_ref[j, 0:1]) for j in range(KERNEL)]

    def depth_rows(r):
        acc = rates[0] * xpad[pl.ds(r, 32), :]
        for j in range(1, KERNEL):
            acc = acc + rates[j] * xpad[pl.ds(r + PAD * j, 32), :]
        e_ref[pl.ds(r, 32), :] = acc.astype(low)

    row_loop(rows, 32, depth_rows)


def project_kernel(place_ref, x_ref, e_ref, wam_ref, wao_ref, wbm_ref, wbo_ref, bm_ref, bo_ref, span_ref,
                   qwkv_ref, u_ref, bias_ref, spant_ref,
                   wa_ref, w3_ref, sems):
    rows, width = x_ref.shape
    half = width // 2

    @pl.when(pl.program_id(0) == 0)
    def _():
        copies = copy_halves(place_ref, wam_ref, wao_ref, wa_ref, sems.at[0], 0, 4 * half)
        copies += copy_halves(place_ref, wbm_ref, wbo_ref, w3_ref, sems.at[1], width, half)
        spant_ref[...] = dot(tap_table(), span_ref[:, 0, :].astype(low)).astype(low)
        hid_dev = bias_ref.shape[1] // bm_ref.shape[0]
        for n in range(bm_ref.shape[0]):
            cols = slice(n * hid_dev, (n + 1) * hid_dev)
            mine, other = bm_ref[n].astype(full)[0:1, 0:hid_dev], bo_ref[n].astype(full)[0:1, 0:hid_dev]
            bias_ref[0:1, cols] = jnp.where(place_ref[0] == 0, mine, other)
            bias_ref[1:2, cols] = jnp.where(place_ref[0] == 0, other, mine)
        for copy in copies:
            copy.wait()

    x = x_ref[...]
    for c in range(4):
        qwkv_ref[:, c * half : (c + 1) * half] = dot(x, wa_ref[:, c * half : (c + 1) * half]).astype(low)
    u_ref[...] = dot(e_ref[...], w3_ref[...]).astype(low)


def mix_kernel(lens_ref, place_ref, qwkv_ref, u_ref, spant_ref, wbm_ref, wbo_ref,
               p_ref, conv_ref, a_ref, ctx_ref, y_ref,
               wpad, taps, wo_ref, spread_ref, sems):
    rows, half = u_ref.shape

    @pl.when(pl.program_id(0) == 0)
    def _():
        copies = copy_halves(place_ref, wbm_ref, wbo_ref, wo_ref, sems, 0, 2 * half)
        spread_ref[...] = spread_table(half)
        for copy in copies:
            copy.wait()

    r = (u_ref[...].astype(full) * qwkv_ref[:, 0:half].astype(full)).astype(low)
    logits = rounded(dot(r, spant_ref[...], NT))
    lt = logits.T[0 : KERNEL * TAP].reshape(KERNEL, TAP, rows)
    top = jnp.max(lt, axis=0, keepdims=True)
    ex = jnp.exp(lt - top)
    pt = (ex / jnp.sum(ex, axis=0, keepdims=True)).reshape(KERNEL * TAP, rows)
    p = jnp.concatenate([pt, jnp.zeros((LANES - KERNEL * TAP, rows), full)], axis=0).T
    p_ref[...] = p
    fill_padded(wpad, qwkv_ref[:, half : 2 * half])
    p_low = p.astype(low)
    for j in range(KERNEL):
        taps[:, j * half : (j + 1) * half] = dot(p_low, spread_ref[:, j * half : (j + 1) * half])

    def conv_rows(r):
        acc = taps[pl.ds(r, 32), 0:half] * wpad[pl.ds(r, 32), :]
        for j in range(1, KERNEL):
            acc = acc + taps[pl.ds(r, 32), j * half : (j + 1) * half] * wpad[pl.ds(r + PAD * j, 32), :]
        conv_ref[pl.ds(r, 32), :] = acc.astype(low)

    row_loop(rows, 32, conv_rows)
    seq_len = lens_ref[pl.program_id(0)]
    lane = lax.broadcasted_iota(jnp.int32, (1, LANES), 1)
    row = lax.broadcasted_iota(jnp.int32, (1, rows), 1)
    live = (row % PAD) * (rows // PAD) + row // PAD < seq_len
    for pair in range(HEADS // 2):
        at = pair * LANES
        q = qwkv_ref[:, at : at + LANES]
        k = qwkv_ref[:, 2 * half + at : 2 * half + at + LANES]
        v = qwkv_ref[:, 3 * half + at : 3 * half + at + LANES]
        outs = []
        for side in range(2):
            pick = jnp.where((lane // HS) == side, HS ** (-0.5), 0.0).astype(low)
            scores = dot(q * pick, k, NT)
            scores = jnp.where(live, scores, -1000000000.0)
            top = jnp.max(scores, axis=1, keepdims=True)
            ex = jnp.exp(scores - top)
            a = (ex * (1.0 / jnp.sum(ex, axis=1, keepdims=True))).astype(low)
            a_ref[0, 2 * pair + side] = a
            outs.append(dot(a, v))
        ctx_ref[:, at : at + LANES] = jnp.where((lane // HS) == 0, outs[0], outs[1]).astype(low)
    y_ref[...] = (dot(ctx_ref[...], wo_ref[0:half, :]) + dot(conv_ref[...], wo_ref[half:, :])).astype(low)


def normed(value):
    centered = value - jnp.mean(value, axis=1, keepdims=True)
    variance = jnp.mean(centered * centered, axis=1, keepdims=True)
    rstd = lax.rsqrt(variance + 1e-12)
    return centered * rstd, rstd


def feed_kernel(count, up_parts, down_parts, place_ref, norm_ref, bias_ref, y_hbm, x_hbm, g_hbm, ctx_hbm, conv_hbm, wbm_hbm, wbo_hbm, *refs):
    ups, downs = refs[: 2 * up_parts], refs[2 * up_parts : 2 * (up_parts + down_parts)]
    (small_ref, res_hbm, gb_hbm, gm_hbm, keep_hbm, piece_hbm, small_s, y_s, x_s, g_s, m_s, up_s, down_s, wo_s, act_s, gpre_s,
     res_s, gb_s, gm_s, ft_s, got_s, df_s, do_s, in_sems, out_sems) = refs[2 * (up_parts + down_parts) :]
    tokens, width = y_s.shape
    half = width // 2
    hid = bias_ref.shape[1]
    length = tokens // count
    waits, outs = {}, []

    def fetch(name, source, target):
        copy = pltpu.make_async_copy(source, target, in_sems.at[len(waits)])
        copy.start()
        waits[name] = copy

    def put(source, target):
        copy = pltpu.make_async_copy(source, target, out_sems.at[len(outs)])
        copy.start()
        outs.append(copy)

    seqs = [slice(n * length, (n + 1) * length) for n in range(count)]
    for n, rows in enumerate(seqs):
        fetch(("y", n), y_hbm.at[rows], y_s.at[rows])
        fetch(("x", n), x_hbm.at[rows], x_s.at[rows])
        if n == 0:
            for i, at in enumerate((place_ref[0], 1 - place_ref[0])):
                for k in range(up_parts):
                    fetch(("up", i, k), ups[i * up_parts + k], up_s.at[at, :, :, place_ref[3] ^ k])
            for i, at in enumerate((place_ref[0], 1 - place_ref[0])):
                for k in range(down_parts):
                    fetch(("down", i, k), downs[i * down_parts + k], down_s.at[at, :, place_ref[2] ^ k])
        fetch(("g", n), g_hbm.at[rows], g_s.at[rows])
        if n == 0:
            for i, (part, at) in enumerate(((wbm_hbm, place_ref[0]), (wbo_hbm, 1 - place_ref[0]))):
                fetch(("wo", i), part.at[:, pl.ds(0, width)], wo_s.at[pl.ds(pl.multiple_of(at * half, half), half), :])
    fetch("ctx", ctx_hbm, m_s.at[:, pl.ds(0, half)])
    fetch("conv", conv_hbm, m_s.at[:, pl.ds(half, half)])

    g1, c1, g2, c2 = (norm_ref[0, i : i + 1] for i in range(4))
    sums = [jnp.zeros((1, width), full) for _ in range(4)]
    dbias = [jnp.zeros((1, hid), full) for _ in range(2)]
    groups = [(slice(g * hid, (g + 1) * hid), slice(g * half, (g + 1) * half)) for g in range(2)]
    kept = [{} for _ in seqs]

    def wait(name):
        if name in waits:
            waits.pop(name).wait()

    def wait_all(name):
        for key in [key for key in waits if key[0] == name]:
            wait(key)

    def enter(n):
        wait(("y", n))
        wait(("x", n))
        zh1, rstd1 = normed(y_s[seqs[n]].astype(full) + x_s[seqs[n]].astype(full))
        f = (zh1 * g1 + c1).astype(low)
        kept[n].update(zh1=zh1, rstd1=rstd1, f=f, parts=[])
        ft_s[:, seqs[n]] = f.T

    def ahead(n, g):
        hidden, cols = groups[g]
        wait_all("up")
        pre = dot(kept[n]["f"][:, cols], up_s[g].reshape(hid, half), NT) + bias_ref[g : g + 1, :]
        cdf = 0.5 * (1.0 + lax.erf(pre * 2.0 ** (-0.5)))
        act_s[seqs[n], hidden] = (pre * cdf).astype(low)
        gpre_s[seqs[n], hidden] = (cdf + pre * (jnp.exp(-0.5 * pre * pre) * 0.3989422804014327)).astype(low)
        wait_all("down")
        kept[n]["parts"].append(rounded(dot(act_s[seqs[n], hidden], down_s[g].reshape(hid, half))))

    def turn(n):
        rows = seqs[n]
        h1 = kept[n]["zh1"] * g1 + c1
        zh2, rstd2 = normed(h1 + jnp.concatenate(kept[n]["parts"], axis=1))
        result = (zh2 * g2 + c2).astype(low)
        res_s[rows] = dot(order_matrix(length, True), result).astype(low)
        put(res_s.at[rows], res_hbm.at[rows])
        wait(("g", n))
        grad = g_s[rows].astype(full)
        sums[2] = sums[2] + jnp.sum(grad * zh2, axis=0, keepdims=True)
        sums[3] = sums[3] + jnp.sum(grad, axis=0, keepdims=True)
        dz = grad * g2
        gz = (dz - jnp.mean(dz, axis=1, keepdims=True) - zh2 * jnp.mean(dz * zh2, axis=1, keepdims=True)) * rstd2
        go = gz.astype(low)
        got_s[:, rows] = go.T
        kept[n].update(gz=gz, go=go, parts=[])

    def behind(n, g):
        hidden, cols = groups[g]
        slope = gpre_s[seqs[n], hidden].astype(full)
        gpre = (dot(kept[n]["go"][:, cols], down_s[g].reshape(hid, half), NT) * slope).astype(low)
        gpre_s[seqs[n], hidden] = gpre
        dbias[g] = dbias[g] + jnp.sum(gpre.astype(full), axis=0, keepdims=True)
        kept[n]["parts"].append(rounded(dot(gpre, up_s[g].reshape(hid, half))))

    def leave(n):
        rows, zh1 = seqs[n], kept[n]["zh1"]
        gh1 = kept[n]["gz"] + jnp.concatenate(kept[n]["parts"], axis=1)
        sums[0] = sums[0] + jnp.sum(gh1 * zh1, axis=0, keepdims=True)
        sums[1] = sums[1] + jnp.sum(gh1, axis=0, keepdims=True)
        dz1 = gh1 * g1
        gy = (dz1 - jnp.mean(dz1, axis=1, keepdims=True) - zh1 * jnp.mean(dz1 * zh1, axis=1, keepdims=True)) * kept[n]["rstd1"]
        gb_s[rows] = gy.astype(low)
        put(gb_s.at[rows], gb_hbm.at[rows])

    def through(n):
        rows = seqs[n]
        wait(("wo", 0))
        wait(("wo", 1))
        gm_s[rows] = dot(gb_s[rows], wo_s[...], NT).astype(low)
        put(gm_s.at[rows], gm_hbm.at[rows])

    first, *rest = range(count)
    enter(first)
    ahead(first, 0)
    for n in rest:
        enter(n)
    ahead(first, 1)
    for n in rest:
        ahead(n, 0)
        turn(n - 1)
        ahead(n, 1)
        behind(n - 1, 0)
        if n == rest[-1]:
            turn(n)
        behind(n - 1, 1)
        if n == rest[-1]:
            behind(n, 0)
        leave(n - 1)
        if n == rest[-1]:
            behind(n, 1)
        through(n - 1)
    if not rest:
        turn(first)
        behind(first, 0)
        behind(first, 1)
    leave(count - 1)
    through(count - 1)

    wait("ctx")
    wait("conv")
    do_s[...] = dot(m_s[...].T, gb_s[...]).astype(low)
    devices = keep_hbm.shape[0]
    hid_dev, rows_dev = hid // devices, half // devices
    for i, (at, target) in enumerate(((1 - place_ref[0], piece_hbm), (place_ref[0], keep_hbm))):
        hidden = pl.ds(pl.multiple_of(at * hid, LANES), hid)
        cols = pl.ds(pl.multiple_of(at * half, half), half)
        up = dot(ft_s[cols, :], gpre_s[:, hidden]).astype(low).T
        down = dot(got_s[cols, :], act_s[:, hidden]).astype(low).T
        out = do_s[cols, :]
        for n in range(devices):
            first = 0
            for value, size in ((up, hid_dev), (out[:, 0:half], rows_dev), (down, hid_dev), (out[:, half:], rows_dev)):
                df_s[i, n, first : first + size, :] = value[n * size : (n + 1) * size]
                first += size
        put(df_s.at[i], target)
    for i in range(4):
        g, side = divmod(i, 2)
        for j in range(2):
            small_s[8 * j + i : 8 * j + i + 1, :] = sums[i][:, j * half : (j + 1) * half]
            at = side * width + j * half
            small_s[8 * j + 4 + i : 8 * j + 5 + i, :] = dbias[g][:, at : at + half]
    small_ref[...] = small_s[...].astype(low)
    for copy in outs:
        copy.wait()


def mixer_back_kernel(place_ref, qwkv_ref, a_ref, gm_ref, u_ref, p_ref, wbm_ref, wbo_ref, spant_ref,
                      gqw_ref, gkv_ref, gu_ref, ge_ref, dspan_ref,
                      gqa, wpad, gpad, taps, prods, w3_ref, spread_ref, sems):
    rows, half = u_ref.shape

    @pl.when(pl.program_id(0) == 0)
    def _():
        copies = copy_halves(place_ref, wbm_ref, wbo_ref, w3_ref, sems, 2 * half, half)
        dspan_ref[...] = jnp.zeros_like(dspan_ref)
        spread_ref[...] = spread_table(half)
        for copy in copies:
            copy.wait()

    lane = lax.broadcasted_iota(jnp.int32, (1, LANES), 1)
    for pair in range(HEADS // 2):
        at = pair * LANES
        q = qwkv_ref[:, at : at + LANES]
        k = qwkv_ref[:, 2 * half + at : 2 * half + at + LANES]
        v = qwkv_ref[:, 3 * half + at : 3 * half + at + LANES]
        gctx = gm_ref[:, at : at + LANES]
        qt, gctxt = q.T, gctx.T
        gqs, gks, gvs = [], [], []
        for side in range(2):
            pick = jnp.where((lane // HS) == side, 1.0, 0.0).astype(low)
            a_low = a_ref[0, 2 * pair + side]
            a = a_low.astype(full)
            ga = dot(gctx * pick, v, NT)
            gs = (a * (ga - jnp.sum(a * ga, axis=1, keepdims=True))).astype(low)
            gqs.append(dot(gs, k))
            gks.append(dot(qt, gs))
            gvs.append(dot(gctxt, a_low))
        first = (lane // HS) == 0
        gqa[:, at : at + LANES] = jnp.where(first, gqs[0], gqs[1]) * HS ** (-0.5)
        gk = jnp.concatenate([gks[0][0:HS], gks[1][HS:]], axis=0) * HS ** (-0.5)
        gv = jnp.concatenate([gvs[0][0:HS], gvs[1][HS:]], axis=0)
        gkv_ref[:, at : at + LANES] = gk.T.astype(low)
        gkv_ref[:, half + at : half + at + LANES] = gv.T.astype(low)
    fill_padded(wpad, qwkv_ref[:, half : 2 * half])
    fill_padded(gpad, gm_ref[:, half:])
    p = p_ref[...]
    p_low = p.astype(low)
    for j in range(KERNEL):
        cols = slice(j * half, (j + 1) * half)
        fill_padded(taps.at[:, cols], dot(p_low, spread_ref[:, cols]))

    def conv_rows(r):
        here = gpad[pl.ds(r + EDGE, 32), :]
        acc = None
        for j in range(KERNEL):
            cols = slice(j * half, (j + 1) * half)
            prods[pl.ds(r, 32), cols] = (here * wpad[pl.ds(r + PAD * j, 32), :]).astype(low)
            back = pl.ds(r + PAD * (2 * REACH - j), 32)
            term = taps[back, cols] * gpad[back, :]
            acc = term if acc is None else acc + term
        gqw_ref[pl.ds(r, 32), half:] = acc.astype(low)

    row_loop(rows, 32, conv_rows)
    gp = dot(prods[...], spread_ref[...], NT)
    gpt = gp.T[0 : KERNEL * TAP].reshape(KERNEL, TAP, rows)
    pt = p.T[0 : KERNEL * TAP].reshape(KERNEL, TAP, rows)
    glt = pt * (gpt - jnp.sum(pt * gpt, axis=0, keepdims=True))
    glt = jnp.concatenate([glt.reshape(KERNEL * TAP, rows), jnp.zeros((LANES - KERNEL * TAP, rows), full)], axis=0)
    gl = glt.T.astype(low)
    q = qwkv_ref[:, 0:half].astype(full)
    u = u_ref[...].astype(full)
    r = (u * q).astype(low)
    dspan_ref[...] += dot(glt.astype(low), r)
    gr = rounded(dot(gl, spant_ref[...]))
    gqw_ref[:, 0:half] = (gqa[...] + gr * u).astype(low)
    gu = (gr * q).astype(low)
    gu_ref[...] = gu
    ge_ref[...] = dot(gu, w3_ref[...], NT).astype(low)


SMALL_ROWS = 2 * KERNEL + HEADS * KERNEL


def weight_kernel(place_ref, x_ref, e_ref, gqw_ref, gkv_ref, gu_ref, ge_ref, dspan_ref,
                  keep_a_ref, piece_a_ref, keep_b_ref, piece_b_ref, small_ref,
                  xpad, acc_a, acc_b, small, rows_s):
    step, last = pl.program_id(0), pl.num_programs(0) - 1
    rows, width = x_ref.shape
    half = width // 2

    @pl.when(step == 0)
    def _():
        acc_a[...] = jnp.zeros_like(acc_a)
        acc_b[...] = jnp.zeros_like(acc_b)
        small[...] = jnp.zeros_like(small)

    x = x_ref[...]
    xt = x.T
    acc_a[:, 0:width] += dot(xt, gqw_ref[...])
    acc_a[:, width:] += dot(xt, gkv_ref[:, 0:half])
    acc_b[:, 0:half] += dot(xt, gkv_ref[:, half:])
    acc_b[:, half:] += dot(e_ref[...].T, gu_ref[...])
    fill_padded(xpad, x)
    for c in range(0, width, LANES):
        cols = slice(c, c + LANES)

        sums = [jnp.zeros((PAD, LANES), full) for _ in range(KERNEL)]
        for r in range(0, rows, 64):
            ge = ge_ref[pl.ds(r, 64), cols].astype(full)
            for j in range(KERNEL):
                prod = ge * xpad[pl.ds(r + PAD * j, 64), cols]
                sums[j] = sums[j] + jnp.sum(prod.reshape(PAD, PAD, LANES), axis=0)
        for j in range(KERNEL):
            small[j : j + 1, cols] += jnp.sum(sums[j], axis=0, keepdims=True)

    @pl.when(step == last)
    def _():
        put_blocks(place_ref, acc_a, keep_a_ref, piece_a_ref)
        put_blocks(place_ref, acc_b, keep_b_ref, piece_b_ref)
        for side in range(2):
            rows_s[side * KERNEL : (side + 1) * KERNEL, :] = small[0:KERNEL, side * half : (side + 1) * half]
        rows_s[2 * KERNEL :, :] = dot(tap_table(), dspan_ref[...].astype(low), TN)
        small_ref[...] = rows_s[...].astype(low)


def input_kernel(place_ref, gb_ref, gqw_ref, gkv_ref, ge_ref, wam_ref, wao_ref, depth_ref,
                 gx_ref, gepad, gx_s, wa_ref, sems):
    rows, width = gb_ref.shape

    @pl.when(pl.program_id(0) == 0)
    def _():
        for copy in copy_halves(place_ref, wam_ref, wao_ref, wa_ref, sems, 0, 2 * width):
            copy.wait()

    fill_padded(gepad, ge_ref[...])
    gx_s[...] = gb_ref[...].astype(full) + dot(gqw_ref[...], wa_ref[:, 0:width], NT) + dot(gkv_ref[...], wa_ref[:, width:], NT)

    rates = [rounded(depth_ref[j, 0:1]) for j in range(KERNEL)]

    def shift_rows(r):
        acc = gx_s[pl.ds(r, 32), :]
        for j in range(KERNEL):
            acc = acc + rates[j] * gepad[pl.ds(r + PAD * (2 * REACH - j), 32), :]
        gx_s[pl.ds(r, 32), :] = acc

    row_loop(rows, 32, shift_rows)
    gx_ref[...] = dot(order_matrix(rows, True), gx_s[...].astype(low)).astype(low)


def adam_step(old, one, two, mean, grad, step_rate, wd_rate):
    moment_one = beta_one * one + (1.0 - beta_one) * grad
    moment_two = beta_two * two + (1.0 - beta_two) * grad * grad
    scaled_one = moment_one / (1.0 - beta_one**STEP)
    scaled_two = moment_two / (1.0 - beta_two**STEP)
    weight = old - step_rate * (scaled_one / (jnp.sqrt(scaled_two) + adam_eps) + wd_rate * old)
    return weight, ema_rate * mean + (1.0 - ema_rate) * weight, moment_one, moment_two


def adam_at(state, new, moments, at, grad, step_rate, wd_rate):
    values = adam_step(*(state[at(slot)] for slot in range(4)), grad, step_rate, wd_rate)
    new[at(0)], new[at(1)], moments[at(0)], moments[at(1)] = values


def adam_mix_kernel(mix, depth, span, ga_ref, gb_ref, small,
                    mix_new, mix_moments, depth_new, depth_moments, span_new, span_moments):
    rows = mix.shape[2]
    sources = [(ga_ref, 0), (ga_ref, 2), (gb_ref, 0), (gb_ref, 1), (ga_ref, 1)]
    for i, (ref, at) in enumerate(sources):
        adam_at(mix, mix_new, mix_moments, lambda slot: (slot, i), ref[at * rows : (at + 1) * rows, :], rate_mix, decay_rate)
    grad = jnp.concatenate([small[0:KERNEL], small[KERNEL : 2 * KERNEL]], axis=1)
    adam_at(depth, depth_new, depth_moments, lambda slot: (slice(None), slot), grad, rate_depth, decay_rate)
    adam_at(span, span_new, span_moments, lambda slot: (slice(None), slot), small[2 * KERNEL :], rate_span, decay_rate)


def adam_feed_kernel(place_ref, out, norm, up, bias, down, ga_ref, gb_ref, small,
                     out_new, out_moments, norm_new, norm_moments,
                     up_new, up_moments, bias_new, bias_moments, down_new, down_moments):
    half = down.shape[3]
    width = 2 * half
    hid_dev = down.shape[2]
    adam_at(up, up_new, up_moments, lambda slot: (slot, 0), ga_ref[0:hid_dev, :], rate_up, decay_rate)
    adam_at(down, down_new, down_moments, lambda slot: (slot, 0), gb_ref[0:hid_dev, :], rate_down, decay_rate)
    grad = jnp.concatenate([ga_ref[hid_dev:, :], gb_ref[hid_dev:, :]], axis=1)
    adam_at(out, out_new, out_moments, lambda slot: slot, grad, rate_out, decay_rate)
    lines = jnp.concatenate([small[0:8], small[8:16]], axis=1)
    adam_at(norm, norm_new, norm_moments, lambda slot: slot, lines[0:4], rate_norm, 0.0)
    row = lax.broadcasted_iota(jnp.int32, (width, hid_dev), 0)
    col = lax.broadcasted_iota(jnp.int32, (width, hid_dev), 1)
    grad = jnp.zeros((1, hid_dev), full)
    for i in range(4):
        group, side = divmod(i, 2)
        line = jnp.where(place_ref[0] == group, lines[4 + i : 5 + i, :], 0.0)
        here = (row + side * width == col + place_ref[1] * hid_dev).astype(full).astype(low)
        high = line.astype(low)
        rest = (line - high.astype(full)).astype(low)
        both = dot(jnp.concatenate([high, rest] + [jnp.zeros_like(high)] * 6, axis=0), here)
        grad = grad + both[0:1] + both[1:2]
    adam_at(bias, bias_new, bias_moments, lambda slot: slot, grad, rate_bias, 0.0)


def adam_call(kernel, inputs, shapes, scalars=0):
    vmem = pl.BlockSpec(memory_space=pltpu.VMEM)
    moved = sum(value.size for value in inputs) * 6
    return pl.pallas_call(
        kernel,
        in_specs=[pl.BlockSpec(memory_space=pltpu.SMEM)] * scalars + [vmem] * (len(inputs) - scalars),
        out_specs=[vmem] * len(shapes),
        out_shape=[struct(shape, full) for shape in shapes],
        compiler_params=pltpu.CompilerParams(vmem_limit_bytes=40 << 20),
        cost_estimate=pl.CostEstimate(flops=2 * moved, transcendentals=0, bytes_accessed=moved),
    )(*inputs)


def struct(shape, dtype):
    return jax.ShapeDtypeStruct(shape, dtype)


def rows_spec(rows, width, at=0):
    return pl.BlockSpec((rows, width), lambda i, *_: (i, at))


def whole(shape, index=None):
    index = index or (0,) * len(shape)
    return pl.BlockSpec(shape, lambda i, *_: index)


def call(kernel, grid, in_specs, out_specs, out_shape, scratch, flops, moved, limit, prefetch=0):
    return pl.pallas_call(
        kernel,
        grid_spec=pltpu.PrefetchScalarGridSpec(
            num_scalar_prefetch=prefetch, grid=grid, in_specs=in_specs, out_specs=out_specs, scratch_shapes=scratch),
        out_shape=out_shape,
        compiler_params=pltpu.CompilerParams(dimension_semantics=("arbitrary",), vmem_limit_bytes=limit << 20),
        cost_estimate=pl.CostEstimate(flops=int(flops), transcendentals=0, bytes_accessed=int(moved)),
    )


def once(shape, index=None):
    index = index or (0,) * len(shape)
    return pl.BlockSpec(shape, lambda i, *_: index, pipeline_mode=pl.Buffered(1))


class Tokens:
    def __init__(self, tokens, width, count, place):
        self.tokens, self.width, self.count, self.place = tokens, width, count, place
        self.length = length = tokens // count
        self.half = half = width // 2
        self.padded = length + 2 * EDGE
        self.wide, self.slim, self.lane = rows_spec(length, width), rows_spec(length, half), rows_spec(length, LANES)
        self.all_cols = rows_spec(length, 4 * half)
        self.heads = pl.BlockSpec((1, HEADS, length, length), lambda i, *_: (i, 0, 0, 0))
        self.any = pl.BlockSpec(memory_space=pl.ANY)
        self.low_wide, self.low_slim = struct((tokens, width), low), struct((tokens, half), low)
        self.low_half = struct((half, width), low)

    def order(self, hidden, grad_out, depth):
        return call(
            order_kernel, (self.count,),
            [self.wide, self.wide, once(depth.shape)],
            [self.wide] * 3, [self.low_wide] * 3,
            [pltpu.VMEM((self.padded, self.width), full)], 4e9, 8e6, 60,
        )(hidden, grad_out, depth)

    def project(self, hidden, e, wa, wb, span, hid):
        tokens, width, half = self.tokens, self.width, self.half
        V = pltpu.VMEM
        devices = 2 * hid // self.hid_dev
        blocks = [value.reshape(devices // 2, -1, value.shape[1]) for value in wa]
        bias = pl.BlockSpec((devices // 2, blocks[0].shape[1], LANES), lambda i, *_: (0, 0, 4 * half // LANES),
                            pipeline_mode=pl.Buffered(1))
        return call(
            project_kernel, (self.count,),
            [self.wide, self.wide] + [self.any] * 4 + [bias, bias, once(span.shape)],
            [self.all_cols, self.slim, whole((2, hid)), whole((LANES, half))],
            [struct((tokens, 4 * half), low), self.low_slim, struct((2, hid), full), struct((LANES, half), low)],
            [V((width, 4 * half), low), V((width, half), low), pltpu.SemaphoreType.DMA((2, 2))],
            8e9, 10e6, 24, prefetch=1,
        )(self.place, hidden, e, *wa, *wb, *blocks, span)

    def mix(self, lens, qwkv, u, spant, wb):
        tokens, length, width, half = self.tokens, self.length, self.width, self.half
        V = pltpu.VMEM
        return call(
            mix_kernel, (self.count,),
            [self.all_cols, self.slim, once((LANES, half)), self.any, self.any],
            [self.lane, self.slim, self.heads, self.slim, self.wide],
            [pltpu.HBM(shape, dtype) for shape, dtype in (
                ((tokens, LANES), full), ((tokens, half), low), ((self.count, HEADS, length, length), low),
                ((tokens, half), low), ((tokens, width), low))],
            [V((self.padded, half), full), V((length, KERNEL * half), full), V((width, width), low),
             V((LANES, KERNEL * half), low), pltpu.SemaphoreType.DMA((2,))],
            20e9, 18e6, 44, prefetch=2,
        )(lens, self.place, qwkv, u, spant, *wb)

    def feed(self, y, hidden, grad_out, norm, ups, downs, bias, ctx, conv, wb):
        tokens, width, half = self.tokens, self.width, self.half
        hid = bias.shape[1]
        V = pltpu.VMEM
        vmem = pl.BlockSpec(memory_space=V)
        wide = V((tokens, width), low)
        ups = [value.reshape(value.shape[1:3] + value.shape[4:]) for value in ups]
        downs = [value.reshape((value.shape[1],) + value.shape[3:]) for value in downs]
        deep, tall, hid_dev = ups[0].shape[:3]
        across = downs[0].shape[1]
        devices = deep * tall * across
        weights = V((2, deep, tall, across, hid_dev, half), low)
        block = (devices, 2 * (hid + half) // devices, half)
        copies = len(ups) + len(downs) + 4 + 3 * self.count
        return pl.pallas_call(
            functools.partial(feed_kernel, self.count, len(ups) // 2, len(downs) // 2),
            in_specs=[pl.BlockSpec(memory_space=pltpu.SMEM), vmem, vmem] + [self.any] * (7 + len(ups) + len(downs)),
            out_specs=[vmem] + [self.any] * 5,
            out_shape=[struct((16, half), low)] + [self.low_wide] * 3 + [struct(block, low)] * 2,
            scratch_shapes=[V((16, half), full), wide, wide, wide, wide, weights, weights, V((width, width), low),
                            V((tokens, 2 * hid), low), V((tokens, 2 * hid), low), wide, wide, wide,
                            V((width, tokens), low), V((width, tokens), low), V((2,) + block, low), V((width, width), low),
                            pltpu.SemaphoreType.DMA((copies,)), pltpu.SemaphoreType.DMA((2 + 3 * self.count,))],
            compiler_params=pltpu.CompilerParams(vmem_limit_bytes=63 << 20),
            cost_estimate=pl.CostEstimate(flops=int(30e9), transcendentals=0, bytes_accessed=int(25e6)),
        )(self.place, norm, bias, y, hidden, grad_out, ctx, conv, *wb, *ups, *downs)

    def mixer_back(self, qwkv, a, gm, u, p, wb, spant):
        length, width, half = self.length, self.width, self.half
        V = pltpu.VMEM
        return call(
            mixer_back_kernel, (self.count,),
            [self.all_cols, self.heads, self.wide, self.slim, self.lane, self.any, self.any, once((LANES, half))],
            [self.wide, self.wide, self.slim, self.wide, whole((LANES, half))],
            [self.low_wide, self.low_wide, self.low_slim, self.low_wide, struct((LANES, half), full)],
            [V((length, half), full), V((self.padded, half), full), V((self.padded, half), full), V((self.padded, KERNEL * half), full),
             V((length, KERNEL * half), low), V((width, half), low), V((LANES, KERNEL * half), low), pltpu.SemaphoreType.DMA((2,))],
            30e9, 22e6, 44, prefetch=1,
        )(self.place, qwkv, a, gm, u, p, *wb, spant)

    def weights(self, hidden, e, gqw, gkv, gu, ge, d_span, devices):
        width, half = self.width, self.half
        shapes = [(devices, parts * half // devices, half) for parts in (3, 3, 2, 2)]
        V = pltpu.VMEM
        return call(
            weight_kernel, (self.count,),
            [self.wide, self.wide, self.wide, self.wide, self.slim, self.wide, whole((LANES, half))],
            [whole(shape) for shape in shapes] + [whole((SMALL_ROWS, half))],
            [struct(shape, low) for shape in shapes] + [struct((SMALL_ROWS, half), low)],
            [V((self.padded, width), full), V((width, 3 * half), full), V((width, width), full), V((16, width), full), V((SMALL_ROWS, half), full)],
            12e9, 16e6, 40, prefetch=1,
        )(self.place, hidden, e, gqw, gkv, gu, ge, d_span)

    def input_grad(self, gb, gqw, gkv, ge, wa, depth):
        length, width = self.length, self.width
        V = pltpu.VMEM
        return call(
            input_kernel, (self.count,),
            [self.wide, self.wide, self.wide, self.wide, self.any, self.any, once(depth.shape)],
            [self.wide], [self.low_wide],
            [V((self.padded, width), full), V((length, width), full), V((width, 2 * width), low), pltpu.SemaphoreType.DMA((2,))],
            10e9, 14e6, 36, prefetch=1,
        )(self.place, gb, gqw, gkv, ge, *wa, depth)[0]


class Links:
    def __init__(self, mesh):
        self.size = mesh.shape["dp"]
        self.grp = mesh.shape["grp"]
        deep = 4 if self.size % 4 == 0 else 1
        rest = self.size // deep
        wide = 1 << ((rest.bit_length() - 1) // 2)
        self.shape = (1, deep, rest // wide, wide)
        self.axes = {"z": (deep, rest, 1), "y": (rest // wide, wide, 2), "x": (wide, 1, 3),
                     "zl": (2, rest, 1), "zh": (deep // 2, 2 * rest, 1)}

    def place(self, name):
        if name == "grp":
            return lax.axis_index("grp")
        size, stride, _ = self.axes[name]
        return (lax.axis_index("dp") // stride) % size

    def swap(self, value, name, shift):
        if name == "grp":
            return lax.ppermute(value, "grp", [(i, i ^ shift) for i in range(self.grp)])
        size, stride, _ = self.axes[name]
        pairs = []
        for i in range(self.size):
            at = (i // stride) % size
            pairs.append((i, i + ((at ^ shift) - at) * stride))
        return lax.ppermute(value, "dp", pairs)

    def fetch(self, block, name):
        return [block] + [self.swap(block, name, k) for k in range(1, self.axes[name][0])]

    def merge(self, got, name):
        size, _, dim = self.axes[name]
        here = self.place(name)
        slots = []
        for j in range(size):
            value = got[size - 1]
            for k in range(size - 1):
                value = jnp.where(here == (j ^ k), got[k], value)
            slots.append(value)
        return jnp.concatenate(slots, axis=dim)

    def gather(self, block, name):
        return self.merge(self.fetch(block, name), name)

    def slices(self, block, name):
        size, _, dim = self.axes[name]
        here = self.place(name)
        if name == "zl":
            halves = block.reshape((1, block.shape[1] // 2, 2) + block.shape[2:])
            return [jnp.squeeze(lax.dynamic_slice_in_dim(halves, here ^ k, 1, 2), 2) for k in range(size)]
        return [lax.dynamic_slice_in_dim(block, here ^ k, 1, dim) for k in range(size)]

    def join(self, keep, piece):
        return keep.astype(full) + self.swap(piece, "grp", 1).astype(full)

    def send(self, a, b, small, name_a, name_b):
        cols = b.shape[-1]
        parts_a, parts_b = self.slices(a, name_a), self.slices(b, name_b)
        own = [parts_a[0], parts_b[0], small]
        apart = [] if name_a == name_b else [self.swap(part, name_a, k + 1) for k, part in enumerate(parts_a[1:])]
        messages = []
        for k in range(1, len(parts_b)):
            pieces = [parts_b[k].reshape(-1, cols), small]
            if name_a == name_b:
                pieces = [parts_a[k].reshape(-1, cols)] + pieces
            messages.append(self.swap(jnp.concatenate(pieces, axis=0), name_b, k))
        return own, apart, messages

    def finish(self, sent, end=low):
        (own_a, own_b, own_small), apart, messages = sent
        cols = own_b.shape[-1]
        sums_a, sums_b, sums = [own_a] + apart, [own_b], [own_small]
        for message in messages:
            for value, kept in ((own_a, sums_a), (own_b, sums_b), (own_small, sums)):
                if value is own_a and apart:
                    continue
                size = value.size // cols
                kept.append(message[:size].reshape(value.shape))
                message = message[size:]

        def add(got):
            got = [value.astype(full) for value in got]
            while len(got) > 1:
                got = [got[i] + got[i + 1] for i in range(0, len(got), 2)]
            return got[0].astype(end)

        return add(sums_a), add(sums_b), add(sums)


def on_device(links, hidden, grad_out, seq_lens, mix_state, out_state, depth_state, span_state, norm_state,
              up_state, bias_state, down_state):
    barrier = lax.optimization_barrier
    width = hidden.shape[1]
    half = width // 2
    hid_dev = up_state.shape[3]
    rows_dev = mix_state.shape[2]
    up_state = jnp.swapaxes(up_state, 2, 3)
    depth_state = jnp.swapaxes(depth_state, 0, 1)
    span_state = jnp.transpose(span_state, (2, 0, 1))
    place = jnp.stack([links.place("grp"), lax.axis_index("dp"), links.place("y"), links.place("x")]).astype(jnp.int32)
    tokens = Tokens(hidden.shape[0], width, seq_lens.shape[0], place)
    tokens.hid_dev = hid_dev

    mix_low = mix_state[0].astype(low)
    bias_row = jnp.pad(bias_state[0].astype(low), ((0, rows_dev - 1), (0, LANES - hid_dev)))
    shard = jnp.concatenate(
        [mix_low[0], mix_low[4], mix_low[1], mix_low[2], bias_row, out_state[0].astype(low), mix_low[3]], axis=1)
    feed_shard = jnp.concatenate([up_state[0, 0], down_state[0, 0]], axis=1).astype(low)

    def block(value):
        return value.reshape((1, 1, 1, 1) + value.shape)

    def both_cores(value):
        value = value.reshape(-1, value.shape[-1])
        return value, links.swap(value, "grp", 1)

    mixer = links.fetch(block(shard), "z")
    mixer, hidden_o, grad_o, e = barrier((mixer, *tokens.order(hidden, grad_out, depth_state)))
    mixer = links.merge(mixer, "z")
    split = 4 * half + LANES
    wa, wb = mixer[..., :split], mixer[..., split:]
    wa, wb = links.gather(wa, "y"), links.gather(wb, "x")
    wa, wb, feed_shard = barrier((wa, wb, feed_shard))
    wa, wb, feed = barrier((links.fetch(wa, "x"), links.fetch(wb, "y"), links.fetch(block(feed_shard), "z")))
    wa, wb = both_cores(links.merge(wa, "x")), both_cores(links.merge(wb, "y"))
    feed = links.merge(feed, "z")
    up, down = links.fetch(feed[..., :half], "y"), links.fetch(feed[..., half:], "x")

    qwkv, u, bias, spant = tokens.project(hidden_o, e, wa, wb, span_state, hid_dev * links.size)
    up, down, qwkv, u = barrier((up, down, qwkv, u))
    up, down = links.merge(up, "y"), links.merge(down, "x")
    ups, downs = links.fetch(up, "x"), links.fetch(down, "y")
    others = [links.swap(up, "grp", 1)], [links.swap(down, "grp", 1)]
    p, conv, a, ctx, y = tokens.mix(seq_lens, qwkv, u, spant, wb)
    ups, downs, others, y = barrier((ups, downs, others, y))
    ups = ups + others[0] + [links.swap(value, "grp", 1) for value in ups[1:]]
    downs = downs + others[1] + [links.swap(value, "grp", 1) for value in downs[1:]]
    small, result, gb, gm, keep, piece = tokens.feed(
        y, hidden_o, grad_o, norm_state, ups, downs, bias, ctx, conv, wb)

    def blocks(value):
        return value.reshape(links.shape + (-1, value.shape[-1]))

    rows = blocks(links.join(keep, piece).astype(low))
    cut = rows.shape[4] // 2
    sums = rows[..., :cut, :], rows[..., cut:, :], links.join(small, small).astype(low)
    *sums, gm = barrier((*sums, gm))
    sent = links.send(*sums, "x", "y")
    gqw, gkv, gu, ge, d_span = tokens.mixer_back(qwkv, a, gm, u, p, wb, spant)
    sent, gqw, gkv, gu, ge, d_span = barrier((sent, gqw, gkv, gu, ge, d_span))
    sent = links.send(*links.finish(sent), "y", "x")
    keep_a, piece_a, keep_b, piece_b, small = tokens.weights(hidden_o, e, gqw, gkv, gu, ge, d_span, links.size)
    sent, keep_a, piece_a, keep_b, piece_b, small = barrier((sent, keep_a, piece_a, keep_b, piece_b, small))

    feed_sent = links.send(*links.finish(sent), "z", "z")
    sums = (blocks(links.join(keep_a, piece_a).astype(low)), blocks(links.join(keep_b, piece_b).astype(low)),
            links.join(small, small).astype(low))
    sums, gqw, ge = barrier((sums, gqw, ge))
    sent = links.send(*sums, "x", "y")
    gx = tokens.input_grad(gb, gqw, gkv, ge, wa, depth_state)
    sent, gx = barrier((sent, gx))
    feed_sent, sums = barrier((feed_sent, links.finish(links.send(*links.finish(sent), "y", "x"))))
    feed_sums = links.finish(feed_sent, full)
    grad_a, grad_b, small = links.finish(links.send(*sums, "z", "z"), full)

    def twice(state, at=0):
        shape = state.shape[:at] + (2,) + state.shape[at + 1 :]
        return [shape, shape]

    def flat(value):
        return value.reshape(-1, value.shape[-1])

    feed_a, feed_b, feed_small = feed_sums
    feed_out = adam_call(
        adam_feed_kernel,
        [place, out_state, norm_state, up_state, bias_state, down_state, flat(feed_a), flat(feed_b), feed_small],
        twice(out_state) + twice(norm_state) + twice(up_state) + twice(bias_state) + twice(down_state), scalars=1)
    mixed = adam_call(
        adam_mix_kernel,
        [mix_state, depth_state, span_state, flat(grad_a), flat(grad_b), small],
        twice(mix_state) + twice(depth_state, 1) + twice(span_state, 1))
    depth_out = [jnp.swapaxes(value, 0, 1) for value in mixed[2:4]]
    span_out = [jnp.transpose(value, (1, 2, 0)) for value in mixed[4:]]
    up_out = [jnp.swapaxes(value, 2, 3) for value in feed_out[4:6]]
    return (result, gx, *mixed[:2], *feed_out[:2], *depth_out, *span_out, *feed_out[2:4], *up_out, *feed_out[6:])


def solution(mesh):
    both = ("grp", "dp")
    mix, out = P(None, None, both, None), P(None, both, None)
    up, bias, down = P(None, "grp", None, "dp"), P(None, "grp", "dp"), P(None, "grp", "dp", None)
    rows = P(both, None)
    return jax.shard_map(
        functools.partial(on_device, Links(mesh)),
        mesh=mesh,
        in_specs=(rows, rows, P(both), mix, out, P(), P(), P(), up, bias, down),
        out_specs=(rows, rows, mix, mix, out, out, P(), P(), P(), P(), P(), P(), up, up, bias, bias, down, down),
        check_vma=False,
    )
```

```python
import functools

import jax
import jax.numpy as jnp
from jax import lax
from jax.experimental import pallas as pl
from jax.experimental.pallas import tpu as pltpu
from jax.sharding import PartitionSpec as P

HEADS = 6
HS = 64
KERNEL = 9
STEP = 7
REACH = KERNEL // 2
TAP = 8
LANES = 128
PAD = 8
EDGE = REACH * PAD

beta_one = 0.9
beta_two = 0.999
adam_eps = 1e-06
ema_rate = 0.99
decay_rate = 0.01
rate_mix = 0.06
rate_out = 0.12
rate_depth = 0.4
rate_span = 0.08
rate_norm = 0.5
rate_up = 0.08
rate_bias = 0.3
rate_down = 0.04

low = jnp.bfloat16
full = jnp.float32
NN = (((1,), (0,)), ((), ()))
NT = (((1,), (1,)), ((), ()))
TN = (((0,), (0,)), ((), ()))


def dot(left, right, dims=NN):
    return lax.dot_general(left, right, dims, preferred_element_type=full)


def rounded(value):
    return value.astype(low).astype(full)


def row_loop(rows, chunk, body):
    for r in range(0, rows, chunk):
        body(r)


def spread_table(width):
    row = lax.broadcasted_iota(jnp.int32, (LANES, 1), 0)
    col = lax.broadcasted_iota(jnp.int32, (1, KERNEL * width), 1)
    head = row % TAP
    first = (row // TAP) * width + head * HS
    first = jnp.where(head < HEADS, first, -HS)
    return ((col >= first) & (col < first + HS)).astype(full).astype(low)


def tap_table():
    row = lax.broadcasted_iota(jnp.int32, (LANES, HEADS * KERNEL), 0)
    col = lax.broadcasted_iota(jnp.int32, (LANES, HEADS * KERNEL), 1)
    return ((col % KERNEL) * TAP + col // KERNEL == row).astype(full).astype(low)


def copy_halves(place_ref, mine, other, target, sems, first, cols):
    rows = mine.shape[0]
    copies = []
    for i, (half, at) in enumerate(((mine, place_ref[0]), (other, 1 - place_ref[0]))):
        copy = pltpu.make_async_copy(
            half.at[:, pl.ds(first, cols)], target.at[pl.ds(pl.multiple_of(at * rows, rows), rows), :], sems.at[i])
        copy.start()
        copies.append(copy)
    return copies


def put_blocks(place_ref, value_ref, keep_ref, piece_ref):
    devices, _, half = keep_ref.shape
    parts = value_ref.shape[1] // half
    rows = half // devices
    for ref, at in ((keep_ref, place_ref[0]), (piece_ref, 1 - place_ref[0])):
        for m in range(parts):
            value = value_ref[pl.ds(pl.multiple_of(at * half, half), half), m * half : (m + 1) * half]
            for n in range(devices):
                ref[n, m * rows : (m + 1) * rows, :] = value[n * rows : (n + 1) * rows].astype(low)


def fill_padded(ref, value):
    rows = value.shape[0]
    value = value.astype(full)
    place = lax.broadcasted_iota(jnp.int32, (PAD, 1), 0)
    ref[EDGE : EDGE + rows, :] = value
    for i in range(REACH):
        before = value[rows - EDGE + i * PAD : rows - EDGE + (i + 1) * PAD]
        ref[i * PAD : (i + 1) * PAD, :] = jnp.where(place == 0, 0.0, pltpu.roll(before, 1, 0))
        after = value[i * PAD : (i + 1) * PAD]
        ref[EDGE + rows + i * PAD : EDGE + rows + (i + 1) * PAD, :] = jnp.where(
            place == PAD - 1, 0.0, pltpu.roll(after, PAD - 1, 0))


def order_matrix(rows, back=False):
    row = lax.broadcasted_iota(jnp.int32, (rows, rows), 0)
    col = lax.broadcasted_iota(jnp.int32, (1, rows), 1)
    places = rows // PAD
    at = (col % PAD) * places + col // PAD if back else (col % places) * PAD + col // places
    return (row == at).astype(full).astype(low)


def order_kernel(x_ref, g_ref, depth_ref, xo_ref, go_ref, e_ref, xpad):
    rows, width = x_ref.shape
    order = order_matrix(rows)
    x = dot(order, x_ref[...])
    xo_ref[...] = x.astype(low)
    go_ref[...] = dot(order, g_ref[...]).astype(low)
    fill_padded(xpad, x)

    rates = [rounded(depth_ref[j, 0:1]) for j in range(KERNEL)]

    def depth_rows(r):
        acc = rates[0] * xpad[pl.ds(r, 32), :]
        for j in range(1, KERNEL):
            acc = acc + rates[j] * xpad[pl.ds(r + PAD * j, 32), :]
        e_ref[pl.ds(r, 32), :] = acc.astype(low)

    row_loop(rows, 32, depth_rows)


def project_kernel(place_ref, x_ref, e_ref, wam_ref, wao_ref, wbm_ref, wbo_ref, bm_ref, bo_ref, span_ref,
                   qwkv_ref, u_ref, bias_ref, spant_ref,
                   wa_ref, w3_ref, sems):
    rows, width = x_ref.shape
    half = width // 2

    @pl.when(pl.program_id(0) == 0)
    def _():
        copies = copy_halves(place_ref, wam_ref, wao_ref, wa_ref, sems.at[0], 0, 4 * half)
        copies += copy_halves(place_ref, wbm_ref, wbo_ref, w3_ref, sems.at[1], width, half)
        spant_ref[...] = dot(tap_table(), span_ref[:, 0, :].astype(low)).astype(low)
        hid_dev = bias_ref.shape[1] // bm_ref.shape[0]
        for n in range(bm_ref.shape[0]):
            cols = slice(n * hid_dev, (n + 1) * hid_dev)
            mine, other = bm_ref[n].astype(full)[0:1, 0:hid_dev], bo_ref[n].astype(full)[0:1, 0:hid_dev]
            bias_ref[0:1, cols] = jnp.where(place_ref[0] == 0, mine, other)
            bias_ref[1:2, cols] = jnp.where(place_ref[0] == 0, other, mine)
        for copy in copies:
            copy.wait()

    x = x_ref[...]
    for c in range(4):
        qwkv_ref[:, c * half : (c + 1) * half] = dot(x, wa_ref[:, c * half : (c + 1) * half]).astype(low)
    u_ref[...] = dot(e_ref[...], w3_ref[...]).astype(low)


def mix_kernel(lens_ref, place_ref, qwkv_ref, u_ref, spant_ref, wbm_ref, wbo_ref,
               p_ref, conv_ref, a_ref, ctx_ref, y_ref,
               wpad, taps, wo_ref, spread_ref, sems):
    rows, half = u_ref.shape

    @pl.when(pl.program_id(0) == 0)
    def _():
        copies = copy_halves(place_ref, wbm_ref, wbo_ref, wo_ref, sems, 0, 2 * half)
        spread_ref[...] = spread_table(half)
        for copy in copies:
            copy.wait()

    r = (u_ref[...].astype(full) * qwkv_ref[:, 0:half].astype(full)).astype(low)
    logits = rounded(dot(r, spant_ref[...], NT))
    lt = logits.T[0 : KERNEL * TAP].reshape(KERNEL, TAP, rows)
    top = jnp.max(lt, axis=0, keepdims=True)
    ex = jnp.exp(lt - top)
    pt = (ex / jnp.sum(ex, axis=0, keepdims=True)).reshape(KERNEL * TAP, rows)
    p = jnp.concatenate([pt, jnp.zeros((LANES - KERNEL * TAP, rows), full)], axis=0).T
    p_ref[...] = p
    fill_padded(wpad, qwkv_ref[:, half : 2 * half])
    p_low = p.astype(low)
    for j in range(KERNEL):
        taps[:, j * half : (j + 1) * half] = dot(p_low, spread_ref[:, j * half : (j + 1) * half])

    def conv_rows(r):
        acc = taps[pl.ds(r, 32), 0:half] * wpad[pl.ds(r, 32), :]
        for j in range(1, KERNEL):
            acc = acc + taps[pl.ds(r, 32), j * half : (j + 1) * half] * wpad[pl.ds(r + PAD * j, 32), :]
        conv_ref[pl.ds(r, 32), :] = acc.astype(low)

    row_loop(rows, 32, conv_rows)
    seq_len = lens_ref[pl.program_id(0)]
    lane = lax.broadcasted_iota(jnp.int32, (1, LANES), 1)
    row = lax.broadcasted_iota(jnp.int32, (1, rows), 1)
    live = (row % PAD) * (rows // PAD) + row // PAD < seq_len
    for pair in range(HEADS // 2):
        at = pair * LANES
        q = qwkv_ref[:, at : at + LANES]
        k = qwkv_ref[:, 2 * half + at : 2 * half + at + LANES]
        v = qwkv_ref[:, 3 * half + at : 3 * half + at + LANES]
        outs = []
        for side in range(2):
            pick = jnp.where((lane // HS) == side, HS ** (-0.5), 0.0).astype(low)
            scores = dot(q * pick, k, NT)
            scores = jnp.where(live, scores, -1000000000.0)
            top = jnp.max(scores, axis=1, keepdims=True)
            ex = jnp.exp(scores - top)
            a = (ex * (1.0 / jnp.sum(ex, axis=1, keepdims=True))).astype(low)
            a_ref[0, 2 * pair + side] = a
            outs.append(dot(a, v))
        ctx_ref[:, at : at + LANES] = jnp.where((lane // HS) == 0, outs[0], outs[1]).astype(low)
    y_ref[...] = (dot(ctx_ref[...], wo_ref[0:half, :]) + dot(conv_ref[...], wo_ref[half:, :])).astype(low)


def normed(value):
    centered = value - jnp.mean(value, axis=1, keepdims=True)
    variance = jnp.mean(centered * centered, axis=1, keepdims=True)
    rstd = lax.rsqrt(variance + 1e-12)
    return centered * rstd, rstd


def feed_kernel(count, up_parts, down_parts, place_ref, norm_ref, bias_ref, y_hbm, x_hbm, g_hbm, ctx_hbm, conv_hbm, wbm_hbm, wbo_hbm, *refs):
    ups, downs = refs[: 2 * up_parts], refs[2 * up_parts : 2 * (up_parts + down_parts)]
    (small_ref, res_hbm, gb_hbm, gm_hbm, keep_hbm, piece_hbm, small_s, y_s, x_s, g_s, m_s, up_s, down_s, wo_s, act_s, gpre_s,
     res_s, gb_s, gm_s, ft_s, got_s, df_s, do_s, in_sems, out_sems) = refs[2 * (up_parts + down_parts) :]
    tokens, width = y_s.shape
    half = width // 2
    hid = bias_ref.shape[1]
    length = tokens // count
    waits, outs = {}, []

    def fetch(name, source, target):
        copy = pltpu.make_async_copy(source, target, in_sems.at[len(waits)])
        copy.start()
        waits[name] = copy

    def put(source, target):
        copy = pltpu.make_async_copy(source, target, out_sems.at[len(outs)])
        copy.start()
        outs.append(copy)

    seqs = [slice(n * length, (n + 1) * length) for n in range(count)]
    for n, rows in enumerate(seqs):
        fetch(("y", n), y_hbm.at[rows], y_s.at[rows])
        fetch(("x", n), x_hbm.at[rows], x_s.at[rows])
        if n == 0:
            for i, at in enumerate((place_ref[0], 1 - place_ref[0])):
                for k in range(up_parts):
                    fetch(("up", i, k), ups[i * up_parts + k], up_s.at[at, :, :, place_ref[3] ^ k])
            for i, at in enumerate((place_ref[0], 1 - place_ref[0])):
                for k in range(down_parts):
                    fetch(("down", i, k), downs[i * down_parts + k], down_s.at[at, :, place_ref[2] ^ k])
        fetch(("g", n), g_hbm.at[rows], g_s.at[rows])
        if n == 0:
            for i, (part, at) in enumerate(((wbm_hbm, place_ref[0]), (wbo_hbm, 1 - place_ref[0]))):
                fetch(("wo", i), part.at[:, pl.ds(0, width)], wo_s.at[pl.ds(pl.multiple_of(at * half, half), half), :])
    fetch("ctx", ctx_hbm, m_s.at[:, pl.ds(0, half)])
    fetch("conv", conv_hbm, m_s.at[:, pl.ds(half, half)])

    g1, c1, g2, c2 = (norm_ref[0, i : i + 1] for i in range(4))
    sums = [jnp.zeros((1, width), full) for _ in range(4)]
    dbias = [jnp.zeros((1, hid), full) for _ in range(2)]
    groups = [(slice(g * hid, (g + 1) * hid), slice(g * half, (g + 1) * half)) for g in range(2)]
    kept = [{} for _ in seqs]

    def wait(name):
        if name in waits:
            waits.pop(name).wait()

    def wait_all(name):
        for key in [key for key in waits if key[0] == name]:
            wait(key)

    def enter(n):
        wait(("y", n))
        wait(("x", n))
        zh1, rstd1 = normed(y_s[seqs[n]].astype(full) + x_s[seqs[n]].astype(full))
        f = (zh1 * g1 + c1).astype(low)
        kept[n].update(zh1=zh1, rstd1=rstd1, f=f, parts=[])
        ft_s[:, seqs[n]] = f.T

    def ahead(n, g):
        hidden, cols = groups[g]
        wait_all("up")
        pre = dot(kept[n]["f"][:, cols], up_s[g].reshape(hid, half), NT) + bias_ref[g : g + 1, :]
        cdf = 0.5 * (1.0 + lax.erf(pre * 2.0 ** (-0.5)))
        act_s[seqs[n], hidden] = (pre * cdf).astype(low)
        gpre_s[seqs[n], hidden] = (cdf + pre * (jnp.exp(-0.5 * pre * pre) * 0.3989422804014327)).astype(low)
        wait_all("down")
        kept[n]["parts"].append(rounded(dot(act_s[seqs[n], hidden], down_s[g].reshape(hid, half))))

    def turn(n):
        rows = seqs[n]
        h1 = kept[n]["zh1"] * g1 + c1
        zh2, rstd2 = normed(h1 + jnp.concatenate(kept[n]["parts"], axis=1))
        result = (zh2 * g2 + c2).astype(low)
        res_s[rows] = dot(order_matrix(length, True), result).astype(low)
        put(res_s.at[rows], res_hbm.at[rows])
        wait(("g", n))
        grad = g_s[rows].astype(full)
        sums[2] = sums[2] + jnp.sum(grad * zh2, axis=0, keepdims=True)
        sums[3] = sums[3] + jnp.sum(grad, axis=0, keepdims=True)
        dz = grad * g2
        gz = (dz - jnp.mean(dz, axis=1, keepdims=True) - zh2 * jnp.mean(dz * zh2, axis=1, keepdims=True)) * rstd2
        go = gz.astype(low)
        got_s[:, rows] = go.T
        kept[n].update(gz=gz, go=go, parts=[])

    def behind(n, g):
        hidden, cols = groups[g]
        slope = gpre_s[seqs[n], hidden].astype(full)
        gpre = (dot(kept[n]["go"][:, cols], down_s[g].reshape(hid, half), NT) * slope).astype(low)
        gpre_s[seqs[n], hidden] = gpre
        dbias[g] = dbias[g] + jnp.sum(gpre.astype(full), axis=0, keepdims=True)
        kept[n]["parts"].append(rounded(dot(gpre, up_s[g].reshape(hid, half))))

    def leave(n):
        rows, zh1 = seqs[n], kept[n]["zh1"]
        gh1 = kept[n]["gz"] + jnp.concatenate(kept[n]["parts"], axis=1)
        sums[0] = sums[0] + jnp.sum(gh1 * zh1, axis=0, keepdims=True)
        sums[1] = sums[1] + jnp.sum(gh1, axis=0, keepdims=True)
        dz1 = gh1 * g1
        gy = (dz1 - jnp.mean(dz1, axis=1, keepdims=True) - zh1 * jnp.mean(dz1 * zh1, axis=1, keepdims=True)) * kept[n]["rstd1"]
        gb_s[rows] = gy.astype(low)
        put(gb_s.at[rows], gb_hbm.at[rows])

    def through(n):
        rows = seqs[n]
        wait(("wo", 0))
        wait(("wo", 1))
        gm_s[rows] = dot(gb_s[rows], wo_s[...], NT).astype(low)
        put(gm_s.at[rows], gm_hbm.at[rows])

    first, *rest = range(count)
    enter(first)
    ahead(first, 0)
    for n in rest:
        enter(n)
    ahead(first, 1)
    for n in rest:
        ahead(n, 0)
        turn(n - 1)
        ahead(n, 1)
        behind(n - 1, 0)
        if n == rest[-1]:
            turn(n)
        behind(n - 1, 1)
        if n == rest[-1]:
            behind(n, 0)
        leave(n - 1)
        if n == rest[-1]:
            behind(n, 1)
        through(n - 1)
    if not rest:
        turn(first)
        behind(first, 0)
        behind(first, 1)
    leave(count - 1)
    through(count - 1)

    wait("ctx")
    wait("conv")
    do_s[...] = dot(m_s[...].T, gb_s[...]).astype(low)
    devices = keep_hbm.shape[0]
    hid_dev, rows_dev = hid // devices, half // devices
    for i, (at, target) in enumerate(((1 - place_ref[0], piece_hbm), (place_ref[0], keep_hbm))):
        hidden = pl.ds(pl.multiple_of(at * hid, LANES), hid)
        cols = pl.ds(pl.multiple_of(at * half, half), half)
        up = dot(ft_s[cols, :], gpre_s[:, hidden]).astype(low).T
        down = dot(got_s[cols, :], act_s[:, hidden]).astype(low).T
        out = do_s[cols, :]
        for n in range(devices):
            first = 0
            for value, size in ((up, hid_dev), (out[:, 0:half], rows_dev), (down, hid_dev), (out[:, half:], rows_dev)):
                df_s[i, n, first : first + size, :] = value[n * size : (n + 1) * size]
                first += size
        put(df_s.at[i], target)
    for i in range(4):
        g, side = divmod(i, 2)
        for j in range(2):
            small_s[8 * j + i : 8 * j + i + 1, :] = sums[i][:, j * half : (j + 1) * half]
            at = side * width + j * half
            small_s[8 * j + 4 + i : 8 * j + 5 + i, :] = dbias[g][:, at : at + half]
    small_ref[...] = small_s[...].astype(low)
    for copy in outs:
        copy.wait()


def mixer_back_kernel(place_ref, qwkv_ref, a_ref, gm_ref, u_ref, p_ref, wbm_ref, wbo_ref, spant_ref,
                      gqw_ref, gkv_ref, gu_ref, ge_ref, dspan_ref,
                      gqa, wpad, gpad, taps, prods, w3_ref, spread_ref, sems):
    rows, half = u_ref.shape

    @pl.when(pl.program_id(0) == 0)
    def _():
        copies = copy_halves(place_ref, wbm_ref, wbo_ref, w3_ref, sems, 2 * half, half)
        dspan_ref[...] = jnp.zeros_like(dspan_ref)
        spread_ref[...] = spread_table(half)
        for copy in copies:
            copy.wait()

    lane = lax.broadcasted_iota(jnp.int32, (1, LANES), 1)
    for pair in range(HEADS // 2):
        at = pair * LANES
        q = qwkv_ref[:, at : at + LANES]
        k = qwkv_ref[:, 2 * half + at : 2 * half + at + LANES]
        v = qwkv_ref[:, 3 * half + at : 3 * half + at + LANES]
        gctx = gm_ref[:, at : at + LANES]
        qt, gctxt = q.T, gctx.T
        gqs, gks, gvs = [], [], []
        for side in range(2):
            pick = jnp.where((lane // HS) == side, 1.0, 0.0).astype(low)
            a_low = a_ref[0, 2 * pair + side]
            a = a_low.astype(full)
            ga = dot(gctx * pick, v, NT)
            gs = (a * (ga - jnp.sum(a * ga, axis=1, keepdims=True))).astype(low)
            gqs.append(dot(gs, k))
            gks.append(dot(qt, gs))
            gvs.append(dot(gctxt, a_low))
        first = (lane // HS) == 0
        gqa[:, at : at + LANES] = jnp.where(first, gqs[0], gqs[1]) * HS ** (-0.5)
        gk = jnp.concatenate([gks[0][0:HS], gks[1][HS:]], axis=0) * HS ** (-0.5)
        gv = jnp.concatenate([gvs[0][0:HS], gvs[1][HS:]], axis=0)
        gkv_ref[:, at : at + LANES] = gk.T.astype(low)
        gkv_ref[:, half + at : half + at + LANES] = gv.T.astype(low)
    fill_padded(wpad, qwkv_ref[:, half : 2 * half])
    fill_padded(gpad, gm_ref[:, half:])
    p = p_ref[...]
    p_low = p.astype(low)
    for j in range(KERNEL):
        cols = slice(j * half, (j + 1) * half)
        fill_padded(taps.at[:, cols], dot(p_low, spread_ref[:, cols]))

    def conv_rows(r):
        here = gpad[pl.ds(r + EDGE, 32), :]
        acc = None
        for j in range(KERNEL):
            cols = slice(j * half, (j + 1) * half)
            prods[pl.ds(r, 32), cols] = (here * wpad[pl.ds(r + PAD * j, 32), :]).astype(low)
            back = pl.ds(r + PAD * (2 * REACH - j), 32)
            term = taps[back, cols] * gpad[back, :]
            acc = term if acc is None else acc + term
        gqw_ref[pl.ds(r, 32), half:] = acc.astype(low)

    row_loop(rows, 32, conv_rows)
    gp = dot(prods[...], spread_ref[...], NT)
    gpt = gp.T[0 : KERNEL * TAP].reshape(KERNEL, TAP, rows)
    pt = p.T[0 : KERNEL * TAP].reshape(KERNEL, TAP, rows)
    glt = pt * (gpt - jnp.sum(pt * gpt, axis=0, keepdims=True))
    glt = jnp.concatenate([glt.reshape(KERNEL * TAP, rows), jnp.zeros((LANES - KERNEL * TAP, rows), full)], axis=0)
    gl = glt.T.astype(low)
    q = qwkv_ref[:, 0:half].astype(full)
    u = u_ref[...].astype(full)
    r = (u * q).astype(low)
    dspan_ref[...] += dot(glt.astype(low), r)
    gr = rounded(dot(gl, spant_ref[...]))
    gqw_ref[:, 0:half] = (gqa[...] + gr * u).astype(low)
    gu = (gr * q).astype(low)
    gu_ref[...] = gu
    ge_ref[...] = dot(gu, w3_ref[...], NT).astype(low)


SMALL_ROWS = 2 * KERNEL + HEADS * KERNEL


def weight_kernel(place_ref, x_ref, e_ref, gqw_ref, gkv_ref, gu_ref, ge_ref, dspan_ref,
                  keep_a_ref, piece_a_ref, keep_b_ref, piece_b_ref, small_ref,
                  xpad, acc_a, acc_b, small, rows_s):
    step, last = pl.program_id(0), pl.num_programs(0) - 1
    rows, width = x_ref.shape
    half = width // 2

    @pl.when(step == 0)
    def _():
        acc_a[...] = jnp.zeros_like(acc_a)
        acc_b[...] = jnp.zeros_like(acc_b)
        small[...] = jnp.zeros_like(small)

    x = x_ref[...]
    xt = x.T
    acc_a[:, 0:width] += dot(xt, gqw_ref[...])
    acc_a[:, width:] += dot(xt, gkv_ref[:, 0:half])
    acc_b[:, 0:half] += dot(xt, gkv_ref[:, half:])
    acc_b[:, half:] += dot(e_ref[...].T, gu_ref[...])
    fill_padded(xpad, x)
    for c in range(0, width, LANES):
        cols = slice(c, c + LANES)

        sums = [jnp.zeros((PAD, LANES), full) for _ in range(KERNEL)]
        for r in range(0, rows, 64):
            ge = ge_ref[pl.ds(r, 64), cols].astype(full)
            for j in range(KERNEL):
                prod = ge * xpad[pl.ds(r + PAD * j, 64), cols]
                sums[j] = sums[j] + jnp.sum(prod.reshape(PAD, PAD, LANES), axis=0)
        for j in range(KERNEL):
            small[j : j + 1, cols] += jnp.sum(sums[j], axis=0, keepdims=True)

    @pl.when(step == last)
    def _():
        put_blocks(place_ref, acc_a, keep_a_ref, piece_a_ref)
        put_blocks(place_ref, acc_b, keep_b_ref, piece_b_ref)
        for side in range(2):
            rows_s[side * KERNEL : (side + 1) * KERNEL, :] = small[0:KERNEL, side * half : (side + 1) * half]
        rows_s[2 * KERNEL :, :] = dot(tap_table(), dspan_ref[...].astype(low), TN)
        small_ref[...] = rows_s[...].astype(low)


def input_kernel(place_ref, gb_ref, gqw_ref, gkv_ref, ge_ref, wam_ref, wao_ref, depth_ref,
                 gx_ref, gepad, gx_s, wa_ref, sems):
    rows, width = gb_ref.shape

    @pl.when(pl.program_id(0) == 0)
    def _():
        for copy in copy_halves(place_ref, wam_ref, wao_ref, wa_ref, sems, 0, 2 * width):
            copy.wait()

    fill_padded(gepad, ge_ref[...])
    gx_s[...] = gb_ref[...].astype(full) + dot(gqw_ref[...], wa_ref[:, 0:width], NT) + dot(gkv_ref[...], wa_ref[:, width:], NT)

    rates = [rounded(depth_ref[j, 0:1]) for j in range(KERNEL)]

    def shift_rows(r):
        acc = gx_s[pl.ds(r, 32), :]
        for j in range(KERNEL):
            acc = acc + rates[j] * gepad[pl.ds(r + PAD * (2 * REACH - j), 32), :]
        gx_s[pl.ds(r, 32), :] = acc

    row_loop(rows, 32, shift_rows)
    gx_ref[...] = dot(order_matrix(rows, True), gx_s[...].astype(low)).astype(low)


def join_kernel(shape, place_ref, keep, came, small, small_came, *outs):
    deep, tall, wide = shape
    cut = keep.shape[1] // 2
    parts_a, (own_b, *messages, small_sum) = outs[:wide], outs[wide:]

    def total(n, first):
        rows = pl.ds(first, cut)
        return (keep[n, rows].astype(full) + came[n, rows].astype(full)).astype(low)

    small_now = (small[...].astype(full) + small_came[...].astype(full)).astype(low)
    small_sum[...] = small_now
    for line in range(deep * tall):
        for k in range(wide):
            parts_a[k][line] = total(line * wide + (place_ref[3] ^ k), 0)
    for z in range(deep):
        for x in range(wide):
            at = z * wide + x
            for k in range(tall):
                value = total((z * tall + (place_ref[2] ^ k)) * wide + x, cut)
                if k == 0:
                    own_b[at] = value
                else:
                    messages[k - 1][at * cut : (at + 1) * cut, :] = value
    for message in messages:
        message[deep * wide * cut :, :] = small_now


def join(shape, place, keep, came, small, small_came):
    deep, tall, wide = shape
    cut, half = keep.shape[1] // 2, keep.shape[2]
    vmem = pl.BlockSpec(memory_space=pltpu.VMEM)
    shapes = [(deep * tall, cut, half)] * wide + [(deep * wide, cut, half)]
    shapes += [(deep * wide * cut + small.shape[0], half)] * (tall - 1) + [small.shape]
    outs = pl.pallas_call(
        functools.partial(join_kernel, shape),
        in_specs=[pl.BlockSpec(memory_space=pltpu.SMEM)] + [vmem] * 4,
        out_specs=[vmem] * len(shapes),
        out_shape=[struct(value, low) for value in shapes],
        compiler_params=pltpu.CompilerParams(vmem_limit_bytes=24 << 20),
        cost_estimate=pl.CostEstimate(flops=keep.size, transcendentals=0, bytes_accessed=6 * keep.size),
    )(place, keep, came, small, small_came)
    parts_a = [value.reshape(1, deep, tall, 1, cut, half) for value in outs[:wide]]
    return parts_a, outs[wide].reshape(1, deep, 1, wide, cut, half), outs[wide + 1 : -1], outs[-1]


def adam_step(old, one, two, mean, grad, step_rate, wd_rate):
    moment_one = beta_one * one + (1.0 - beta_one) * grad
    moment_two = beta_two * two + (1.0 - beta_two) * grad * grad
    scaled_one = moment_one / (1.0 - beta_one**STEP)
    scaled_two = moment_two / (1.0 - beta_two**STEP)
    weight = old - step_rate * (scaled_one / (jnp.sqrt(scaled_two) + adam_eps) + wd_rate * old)
    return weight, ema_rate * mean + (1.0 - ema_rate) * weight, moment_one, moment_two


def adam_at(state, new, moments, at, grad, step_rate, wd_rate):
    values = adam_step(*(state[at(slot)] for slot in range(4)), grad, step_rate, wd_rate)
    new[at(0)], new[at(1)], moments[at(0)], moments[at(1)] = values


def adam_mix_kernel(mix, depth, span, ga_ref, gb_ref, small,
                    mix_new, mix_moments, depth_new, depth_moments, span_new, span_moments):
    rows = mix.shape[2]
    sources = [(ga_ref, 0), (ga_ref, 2), (gb_ref, 0), (gb_ref, 1), (ga_ref, 1)]
    for i, (ref, at) in enumerate(sources):
        adam_at(mix, mix_new, mix_moments, lambda slot: (slot, i), ref[at * rows : (at + 1) * rows, :], rate_mix, decay_rate)
    grad = jnp.concatenate([small[0:KERNEL], small[KERNEL : 2 * KERNEL]], axis=1)
    adam_at(depth, depth_new, depth_moments, lambda slot: (slice(None), slot), grad, rate_depth, decay_rate)
    adam_at(span, span_new, span_moments, lambda slot: (slice(None), slot), small[2 * KERNEL :], rate_span, decay_rate)


def adam_feed_kernel(place_ref, out, norm, up, bias, down, ga_ref, gb_ref, small,
                     out_new, out_moments, norm_new, norm_moments,
                     up_new, up_moments, bias_new, bias_moments, down_new, down_moments):
    half = down.shape[3]
    width = 2 * half
    hid_dev = down.shape[2]
    adam_at(up, up_new, up_moments, lambda slot: (slot, 0), ga_ref[0:hid_dev, :], rate_up, decay_rate)
    adam_at(down, down_new, down_moments, lambda slot: (slot, 0), gb_ref[0:hid_dev, :], rate_down, decay_rate)
    grad = jnp.concatenate([ga_ref[hid_dev:, :], gb_ref[hid_dev:, :]], axis=1)
    adam_at(out, out_new, out_moments, lambda slot: slot, grad, rate_out, decay_rate)
    lines = jnp.concatenate([small[0:8], small[8:16]], axis=1)
    adam_at(norm, norm_new, norm_moments, lambda slot: slot, lines[0:4], rate_norm, 0.0)
    row = lax.broadcasted_iota(jnp.int32, (width, hid_dev), 0)
    col = lax.broadcasted_iota(jnp.int32, (width, hid_dev), 1)
    grad = jnp.zeros((1, hid_dev), full)
    for i in range(4):
        group, side = divmod(i, 2)
        line = jnp.where(place_ref[0] == group, lines[4 + i : 5 + i, :], 0.0)
        here = (row + side * width == col + place_ref[1] * hid_dev).astype(full).astype(low)
        high = line.astype(low)
        rest = (line - high.astype(full)).astype(low)
        both = dot(jnp.concatenate([high, rest] + [jnp.zeros_like(high)] * 6, axis=0), here)
        grad = grad + both[0:1] + both[1:2]
    adam_at(bias, bias_new, bias_moments, lambda slot: slot, grad, rate_bias, 0.0)


def adam_call(kernel, inputs, shapes, scalars=0):
    vmem = pl.BlockSpec(memory_space=pltpu.VMEM)
    moved = sum(value.size for value in inputs) * 6
    return pl.pallas_call(
        kernel,
        in_specs=[pl.BlockSpec(memory_space=pltpu.SMEM)] * scalars + [vmem] * (len(inputs) - scalars),
        out_specs=[vmem] * len(shapes),
        out_shape=[struct(shape, full) for shape in shapes],
        compiler_params=pltpu.CompilerParams(vmem_limit_bytes=40 << 20),
        cost_estimate=pl.CostEstimate(flops=2 * moved, transcendentals=0, bytes_accessed=moved),
    )(*inputs)


def struct(shape, dtype):
    return jax.ShapeDtypeStruct(shape, dtype)


def rows_spec(rows, width, at=0):
    return pl.BlockSpec((rows, width), lambda i, *_: (i, at))


def whole(shape, index=None):
    index = index or (0,) * len(shape)
    return pl.BlockSpec(shape, lambda i, *_: index)


def call(kernel, grid, in_specs, out_specs, out_shape, scratch, flops, moved, limit, prefetch=0):
    return pl.pallas_call(
        kernel,
        grid_spec=pltpu.PrefetchScalarGridSpec(
            num_scalar_prefetch=prefetch, grid=grid, in_specs=in_specs, out_specs=out_specs, scratch_shapes=scratch),
        out_shape=out_shape,
        compiler_params=pltpu.CompilerParams(dimension_semantics=("arbitrary",), vmem_limit_bytes=limit << 20),
        cost_estimate=pl.CostEstimate(flops=int(flops), transcendentals=0, bytes_accessed=int(moved)),
    )


def once(shape, index=None):
    index = index or (0,) * len(shape)
    return pl.BlockSpec(shape, lambda i, *_: index, pipeline_mode=pl.Buffered(1))


class Tokens:
    def __init__(self, tokens, width, count, place):
        self.tokens, self.width, self.count, self.place = tokens, width, count, place
        self.length = length = tokens // count
        self.half = half = width // 2
        self.padded = length + 2 * EDGE
        self.wide, self.slim, self.lane = rows_spec(length, width), rows_spec(length, half), rows_spec(length, LANES)
        self.all_cols = rows_spec(length, 4 * half)
        self.heads = pl.BlockSpec((1, HEADS, length, length), lambda i, *_: (i, 0, 0, 0))
        self.any = pl.BlockSpec(memory_space=pl.ANY)
        self.low_wide, self.low_slim = struct((tokens, width), low), struct((tokens, half), low)
        self.low_half = struct((half, width), low)

    def order(self, hidden, grad_out, depth):
        return call(
            order_kernel, (self.count,),
            [self.wide, self.wide, once(depth.shape)],
            [self.wide] * 3, [self.low_wide] * 3,
            [pltpu.VMEM((self.padded, self.width), full)], 4e9, 8e6, 60,
        )(hidden, grad_out, depth)

    def project(self, hidden, e, wa, wb, span, hid):
        tokens, width, half = self.tokens, self.width, self.half
        V = pltpu.VMEM
        devices = 2 * hid // self.hid_dev
        blocks = [value.reshape(devices // 2, -1, value.shape[1]) for value in wa]
        bias = pl.BlockSpec((devices // 2, blocks[0].shape[1], LANES), lambda i, *_: (0, 0, 4 * half // LANES),
                            pipeline_mode=pl.Buffered(1))
        return call(
            project_kernel, (self.count,),
            [self.wide, self.wide] + [self.any] * 4 + [bias, bias, once(span.shape)],
            [self.all_cols, self.slim, whole((2, hid)), whole((LANES, half))],
            [struct((tokens, 4 * half), low), self.low_slim, struct((2, hid), full), struct((LANES, half), low)],
            [V((width, 4 * half), low), V((width, half), low), pltpu.SemaphoreType.DMA((2, 2))],
            8e9, 10e6, 24, prefetch=1,
        )(self.place, hidden, e, *wa, *wb, *blocks, span)

    def mix(self, lens, qwkv, u, spant, wb):
        tokens, length, width, half = self.tokens, self.length, self.width, self.half
        V = pltpu.VMEM
        return call(
            mix_kernel, (self.count,),
            [self.all_cols, self.slim, once((LANES, half)), self.any, self.any],
            [self.lane, self.slim, self.heads, self.slim, self.wide],
            [pltpu.HBM(shape, dtype) for shape, dtype in (
                ((tokens, LANES), full), ((tokens, half), low), ((self.count, HEADS, length, length), low),
                ((tokens, half), low), ((tokens, width), low))],
            [V((self.padded, half), full), V((length, KERNEL * half), full), V((width, width), low),
             V((LANES, KERNEL * half), low), pltpu.SemaphoreType.DMA((2,))],
            20e9, 18e6, 44, prefetch=2,
        )(lens, self.place, qwkv, u, spant, *wb)

    def feed(self, y, hidden, grad_out, norm, ups, downs, bias, ctx, conv, wb):
        tokens, width, half = self.tokens, self.width, self.half
        hid = bias.shape[1]
        V = pltpu.VMEM
        vmem = pl.BlockSpec(memory_space=V)
        wide = V((tokens, width), low)
        ups = [value.reshape(value.shape[1:3] + value.shape[4:]) for value in ups]
        downs = [value.reshape((value.shape[1],) + value.shape[3:]) for value in downs]
        deep, tall, hid_dev = ups[0].shape[:3]
        across = downs[0].shape[1]
        devices = deep * tall * across
        weights = V((2, deep, tall, across, hid_dev, half), low)
        block = (devices, 2 * (hid + half) // devices, half)
        copies = len(ups) + len(downs) + 4 + 3 * self.count
        return pl.pallas_call(
            functools.partial(feed_kernel, self.count, len(ups) // 2, len(downs) // 2),
            in_specs=[pl.BlockSpec(memory_space=pltpu.SMEM), vmem, vmem] + [self.any] * (7 + len(ups) + len(downs)),
            out_specs=[vmem] + [self.any] * 5,
            out_shape=[struct((16, half), low)] + [self.low_wide] * 3 + [struct(block, low)] * 2,
            scratch_shapes=[V((16, half), full), wide, wide, wide, wide, weights, weights, V((width, width), low),
                            V((tokens, 2 * hid), low), V((tokens, 2 * hid), low), wide, wide, wide,
                            V((width, tokens), low), V((width, tokens), low), V((2,) + block, low), V((width, width), low),
                            pltpu.SemaphoreType.DMA((copies,)), pltpu.SemaphoreType.DMA((2 + 3 * self.count,))],
            compiler_params=pltpu.CompilerParams(vmem_limit_bytes=63 << 20),
            cost_estimate=pl.CostEstimate(flops=int(30e9), transcendentals=0, bytes_accessed=int(25e6)),
        )(self.place, norm, bias, y, hidden, grad_out, ctx, conv, *wb, *ups, *downs)

    def mixer_back(self, qwkv, a, gm, u, p, wb, spant):
        length, width, half = self.length, self.width, self.half
        V = pltpu.VMEM
        return call(
            mixer_back_kernel, (self.count,),
            [self.all_cols, self.heads, self.wide, self.slim, self.lane, self.any, self.any, once((LANES, half))],
            [self.wide, self.wide, self.slim, self.wide, whole((LANES, half))],
            [self.low_wide, self.low_wide, self.low_slim, self.low_wide, struct((LANES, half), full)],
            [V((length, half), full), V((self.padded, half), full), V((self.padded, half), full), V((self.padded, KERNEL * half), full),
             V((length, KERNEL * half), low), V((width, half), low), V((LANES, KERNEL * half), low), pltpu.SemaphoreType.DMA((2,))],
            30e9, 22e6, 44, prefetch=1,
        )(self.place, qwkv, a, gm, u, p, *wb, spant)

    def weights(self, hidden, e, gqw, gkv, gu, ge, d_span, devices):
        width, half = self.width, self.half
        shapes = [(devices, parts * half // devices, half) for parts in (3, 3, 2, 2)]
        V = pltpu.VMEM
        return call(
            weight_kernel, (self.count,),
            [self.wide, self.wide, self.wide, self.wide, self.slim, self.wide, whole((LANES, half))],
            [whole(shape) for shape in shapes] + [whole((SMALL_ROWS, half))],
            [struct(shape, low) for shape in shapes] + [struct((SMALL_ROWS, half), low)],
            [V((self.padded, width), full), V((width, 3 * half), full), V((width, width), full), V((16, width), full), V((SMALL_ROWS, half), full)],
            12e9, 16e6, 40, prefetch=1,
        )(self.place, hidden, e, gqw, gkv, gu, ge, d_span)

    def input_grad(self, gb, gqw, gkv, ge, wa, depth):
        length, width = self.length, self.width
        V = pltpu.VMEM
        return call(
            input_kernel, (self.count,),
            [self.wide, self.wide, self.wide, self.wide, self.any, self.any, once(depth.shape)],
            [self.wide], [self.low_wide],
            [V((self.padded, width), full), V((length, width), full), V((width, 2 * width), low), pltpu.SemaphoreType.DMA((2,))],
            10e9, 14e6, 36, prefetch=1,
        )(self.place, gb, gqw, gkv, ge, *wa, depth)[0]


class Links:
    def __init__(self, mesh):
        self.size = mesh.shape["dp"]
        self.grp = mesh.shape["grp"]
        deep = 4 if self.size % 4 == 0 else 1
        rest = self.size // deep
        wide = 1 << ((rest.bit_length() - 1) // 2)
        self.shape = (1, deep, rest // wide, wide)
        self.axes = {"z": (deep, rest, 1), "y": (rest // wide, wide, 2), "x": (wide, 1, 3),
                     "zl": (2, rest, 1), "zh": (deep // 2, 2 * rest, 1)}

    def place(self, name):
        if name == "grp":
            return lax.axis_index("grp")
        size, stride, _ = self.axes[name]
        return (lax.axis_index("dp") // stride) % size

    def swap(self, value, name, shift):
        if name == "grp":
            return lax.ppermute(value, "grp", [(i, i ^ shift) for i in range(self.grp)])
        size, stride, _ = self.axes[name]
        pairs = []
        for i in range(self.size):
            at = (i // stride) % size
            pairs.append((i, i + ((at ^ shift) - at) * stride))
        return lax.ppermute(value, "dp", pairs)

    def fetch(self, block, name):
        return [block] + [self.swap(block, name, k) for k in range(1, self.axes[name][0])]

    def merge(self, got, name):
        size, _, dim = self.axes[name]
        here = self.place(name)
        slots = []
        for j in range(size):
            value = got[size - 1]
            for k in range(size - 1):
                value = jnp.where(here == (j ^ k), got[k], value)
            slots.append(value)
        return jnp.concatenate(slots, axis=dim)

    def gather(self, block, name):
        return self.merge(self.fetch(block, name), name)

    def slices(self, block, name):
        size, _, dim = self.axes[name]
        here = self.place(name)
        if name == "zl":
            halves = block.reshape((1, block.shape[1] // 2, 2) + block.shape[2:])
            return [jnp.squeeze(lax.dynamic_slice_in_dim(halves, here ^ k, 1, 2), 2) for k in range(size)]
        return [lax.dynamic_slice_in_dim(block, here ^ k, 1, dim) for k in range(size)]

    def join(self, keep, piece):
        return keep.astype(full) + self.swap(piece, "grp", 1).astype(full)

    def send(self, a, b, small, name_a, name_b):
        cols = b.shape[-1]
        parts_a, parts_b = self.slices(a, name_a), self.slices(b, name_b)
        own = [parts_a[0], parts_b[0], small]
        apart = [] if name_a == name_b else [self.swap(part, name_a, k + 1) for k, part in enumerate(parts_a[1:])]
        messages = []
        for k in range(1, len(parts_b)):
            pieces = [parts_b[k].reshape(-1, cols), small]
            if name_a == name_b:
                pieces = [parts_a[k].reshape(-1, cols)] + pieces
            messages.append(self.swap(jnp.concatenate(pieces, axis=0), name_b, k))
        return own, apart, messages

    def finish(self, sent, end=low):
        (own_a, own_b, own_small), apart, messages = sent
        cols = own_b.shape[-1]
        sums_a, sums_b, sums = [own_a] + apart, [own_b], [own_small]
        for message in messages:
            for value, kept in ((own_a, sums_a), (own_b, sums_b), (own_small, sums)):
                if value is own_a and apart:
                    continue
                size = value.size // cols
                kept.append(message[:size].reshape(value.shape))
                message = message[size:]

        def add(got):
            got = [value.astype(full) for value in got]
            while len(got) > 1:
                got = [got[i] + got[i + 1] for i in range(0, len(got), 2)]
            return got[0].astype(end)

        return add(sums_a), add(sums_b), add(sums)


def on_device(links, hidden, grad_out, seq_lens, mix_state, out_state, depth_state, span_state, norm_state,
              up_state, bias_state, down_state):
    barrier = lax.optimization_barrier
    width = hidden.shape[1]
    half = width // 2
    hid_dev = up_state.shape[3]
    rows_dev = mix_state.shape[2]
    up_state = jnp.swapaxes(up_state, 2, 3)
    depth_state = jnp.swapaxes(depth_state, 0, 1)
    span_state = jnp.transpose(span_state, (2, 0, 1))
    place = jnp.stack([links.place("grp"), lax.axis_index("dp"), links.place("y"), links.place("x")]).astype(jnp.int32)
    tokens = Tokens(hidden.shape[0], width, seq_lens.shape[0], place)
    tokens.hid_dev = hid_dev

    mix_low = mix_state[0].astype(low)
    bias_row = jnp.pad(bias_state[0].astype(low), ((0, rows_dev - 1), (0, LANES - hid_dev)))
    shard = jnp.concatenate(
        [mix_low[0], mix_low[4], mix_low[1], mix_low[2], bias_row, out_state[0].astype(low), mix_low[3]], axis=1)
    feed_shard = jnp.concatenate([up_state[0, 0], down_state[0, 0]], axis=1).astype(low)

    def block(value):
        return value.reshape((1, 1, 1, 1) + value.shape)

    def both_cores(value):
        value = value.reshape(-1, value.shape[-1])
        return value, links.swap(value, "grp", 1)

    mixer = links.fetch(block(shard), "z")
    mixer, hidden_o, grad_o, e = barrier((mixer, *tokens.order(hidden, grad_out, depth_state)))
    mixer = links.merge(mixer, "z")
    split = 4 * half + LANES
    wa, wb = mixer[..., :split], mixer[..., split:]
    wa, wb = links.gather(wa, "y"), links.gather(wb, "x")
    wa, wb, feed_shard = barrier((wa, wb, feed_shard))
    wa, wb, feed = barrier((links.fetch(wa, "x"), links.fetch(wb, "y"), links.fetch(block(feed_shard), "z")))
    wa, wb = both_cores(links.merge(wa, "x")), both_cores(links.merge(wb, "y"))
    feed = links.merge(feed, "z")
    up, down = links.fetch(feed[..., :half], "y"), links.fetch(feed[..., half:], "x")

    qwkv, u, bias, spant = tokens.project(hidden_o, e, wa, wb, span_state, hid_dev * links.size)
    up, down, qwkv, u = barrier((up, down, qwkv, u))
    up, down = links.merge(up, "y"), links.merge(down, "x")
    ups, downs = links.fetch(up, "x"), links.fetch(down, "y")
    others = [links.swap(up, "grp", 1)], [links.swap(down, "grp", 1)]
    p, conv, a, ctx, y = tokens.mix(seq_lens, qwkv, u, spant, wb)
    ups, downs, others, y = barrier((ups, downs, others, y))
    ups = ups + others[0] + [links.swap(value, "grp", 1) for value in ups[1:]]
    downs = downs + others[1] + [links.swap(value, "grp", 1) for value in downs[1:]]
    small, result, gb, gm, keep, piece = tokens.feed(
        y, hidden_o, grad_o, norm_state, ups, downs, bias, ctx, conv, wb)

    def blocks(value):
        return value.reshape(links.shape + (-1, value.shape[-1]))

    joined = join(links.shape[1:], place, keep, links.swap(piece, "grp", 1), small, links.swap(small, "grp", 1))
    (parts_a, own_b, messages, small), gm = barrier((joined, gm))
    sent = ([parts_a[0], own_b, small], [links.swap(part, "x", k + 1) for k, part in enumerate(parts_a[1:])],
            [links.swap(message, "y", k + 1) for k, message in enumerate(messages)])
    gqw, gkv, gu, ge, d_span = tokens.mixer_back(qwkv, a, gm, u, p, wb, spant)
    sent, gqw, gkv, gu, ge, d_span = barrier((sent, gqw, gkv, gu, ge, d_span))
    sent = links.send(*links.finish(sent), "y", "x")
    keep_a, piece_a, keep_b, piece_b, small = tokens.weights(hidden_o, e, gqw, gkv, gu, ge, d_span, links.size)
    sent, keep_a, piece_a, keep_b, piece_b, small = barrier((sent, keep_a, piece_a, keep_b, piece_b, small))

    feed_sent = links.send(*links.finish(sent), "z", "z")
    sums = (blocks(links.join(keep_a, piece_a).astype(low)), blocks(links.join(keep_b, piece_b).astype(low)),
            links.join(small, small).astype(low))
    sums, gqw, ge = barrier((sums, gqw, ge))
    sent = links.send(*sums, "x", "y")
    gx = tokens.input_grad(gb, gqw, gkv, ge, wa, depth_state)
    sent, gx = barrier((sent, gx))
    feed_sent, sums = barrier((feed_sent, links.finish(links.send(*links.finish(sent), "y", "x"))))
    feed_sums = links.finish(feed_sent, full)
    grad_a, grad_b, small = links.finish(links.send(*sums, "z", "z"), full)

    def twice(state, at=0):
        shape = state.shape[:at] + (2,) + state.shape[at + 1 :]
        return [shape, shape]

    def flat(value):
        return value.reshape(-1, value.shape[-1])

    feed_a, feed_b, feed_small = feed_sums
    feed_out = adam_call(
        adam_feed_kernel,
        [place, out_state, norm_state, up_state, bias_state, down_state, flat(feed_a), flat(feed_b), feed_small],
        twice(out_state) + twice(norm_state) + twice(up_state) + twice(bias_state) + twice(down_state), scalars=1)
    mixed = adam_call(
        adam_mix_kernel,
        [mix_state, depth_state, span_state, flat(grad_a), flat(grad_b), small],
        twice(mix_state) + twice(depth_state, 1) + twice(span_state, 1))
    depth_out = [jnp.swapaxes(value, 0, 1) for value in mixed[2:4]]
    span_out = [jnp.transpose(value, (1, 2, 0)) for value in mixed[4:]]
    up_out = [jnp.swapaxes(value, 2, 3) for value in feed_out[4:6]]
    return (result, gx, *mixed[:2], *feed_out[:2], *depth_out, *span_out, *feed_out[2:4], *up_out, *feed_out[6:])


def solution(mesh):
    both = ("grp", "dp")
    mix, out = P(None, None, both, None), P(None, both, None)
    up, bias, down = P(None, "grp", None, "dp"), P(None, "grp", "dp"), P(None, "grp", "dp", None)
    rows = P(both, None)
    return jax.shard_map(
        functools.partial(on_device, Links(mesh)),
        mesh=mesh,
        in_specs=(rows, rows, P(both), mix, out, P(), P(), P(), up, bias, down),
        out_specs=(rows, rows, mix, mix, out, out, P(), P(), P(), P(), P(), P(), up, up, bias, bias, down, down),
        check_vma=False,
    )
```

```python
import functools

import jax
import jax.numpy as jnp
from jax import lax
from jax.experimental import pallas as pl
from jax.experimental.pallas import tpu as pltpu
from jax.sharding import PartitionSpec as P

HEADS = 6
HS = 64
KERNEL = 9
STEP = 7
REACH = KERNEL // 2
TAP = 8
LANES = 128
PAD = 8
EDGE = REACH * PAD

beta_one = 0.9
beta_two = 0.999
adam_eps = 1e-06
ema_rate = 0.99
decay_rate = 0.01
rate_mix = 0.06
rate_out = 0.12
rate_depth = 0.4
rate_span = 0.08
rate_norm = 0.5
rate_up = 0.08
rate_bias = 0.3
rate_down = 0.04

low = jnp.bfloat16
full = jnp.float32
NN = (((1,), (0,)), ((), ()))
NT = (((1,), (1,)), ((), ()))
TN = (((0,), (0,)), ((), ()))


def dot(left, right, dims=NN):
    return lax.dot_general(left, right, dims, preferred_element_type=full)


def rounded(value):
    return value.astype(low).astype(full)


def row_loop(rows, chunk, body):
    for r in range(0, rows, chunk):
        body(r)


def spread_table(width):
    row = lax.broadcasted_iota(jnp.int32, (LANES, 1), 0)
    col = lax.broadcasted_iota(jnp.int32, (1, KERNEL * width), 1)
    head = row % TAP
    first = (row // TAP) * width + head * HS
    first = jnp.where(head < HEADS, first, -HS)
    return ((col >= first) & (col < first + HS)).astype(full).astype(low)


def tap_table():
    row = lax.broadcasted_iota(jnp.int32, (LANES, HEADS * KERNEL), 0)
    col = lax.broadcasted_iota(jnp.int32, (LANES, HEADS * KERNEL), 1)
    return ((col % KERNEL) * TAP + col // KERNEL == row).astype(full).astype(low)


def copy_halves(place_ref, mine, other, target, sems, first, cols):
    rows = mine.shape[0]
    copies = []
    for i, (half, at) in enumerate(((mine, place_ref[0]), (other, 1 - place_ref[0]))):
        copy = pltpu.make_async_copy(
            half.at[:, pl.ds(first, cols)], target.at[pl.ds(pl.multiple_of(at * rows, rows), rows), :], sems.at[i])
        copy.start()
        copies.append(copy)
    return copies


def put_blocks(place_ref, value_ref, keep_ref, piece_ref):
    devices, _, half = keep_ref.shape
    parts = value_ref.shape[1] // half
    rows = half // devices
    for ref, at in ((keep_ref, place_ref[0]), (piece_ref, 1 - place_ref[0])):
        for m in range(parts):
            value = value_ref[pl.ds(pl.multiple_of(at * half, half), half), m * half : (m + 1) * half]
            for n in range(devices):
                ref[n, m * rows : (m + 1) * rows, :] = value[n * rows : (n + 1) * rows].astype(low)


def fill_padded(ref, value):
    rows = value.shape[0]
    value = value.astype(full)
    place = lax.broadcasted_iota(jnp.int32, (PAD, 1), 0)
    ref[EDGE : EDGE + rows, :] = value
    for i in range(REACH):
        before = value[rows - EDGE + i * PAD : rows - EDGE + (i + 1) * PAD]
        ref[i * PAD : (i + 1) * PAD, :] = jnp.where(place == 0, 0.0, pltpu.roll(before, 1, 0))
        after = value[i * PAD : (i + 1) * PAD]
        ref[EDGE + rows + i * PAD : EDGE + rows + (i + 1) * PAD, :] = jnp.where(
            place == PAD - 1, 0.0, pltpu.roll(after, PAD - 1, 0))


def order_matrix(rows, back=False):
    row = lax.broadcasted_iota(jnp.int32, (rows, rows), 0)
    col = lax.broadcasted_iota(jnp.int32, (1, rows), 1)
    places = rows // PAD
    at = (col % PAD) * places + col // PAD if back else (col % places) * PAD + col // places
    return (row == at).astype(full).astype(low)


def order_kernel(x_ref, g_ref, depth_ref, xo_ref, go_ref, e_ref, xpad):
    rows, width = x_ref.shape
    order = order_matrix(rows)
    x = dot(order, x_ref[...])
    xo_ref[...] = x.astype(low)
    go_ref[...] = dot(order, g_ref[...]).astype(low)
    fill_padded(xpad, x)

    rates = [rounded(depth_ref[j, 0:1]) for j in range(KERNEL)]

    def depth_rows(r):
        acc = rates[0] * xpad[pl.ds(r, 32), :]
        for j in range(1, KERNEL):
            acc = acc + rates[j] * xpad[pl.ds(r + PAD * j, 32), :]
        e_ref[pl.ds(r, 32), :] = acc.astype(low)

    row_loop(rows, 32, depth_rows)


def project_kernel(place_ref, x_ref, e_ref, wam_ref, wao_ref, wbm_ref, wbo_ref, bm_ref, bo_ref, span_ref,
                   qwkv_ref, u_ref, bias_ref, spant_ref,
                   wa_ref, w3_ref, sems):
    rows, width = x_ref.shape
    half = width // 2

    @pl.when(pl.program_id(0) == 0)
    def _():
        copies = copy_halves(place_ref, wam_ref, wao_ref, wa_ref, sems.at[0], 0, 4 * half)
        copies += copy_halves(place_ref, wbm_ref, wbo_ref, w3_ref, sems.at[1], width, half)
        spant_ref[...] = dot(tap_table(), span_ref[:, 0, :].astype(low)).astype(low)
        hid_dev = bias_ref.shape[1] // bm_ref.shape[0]
        for n in range(bm_ref.shape[0]):
            cols = slice(n * hid_dev, (n + 1) * hid_dev)
            mine, other = bm_ref[n].astype(full)[0:1, 0:hid_dev], bo_ref[n].astype(full)[0:1, 0:hid_dev]
            bias_ref[0:1, cols] = jnp.where(place_ref[0] == 0, mine, other)
            bias_ref[1:2, cols] = jnp.where(place_ref[0] == 0, other, mine)
        for copy in copies:
            copy.wait()

    x = x_ref[...]
    for c in range(4):
        qwkv_ref[:, c * half : (c + 1) * half] = dot(x, wa_ref[:, c * half : (c + 1) * half]).astype(low)
    u_ref[...] = dot(e_ref[...], w3_ref[...]).astype(low)


def mix_kernel(lens_ref, place_ref, qwkv_ref, u_ref, spant_ref, wbm_ref, wbo_ref,
               p_ref, conv_ref, a_ref, ctx_ref, y_ref,
               wpad, taps, wo_ref, spread_ref, sems):
    rows, half = u_ref.shape

    @pl.when(pl.program_id(0) == 0)
    def _():
        copies = copy_halves(place_ref, wbm_ref, wbo_ref, wo_ref, sems, 0, 2 * half)
        spread_ref[...] = spread_table(half)
        for copy in copies:
            copy.wait()

    r = (u_ref[...].astype(full) * qwkv_ref[:, 0:half].astype(full)).astype(low)
    logits = rounded(dot(r, spant_ref[...], NT))
    lt = logits.T[0 : KERNEL * TAP].reshape(KERNEL, TAP, rows)
    top = jnp.max(lt, axis=0, keepdims=True)
    ex = jnp.exp(lt - top)
    pt = (ex / jnp.sum(ex, axis=0, keepdims=True)).reshape(KERNEL * TAP, rows)
    p = jnp.concatenate([pt, jnp.zeros((LANES - KERNEL * TAP, rows), full)], axis=0).T
    p_ref[...] = p
    fill_padded(wpad, qwkv_ref[:, half : 2 * half])
    p_low = p.astype(low)
    for j in range(KERNEL):
        taps[:, j * half : (j + 1) * half] = dot(p_low, spread_ref[:, j * half : (j + 1) * half])

    def conv_rows(r):
        acc = taps[pl.ds(r, 32), 0:half] * wpad[pl.ds(r, 32), :]
        for j in range(1, KERNEL):
            acc = acc + taps[pl.ds(r, 32), j * half : (j + 1) * half] * wpad[pl.ds(r + PAD * j, 32), :]
        conv_ref[pl.ds(r, 32), :] = acc.astype(low)

    row_loop(rows, 32, conv_rows)
    seq_len = lens_ref[pl.program_id(0)]
    lane = lax.broadcasted_iota(jnp.int32, (1, LANES), 1)
    row = lax.broadcasted_iota(jnp.int32, (1, rows), 1)
    live = (row % PAD) * (rows // PAD) + row // PAD < seq_len
    for pair in range(HEADS // 2):
        at = pair * LANES
        q = qwkv_ref[:, at : at + LANES]
        k = qwkv_ref[:, 2 * half + at : 2 * half + at + LANES]
        v = qwkv_ref[:, 3 * half + at : 3 * half + at + LANES]
        outs = []
        for side in range(2):
            pick = jnp.where((lane // HS) == side, HS ** (-0.5), 0.0).astype(low)
            scores = dot(q * pick, k, NT)
            scores = jnp.where(live, scores, -1000000000.0)
            top = jnp.max(scores, axis=1, keepdims=True)
            ex = jnp.exp(scores - top)
            a = (ex * (1.0 / jnp.sum(ex, axis=1, keepdims=True))).astype(low)
            a_ref[0, 2 * pair + side] = a
            outs.append(dot(a, v))
        ctx_ref[:, at : at + LANES] = jnp.where((lane // HS) == 0, outs[0], outs[1]).astype(low)
    y_ref[...] = (dot(ctx_ref[...], wo_ref[0:half, :]) + dot(conv_ref[...], wo_ref[half:, :])).astype(low)


def normed(value):
    centered = value - jnp.mean(value, axis=1, keepdims=True)
    variance = jnp.mean(centered * centered, axis=1, keepdims=True)
    rstd = lax.rsqrt(variance + 1e-12)
    return centered * rstd, rstd


def feed_kernel(count, up_parts, down_parts, place_ref, norm_ref, bias_ref, y_hbm, x_hbm, g_hbm, ctx_hbm, conv_hbm, wbm_hbm, wbo_hbm, *refs):
    ups, downs = refs[: 2 * up_parts], refs[2 * up_parts : 2 * (up_parts + down_parts)]
    (small_ref, res_hbm, gb_hbm, gm_hbm, keep_hbm, piece_hbm, small_s, y_s, x_s, g_s, m_s, up_s, down_s, wo_s, act_s, gpre_s,
     res_s, gb_s, gm_s, ft_s, got_s, df_s, do_s, in_sems, out_sems) = refs[2 * (up_parts + down_parts) :]
    tokens, width = y_s.shape
    half = width // 2
    hid = bias_ref.shape[1]
    length = tokens // count
    waits, outs = {}, []

    def fetch(name, source, target):
        copy = pltpu.make_async_copy(source, target, in_sems.at[len(waits)])
        copy.start()
        waits[name] = copy

    def put(source, target):
        copy = pltpu.make_async_copy(source, target, out_sems.at[len(outs)])
        copy.start()
        outs.append(copy)

    seqs = [slice(n * length, (n + 1) * length) for n in range(count)]
    for n, rows in enumerate(seqs):
        fetch(("y", n), y_hbm.at[rows], y_s.at[rows])
        fetch(("x", n), x_hbm.at[rows], x_s.at[rows])
        if n == 0:
            for i, at in enumerate((place_ref[0], 1 - place_ref[0])):
                for k in range(up_parts):
                    fetch(("up", i, k), ups[i * up_parts + k], up_s.at[at, :, :, place_ref[3] ^ k])
            for i, at in enumerate((place_ref[0], 1 - place_ref[0])):
                for k in range(down_parts):
                    fetch(("down", i, k), downs[i * down_parts + k], down_s.at[at, :, place_ref[2] ^ k])
        fetch(("g", n), g_hbm.at[rows], g_s.at[rows])
        if n == 0:
            for i, (part, at) in enumerate(((wbm_hbm, place_ref[0]), (wbo_hbm, 1 - place_ref[0]))):
                fetch(("wo", i), part.at[:, pl.ds(0, width)], wo_s.at[pl.ds(pl.multiple_of(at * half, half), half), :])
    fetch("ctx", ctx_hbm, m_s.at[:, pl.ds(0, half)])
    fetch("conv", conv_hbm, m_s.at[:, pl.ds(half, half)])

    g1, c1, g2, c2 = (norm_ref[0, i : i + 1] for i in range(4))
    sums = [jnp.zeros((1, width), full) for _ in range(4)]
    dbias = [jnp.zeros((1, hid), full) for _ in range(2)]
    groups = [(slice(g * hid, (g + 1) * hid), slice(g * half, (g + 1) * half)) for g in range(2)]
    kept = [{} for _ in seqs]

    def wait(name):
        if name in waits:
            waits.pop(name).wait()

    def wait_all(name):
        for key in [key for key in waits if key[0] == name]:
            wait(key)

    def enter(n):
        wait(("y", n))
        wait(("x", n))
        zh1, rstd1 = normed(y_s[seqs[n]].astype(full) + x_s[seqs[n]].astype(full))
        f = (zh1 * g1 + c1).astype(low)
        kept[n].update(zh1=zh1, rstd1=rstd1, f=f, parts=[])
        ft_s[:, seqs[n]] = f.T

    def ahead(n, g):
        hidden, cols = groups[g]
        wait_all("up")
        pre = dot(kept[n]["f"][:, cols], up_s[g].reshape(hid, half), NT) + bias_ref[g : g + 1, :]
        cdf = 0.5 * (1.0 + lax.erf(pre * 2.0 ** (-0.5)))
        act_s[seqs[n], hidden] = (pre * cdf).astype(low)
        gpre_s[seqs[n], hidden] = (cdf + pre * (jnp.exp(-0.5 * pre * pre) * 0.3989422804014327)).astype(low)
        wait_all("down")
        kept[n]["parts"].append(rounded(dot(act_s[seqs[n], hidden], down_s[g].reshape(hid, half))))

    def turn(n):
        rows = seqs[n]
        h1 = kept[n]["zh1"] * g1 + c1
        zh2, rstd2 = normed(h1 + jnp.concatenate(kept[n]["parts"], axis=1))
        result = (zh2 * g2 + c2).astype(low)
        res_s[rows] = dot(order_matrix(length, True), result).astype(low)
        put(res_s.at[rows], res_hbm.at[rows])
        wait(("g", n))
        grad = g_s[rows].astype(full)
        sums[2] = sums[2] + jnp.sum(grad * zh2, axis=0, keepdims=True)
        sums[3] = sums[3] + jnp.sum(grad, axis=0, keepdims=True)
        dz = grad * g2
        gz = (dz - jnp.mean(dz, axis=1, keepdims=True) - zh2 * jnp.mean(dz * zh2, axis=1, keepdims=True)) * rstd2
        go = gz.astype(low)
        got_s[:, rows] = go.T
        kept[n].update(gz=gz, go=go, parts=[])

    def behind(n, g):
        hidden, cols = groups[g]
        slope = gpre_s[seqs[n], hidden].astype(full)
        gpre = (dot(kept[n]["go"][:, cols], down_s[g].reshape(hid, half), NT) * slope).astype(low)
        gpre_s[seqs[n], hidden] = gpre
        dbias[g] = dbias[g] + jnp.sum(gpre.astype(full), axis=0, keepdims=True)
        kept[n]["parts"].append(rounded(dot(gpre, up_s[g].reshape(hid, half))))

    def leave(n):
        rows, zh1 = seqs[n], kept[n]["zh1"]
        gh1 = kept[n]["gz"] + jnp.concatenate(kept[n]["parts"], axis=1)
        sums[0] = sums[0] + jnp.sum(gh1 * zh1, axis=0, keepdims=True)
        sums[1] = sums[1] + jnp.sum(gh1, axis=0, keepdims=True)
        dz1 = gh1 * g1
        gy = (dz1 - jnp.mean(dz1, axis=1, keepdims=True) - zh1 * jnp.mean(dz1 * zh1, axis=1, keepdims=True)) * kept[n]["rstd1"]
        gb_s[rows] = gy.astype(low)
        put(gb_s.at[rows], gb_hbm.at[rows])

    def through(n):
        rows = seqs[n]
        wait(("wo", 0))
        wait(("wo", 1))
        gm_s[rows] = dot(gb_s[rows], wo_s[...], NT).astype(low)
        put(gm_s.at[rows], gm_hbm.at[rows])

    first, *rest = range(count)
    enter(first)
    ahead(first, 0)
    for n in rest:
        enter(n)
    ahead(first, 1)
    for n in rest:
        ahead(n, 0)
        turn(n - 1)
        ahead(n, 1)
        behind(n - 1, 0)
        if n == rest[-1]:
            turn(n)
        behind(n - 1, 1)
        if n == rest[-1]:
            behind(n, 0)
        leave(n - 1)
        if n == rest[-1]:
            behind(n, 1)
        through(n - 1)
    if not rest:
        turn(first)
        behind(first, 0)
        behind(first, 1)
    leave(count - 1)
    through(count - 1)

    wait("ctx")
    wait("conv")
    do_s[...] = dot(m_s[...].T, gb_s[...]).astype(low)
    devices = keep_hbm.shape[0]
    hid_dev, rows_dev = hid // devices, half // devices
    for i, (at, target) in enumerate(((1 - place_ref[0], piece_hbm), (place_ref[0], keep_hbm))):
        hidden = pl.ds(pl.multiple_of(at * hid, LANES), hid)
        cols = pl.ds(pl.multiple_of(at * half, half), half)
        up = dot(ft_s[cols, :], gpre_s[:, hidden]).astype(low).T
        down = dot(got_s[cols, :], act_s[:, hidden]).astype(low).T
        out = do_s[cols, :]
        for n in range(devices):
            first = 0
            for value, size in ((up, hid_dev), (out[:, 0:half], rows_dev), (down, hid_dev), (out[:, half:], rows_dev)):
                df_s[i, n, first : first + size, :] = value[n * size : (n + 1) * size]
                first += size
        put(df_s.at[i], target)
    for i in range(4):
        g, side = divmod(i, 2)
        for j in range(2):
            small_s[8 * j + i : 8 * j + i + 1, :] = sums[i][:, j * half : (j + 1) * half]
            at = side * width + j * half
            small_s[8 * j + 4 + i : 8 * j + 5 + i, :] = dbias[g][:, at : at + half]
    small_ref[...] = small_s[...].astype(low)
    for copy in outs:
        copy.wait()


def mixer_back_kernel(place_ref, qwkv_ref, a_ref, gm_ref, u_ref, p_ref, wbm_ref, wbo_ref, spant_ref,
                      gqw_ref, gkv_ref, gu_ref, ge_ref, dspan_ref,
                      gqa, wpad, gpad, taps, prods, w3_ref, spread_ref, sems):
    rows, half = u_ref.shape

    @pl.when(pl.program_id(0) == 0)
    def _():
        copies = copy_halves(place_ref, wbm_ref, wbo_ref, w3_ref, sems, 2 * half, half)
        dspan_ref[...] = jnp.zeros_like(dspan_ref)
        spread_ref[...] = spread_table(half)
        for copy in copies:
            copy.wait()

    lane = lax.broadcasted_iota(jnp.int32, (1, LANES), 1)
    for pair in range(HEADS // 2):
        at = pair * LANES
        q = qwkv_ref[:, at : at + LANES]
        k = qwkv_ref[:, 2 * half + at : 2 * half + at + LANES]
        v = qwkv_ref[:, 3 * half + at : 3 * half + at + LANES]
        gctx = gm_ref[:, at : at + LANES]
        qt, gctxt = q.T, gctx.T
        gqs, gks, gvs = [], [], []
        for side in range(2):
            pick = jnp.where((lane // HS) == side, 1.0, 0.0).astype(low)
            a_low = a_ref[0, 2 * pair + side]
            a = a_low.astype(full)
            ga = dot(gctx * pick, v, NT)
            gs = (a * (ga - jnp.sum(a * ga, axis=1, keepdims=True))).astype(low)
            gqs.append(dot(gs, k))
            gks.append(dot(qt, gs))
            gvs.append(dot(gctxt, a_low))
        first = (lane // HS) == 0
        gqa[:, at : at + LANES] = jnp.where(first, gqs[0], gqs[1]) * HS ** (-0.5)
        gk = jnp.concatenate([gks[0][0:HS], gks[1][HS:]], axis=0) * HS ** (-0.5)
        gv = jnp.concatenate([gvs[0][0:HS], gvs[1][HS:]], axis=0)
        gkv_ref[:, at : at + LANES] = gk.T.astype(low)
        gkv_ref[:, half + at : half + at + LANES] = gv.T.astype(low)
    fill_padded(wpad, qwkv_ref[:, half : 2 * half])
    fill_padded(gpad, gm_ref[:, half:])
    p = p_ref[...]
    p_low = p.astype(low)
    for j in range(KERNEL):
        cols = slice(j * half, (j + 1) * half)
        fill_padded(taps.at[:, cols], dot(p_low, spread_ref[:, cols]))

    def conv_rows(r):
        here = gpad[pl.ds(r + EDGE, 32), :]
        acc = None
        for j in range(KERNEL):
            cols = slice(j * half, (j + 1) * half)
            prods[pl.ds(r, 32), cols] = (here * wpad[pl.ds(r + PAD * j, 32), :]).astype(low)
            back = pl.ds(r + PAD * (2 * REACH - j), 32)
            term = taps[back, cols] * gpad[back, :]
            acc = term if acc is None else acc + term
        gqw_ref[pl.ds(r, 32), half:] = acc.astype(low)

    row_loop(rows, 32, conv_rows)
    gp = dot(prods[...], spread_ref[...], NT)
    gpt = gp.T[0 : KERNEL * TAP].reshape(KERNEL, TAP, rows)
    pt = p.T[0 : KERNEL * TAP].reshape(KERNEL, TAP, rows)
    glt = pt * (gpt - jnp.sum(pt * gpt, axis=0, keepdims=True))
    glt = jnp.concatenate([glt.reshape(KERNEL * TAP, rows), jnp.zeros((LANES - KERNEL * TAP, rows), full)], axis=0)
    gl = glt.T.astype(low)
    q = qwkv_ref[:, 0:half].astype(full)
    u = u_ref[...].astype(full)
    r = (u * q).astype(low)
    dspan_ref[...] += dot(glt.astype(low), r)
    gr = rounded(dot(gl, spant_ref[...]))
    gqw_ref[:, 0:half] = (gqa[...] + gr * u).astype(low)
    gu = (gr * q).astype(low)
    gu_ref[...] = gu
    ge_ref[...] = dot(gu, w3_ref[...], NT).astype(low)


SMALL_ROWS = 2 * KERNEL + HEADS * KERNEL


def weight_kernel(place_ref, x_ref, e_ref, gqw_ref, gkv_ref, gu_ref, ge_ref, dspan_ref,
                  keep_a_ref, piece_a_ref, keep_b_ref, piece_b_ref, small_ref,
                  xpad, acc_a, acc_b, small, rows_s):
    step, last = pl.program_id(0), pl.num_programs(0) - 1
    rows, width = x_ref.shape
    half = width // 2

    @pl.when(step == 0)
    def _():
        acc_a[...] = jnp.zeros_like(acc_a)
        acc_b[...] = jnp.zeros_like(acc_b)
        small[...] = jnp.zeros_like(small)

    x = x_ref[...]
    xt = x.T
    acc_a[:, 0:width] += dot(xt, gqw_ref[...])
    acc_a[:, width:] += dot(xt, gkv_ref[:, 0:half])
    acc_b[:, 0:half] += dot(xt, gkv_ref[:, half:])
    acc_b[:, half:] += dot(e_ref[...].T, gu_ref[...])
    fill_padded(xpad, x)
    for c in range(0, width, LANES):
        cols = slice(c, c + LANES)

        sums = [jnp.zeros((PAD, LANES), full) for _ in range(KERNEL)]
        for r in range(0, rows, 64):
            ge = ge_ref[pl.ds(r, 64), cols].astype(full)
            for j in range(KERNEL):
                prod = ge * xpad[pl.ds(r + PAD * j, 64), cols]
                sums[j] = sums[j] + jnp.sum(prod.reshape(PAD, PAD, LANES), axis=0)
        for j in range(KERNEL):
            small[j : j + 1, cols] += jnp.sum(sums[j], axis=0, keepdims=True)

    @pl.when(step == last)
    def _():
        put_blocks(place_ref, acc_a, keep_a_ref, piece_a_ref)
        put_blocks(place_ref, acc_b, keep_b_ref, piece_b_ref)
        for side in range(2):
            rows_s[side * KERNEL : (side + 1) * KERNEL, :] = small[0:KERNEL, side * half : (side + 1) * half]
        rows_s[2 * KERNEL :, :] = dot(tap_table(), dspan_ref[...].astype(low), TN)
        small_ref[...] = rows_s[...].astype(low)


def input_kernel(place_ref, gb_ref, gqw_ref, gkv_ref, ge_ref, wam_ref, wao_ref, depth_ref,
                 gx_ref, gepad, gx_s, wa_ref, sems):
    rows, width = gb_ref.shape

    @pl.when(pl.program_id(0) == 0)
    def _():
        for copy in copy_halves(place_ref, wam_ref, wao_ref, wa_ref, sems, 0, 2 * width):
            copy.wait()

    fill_padded(gepad, ge_ref[...])
    gx_s[...] = gb_ref[...].astype(full) + dot(gqw_ref[...], wa_ref[:, 0:width], NT) + dot(gkv_ref[...], wa_ref[:, width:], NT)

    rates = [rounded(depth_ref[j, 0:1]) for j in range(KERNEL)]

    def shift_rows(r):
        acc = gx_s[pl.ds(r, 32), :]
        for j in range(KERNEL):
            acc = acc + rates[j] * gepad[pl.ds(r + PAD * (2 * REACH - j), 32), :]
        gx_s[pl.ds(r, 32), :] = acc

    row_loop(rows, 32, shift_rows)
    gx_ref[...] = dot(order_matrix(rows, True), gx_s[...].astype(low)).astype(low)


def join_kernel(shape, place_ref, keep, came, small, small_came, *outs):
    deep, tall, wide = shape
    cut = keep.shape[1] // 2
    parts_a, (own_b, *messages, small_sum) = outs[:wide], outs[wide:]

    def total(n, first):
        rows = pl.ds(first, cut)
        return (keep[n, rows].astype(full) + came[n, rows].astype(full)).astype(low)

    small_now = (small[...].astype(full) + small_came[...].astype(full)).astype(low)
    small_sum[...] = small_now
    for line in range(deep * tall):
        for k in range(wide):
            parts_a[k][line] = total(line * wide + (place_ref[3] ^ k), 0)
    for z in range(deep):
        for x in range(wide):
            at = z * wide + x
            for k in range(tall):
                value = total((z * tall + (place_ref[2] ^ k)) * wide + x, cut)
                if k == 0:
                    own_b[at] = value
                else:
                    messages[k - 1][at * cut : (at + 1) * cut, :] = value
    for message in messages:
        message[deep * wide * cut :, :] = small_now


def join(shape, place, keep, came, small, small_came):
    deep, tall, wide = shape
    cut, half = keep.shape[1] // 2, keep.shape[2]
    vmem = pl.BlockSpec(memory_space=pltpu.VMEM)
    shapes = [(deep * tall, cut, half)] * wide + [(deep * wide, cut, half)]
    shapes += [(deep * wide * cut + small.shape[0], half)] * (tall - 1) + [small.shape]
    outs = pl.pallas_call(
        functools.partial(join_kernel, shape),
        in_specs=[pl.BlockSpec(memory_space=pltpu.SMEM)] + [vmem] * 4,
        out_specs=[vmem] * len(shapes),
        out_shape=[struct(value, low) for value in shapes],
        compiler_params=pltpu.CompilerParams(vmem_limit_bytes=24 << 20),
        cost_estimate=pl.CostEstimate(flops=keep.size, transcendentals=0, bytes_accessed=6 * keep.size),
    )(place, keep, came, small, small_came)
    parts_a = [value.reshape(1, deep, tall, 1, cut, half) for value in outs[:wide]]
    return parts_a, outs[wide].reshape(1, deep, 1, wide, cut, half), outs[wide + 1 : -1], outs[-1]


def adam_step(old, one, two, mean, grad, step_rate, wd_rate):
    moment_one = beta_one * one + (1.0 - beta_one) * grad
    moment_two = beta_two * two + (1.0 - beta_two) * grad * grad
    scaled_one = moment_one / (1.0 - beta_one**STEP)
    scaled_two = moment_two / (1.0 - beta_two**STEP)
    weight = old - step_rate * (scaled_one / (jnp.sqrt(scaled_two) + adam_eps) + wd_rate * old)
    return weight, ema_rate * mean + (1.0 - ema_rate) * weight, moment_one, moment_two


def adam_at(state, new, moments, at, grad, step_rate, wd_rate):
    values = adam_step(*(state[at(slot)] for slot in range(4)), grad, step_rate, wd_rate)
    new[at(0)], new[at(1)], moments[at(0)], moments[at(1)] = values


def adam_mix_kernel(mix, depth, span, ga_ref, gb_ref, small,
                    mix_new, mix_moments, depth_new, depth_moments, span_new, span_moments):
    rows = mix.shape[2]
    sources = [(ga_ref, 0), (ga_ref, 2), (gb_ref, 0), (gb_ref, 1), (ga_ref, 1)]
    for i, (ref, at) in enumerate(sources):
        adam_at(mix, mix_new, mix_moments, lambda slot: (slot, i), ref[at * rows : (at + 1) * rows, :], rate_mix, decay_rate)
    grad = jnp.concatenate([small[0:KERNEL], small[KERNEL : 2 * KERNEL]], axis=1)
    adam_at(depth, depth_new, depth_moments, lambda slot: (slice(None), slot), grad, rate_depth, decay_rate)
    adam_at(span, span_new, span_moments, lambda slot: (slice(None), slot), small[2 * KERNEL :], rate_span, decay_rate)


def adam_feed_kernel(place_ref, out, norm, up, bias, down, ga_ref, gb_ref, small,
                     out_new, out_moments, norm_new, norm_moments,
                     up_new, up_moments, bias_new, bias_moments, down_new, down_moments):
    half = down.shape[3]
    width = 2 * half
    hid_dev = down.shape[2]
    adam_at(up, up_new, up_moments, lambda slot: (slot, 0), ga_ref[0:hid_dev, :], rate_up, decay_rate)
    adam_at(down, down_new, down_moments, lambda slot: (slot, 0), gb_ref[0:hid_dev, :], rate_down, decay_rate)
    grad = jnp.concatenate([ga_ref[hid_dev:, :], gb_ref[hid_dev:, :]], axis=1)
    adam_at(out, out_new, out_moments, lambda slot: slot, grad, rate_out, decay_rate)
    lines = jnp.concatenate([small[0:8], small[8:16]], axis=1)
    adam_at(norm, norm_new, norm_moments, lambda slot: slot, lines[0:4], rate_norm, 0.0)
    row = lax.broadcasted_iota(jnp.int32, (width, hid_dev), 0)
    col = lax.broadcasted_iota(jnp.int32, (width, hid_dev), 1)
    grad = jnp.zeros((1, hid_dev), full)
    for i in range(4):
        group, side = divmod(i, 2)
        line = jnp.where(place_ref[0] == group, lines[4 + i : 5 + i, :], 0.0)
        here = (row + side * width == col + place_ref[1] * hid_dev).astype(full).astype(low)
        high = line.astype(low)
        rest = (line - high.astype(full)).astype(low)
        both = dot(jnp.concatenate([high, rest] + [jnp.zeros_like(high)] * 6, axis=0), here)
        grad = grad + both[0:1] + both[1:2]
    adam_at(bias, bias_new, bias_moments, lambda slot: slot, grad, rate_bias, 0.0)


def adam_call(kernel, inputs, shapes, scalars=0):
    vmem = pl.BlockSpec(memory_space=pltpu.VMEM)
    moved = sum(value.size for value in inputs) * 6
    return pl.pallas_call(
        kernel,
        in_specs=[pl.BlockSpec(memory_space=pltpu.SMEM)] * scalars + [vmem] * (len(inputs) - scalars),
        out_specs=[vmem] * len(shapes),
        out_shape=[struct(shape, full) for shape in shapes],
        compiler_params=pltpu.CompilerParams(vmem_limit_bytes=40 << 20),
        cost_estimate=pl.CostEstimate(flops=2 * moved, transcendentals=0, bytes_accessed=moved),
    )(*inputs)


def struct(shape, dtype):
    return jax.ShapeDtypeStruct(shape, dtype)


def rows_spec(rows, width, at=0):
    return pl.BlockSpec((rows, width), lambda i, *_: (i, at))


def whole(shape, index=None):
    index = index or (0,) * len(shape)
    return pl.BlockSpec(shape, lambda i, *_: index)


def call(kernel, grid, in_specs, out_specs, out_shape, scratch, flops, moved, limit, prefetch=0):
    return pl.pallas_call(
        kernel,
        grid_spec=pltpu.PrefetchScalarGridSpec(
            num_scalar_prefetch=prefetch, grid=grid, in_specs=in_specs, out_specs=out_specs, scratch_shapes=scratch),
        out_shape=out_shape,
        compiler_params=pltpu.CompilerParams(dimension_semantics=("arbitrary",), vmem_limit_bytes=limit << 20),
        cost_estimate=pl.CostEstimate(flops=int(flops), transcendentals=0, bytes_accessed=int(moved)),
    )


def once(shape, index=None):
    index = index or (0,) * len(shape)
    return pl.BlockSpec(shape, lambda i, *_: index, pipeline_mode=pl.Buffered(1))


class Tokens:
    def __init__(self, tokens, width, count, place):
        self.tokens, self.width, self.count, self.place = tokens, width, count, place
        self.length = length = tokens // count
        self.half = half = width // 2
        self.padded = length + 2 * EDGE
        self.wide, self.slim, self.lane = rows_spec(length, width), rows_spec(length, half), rows_spec(length, LANES)
        self.all_cols = rows_spec(length, 4 * half)
        self.heads = pl.BlockSpec((1, HEADS, length, length), lambda i, *_: (i, 0, 0, 0))
        self.any = pl.BlockSpec(memory_space=pl.ANY)
        self.low_wide, self.low_slim = struct((tokens, width), low), struct((tokens, half), low)
        self.low_half = struct((half, width), low)

    def order(self, hidden, grad_out, depth):
        return call(
            order_kernel, (self.count,),
            [self.wide, self.wide, once(depth.shape)],
            [self.wide] * 3, [self.low_wide] * 3,
            [pltpu.VMEM((self.padded, self.width), full)], 4e9, 8e6, 60,
        )(hidden, grad_out, depth)

    def project(self, hidden, e, wa, wb, span, hid):
        tokens, width, half = self.tokens, self.width, self.half
        V = pltpu.VMEM
        devices = 2 * hid // self.hid_dev
        blocks = [value.reshape(devices // 2, -1, value.shape[1]) for value in wa]
        bias = pl.BlockSpec((devices // 2, blocks[0].shape[1], LANES), lambda i, *_: (0, 0, 4 * half // LANES),
                            pipeline_mode=pl.Buffered(1))
        return call(
            project_kernel, (self.count,),
            [self.wide, self.wide] + [self.any] * 4 + [bias, bias, once(span.shape)],
            [self.all_cols, self.slim, whole((2, hid)), whole((LANES, half))],
            [struct((tokens, 4 * half), low), self.low_slim, struct((2, hid), full), struct((LANES, half), low)],
            [V((width, 4 * half), low), V((width, half), low), pltpu.SemaphoreType.DMA((2, 2))],
            8e9, 10e6, 24, prefetch=1,
        )(self.place, hidden, e, *wa, *wb, *blocks, span)

    def mix(self, lens, qwkv, u, spant, wb):
        tokens, length, width, half = self.tokens, self.length, self.width, self.half
        V = pltpu.VMEM
        return call(
            mix_kernel, (self.count,),
            [self.all_cols, self.slim, once((LANES, half)), self.any, self.any],
            [self.lane, self.slim, self.heads, self.slim, self.wide],
            [pltpu.HBM(shape, dtype) for shape, dtype in (
                ((tokens, LANES), full), ((tokens, half), low), ((self.count, HEADS, length, length), low),
                ((tokens, half), low), ((tokens, width), low))],
            [V((self.padded, half), full), V((length, KERNEL * half), full), V((width, width), low),
             V((LANES, KERNEL * half), low), pltpu.SemaphoreType.DMA((2,))],
            20e9, 18e6, 44, prefetch=2,
        )(lens, self.place, qwkv, u, spant, *wb)

    def feed(self, y, hidden, grad_out, norm, ups, downs, bias, ctx, conv, wb):
        tokens, width, half = self.tokens, self.width, self.half
        hid = bias.shape[1]
        V = pltpu.VMEM
        vmem = pl.BlockSpec(memory_space=V)
        wide = V((tokens, width), low)
        ups = [value.reshape(value.shape[1:3] + value.shape[4:]) for value in ups]
        downs = [value.reshape((value.shape[1],) + value.shape[3:]) for value in downs]
        deep, tall, hid_dev = ups[0].shape[:3]
        across = downs[0].shape[1]
        devices = deep * tall * across
        weights = V((2, deep, tall, across, hid_dev, half), low)
        block = (devices, 2 * (hid + half) // devices, half)
        copies = len(ups) + len(downs) + 4 + 3 * self.count
        return pl.pallas_call(
            functools.partial(feed_kernel, self.count, len(ups) // 2, len(downs) // 2),
            in_specs=[pl.BlockSpec(memory_space=pltpu.SMEM), vmem, vmem] + [self.any] * (7 + len(ups) + len(downs)),
            out_specs=[vmem] + [self.any] * 5,
            out_shape=[struct((16, half), low)] + [self.low_wide] * 3 + [struct(block, low)] * 2,
            scratch_shapes=[V((16, half), full), wide, wide, wide, wide, weights, weights, V((width, width), low),
                            V((tokens, 2 * hid), low), V((tokens, 2 * hid), low), wide, wide, wide,
                            V((width, tokens), low), V((width, tokens), low), V((2,) + block, low), V((width, width), low),
                            pltpu.SemaphoreType.DMA((copies,)), pltpu.SemaphoreType.DMA((2 + 3 * self.count,))],
            compiler_params=pltpu.CompilerParams(vmem_limit_bytes=63 << 20),
            cost_estimate=pl.CostEstimate(flops=int(30e9), transcendentals=0, bytes_accessed=int(25e6)),
        )(self.place, norm, bias, y, hidden, grad_out, ctx, conv, *wb, *ups, *downs)

    def mixer_back(self, qwkv, a, gm, u, p, wb, spant):
        length, width, half = self.length, self.width, self.half
        V = pltpu.VMEM
        return call(
            mixer_back_kernel, (self.count,),
            [self.all_cols, self.heads, self.wide, self.slim, self.lane, self.any, self.any, once((LANES, half))],
            [self.wide, self.wide, self.slim, self.wide, whole((LANES, half))],
            [self.low_wide, self.low_wide, self.low_slim, self.low_wide, struct((LANES, half), full)],
            [V((length, half), full), V((self.padded, half), full), V((self.padded, half), full), V((self.padded, KERNEL * half), full),
             V((length, KERNEL * half), low), V((width, half), low), V((LANES, KERNEL * half), low), pltpu.SemaphoreType.DMA((2,))],
            30e9, 22e6, 44, prefetch=1,
        )(self.place, *(pltpu.with_memory_space_constraint(value, V) for value in (qwkv, a, gm)), u, p, *wb, spant)

    def weights(self, hidden, e, gqw, gkv, gu, ge, d_span, devices):
        width, half = self.width, self.half
        shapes = [(devices, parts * half // devices, half) for parts in (3, 3, 2, 2)]
        V = pltpu.VMEM
        return call(
            weight_kernel, (self.count,),
            [self.wide, self.wide, self.wide, self.wide, self.slim, self.wide, whole((LANES, half))],
            [whole(shape) for shape in shapes] + [whole((SMALL_ROWS, half))],
            [struct(shape, low) for shape in shapes] + [struct((SMALL_ROWS, half), low)],
            [V((self.padded, width), full), V((width, 3 * half), full), V((width, width), full), V((16, width), full), V((SMALL_ROWS, half), full)],
            12e9, 16e6, 40, prefetch=1,
        )(self.place, hidden, e, gqw, gkv, gu, ge, d_span)

    def input_grad(self, gb, gqw, gkv, ge, wa, depth):
        length, width = self.length, self.width
        V = pltpu.VMEM
        return call(
            input_kernel, (self.count,),
            [self.wide, self.wide, self.wide, self.wide, self.any, self.any, once(depth.shape)],
            [self.wide], [self.low_wide],
            [V((self.padded, width), full), V((length, width), full), V((width, 2 * width), low), pltpu.SemaphoreType.DMA((2,))],
            10e9, 14e6, 36, prefetch=1,
        )(self.place, gb, gqw, gkv, ge, *wa, depth)[0]


class Links:
    def __init__(self, mesh):
        self.size = mesh.shape["dp"]
        self.grp = mesh.shape["grp"]
        deep = 4 if self.size % 4 == 0 else 1
        rest = self.size // deep
        wide = 1 << ((rest.bit_length() - 1) // 2)
        self.shape = (1, deep, rest // wide, wide)
        self.axes = {"z": (deep, rest, 1), "y": (rest // wide, wide, 2), "x": (wide, 1, 3),
                     "zl": (2, rest, 1), "zh": (deep // 2, 2 * rest, 1)}

    def place(self, name):
        if name == "grp":
            return lax.axis_index("grp")
        size, stride, _ = self.axes[name]
        return (lax.axis_index("dp") // stride) % size

    def swap(self, value, name, shift):
        if name == "grp":
            return lax.ppermute(value, "grp", [(i, i ^ shift) for i in range(self.grp)])
        size, stride, _ = self.axes[name]
        pairs = []
        for i in range(self.size):
            at = (i // stride) % size
            pairs.append((i, i + ((at ^ shift) - at) * stride))
        return lax.ppermute(value, "dp", pairs)

    def fetch(self, block, name):
        return [block] + [self.swap(block, name, k) for k in range(1, self.axes[name][0])]

    def merge(self, got, name):
        size, _, dim = self.axes[name]
        here = self.place(name)
        slots = []
        for j in range(size):
            value = got[size - 1]
            for k in range(size - 1):
                value = jnp.where(here == (j ^ k), got[k], value)
            slots.append(value)
        return jnp.concatenate(slots, axis=dim)

    def gather(self, block, name):
        return self.merge(self.fetch(block, name), name)

    def slices(self, block, name):
        size, _, dim = self.axes[name]
        here = self.place(name)
        if name == "zl":
            halves = block.reshape((1, block.shape[1] // 2, 2) + block.shape[2:])
            return [jnp.squeeze(lax.dynamic_slice_in_dim(halves, here ^ k, 1, 2), 2) for k in range(size)]
        return [lax.dynamic_slice_in_dim(block, here ^ k, 1, dim) for k in range(size)]

    def join(self, keep, piece):
        return keep.astype(full) + self.swap(piece, "grp", 1).astype(full)

    def send(self, a, b, small, name_a, name_b):
        cols = b.shape[-1]
        parts_a, parts_b = self.slices(a, name_a), self.slices(b, name_b)
        own = [parts_a[0], parts_b[0], small]
        apart = [] if name_a == name_b else [self.swap(part, name_a, k + 1) for k, part in enumerate(parts_a[1:])]
        messages = []
        for k in range(1, len(parts_b)):
            pieces = [parts_b[k].reshape(-1, cols), small]
            if name_a == name_b:
                pieces = [parts_a[k].reshape(-1, cols)] + pieces
            messages.append(self.swap(jnp.concatenate(pieces, axis=0), name_b, k))
        return own, apart, messages

    def finish(self, sent, end=low):
        (own_a, own_b, own_small), apart, messages = sent
        cols = own_b.shape[-1]
        sums_a, sums_b, sums = [own_a] + apart, [own_b], [own_small]
        for message in messages:
            for value, kept in ((own_a, sums_a), (own_b, sums_b), (own_small, sums)):
                if value is own_a and apart:
                    continue
                size = value.size // cols
                kept.append(message[:size].reshape(value.shape))
                message = message[size:]

        def add(got):
            got = [value.astype(full) for value in got]
            while len(got) > 1:
                got = [got[i] + got[i + 1] for i in range(0, len(got), 2)]
            return got[0].astype(end)

        return add(sums_a), add(sums_b), add(sums)


def on_device(links, hidden, grad_out, seq_lens, mix_state, out_state, depth_state, span_state, norm_state,
              up_state, bias_state, down_state):
    barrier = lax.optimization_barrier
    width = hidden.shape[1]
    half = width // 2
    hid_dev = up_state.shape[3]
    rows_dev = mix_state.shape[2]
    up_state = jnp.swapaxes(up_state, 2, 3)
    depth_state = jnp.swapaxes(depth_state, 0, 1)
    span_state = jnp.transpose(span_state, (2, 0, 1))
    place = jnp.stack([links.place("grp"), lax.axis_index("dp"), links.place("y"), links.place("x")]).astype(jnp.int32)
    tokens = Tokens(hidden.shape[0], width, seq_lens.shape[0], place)
    tokens.hid_dev = hid_dev

    mix_low = mix_state[0].astype(low)
    bias_row = jnp.pad(bias_state[0].astype(low), ((0, rows_dev - 1), (0, LANES - hid_dev)))
    shard = jnp.concatenate(
        [mix_low[0], mix_low[4], mix_low[1], mix_low[2], bias_row, out_state[0].astype(low), mix_low[3]], axis=1)
    feed_shard = jnp.concatenate([up_state[0, 0], down_state[0, 0]], axis=1).astype(low)

    def block(value):
        return value.reshape((1, 1, 1, 1) + value.shape)

    def both_cores(value):
        value = value.reshape(-1, value.shape[-1])
        return value, links.swap(value, "grp", 1)

    mixer = links.fetch(block(shard), "z")
    mixer, hidden_o, grad_o, e = barrier((mixer, *tokens.order(hidden, grad_out, depth_state)))
    mixer = links.merge(mixer, "z")
    split = 4 * half + LANES
    wa, wb = mixer[..., :split], mixer[..., split:]
    wa, wb = links.gather(wa, "y"), links.gather(wb, "x")
    wa, wb, feed_shard = barrier((wa, wb, feed_shard))
    wa, wb, feed = barrier((links.fetch(wa, "x"), links.fetch(wb, "y"), links.fetch(block(feed_shard), "z")))
    wa, wb = both_cores(links.merge(wa, "x")), both_cores(links.merge(wb, "y"))
    feed = links.merge(feed, "z")
    up, down = links.fetch(feed[..., :half], "y"), links.fetch(feed[..., half:], "x")

    qwkv, u, bias, spant = tokens.project(hidden_o, e, wa, wb, span_state, hid_dev * links.size)
    up, down, qwkv, u = barrier((up, down, qwkv, u))
    up, down = links.merge(up, "y"), links.merge(down, "x")
    ups, downs = links.fetch(up, "x"), links.fetch(down, "y")
    others = [links.swap(up, "grp", 1)], [links.swap(down, "grp", 1)]
    p, conv, a, ctx, y = tokens.mix(seq_lens, qwkv, u, spant, wb)
    ups, downs, others, y = barrier((ups, downs, others, y))
    ups = ups + others[0] + [links.swap(value, "grp", 1) for value in ups[1:]]
    downs = downs + others[1] + [links.swap(value, "grp", 1) for value in downs[1:]]
    small, result, gb, gm, keep, piece = tokens.feed(
        y, hidden_o, grad_o, norm_state, ups, downs, bias, ctx, conv, wb)

    def blocks(value):
        return value.reshape(links.shape + (-1, value.shape[-1]))

    joined = join(links.shape[1:], place, keep, links.swap(piece, "grp", 1), small, links.swap(small, "grp", 1))
    (parts_a, own_b, messages, small), gm = barrier((joined, gm))
    sent = ([parts_a[0], own_b, small], [links.swap(part, "x", k + 1) for k, part in enumerate(parts_a[1:])],
            [links.swap(message, "y", k + 1) for k, message in enumerate(messages)])
    gqw, gkv, gu, ge, d_span = tokens.mixer_back(qwkv, a, gm, u, p, wb, spant)
    sent, gqw, gkv, gu, ge, d_span = barrier((sent, gqw, gkv, gu, ge, d_span))
    sent = links.send(*links.finish(sent), "y", "x")
    keep_a, piece_a, keep_b, piece_b, small = tokens.weights(hidden_o, e, gqw, gkv, gu, ge, d_span, links.size)
    sent, keep_a, piece_a, keep_b, piece_b, small = barrier((sent, keep_a, piece_a, keep_b, piece_b, small))

    feed_sent = links.send(*links.finish(sent), "z", "z")
    sums = (blocks(links.join(keep_a, piece_a).astype(low)), blocks(links.join(keep_b, piece_b).astype(low)),
            links.join(small, small).astype(low))
    sums, gqw, ge = barrier((sums, gqw, ge))
    sent = links.send(*sums, "x", "y")
    gx = tokens.input_grad(gb, gqw, gkv, ge, wa, depth_state)
    sent, gx = barrier((sent, gx))
    feed_sent, sums = barrier((feed_sent, links.finish(links.send(*links.finish(sent), "y", "x"))))
    feed_sums = links.finish(feed_sent, full)
    grad_a, grad_b, small = links.finish(links.send(*sums, "z", "z"), full)

    def twice(state, at=0):
        shape = state.shape[:at] + (2,) + state.shape[at + 1 :]
        return [shape, shape]

    def flat(value):
        return value.reshape(-1, value.shape[-1])

    feed_a, feed_b, feed_small = feed_sums
    feed_out = adam_call(
        adam_feed_kernel,
        [place, out_state, norm_state, up_state, bias_state, down_state, flat(feed_a), flat(feed_b), feed_small],
        twice(out_state) + twice(norm_state) + twice(up_state) + twice(bias_state) + twice(down_state), scalars=1)
    mixed = adam_call(
        adam_mix_kernel,
        [mix_state, depth_state, span_state, flat(grad_a), flat(grad_b), small],
        twice(mix_state) + twice(depth_state, 1) + twice(span_state, 1))
    depth_out = [jnp.swapaxes(value, 0, 1) for value in mixed[2:4]]
    span_out = [jnp.transpose(value, (1, 2, 0)) for value in mixed[4:]]
    up_out = [jnp.swapaxes(value, 2, 3) for value in feed_out[4:6]]
    return (result, gx, *mixed[:2], *feed_out[:2], *depth_out, *span_out, *feed_out[2:4], *up_out, *feed_out[6:])


def solution(mesh):
    both = ("grp", "dp")
    mix, out = P(None, None, both, None), P(None, both, None)
    up, bias, down = P(None, "grp", None, "dp"), P(None, "grp", "dp"), P(None, "grp", "dp", None)
    rows = P(both, None)
    return jax.shard_map(
        functools.partial(on_device, Links(mesh)),
        mesh=mesh,
        in_specs=(rows, rows, P(both), mix, out, P(), P(), P(), up, bias, down),
        out_specs=(rows, rows, mix, mix, out, out, P(), P(), P(), P(), P(), P(), up, up, bias, bias, down, down),
        check_vma=False,
    )
```
